32 devices in a mesh: dp: 8 (over y, x, core), tensor: 4 (over z).
Axes of the slice: x: 2, y: 2, z: 4, core: 2. Of those that a mesh axis runs over, the one named last changes fastest.
Arguments:
- tokens: bfloat16 [32768, 768], P(('dp', 'tensor')), may hold values from -6 to 6
- norm1_gain: float32 [768], replicated, may hold values from 0.5 to 1.5
- qkv_weight: bfloat16 [768, 3, 768], P('dp', None, 'tensor'), may hold values from -0.21875 to 0.21875
- attn_proj: bfloat16 [768, 768], P('tensor', 'dp'), may hold values from -3 to 3
- norm2_gain: float32 [768], replicated, may hold values from 0.5 to 1.5
- router_proj: float32 [768, 16], replicated, may hold values from -0.21875 to 0.21875
- expert_embed: float32 [4, 16], replicated, may hold values from -6 to 6
- expert_in: bfloat16 [768, 12288], P(None, 'dp'), may hold values from -0.21875 to 0.21875
- expert_out: bfloat16 [12288, 768], P('dp'), may hold values from -0.4375 to 0.4375
- routes: int32 [32768, 1], P(('dp', 'tensor')), may hold values from 0 to 3
- orders: int32 [32, 1024], P(('dp', 'tensor')), may hold values from 0 to 1023, each once within a row
- leaf_parent: int32 [8, 8], P('dp'), may hold values from 1 to 4, as said below
- cotangent: bfloat16 [32768, 768], P(('dp', 'tensor')), may hold values from -6 to 6
Outputs:
- output: bfloat16 [32768, 768], P(('dp', 'tensor'))
- grad_tokens: float32 [32768, 768], P(('dp', 'tensor'))
- grad_norm1: float32 [768], replicated
- grad_qkv: float32 [768, 3, 768], P('dp', None, 'tensor')
- grad_attn_proj: float32 [768, 768], P('tensor', 'dp')
- grad_norm2: float32 [768], replicated
- grad_router: float32 [768, 16], replicated
- grad_embed: float32 [4, 16], replicated
- grad_expert_in: float32 [768, 12288], P(None, ('dp', 'tensor'))
- grad_expert_out: float32 [12288, 768], P(('dp', 'tensor'))
The draws below stay inside these ranges and needn't reach their ends.
Inputs may be any that keep to these rules, and one draw needn't show every extreme that they name: `leaf_parent`: in each tree, each branch segment 1 to 4 is the parent of exactly two of the 8 leaves.
All inputs are finite; a program needn't handle non-finite values.
Results may differ from the reference program's by a relative error of at most 0.014.
Values may be sent and summed in bfloat16 or wider, within the bound.
A program may use at most 256 MiB of HBM per device.

```python
import jax
import jax.numpy as jnp
from jax import lax

D = 768
HEADS = 12
HEAD_DIM = 64
FF = 3072
ROUTE = 16
TRUNK = 1024
BRANCH = 256
BRANCHES = 4
QBLOCK = 512
LEAVES = 8
TREE = 4096
TREES = 8
TOK_DEV = 1024
TOKENS = 32768
GROUPS = 32
EXPERTS = 4
CAP = 256
N_DP = 8
N_TENSOR = 4


def draw_leaf_parent(key, part):
    tree_keys = jax.random.split(jax.random.fold_in(key, 11), TREES)

    def one_tree(tree_key):
        return (jax.random.permutation(tree_key, LEAVES) // 2 + 1).astype(jnp.int32)
    return jax.vmap(one_tree)(tree_keys)


def block_scale(key, dims, shards, low, largest):
    def one(axis_at, shards_of):
        draws = jax.random.uniform(jax.random.fold_in(jax.random.fold_in(key, 6), axis_at), (shards_of,), jnp.float32, low / len(shards), largest / len(shards))
        return jnp.repeat(jnp.exp(draws), dims[axis_at] // shards_of).reshape((-1,) + (1,) * (len(dims) - axis_at - 1))

    loudness = one(*shards[0])
    for cut in shards[1:]:
        loudness = loudness * one(*cut)
    return loudness


def distinct(key, rows, count, top, lift):
    order = jax.random.permutation(jax.random.fold_in(key, 1), count)
    boost = order
    for power in range(3):
        boost = boost * boost // count
    boost = boost * lift // count
    tickets = jax.random.randint(jax.random.fold_in(key, 2), (rows, count), 0, 4096) + boost
    holders = jax.random.permutation(jax.random.fold_in(key, 3), rows)[jnp.arange(count) % rows]
    tickets = jnp.where(jnp.arange(rows)[:, None] == holders[None, :], 1 << 14, tickets)
    priority = tickets * count + jnp.arange(count)
    return lax.top_k(priority.astype(jnp.int32), top)[1].astype(jnp.int32)


def noise(own_key, shape, width, reach, cuts=(), held_as=jnp.bfloat16):
    result = width * jax.random.normal(own_key, shape, jnp.float32)
    if cuts:
        result = result * block_scale(own_key, shape, cuts, -0.22, 0.18)
    return jnp.clip(result, -reach, reach).astype(held_as)


def setup_inputs(seed: int = 0) -> dict:
    arg_keys = jax.random.split(jax.random.key(seed), 14)
    return {
        "tokens": noise(arg_keys[0], (TOKENS, D), 1.0, 6.0, ((0, 32),)),
        "norm1_gain": jnp.clip(1.0 + 0.1 * jax.random.normal(arg_keys[1], (D,), jnp.float32), 0.5, 1.5),
        "qkv_weight": noise(arg_keys[2], (D, 3, D), D ** -0.5, 0.21875, ((0, 8), (2, 4))),
        "attn_proj": noise(arg_keys[3], (D, D), 4 ** -0.5, 3.0, ((0, 4), (1, 8))),
        "norm2_gain": jnp.clip(1.0 + 0.1 * jax.random.normal(arg_keys[4], (D,), jnp.float32), 0.5, 1.5),
        "router_proj": noise(arg_keys[5], (D, ROUTE), D ** -0.5, 0.21875, (), jnp.float32),
        "expert_embed": noise(arg_keys[6], (EXPERTS, ROUTE), 1.0, 6.0, (), jnp.float32),
        "expert_in": noise(arg_keys[7], (D, EXPERTS * FF), D ** -0.5, 0.21875, ((1, 8),)),
        "expert_out": noise(arg_keys[8], (EXPERTS * FF, D), (max(1, FF // (EXPERTS * EXPERTS))) ** -0.5, 0.4375, ((0, 8),)),
        "routes": distinct(arg_keys[9], TOKENS, EXPERTS, 1, 2048),
        "orders": jax.vmap(lambda own: jax.random.permutation(own, TOK_DEV))(jax.random.split(arg_keys[10], GROUPS)).reshape((GROUPS, TOK_DEV)).astype(jnp.int32),
        "leaf_parent": draw_leaf_parent(jax.random.fold_in(arg_keys[13], 71), 0),
        "cotangent": noise(arg_keys[12], (TOKENS, D), 1.0, 6.0, ((0, 32),)),
    }


norm_eps = 1e-05
route_scale = 3.0
masked_score = -1e+30
highest = lax.Precision.HIGHEST

@jax.custom_vjp
def low(v):
    return lax.optimization_barrier(v.astype(jnp.bfloat16)).astype(jnp.float32)

@jax.custom_vjp
def low_back(v):
    return v

def low_keep(v):
    return (low(v), None)

def low_pass(kept, grad):
    return (grad,)

def back_keep(v):
    return (v, None)

def back_low(kept, grad):
    return (low(grad),)
low.defvjp(low_keep, low_pass)
low_back.defvjp(back_keep, back_low)

def layer_norm(values, norm_gain):
    centred = values - lax.optimization_barrier(jnp.mean(values, axis=-1, keepdims=True))
    spread = lax.optimization_barrier(jnp.mean(centred * centred, axis=-1, keepdims=True))
    return centred * lax.rsqrt(spread + norm_eps) * norm_gain

def unit_rows(values):
    return values * lax.rsqrt(lax.optimization_barrier(jnp.sum(values * values, axis=-1, keepdims=True)) + 1.0)

def router_gate(normed, router_proj, expert_embed, picked):
    routed = jnp.dot(normed, router_proj, precision=highest)
    logits = route_scale * jnp.dot(unit_rows(routed), unit_rows(expert_embed).T, precision=highest)
    return lax.optimization_barrier(jnp.sum(jax.nn.softmax(logits, axis=-1) * picked, axis=-1))

def gelu_exact(values):
    return jax.nn.gelu(values, approximate=False)

def segment_of(positions):
    past_trunk = positions - TRUNK
    past_branches = past_trunk - BRANCHES * BRANCH
    inner = jnp.where(past_branches < 0, 1 + past_trunk // BRANCH, 1 + BRANCHES + past_branches // BRANCH)
    return jnp.where(positions < TRUNK, 0, inner).astype(jnp.int32)

def parent_of(segments, leaf_parents):
    leaf_index = segments - 1 - BRANCHES
    matches = leaf_index[:, None] == jnp.arange(LEAVES)[None, :]
    return lax.optimization_barrier(jnp.sum(jnp.where(matches, leaf_parents[None, :], 0), axis=1)).astype(jnp.int32)

def visible(query_pos, key_pos, leaf_parents):
    query_seg = segment_of(query_pos)
    query_parent = parent_of(query_seg, leaf_parents)
    key_seg = segment_of(key_pos)[None, :]
    related = (key_seg == 0) | (key_seg == query_seg[:, None]) | (key_seg == query_parent[:, None])
    return related & (key_pos[None, :] <= query_pos[:, None])

def slot_table(route_ids, order_ids, experts, capacity):
    same_expert = route_ids[:, None] == route_ids[None, :]
    earlier = order_ids[None, :] < order_ids[:, None]
    ranking = lax.optimization_barrier(jnp.sum(jnp.where(same_expert & earlier, 1, 0), axis=1)).astype(jnp.int32)
    kept_mask = ranking < capacity
    column = (route_ids * capacity + jnp.minimum(ranking, capacity - 1)).astype(jnp.int32)
    return (column, kept_mask)

def attend_block(block_id, queries, key_rows, value_rows, leaf_parents):
    first_row = block_id * QBLOCK
    block_queries = lax.dynamic_slice_in_dim(queries, first_row, QBLOCK, 0)
    allowed = visible(first_row + jnp.arange(QBLOCK), jnp.arange(TREE), leaf_parents)
    scores = low_back(jnp.einsum('qhc,khc->hqk', block_queries, key_rows, precision=highest) * HEAD_DIM ** (-0.5))
    scores = jnp.where(allowed[None], scores, masked_score)
    attn_probs = jax.nn.softmax(scores, axis=-1)
    return jnp.einsum('hqk,khc->qhc', low(attn_probs), value_rows, precision=highest)

def tree_layer(hidden, norm1_gain, qkv_weight, attn_proj, norm2_gain, router_proj, expert_embed, expert_in, expert_out, route_ids, order_ids, leaf_parents):
    tree_in = low(layer_norm(hidden, norm1_gain))
    projected = low(low_back(jnp.einsum('sd,dkc->skc', tree_in, qkv_weight, precision=highest)))
    queries = projected[:, 0].reshape(TREE, HEADS, HEAD_DIM)
    key_rows = projected[:, 1].reshape(TREE, HEADS, HEAD_DIM)
    value_rows = projected[:, 2].reshape(TREE, HEADS, HEAD_DIM)
    checked = jax.checkpoint(attend_block)
    attended = lax.map(lambda block_id: checked(block_id, queries, key_rows, value_rows, leaf_parents), jnp.arange(TREE // QBLOCK))
    attended = low(low_back(attended.reshape(TREE, D)))
    mid_stream = hidden + low_back(jnp.dot(attended, attn_proj, precision=highest))
    moe_in = low(layer_norm(mid_stream, norm2_gain))
    picked = (route_ids.reshape(TREE)[:, None] == jnp.arange(EXPERTS)[None, :]).astype(jnp.float32)
    gate_value = router_gate(moe_in, router_proj, expert_embed, picked)
    column, kept_mask = jax.vmap(lambda group_routes, group_orders: slot_table(group_routes, group_orders, EXPERTS, CAP))(route_ids, order_ids)
    select = ((column[..., None] == jnp.arange(EXPERTS * CAP)[None, None, :]) & kept_mask[..., None]).astype(jnp.float32)
    grouped = moe_in.reshape(N_TENSOR, TOK_DEV, D)
    slot_rows = jnp.einsum('gts,gtd->gsd', select, grouped, precision=highest)
    slot_rows = slot_rows.reshape(N_TENSOR, EXPERTS, CAP, D).transpose(1, 0, 2, 3).reshape(EXPERTS, N_TENSOR * CAP, D)
    up_values = low_back(jnp.einsum('end,def->enf', slot_rows, expert_in.reshape(D, EXPERTS, FF), precision=highest))
    active = low(gelu_exact(up_values))
    expert_rows = low_back(jnp.einsum('enf,efd->end', active, expert_out.reshape(EXPERTS, FF, D), precision=highest))
    expert_rows = expert_rows.reshape(EXPERTS, N_TENSOR, CAP, D).transpose(1, 0, 2, 3).reshape(N_TENSOR, EXPERTS * CAP, D)
    gathered = jax.vmap(lambda slot_group, column_group, kept_group: jnp.take(slot_group, column_group, axis=0) * kept_group[:, None].astype(jnp.float32))(expert_rows, column, kept_mask)
    return mid_stream + gate_value[:, None] * gathered.reshape(TREE, D)

def reference(tokens, norm1_gain, qkv_weight, attn_proj, norm2_gain, router_proj, expert_embed, expert_in, expert_out, routes, orders, leaf_parent, cotangent):
    weights = tuple((weight_arg.astype(jnp.float32) for weight_arg in (norm1_gain, qkv_weight, attn_proj, norm2_gain, router_proj, expert_embed, expert_in, expert_out)))
    token_trees = tokens.astype(jnp.float32).reshape(N_DP, TREE, D)
    grad_trees = cotangent.astype(jnp.float32).reshape(N_DP, TREE, D)
    route_trees = routes.reshape(N_DP, N_TENSOR, TOK_DEV)
    order_trees = orders.reshape(N_DP, N_TENSOR, TOK_DEV)

    def per_tree(running_sums, tree_inputs):
        hidden, upstream, route_ids, order_ids, leaf_parents = tree_inputs

        def layer_of(hidden_in, *params):
            return tree_layer(hidden_in, *params, route_ids, order_ids, leaf_parents)
        output, pullback = jax.vjp(layer_of, hidden, *weights)
        gradients = pullback(upstream)
        updated = tuple((running + gradient for running, gradient in zip(running_sums, gradients[1:])))
        return (updated, (output.astype(jnp.bfloat16), gradients[0]))
    starting = tuple((jnp.zeros_like(weight_arg) for weight_arg in weights))
    totals, (outputs, token_grads) = lax.scan(per_tree, starting, (token_trees, grad_trees, route_trees, order_trees, leaf_parent))
    return (outputs.reshape(TOKENS, D), token_grads.reshape(TOKENS, D), totals[0], totals[1], totals[2], totals[3], totals[4], totals[5], totals[6], totals[7])
```

```python
import math

import jax
import jax.numpy as jnp
from jax import lax
from jax.experimental import pallas as pl
from jax.experimental.pallas import tpu as pltpu
from jax.sharding import PartitionSpec as P

HEAD_DIM = 64
TRUNK = 1024
BRANCH = 256
MASKED = -1e30
LOG2E = math.log2(math.e)
EXP_SCALE = HEAD_DIM ** (-0.5) * LOG2E

NT = (((1,), (1,)), ((), ()))
NN = (((1,), (0,)), ((), ()))


def dot_nt(a, b):
    return lax.dot_general(a, b, NT, preferred_element_type=jnp.float32)


def dot_nn(a, b):
    return lax.dot_general(a, b, NN, preferred_element_type=jnp.float32)


def head_lanes(shape, dim, head):
    return lax.broadcasted_iota(jnp.int32, shape, dim) // HEAD_DIM == head


def fwd_kernel(meta_ref, q_ref, k_ref, v_ref, o_ref, lse_ref, vt_ref):
    block = pl.program_id(1)
    place = meta_ref[0]
    parent_row = pl.multiple_of(TRUNK + meta_ref[1 + block] * BRANCH, BRANCH)
    own_row = pl.multiple_of(2 * TRUNK + block * BRANCH, BRANCH)
    width = k_ref.shape[1]

    @pl.when(block == 0)
    def _():
        flipped = v_ref[...].T
        for head in range(2):
            vt_ref[head] = jnp.where(
                head_lanes(flipped.shape, 0, head), flipped, jnp.ones_like(flipped)
            )

    queries = q_ref[...]

    def finish(outs):
        rows = []
        for head, (acc, top) in enumerate(outs):
            mine, other = head * HEAD_DIM, (1 - head) * HEAD_DIM
            total = acc[other : other + 1]
            rows.append(acc[mine : mine + HEAD_DIM] / total)
            lse_ref[0, head : head + 1, :] = top * EXP_SCALE + jnp.log2(total)
        o_ref[...] = jnp.concatenate(rows, axis=0).T.astype(o_ref.dtype)

    def probs(scores, top):
        return jnp.exp2(scores * EXP_SCALE - top * EXP_SCALE).astype(jnp.bfloat16)

    def masked_queries(head):
        return jnp.where(head_lanes(queries.shape, 1, head), queries, jnp.zeros_like(queries))

    @pl.when(place == 0)
    def _():
        outs = []
        for head in range(2):
            scores = dot_nt(k_ref[0:TRUNK], masked_queries(head))
            keys = lax.broadcasted_iota(jnp.int32, scores.shape, 0)
            rows = lax.broadcasted_iota(jnp.int32, scores.shape, 1) + block * BRANCH
            scores = jnp.where(keys <= rows, scores, MASKED)
            top = jnp.max(scores, axis=0, keepdims=True)
            outs.append((dot_nn(vt_ref[head, :, 0:TRUNK], probs(scores, top)), top))
        finish(outs)

    @pl.when(place > 0)
    def _():
        outs = []
        for head in range(2):
            qm = masked_queries(head)
            trunk = dot_nt(k_ref[0:TRUNK], qm)
            parent = dot_nt(k_ref[pl.ds(parent_row, BRANCH)], qm)
            parent = jnp.where(place > 1, parent, MASKED)
            own = dot_nt(k_ref[pl.ds(own_row, BRANCH)], qm)
            keys = lax.broadcasted_iota(jnp.int32, own.shape, 0)
            rows = lax.broadcasted_iota(jnp.int32, own.shape, 1)
            own = jnp.where(keys <= rows, own, MASKED)
            top = jnp.maximum(
                jnp.maximum(
                    jnp.max(trunk, axis=0, keepdims=True), jnp.max(parent, axis=0, keepdims=True)
                ),
                jnp.max(own, axis=0, keepdims=True),
            )
            acc = dot_nn(vt_ref[head, :, 0:TRUNK], probs(trunk, top))
            acc = acc + dot_nn(vt_ref[head, :, pl.ds(parent_row, BRANCH)], probs(parent, top))
            acc = acc + dot_nn(vt_ref[head, :, pl.ds(own_row, BRANCH)], probs(own, top))
            outs.append((acc, top))
        finish(outs)


def attend(meta, q, k, v):
    rows, width = q.shape
    keys = k.shape[0]
    pairs = width // 128
    blocks = rows // BRANCH
    return pl.pallas_call(
        fwd_kernel,
        out_shape=(
            jax.ShapeDtypeStruct((rows, width), jnp.bfloat16),
            jax.ShapeDtypeStruct((pairs, 2, rows), jnp.float32),
        ),
        grid_spec=pltpu.PrefetchScalarGridSpec(
            num_scalar_prefetch=1,
            grid=(pairs, blocks),
            in_specs=[
                pl.BlockSpec((BRANCH, 128), lambda p, i, m: (i, p)),
                pl.BlockSpec((keys, 128), lambda p, i, m: (0, p)),
                pl.BlockSpec((keys, 128), lambda p, i, m: (0, p)),
            ],
            out_specs=[
                pl.BlockSpec((BRANCH, 128), lambda p, i, m: (i, p)),
                pl.BlockSpec((1, 2, BRANCH), lambda p, i, m: (p, 0, i)),
            ],
            scratch_shapes=[pltpu.VMEM((2, 128, keys), jnp.bfloat16)],
        ),
        compiler_params=pltpu.CompilerParams(vmem_limit_bytes=40 << 20),
        name="attend_forward",
    )(meta, q, k, v)


def bwd_kernel(meta_ref, q_ref, k_ref, v_ref, o_ref, g_ref, lse_ref,
               dq_ref, dk_ref, dv_ref, kt_ref, qm_ref, gm_ref, delta_ref, dqt_ref, dkp_ref, dvp_ref):
    place = meta_ref[0]
    scale = HEAD_DIM ** (-0.5)
    rows = q_ref.shape[0]
    blocks = rows // BRANCH
    kt_ref[...] = k_ref[...].T
    queries, grads = q_ref[...], g_ref[...]
    for head in range(2):
        lanes = head_lanes(queries.shape, 1, head)
        qm_ref[head] = jnp.where(lanes, queries, jnp.zeros_like(queries))
        gm_ref[head] = jnp.where(lanes, grads, jnp.zeros_like(grads))
    product = (grads.astype(jnp.float32) * o_ref[...].astype(jnp.float32)).T
    for head in range(2):
        delta_ref[head : head + 1, :] = jnp.sum(
            product[head * HEAD_DIM : (head + 1) * HEAD_DIM], axis=0, keepdims=True
        )
    dqt_ref[...] = jnp.zeros_like(dqt_ref)

    def step(key_row, query_row, count, mask_of=None):
        kb = k_ref[pl.ds(key_row, BRANCH)]
        vb = v_ref[pl.ds(key_row, BRANCH)]
        dk = dv = None
        for head in range(2):
            at = pl.ds(query_row, count)
            qm, gm = qm_ref[head, at], gm_ref[head, at]
            scores = dot_nt(kb, qm)
            probs = jnp.exp2(scores * EXP_SCALE - lse_ref[0, head : head + 1, at])
            if mask_of is not None:
                probs = mask_of(probs)
            prob_grad = dot_nt(vb, gm)
            score_grad = (probs * (prob_grad - delta_ref[head : head + 1, at])).astype(jnp.bfloat16)
            dv_part = dot_nn(probs.astype(jnp.bfloat16), gm)
            dk_part = dot_nn(score_grad, qm)
            dv = dv_part if dv is None else dv + dv_part
            dk = dk_part if dk is None else dk + dk_part
            mine = slice(head * HEAD_DIM, (head + 1) * HEAD_DIM)
            dqt_ref[mine, at] += dot_nn(kt_ref[mine, pl.ds(key_row, BRANCH)], score_grad)
        return dk * scale, dv

    def causal(offset):
        def mask_of(probs):
            keys = lax.broadcasted_iota(jnp.int32, probs.shape, 0) + offset
            at = lax.broadcasted_iota(jnp.int32, probs.shape, 1)
            return jnp.where(keys <= at, probs, 0.0)
        return mask_of

    @pl.when(place == 0)
    def _():
        @pl.loop(0, TRUNK // BRANCH)
        def _(b):
            row = pl.multiple_of(b * BRANCH, BRANCH)
            dk, dv = step(row, 0, rows, causal(row))
            dk_ref[pl.ds(row, BRANCH)] = dk.astype(dk_ref.dtype)
            dv_ref[pl.ds(row, BRANCH)] = dv.astype(dv_ref.dtype)
        rest = (dk_ref.shape[0] - TRUNK, dk_ref.shape[1])
        dk_ref[TRUNK:] = jnp.zeros(rest, dk_ref.dtype)
        dv_ref[TRUNK:] = jnp.zeros(rest, dv_ref.dtype)

    @pl.when(place > 0)
    def _():
        @pl.loop(0, TRUNK // BRANCH)
        def _(b):
            row = pl.multiple_of(b * BRANCH, BRANCH)
            dk, dv = step(row, 0, rows)
            dk_ref[pl.ds(row, BRANCH)] = dk.astype(dk_ref.dtype)
            dv_ref[pl.ds(row, BRANCH)] = dv.astype(dv_ref.dtype)

        dkp_ref[...] = jnp.zeros_like(dkp_ref)
        dvp_ref[...] = jnp.zeros_like(dvp_ref)

        @pl.loop(0, blocks)
        def _(b):
            at = pl.multiple_of(b * BRANCH, BRANCH)
            parent = pl.multiple_of(meta_ref[1 + b] * BRANCH, BRANCH)
            dk, dv = step(TRUNK + parent, at, BRANCH, lambda probs: jnp.where(place > 1, probs, 0.0))
            dkp_ref[pl.ds(parent, BRANCH)] += dk
            dvp_ref[pl.ds(parent, BRANCH)] += dv
            own = pl.multiple_of(2 * TRUNK + at, BRANCH)
            dk, dv = step(own, at, BRANCH, causal(0))
            dk_ref[pl.ds(own, BRANCH)] = dk.astype(dk_ref.dtype)
            dv_ref[pl.ds(own, BRANCH)] = dv.astype(dv_ref.dtype)

        dk_ref[TRUNK : 2 * TRUNK] = dkp_ref[...].astype(dk_ref.dtype)
        dv_ref[TRUNK : 2 * TRUNK] = dvp_ref[...].astype(dv_ref.dtype)

    dq_ref[...] = (dqt_ref[...] * scale).T.astype(dq_ref.dtype)


def attend_back(meta, q, k, v, o, grad, lse):
    rows, width = q.shape
    keys = k.shape[0]
    pairs = width // 128
    here = pl.BlockSpec((rows, 128), lambda p, m: (0, p))
    wide = pl.BlockSpec((keys, 128), lambda p, m: (0, p))
    return pl.pallas_call(
        bwd_kernel,
        out_shape=(
            jax.ShapeDtypeStruct((rows, width), jnp.bfloat16),
            jax.ShapeDtypeStruct((keys, width), jnp.bfloat16),
            jax.ShapeDtypeStruct((keys, width), jnp.bfloat16),
        ),
        grid_spec=pltpu.PrefetchScalarGridSpec(
            num_scalar_prefetch=1,
            grid=(pairs,),
            in_specs=[here, wide, wide, here, here, pl.BlockSpec((1, 2, rows), lambda p, m: (p, 0, 0))],
            out_specs=[here, wide, wide],
            scratch_shapes=[
                pltpu.VMEM((128, keys), jnp.bfloat16),
                pltpu.VMEM((2, rows, 128), jnp.bfloat16),
                pltpu.VMEM((2, rows, 128), jnp.bfloat16),
                pltpu.VMEM((2, rows), jnp.float32),
                pltpu.VMEM((128, rows), jnp.float32),
                pltpu.VMEM((TRUNK, 128), jnp.float32),
                pltpu.VMEM((TRUNK, 128), jnp.float32),
            ],
        ),
        compiler_params=pltpu.CompilerParams(vmem_limit_bytes=48 << 20),
        name="attend_backward",
    )(meta, q, k, v, o, grad, lse)


norm_eps = 1e-05
route_scale = 3.0
masked_score = -1e30
highest = lax.Precision.HIGHEST


def layer_norm(values, norm_gain):
    centred = values - jnp.mean(values, axis=-1, keepdims=True)
    spread = jnp.mean(centred * centred, axis=-1, keepdims=True)
    return centred * lax.rsqrt(spread + norm_eps) * norm_gain


def unit_rows(values):
    return values * lax.rsqrt(jnp.sum(values * values, axis=-1, keepdims=True) + 1.0)


def router_gate(normed, router_proj, expert_embed, picked):
    routed = jnp.dot(normed, router_proj, precision=highest)
    logits = route_scale * jnp.dot(unit_rows(routed), unit_rows(expert_embed).T, precision=highest)
    return jnp.sum(jax.nn.softmax(logits, axis=-1) * picked, axis=-1)


def gelu_exact(values):
    return jax.nn.gelu(values, approximate=False)


def slot_table(route_ids, order_ids, capacity):
    same_expert = route_ids[:, None] == route_ids[None, :]
    earlier = order_ids[None, :] < order_ids[:, None]
    ranking = jnp.sum(jnp.where(same_expert & earlier, 1, 0), axis=1).astype(jnp.int32)
    kept_mask = ranking < capacity
    column = route_ids * capacity + jnp.minimum(ranking, capacity - 1)
    return (column, kept_mask)


def low_dot(rows, weight):
    return jnp.dot(rows, weight, preferred_element_type=jnp.float32).astype(jnp.bfloat16)


def shards(
    tokens,
    norm1_gain,
    qkv_weight,
    attn_proj,
    norm2_gain,
    router_proj,
    expert_embed,
    expert_in,
    expert_out,
    routes,
    orders,
    leaf_parent,
    cotangent,
):
    rows_here = tokens.shape[0]
    model_width = tokens.shape[1]
    experts = expert_embed.shape[0]
    capacity = rows_here // experts
    dp_size = lax.axis_size("dp")
    leaf_parents = leaf_parent[0]

    def whole_tree(local_rows):
        return lax.all_gather(local_rows, "tensor", axis=0, tiled=True)

    def dispatch(slot_input):
        doubled = jnp.broadcast_to(
            slot_input.reshape(experts, 1, capacity, model_width),
            (experts, 2, capacity, model_width),
        )
        arrived = lax.all_to_all(
            doubled.reshape(dp_size, capacity, model_width),
            "dp",
            split_axis=0,
            concat_axis=0,
            tiled=True,
        )
        return arrived.reshape(dp_size * capacity, model_width)

    def combine(partial_rows):
        returned = lax.all_to_all(
            partial_rows.reshape(dp_size, capacity, model_width),
            "dp",
            split_axis=0,
            concat_axis=0,
            tiled=True,
        )
        summed = jnp.sum(returned.reshape(experts, 2, capacity, model_width), axis=1)
        return summed.reshape(experts * capacity, model_width)

    hidden = tokens.astype(jnp.float32)
    normed_in, norm1_back = jax.vjp(layer_norm, hidden, norm1_gain)
    own_in = normed_in.astype(jnp.bfloat16)
    shared_in = whole_tree(own_in)[: 2 * TRUNK]
    seen_in = jnp.concatenate([shared_in, own_in], axis=0)
    qkv_cols = lax.all_gather(qkv_weight, "tensor", axis=2, tiled=True)
    qkv_full = lax.all_gather(qkv_cols, "dp", axis=0, tiled=True)
    proj_rows = lax.all_gather(attn_proj, "tensor", axis=0, tiled=True)
    proj_full = lax.all_gather(proj_rows, "dp", axis=1, tiled=True)
    query_weight, key_weight, value_weight = (qkv_full[:, part] for part in range(3))
    query_rows = low_dot(own_in, query_weight)
    key_rows = low_dot(seen_in, key_weight)
    value_rows = low_dot(seen_in, value_weight)
    place = lax.axis_index("tensor")
    leaf_blocks = rows_here // BRANCH
    first_leaf = jnp.maximum(place - 2, 0) * leaf_blocks
    parents = lax.dynamic_slice_in_dim(leaf_parents, first_leaf, leaf_blocks, 0) - 1
    meta = jnp.concatenate([place[None], parents]).astype(jnp.int32)
    attended, log_totals = attend(meta, query_rows, key_rows, value_rows)
    branch_out = jnp.dot(attended, proj_full, preferred_element_type=jnp.float32)
    mid_stream = hidden + branch_out
    normed_mid, norm2_back = jax.vjp(layer_norm, mid_stream, norm2_gain)
    moe_in = normed_mid.astype(jnp.bfloat16)
    route_ids = routes[:, 0]
    column, kept_mask = slot_table(route_ids, orders[0], capacity)
    picked = (route_ids[:, None] == jnp.arange(experts)[None, :]).astype(jnp.float32)
    gate_value, gate_back = jax.vjp(
        lambda normed_rows, route_proj, embed_rows: router_gate(
            normed_rows, route_proj, embed_rows, picked
        ),
        moe_in.astype(jnp.float32),
        router_proj,
        expert_embed,
    )
    select = (
        (column[:, None] == jnp.arange(experts * capacity)[None, :]) & kept_mask[:, None]
    ).astype(jnp.bfloat16)
    kept_float = kept_mask[:, None].astype(jnp.float32)

    def to_slots(token_rows):
        return jnp.einsum(
            "ts,td->sd", select, token_rows, preferred_element_type=jnp.float32
        ).astype(jnp.bfloat16)

    def from_slots(slot_rows):
        return jnp.take(slot_rows, column, axis=0) * kept_float

    expert_rows = dispatch(to_slots(moe_in))
    up_values = jnp.dot(expert_rows, expert_in, preferred_element_type=jnp.float32)
    active_full, gelu_back = jax.vjp(gelu_exact, up_values)
    active = active_full.astype(jnp.bfloat16)
    expert_result = from_slots(
        combine(jnp.dot(active, expert_out, preferred_element_type=jnp.float32))
    )
    output = (mid_stream + gate_value[:, None] * expert_result).astype(jnp.bfloat16)
    upstream = cotangent.astype(jnp.float32)
    arrived_grad = dispatch(to_slots((gate_value[:, None] * upstream).astype(jnp.bfloat16)))
    out_weight_grad = jnp.einsum(
        "rf,rd->fd", active, arrived_grad, preferred_element_type=jnp.float32
    )
    active_grad = jnp.einsum(
        "rd,fd->rf", arrived_grad, expert_out, preferred_element_type=jnp.float32
    )
    up_grad = gelu_back(active_grad)[0].astype(jnp.bfloat16)
    in_weight_grad = jnp.einsum(
        "rd,rf->df", expert_rows, up_grad, preferred_element_type=jnp.float32
    )
    moe_grad = from_slots(
        combine(jnp.einsum("rf,df->rd", up_grad, expert_in, preferred_element_type=jnp.float32))
    )
    gate_grad = jnp.sum(upstream * expert_result, axis=-1)
    router_part, proj_grad, embed_grad = gate_back(gate_grad)
    mid_part, gain2_grad = norm2_back(moe_grad + router_part)
    mid_grad = upstream + mid_part
    expert_in_grad, expert_out_grad = (
        lax.psum_scatter(
            in_weight_grad.astype(jnp.bfloat16), "tensor", scatter_dimension=1, tiled=True
        ).astype(jnp.float32),
        lax.psum_scatter(
            out_weight_grad.astype(jnp.bfloat16), "tensor", scatter_dimension=0, tiled=True
        ).astype(jnp.float32),
    )
    branch_grad = mid_grad.astype(jnp.bfloat16)
    proj_grad_full = jnp.einsum(
        "sc,sd->cd", attended, branch_grad, preferred_element_type=jnp.float32
    )
    attn_proj_grad = lax.psum_scatter(
        lax.psum_scatter(proj_grad_full, "dp", scatter_dimension=1, tiled=True),
        "tensor",
        scatter_dimension=0,
        tiled=True,
    )
    attended_grad = jnp.einsum(
        "sd,cd->sc", branch_grad, proj_full, preferred_element_type=jnp.float32
    ).astype(jnp.bfloat16)
    query_grad, key_grad, value_grad = attend_back(
        meta, query_rows, key_rows, value_rows, attended, attended_grad, log_totals
    )

    def weight_grad(rows, row_grads):
        return jnp.einsum("sd,sc->dc", rows, row_grads, preferred_element_type=jnp.float32)

    def row_grad(row_grads, weight):
        return jnp.einsum("sc,dc->sd", row_grads, weight, preferred_element_type=jnp.float32)

    qkv_grad_full = jnp.stack(
        [
            weight_grad(own_in, query_grad),
            weight_grad(seen_in, key_grad),
            weight_grad(seen_in, value_grad),
        ],
        axis=1,
    )
    qkv_grad = lax.psum_scatter(
        lax.psum_scatter(qkv_grad_full, "dp", scatter_dimension=0, tiled=True),
        "tensor",
        scatter_dimension=2,
        tiled=True,
    )
    seen_grad = row_grad(key_grad, key_weight) + row_grad(value_grad, value_weight)
    own_grad = seen_grad[2 * TRUNK :] + row_grad(query_grad, query_weight)
    shared_grad = jnp.concatenate(
        [seen_grad[: 2 * TRUNK], jnp.zeros_like(seen_grad[: 2 * TRUNK])], axis=0
    ).astype(jnp.bfloat16)
    input_grad = own_grad + lax.psum_scatter(
        shared_grad, "tensor", scatter_dimension=0, tiled=True
    ).astype(jnp.float32)
    token_part, gain1_grad = norm1_back(input_grad)
    token_grad = mid_grad + token_part
    gain1_sum, gain2_sum, router_sum, embed_sum = lax.psum(
        (gain1_grad, gain2_grad, proj_grad, embed_grad), ("dp", "tensor")
    )
    return (
        output,
        token_grad,
        gain1_sum,
        qkv_grad,
        attn_proj_grad,
        gain2_sum,
        router_sum,
        embed_sum,
        expert_in_grad,
        expert_out_grad,
    )


def solution(mesh):
    in_specs = (
        P(("dp", "tensor"), None),
        P(),
        P("dp", None, "tensor"),
        P("tensor", "dp"),
        P(),
        P(),
        P(),
        P(None, "dp"),
        P("dp", None),
        P(("dp", "tensor"), None),
        P(("dp", "tensor"), None),
        P("dp", None),
        P(("dp", "tensor"), None),
    )
    out_specs = (
        P(("dp", "tensor"), None),
        P(("dp", "tensor"), None),
        P(),
        P("dp", None, "tensor"),
        P("tensor", "dp"),
        P(),
        P(),
        P(),
        P(None, ("dp", "tensor")),
        P(("dp", "tensor"), None),
    )
    return jax.shard_map(shards, mesh=mesh, in_specs=in_specs, out_specs=out_specs, check_vma=False)
```

```python
import math

import jax
import jax.numpy as jnp
from jax import lax
from jax.experimental import pallas as pl
from jax.experimental.pallas import tpu as pltpu
from jax.sharding import PartitionSpec as P

HEAD_DIM = 64
TRUNK = 1024
BRANCH = 256
MASKED = -1e30
LOG2E = math.log2(math.e)
EXP_SCALE = HEAD_DIM ** (-0.5) * LOG2E

NT = (((1,), (1,)), ((), ()))
NN = (((1,), (0,)), ((), ()))


def dot_nt(a, b):
    return lax.dot_general(a, b, NT, preferred_element_type=jnp.float32)


def dot_nn(a, b):
    return lax.dot_general(a, b, NN, preferred_element_type=jnp.float32)


def head_lanes(shape, dim, head):
    return lax.broadcasted_iota(jnp.int32, shape, dim) // HEAD_DIM == head


def fwd_kernel(meta_ref, q_ref, k_ref, v_ref, o_ref, lse_ref, vt_ref):
    block = pl.program_id(1)
    place = meta_ref[0]
    parent_row = pl.multiple_of(TRUNK + meta_ref[1 + block] * BRANCH, BRANCH)
    own_row = pl.multiple_of(2 * TRUNK + block * BRANCH, BRANCH)
    width = k_ref.shape[1]

    @pl.when(block == 0)
    def _():
        flipped = v_ref[...].T
        for head in range(2):
            vt_ref[head] = jnp.where(
                head_lanes(flipped.shape, 0, head), flipped, jnp.ones_like(flipped)
            )

    queries = q_ref[...]

    def finish(outs):
        rows = []
        for head, (acc, top) in enumerate(outs):
            mine, other = head * HEAD_DIM, (1 - head) * HEAD_DIM
            total = acc[other : other + 1]
            rows.append(acc[mine : mine + HEAD_DIM] / total)
            lse_ref[0, head : head + 1, :] = top * EXP_SCALE + jnp.log2(total)
        o_ref[...] = jnp.concatenate(rows, axis=0).T.astype(o_ref.dtype)

    def probs(scores, top):
        return jnp.exp2(scores * EXP_SCALE - top * EXP_SCALE).astype(jnp.bfloat16)

    def masked_queries(head):
        return jnp.where(head_lanes(queries.shape, 1, head), queries, jnp.zeros_like(queries))

    @pl.when(place == 0)
    def _():
        outs = []
        for head in range(2):
            scores = dot_nt(k_ref[0:TRUNK], masked_queries(head))
            keys = lax.broadcasted_iota(jnp.int32, scores.shape, 0)
            rows = lax.broadcasted_iota(jnp.int32, scores.shape, 1) + block * BRANCH
            scores = jnp.where(keys <= rows, scores, MASKED)
            top = jnp.max(scores, axis=0, keepdims=True)
            outs.append((dot_nn(vt_ref[head, :, 0:TRUNK], probs(scores, top)), top))
        finish(outs)

    @pl.when(place > 0)
    def _():
        outs = []
        for head in range(2):
            qm = masked_queries(head)
            trunk = dot_nt(k_ref[0:TRUNK], qm)
            parent = dot_nt(k_ref[pl.ds(parent_row, BRANCH)], qm)
            parent = jnp.where(place > 1, parent, MASKED)
            own = dot_nt(k_ref[pl.ds(own_row, BRANCH)], qm)
            keys = lax.broadcasted_iota(jnp.int32, own.shape, 0)
            rows = lax.broadcasted_iota(jnp.int32, own.shape, 1)
            own = jnp.where(keys <= rows, own, MASKED)
            top = jnp.maximum(
                jnp.maximum(
                    jnp.max(trunk, axis=0, keepdims=True), jnp.max(parent, axis=0, keepdims=True)
                ),
                jnp.max(own, axis=0, keepdims=True),
            )
            acc = dot_nn(vt_ref[head, :, 0:TRUNK], probs(trunk, top))
            acc = acc + dot_nn(vt_ref[head, :, pl.ds(parent_row, BRANCH)], probs(parent, top))
            acc = acc + dot_nn(vt_ref[head, :, pl.ds(own_row, BRANCH)], probs(own, top))
            outs.append((acc, top))
        finish(outs)


def attend(meta, q, k, v):
    rows, width = q.shape
    keys = k.shape[0]
    pairs = width // 128
    blocks = rows // BRANCH
    return pl.pallas_call(
        fwd_kernel,
        out_shape=(
            jax.ShapeDtypeStruct((rows, width), jnp.bfloat16),
            jax.ShapeDtypeStruct((pairs, 2, rows), jnp.float32),
        ),
        grid_spec=pltpu.PrefetchScalarGridSpec(
            num_scalar_prefetch=1,
            grid=(pairs, blocks),
            in_specs=[
                pl.BlockSpec((BRANCH, 128), lambda p, i, m: (i, p)),
                pl.BlockSpec((keys, 128), lambda p, i, m: (0, p)),
                pl.BlockSpec((keys, 128), lambda p, i, m: (0, p)),
            ],
            out_specs=[
                pl.BlockSpec((BRANCH, 128), lambda p, i, m: (i, p)),
                pl.BlockSpec((1, 2, BRANCH), lambda p, i, m: (p, 0, i)),
            ],
            scratch_shapes=[pltpu.VMEM((2, 128, keys), jnp.bfloat16)],
        ),
        compiler_params=pltpu.CompilerParams(vmem_limit_bytes=40 << 20),
        name="attend_forward",
    )(meta, q, k, v)


def bwd_kernel(meta_ref, q_ref, k_ref, v_ref, o_ref, g_ref, lse_ref,
               dq_ref, dk_ref, dv_ref, kt_ref, qm_ref, gm_ref, delta_ref, dqt_ref, dkp_ref, dvp_ref):
    place = meta_ref[0]
    scale = HEAD_DIM ** (-0.5)
    rows = q_ref.shape[0]
    blocks = rows // BRANCH
    kt_ref[...] = k_ref[...].T
    queries, grads = q_ref[...], g_ref[...]
    for head in range(2):
        lanes = head_lanes(queries.shape, 1, head)
        qm_ref[head] = jnp.where(lanes, queries, jnp.zeros_like(queries))
        gm_ref[head] = jnp.where(lanes, grads, jnp.zeros_like(grads))
    product = (grads.astype(jnp.float32) * o_ref[...].astype(jnp.float32)).T
    for head in range(2):
        delta_ref[head : head + 1, :] = jnp.sum(
            product[head * HEAD_DIM : (head + 1) * HEAD_DIM], axis=0, keepdims=True
        )
    dqt_ref[...] = jnp.zeros_like(dqt_ref)

    def step(key_row, query_row, count, mask_of=None):
        kb = k_ref[pl.ds(key_row, BRANCH)]
        vb = v_ref[pl.ds(key_row, BRANCH)]
        dk = dv = None
        for head in range(2):
            at = pl.ds(query_row, count)
            qm, gm = qm_ref[head, at], gm_ref[head, at]
            scores = dot_nt(kb, qm)
            probs = jnp.exp2(scores * EXP_SCALE - lse_ref[0, head : head + 1, at])
            if mask_of is not None:
                probs = mask_of(probs)
            prob_grad = dot_nt(vb, gm)
            score_grad = (probs * (prob_grad - delta_ref[head : head + 1, at])).astype(jnp.bfloat16)
            dv_part = dot_nn(probs.astype(jnp.bfloat16), gm)
            dk_part = dot_nn(score_grad, qm)
            dv = dv_part if dv is None else dv + dv_part
            dk = dk_part if dk is None else dk + dk_part
            mine = slice(head * HEAD_DIM, (head + 1) * HEAD_DIM)
            dqt_ref[mine, at] += dot_nn(kt_ref[mine, pl.ds(key_row, BRANCH)], score_grad)
        return dk * scale, dv

    def causal(offset):
        def mask_of(probs):
            keys = lax.broadcasted_iota(jnp.int32, probs.shape, 0) + offset
            at = lax.broadcasted_iota(jnp.int32, probs.shape, 1)
            return jnp.where(keys <= at, probs, 0.0)
        return mask_of

    @pl.when(place == 0)
    def _():
        @pl.loop(0, TRUNK // BRANCH)
        def _(b):
            row = pl.multiple_of(b * BRANCH, BRANCH)
            dk, dv = step(row, 0, rows, causal(row))
            dk_ref[pl.ds(row, BRANCH)] = dk.astype(dk_ref.dtype)
            dv_ref[pl.ds(row, BRANCH)] = dv.astype(dv_ref.dtype)
        rest = (dk_ref.shape[0] - TRUNK, dk_ref.shape[1])
        dk_ref[TRUNK:] = jnp.zeros(rest, dk_ref.dtype)
        dv_ref[TRUNK:] = jnp.zeros(rest, dv_ref.dtype)

    @pl.when(place > 0)
    def _():
        @pl.loop(0, TRUNK // BRANCH)
        def _(b):
            row = pl.multiple_of(b * BRANCH, BRANCH)
            dk, dv = step(row, 0, rows)
            dk_ref[pl.ds(row, BRANCH)] = dk.astype(dk_ref.dtype)
            dv_ref[pl.ds(row, BRANCH)] = dv.astype(dv_ref.dtype)

        dkp_ref[...] = jnp.zeros_like(dkp_ref)
        dvp_ref[...] = jnp.zeros_like(dvp_ref)

        @pl.loop(0, blocks)
        def _(b):
            at = pl.multiple_of(b * BRANCH, BRANCH)
            parent = pl.multiple_of(meta_ref[1 + b] * BRANCH, BRANCH)
            dk, dv = step(TRUNK + parent, at, BRANCH, lambda probs: jnp.where(place > 1, probs, 0.0))
            dkp_ref[pl.ds(parent, BRANCH)] += dk
            dvp_ref[pl.ds(parent, BRANCH)] += dv
            own = pl.multiple_of(2 * TRUNK + at, BRANCH)
            dk, dv = step(own, at, BRANCH, causal(0))
            dk_ref[pl.ds(own, BRANCH)] = dk.astype(dk_ref.dtype)
            dv_ref[pl.ds(own, BRANCH)] = dv.astype(dv_ref.dtype)

        dk_ref[TRUNK : 2 * TRUNK] = dkp_ref[...].astype(dk_ref.dtype)
        dv_ref[TRUNK : 2 * TRUNK] = dvp_ref[...].astype(dv_ref.dtype)

    dq_ref[...] = (dqt_ref[...] * scale).T.astype(dq_ref.dtype)


def attend_back(meta, q, k, v, o, grad, lse):
    rows, width = q.shape
    keys = k.shape[0]
    pairs = width // 128
    here = pl.BlockSpec((rows, 128), lambda p, m: (0, p))
    wide = pl.BlockSpec((keys, 128), lambda p, m: (0, p))
    return pl.pallas_call(
        bwd_kernel,
        out_shape=(
            jax.ShapeDtypeStruct((rows, width), jnp.bfloat16),
            jax.ShapeDtypeStruct((keys, width), jnp.bfloat16),
            jax.ShapeDtypeStruct((keys, width), jnp.bfloat16),
        ),
        grid_spec=pltpu.PrefetchScalarGridSpec(
            num_scalar_prefetch=1,
            grid=(pairs,),
            in_specs=[here, wide, wide, here, here, pl.BlockSpec((1, 2, rows), lambda p, m: (p, 0, 0))],
            out_specs=[here, wide, wide],
            scratch_shapes=[
                pltpu.VMEM((128, keys), jnp.bfloat16),
                pltpu.VMEM((2, rows, 128), jnp.bfloat16),
                pltpu.VMEM((2, rows, 128), jnp.bfloat16),
                pltpu.VMEM((2, rows), jnp.float32),
                pltpu.VMEM((128, rows), jnp.float32),
                pltpu.VMEM((TRUNK, 128), jnp.float32),
                pltpu.VMEM((TRUNK, 128), jnp.float32),
            ],
        ),
        compiler_params=pltpu.CompilerParams(vmem_limit_bytes=48 << 20),
        name="attend_backward",
    )(meta, q, k, v, o, grad, lse)


ROWS = 256
HALF_ROOT = math.sqrt(0.5)
PDF_SCALE = 1.0 / math.sqrt(2.0 * math.pi)
CHUNK = 512


def expert_fwd_kernel(x_ref, in_ref, out_ref, active_ref, slope_ref, keep_ref, send_ref):
    step = pl.program_id(0)
    half = pl.num_programs(0) // 2
    rows = x_ref[...]
    total = None
    for first in range(0, in_ref.shape[1], CHUNK):
        cols = slice(first, first + CHUNK)
        up = dot_nn(rows, in_ref[:, cols])
        below = 0.5 * (1.0 + lax.erf(up * HALF_ROOT))
        active = (up * below).astype(jnp.bfloat16)
        slope = below + up * (jnp.exp(-0.5 * up * up) * PDF_SCALE)
        active_ref[:, cols] = active
        slope_ref[:, cols] = slope.astype(jnp.bfloat16)
        part = dot_nn(active, out_ref[cols])
        total = part if total is None else total + part

    @pl.when(step < half)
    def _():
        keep_ref[...] = total

    @pl.when(step >= half)
    def _():
        send_ref[...] = total.astype(send_ref.dtype)


def expert_bwd_kernel(grad_ref, slope_ref, in_ref, out_ref, upgrad_ref, keep_ref, send_ref):
    step = pl.program_id(0)
    half = pl.num_programs(0) // 2
    grads = grad_ref[...]
    total = None
    for first in range(0, in_ref.shape[1], CHUNK):
        cols = slice(first, first + CHUNK)
        active_grad = dot_nt(grads, out_ref[cols])
        up_grad = (active_grad * slope_ref[:, cols].astype(jnp.float32)).astype(jnp.bfloat16)
        upgrad_ref[:, cols] = up_grad
        part = dot_nt(up_grad, in_ref[:, cols])
        total = part if total is None else total + part

    @pl.when(step < half)
    def _():
        keep_ref[...] = total

    @pl.when(step >= half)
    def _():
        send_ref[...] = total.astype(send_ref.dtype)


def split_specs(count, width):
    half = count // 2
    return [
        pl.BlockSpec((ROWS, width), lambda i: (jnp.minimum(i, half - 1), 0)),
        pl.BlockSpec((ROWS, width), lambda i: (jnp.maximum(i - half, 0), 0)),
    ]


def expert_forward(x, w_in, w_out):
    rows, width = x.shape
    hidden = w_in.shape[1]
    count = rows // ROWS
    def wide(cols):
        return pl.BlockSpec((ROWS, cols), lambda i: (i, 0))
    def whole(shape):
        return pl.BlockSpec(shape, lambda i: (0, 0), pipeline_mode=pl.Buffered(1))
    return pl.pallas_call(
        expert_fwd_kernel,
        grid=(count,),
        in_specs=[wide(width), whole(w_in.shape), whole(w_out.shape)],
        out_specs=[wide(hidden), wide(hidden)] + split_specs(count, width),
        out_shape=(
            jax.ShapeDtypeStruct((rows, hidden), jnp.bfloat16),
            jax.ShapeDtypeStruct((rows, hidden), jnp.bfloat16),
            jax.ShapeDtypeStruct((rows // 2, width), jnp.float32),
            jax.ShapeDtypeStruct((rows // 2, width), jnp.bfloat16),
        ),
        cost_estimate=pl.CostEstimate(flops=4 * rows * width * hidden, bytes_accessed=24 << 20, transcendentals=2 * rows * hidden),
        compiler_params=pltpu.CompilerParams(vmem_limit_bytes=40 << 20),
        name="expert_forward",
    )(x, w_in, w_out)


def expert_back(grads, slope, w_in, w_out):
    rows, width = grads.shape
    hidden = w_in.shape[1]
    count = rows // ROWS
    def wide(cols):
        return pl.BlockSpec((ROWS, cols), lambda i: (i, 0))
    def whole(shape):
        return pl.BlockSpec(shape, lambda i: (0, 0), pipeline_mode=pl.Buffered(1))
    return pl.pallas_call(
        expert_bwd_kernel,
        grid=(count,),
        in_specs=[wide(width), wide(hidden), whole(w_in.shape), whole(w_out.shape)],
        out_specs=[wide(hidden)] + split_specs(count, width),
        out_shape=(
            jax.ShapeDtypeStruct((rows, hidden), jnp.bfloat16),
            jax.ShapeDtypeStruct((rows // 2, width), jnp.float32),
            jax.ShapeDtypeStruct((rows // 2, width), jnp.bfloat16),
        ),
        cost_estimate=pl.CostEstimate(flops=4 * rows * width * hidden, bytes_accessed=24 << 20, transcendentals=0),
        compiler_params=pltpu.CompilerParams(vmem_limit_bytes=40 << 20),
        name="expert_backward",
    )(grads, slope, w_in, w_out)


MESH = pl.DeviceIdType.MESH


def total_kernel(ways, tensor, part_ref, out_ref, land_ref, send1, recv1, send2, recv2):
    me = lax.axis_index("dp") * tensor + lax.axis_index("tensor")

    def other(step):
        peer = lax.rem(me + step, ways)
        return peer, (peer // tensor, lax.rem(peer, tensor))

    barrier = pltpu.get_barrier_semaphore()

    @pl.loop(1, ways)
    def _(step):
        pl.semaphore_signal(barrier, inc=1, device_id=other(step)[1], device_id_type=MESH)

    pl.semaphore_wait(barrier, ways - 1)

    def scatter(step):
        peer, where = other(step)
        return pltpu.make_async_remote_copy(
            src_ref=part_ref.at[peer], dst_ref=land_ref.at[me],
            send_sem=send1.at[step], recv_sem=recv1.at[me],
            device_id=where, device_id_type=MESH,
        )

    def arrival(step):
        source = lax.rem(me - step + ways, ways)
        return pltpu.make_async_remote_copy(
            src_ref=part_ref.at[source], dst_ref=land_ref.at[source],
            send_sem=send1.at[step], recv_sem=recv1.at[source],
            device_id=other(step)[1], device_id_type=MESH,
        )

    def spread(step):
        return pltpu.make_async_remote_copy(
            src_ref=out_ref.at[me], dst_ref=out_ref.at[me],
            send_sem=send2.at[step], recv_sem=recv2.at[me],
            device_id=other(step)[1], device_id_type=MESH,
        )

    def landing(step):
        source = lax.rem(me - step + ways, ways)
        return pltpu.make_async_remote_copy(
            src_ref=out_ref.at[source], dst_ref=out_ref.at[source],
            send_sem=send2.at[step], recv_sem=recv2.at[source],
            device_id=other(step)[1], device_id_type=MESH,
        )

    @pl.loop(1, ways)
    def _(step):
        scatter(step).start()

    def add(step, total):
        arrival(step).wait_recv()
        return total + land_ref[lax.rem(me - step + ways, ways)]

    out_ref[me] = lax.fori_loop(1, ways, add, part_ref[me])

    @pl.loop(1, ways)
    def _(step):
        spread(step).start()

    @pl.loop(1, ways)
    def _(step):
        landing(step).wait_recv()

    @pl.loop(1, ways)
    def _(step):
        scatter(step).wait_send()
        spread(step).wait_send()


def total_over_devices(parts):
    tensor = lax.axis_size("tensor")
    ways = lax.axis_size("dp") * tensor
    flat = jnp.concatenate([part.reshape(-1) for part in parts])
    lanes = -(-flat.shape[0] // (ways * 8 * 128)) * 128
    padded = jnp.pad(flat, (0, ways * 8 * lanes - flat.shape[0])).reshape(ways, 8, lanes)
    summed = pl.pallas_call(
        lambda *refs: total_kernel(ways, tensor, *refs),
        out_shape=jax.ShapeDtypeStruct(padded.shape, jnp.float32),
        in_specs=[pl.BlockSpec(memory_space=pltpu.VMEM)],
        out_specs=pl.BlockSpec(memory_space=pltpu.VMEM),
        scratch_shapes=[pltpu.VMEM(padded.shape, jnp.float32)]
        + [pltpu.SemaphoreType.DMA((ways,))] * 4,
        compiler_params=pltpu.CompilerParams(collective_id=1, has_side_effects=True),
        name="total_over_devices",
    )(padded).reshape(-1)
    results, first = [], 0
    for part in parts:
        results.append(summed[first : first + part.size].reshape(part.shape))
        first += part.size
    return results


norm_eps = 1e-05
route_scale = 3.0
masked_score = -1e30
highest = lax.Precision.HIGHEST


def layer_norm(values, norm_gain):
    centred = values - jnp.mean(values, axis=-1, keepdims=True)
    spread = jnp.mean(centred * centred, axis=-1, keepdims=True)
    return centred * lax.rsqrt(spread + norm_eps) * norm_gain


def unit_rows(values):
    return values * lax.rsqrt(jnp.sum(values * values, axis=-1, keepdims=True) + 1.0)


def router_gate(normed, router_proj, expert_embed, picked):
    routed = jnp.dot(normed, router_proj, precision=highest)
    logits = route_scale * jnp.dot(unit_rows(routed), unit_rows(expert_embed).T, precision=highest)
    return jnp.sum(jax.nn.softmax(logits, axis=-1) * picked, axis=-1)


def gelu_exact(values):
    return jax.nn.gelu(values, approximate=False)


def slot_table(route_ids, order_ids, capacity):
    same_expert = route_ids[:, None] == route_ids[None, :]
    earlier = order_ids[None, :] < order_ids[:, None]
    ranking = jnp.sum(jnp.where(same_expert & earlier, 1, 0), axis=1).astype(jnp.int32)
    kept_mask = ranking < capacity
    column = route_ids * capacity + jnp.minimum(ranking, capacity - 1)
    return (column, kept_mask)


def low_dot(rows, weight):
    return jnp.dot(rows, weight, preferred_element_type=jnp.float32).astype(jnp.bfloat16)


def shards(
    tokens,
    norm1_gain,
    qkv_weight,
    attn_proj,
    norm2_gain,
    router_proj,
    expert_embed,
    expert_in,
    expert_out,
    routes,
    orders,
    leaf_parent,
    cotangent,
):
    rows_here = tokens.shape[0]
    model_width = tokens.shape[1]
    experts = expert_embed.shape[0]
    capacity = rows_here // experts
    dp_size = lax.axis_size("dp")
    leaf_parents = leaf_parent[0]

    def whole_tree(local_rows):
        return lax.all_gather(local_rows, "tensor", axis=0, tiled=True)

    def hop(rows, chip_step, core_step):
        route = []
        for source in range(dp_size):
            chip, core = source // 2, source % 2
            route.append((source, (chip ^ chip_step) * 2 + (core ^ core_step)))
        return lax.ppermute(rows, "dp", route)

    def across_chips(rows):
        blocks = rows.reshape(experts, capacity, model_width)
        moved = [blocks[0]] + [hop(blocks[step], step, 0) for step in range(1, experts)]
        return jnp.concatenate(moved, axis=0)

    def dispatch(slot_input):
        arrived = across_chips(slot_input)
        return jnp.concatenate([arrived, hop(arrived, 0, 1)], axis=0)

    def combine(kept_rows, sent_rows):
        paired = (kept_rows + hop(sent_rows, 0, 1).astype(jnp.float32)).astype(jnp.bfloat16)
        return across_chips(paired)

    hidden = tokens.astype(jnp.float32)
    normed_in, norm1_back = jax.vjp(layer_norm, hidden, norm1_gain)
    own_in = normed_in.astype(jnp.bfloat16)
    shared_in = whole_tree(own_in)[: 2 * TRUNK]
    seen_in = jnp.concatenate([shared_in, own_in], axis=0)
    qkv_cols = lax.all_gather(qkv_weight, "tensor", axis=2, tiled=True)
    qkv_full = lax.all_gather(qkv_cols, "dp", axis=0, tiled=True)
    proj_rows = lax.all_gather(attn_proj, "tensor", axis=0, tiled=True)
    proj_full = lax.all_gather(proj_rows, "dp", axis=1, tiled=True)
    query_weight, key_weight, value_weight = (qkv_full[:, part] for part in range(3))
    query_rows = low_dot(own_in, query_weight)
    key_rows = low_dot(seen_in, key_weight)
    value_rows = low_dot(seen_in, value_weight)
    place = lax.axis_index("tensor")
    leaf_blocks = rows_here // BRANCH
    first_leaf = jnp.maximum(place - 2, 0) * leaf_blocks
    parents = lax.dynamic_slice_in_dim(leaf_parents, first_leaf, leaf_blocks, 0) - 1
    meta = jnp.concatenate([place[None], parents]).astype(jnp.int32)
    attended, log_totals = attend(meta, query_rows, key_rows, value_rows)
    branch_out = jnp.dot(attended, proj_full, preferred_element_type=jnp.float32)
    mid_stream = hidden + branch_out
    normed_mid, norm2_back = jax.vjp(layer_norm, mid_stream, norm2_gain)
    moe_in = normed_mid.astype(jnp.bfloat16)
    route_ids = routes[:, 0]
    near_route = route_ids ^ (lax.axis_index("dp") // 2)
    column, kept_mask = slot_table(near_route, orders[0], capacity)
    picked = (route_ids[:, None] == jnp.arange(experts)[None, :]).astype(jnp.float32)
    gate_value, gate_back = jax.vjp(
        lambda normed_rows, route_proj, embed_rows: router_gate(
            normed_rows, route_proj, embed_rows, picked
        ),
        moe_in.astype(jnp.float32),
        router_proj,
        expert_embed,
    )
    select = (
        (column[:, None] == jnp.arange(experts * capacity)[None, :]) & kept_mask[:, None]
    ).astype(jnp.bfloat16)
    def to_slots(token_rows):
        return jnp.einsum(
            "ts,td->sd", select, token_rows, preferred_element_type=jnp.float32
        ).astype(jnp.bfloat16)

    def from_slots(slot_rows):
        return jnp.dot(select, slot_rows, preferred_element_type=jnp.float32)

    upstream = cotangent.astype(jnp.float32)
    expert_rows = dispatch(to_slots(moe_in))
    arrived_grad = dispatch(to_slots((gate_value[:, None] * upstream).astype(jnp.bfloat16)))
    active, slope, kept_result, sent_result = expert_forward(expert_rows, expert_in, expert_out)
    expert_result = from_slots(combine(kept_result, sent_result))
    output = (mid_stream + gate_value[:, None] * expert_result).astype(jnp.bfloat16)
    out_weight_grad = jnp.einsum(
        "rf,rd->fd", active, arrived_grad, preferred_element_type=jnp.float32
    ).astype(jnp.bfloat16)
    up_grad, kept_grad, sent_grad = expert_back(arrived_grad, slope, expert_in, expert_out)
    in_weight_grad = jnp.einsum(
        "rd,rf->df", expert_rows, up_grad, preferred_element_type=jnp.float32
    ).astype(jnp.bfloat16)
    moe_grad = from_slots(combine(kept_grad, sent_grad))
    gate_grad = jnp.sum(upstream * expert_result, axis=-1)
    router_part, proj_grad, embed_grad = gate_back(gate_grad)
    mid_part, gain2_grad = norm2_back(moe_grad + router_part)
    mid_grad = upstream + mid_part
    mid_grad, in_weight_grad, out_weight_grad = lax.optimization_barrier(
        (mid_grad, in_weight_grad, out_weight_grad)
    )
    expert_in_grad, expert_out_grad = (
        lax.psum_scatter(in_weight_grad, "tensor", scatter_dimension=1, tiled=True).astype(
            jnp.float32
        ),
        lax.psum_scatter(out_weight_grad, "tensor", scatter_dimension=0, tiled=True).astype(
            jnp.float32
        ),
    )
    branch_grad = mid_grad.astype(jnp.bfloat16)
    proj_grad_full = jnp.einsum(
        "sc,sd->cd", attended, branch_grad, preferred_element_type=jnp.float32
    )
    attn_proj_grad = lax.psum_scatter(
        lax.psum_scatter(proj_grad_full, "dp", scatter_dimension=1, tiled=True),
        "tensor",
        scatter_dimension=0,
        tiled=True,
    )
    attended_grad = jnp.einsum(
        "sd,cd->sc", branch_grad, proj_full, preferred_element_type=jnp.float32
    ).astype(jnp.bfloat16)
    query_grad, key_grad, value_grad = attend_back(
        meta, query_rows, key_rows, value_rows, attended, attended_grad, log_totals
    )

    def weight_grad(rows, row_grads):
        return jnp.einsum("sd,sc->dc", rows, row_grads, preferred_element_type=jnp.float32)

    def row_grad(row_grads, weight):
        return jnp.einsum("sc,dc->sd", row_grads, weight, preferred_element_type=jnp.float32)

    qkv_grad_full = jnp.stack(
        [
            weight_grad(own_in, query_grad),
            weight_grad(seen_in, key_grad),
            weight_grad(seen_in, value_grad),
        ],
        axis=1,
    ).astype(jnp.bfloat16)
    qkv_grad = lax.psum_scatter(
        lax.psum_scatter(qkv_grad_full, "dp", scatter_dimension=0, tiled=True),
        "tensor",
        scatter_dimension=2,
        tiled=True,
    ).astype(jnp.float32)
    seen_grad = row_grad(key_grad, key_weight) + row_grad(value_grad, value_weight)
    own_grad = seen_grad[2 * TRUNK :] + row_grad(query_grad, query_weight)
    shared_grad = jnp.concatenate(
        [seen_grad[: 2 * TRUNK], jnp.zeros_like(seen_grad[: 2 * TRUNK])], axis=0
    ).astype(jnp.bfloat16)
    input_grad = own_grad + lax.psum_scatter(
        shared_grad, "tensor", scatter_dimension=0, tiled=True
    ).astype(jnp.float32)
    token_part, gain1_grad = norm1_back(input_grad)
    token_grad = mid_grad + token_part
    gain1_sum, gain2_sum, router_sum, embed_sum = total_over_devices(
        (gain1_grad, gain2_grad, proj_grad, embed_grad)
    )
    return (
        output,
        token_grad,
        gain1_sum,
        qkv_grad,
        attn_proj_grad,
        gain2_sum,
        router_sum,
        embed_sum,
        expert_in_grad,
        expert_out_grad,
    )


def solution(mesh):
    in_specs = (
        P(("dp", "tensor"), None),
        P(),
        P("dp", None, "tensor"),
        P("tensor", "dp"),
        P(),
        P(),
        P(),
        P(None, "dp"),
        P("dp", None),
        P(("dp", "tensor"), None),
        P(("dp", "tensor"), None),
        P("dp", None),
        P(("dp", "tensor"), None),
    )
    out_specs = (
        P(("dp", "tensor"), None),
        P(("dp", "tensor"), None),
        P(),
        P("dp", None, "tensor"),
        P("tensor", "dp"),
        P(),
        P(),
        P(),
        P(None, ("dp", "tensor")),
        P(("dp", "tensor"), None),
    )
    return jax.shard_map(shards, mesh=mesh, in_specs=in_specs, out_specs=out_specs, check_vma=False)
```

```python
import math

import jax
import jax.numpy as jnp
from jax import lax
from jax.experimental import pallas as pl
from jax.experimental.pallas import tpu as pltpu
from jax.sharding import PartitionSpec as P

HEAD_DIM = 64
TRUNK = 1024
BRANCH = 256
MASKED = -1e30
LOG2E = math.log2(math.e)
EXP_SCALE = HEAD_DIM ** (-0.5) * LOG2E

NT = (((1,), (1,)), ((), ()))
NN = (((1,), (0,)), ((), ()))


def dot_nt(a, b):
    return lax.dot_general(a, b, NT, preferred_element_type=jnp.float32)


def dot_nn(a, b):
    return lax.dot_general(a, b, NN, preferred_element_type=jnp.float32)


def head_lanes(shape, dim, head):
    return lax.broadcasted_iota(jnp.int32, shape, dim) // HEAD_DIM == head


def fwd_kernel(meta_ref, q_ref, k_ref, v_ref, o_ref, lse_ref, vt_ref):
    block = pl.program_id(1)
    place = meta_ref[0]
    parent_row = pl.multiple_of(TRUNK + meta_ref[1 + block] * BRANCH, BRANCH)
    own_row = pl.multiple_of(2 * TRUNK + block * BRANCH, BRANCH)
    width = k_ref.shape[1]

    @pl.when(block == 0)
    def _():
        flipped = v_ref[...].T
        for head in range(2):
            vt_ref[head] = jnp.where(
                head_lanes(flipped.shape, 0, head), flipped, jnp.ones_like(flipped)
            )

    queries = q_ref[...]

    def finish(outs):
        rows = []
        for head, (acc, top) in enumerate(outs):
            mine, other = head * HEAD_DIM, (1 - head) * HEAD_DIM
            total = acc[other : other + 1]
            rows.append(acc[mine : mine + HEAD_DIM] / total)
            lse_ref[0, head : head + 1, :] = top * EXP_SCALE + jnp.log2(total)
        o_ref[...] = jnp.concatenate(rows, axis=0).T.astype(o_ref.dtype)

    def probs(scores, top):
        return jnp.exp2(scores * EXP_SCALE - top * EXP_SCALE).astype(jnp.bfloat16)

    def masked_queries(head):
        return jnp.where(head_lanes(queries.shape, 1, head), queries, jnp.zeros_like(queries))

    @pl.when(place == 0)
    def _():
        outs = []
        for head in range(2):
            scores = dot_nt(k_ref[0:TRUNK], masked_queries(head))
            keys = lax.broadcasted_iota(jnp.int32, scores.shape, 0)
            rows = lax.broadcasted_iota(jnp.int32, scores.shape, 1) + block * BRANCH
            scores = jnp.where(keys <= rows, scores, MASKED)
            top = jnp.max(scores, axis=0, keepdims=True)
            outs.append((dot_nn(vt_ref[head, :, 0:TRUNK], probs(scores, top)), top))
        finish(outs)

    @pl.when(place > 0)
    def _():
        outs = []
        for head in range(2):
            qm = masked_queries(head)
            trunk = dot_nt(k_ref[0:TRUNK], qm)
            parent = dot_nt(k_ref[pl.ds(parent_row, BRANCH)], qm)
            parent = jnp.where(place > 1, parent, MASKED)
            own = dot_nt(k_ref[pl.ds(own_row, BRANCH)], qm)
            keys = lax.broadcasted_iota(jnp.int32, own.shape, 0)
            rows = lax.broadcasted_iota(jnp.int32, own.shape, 1)
            own = jnp.where(keys <= rows, own, MASKED)
            top = jnp.maximum(
                jnp.maximum(
                    jnp.max(trunk, axis=0, keepdims=True), jnp.max(parent, axis=0, keepdims=True)
                ),
                jnp.max(own, axis=0, keepdims=True),
            )
            acc = dot_nn(vt_ref[head, :, 0:TRUNK], probs(trunk, top))
            acc = acc + dot_nn(vt_ref[head, :, pl.ds(parent_row, BRANCH)], probs(parent, top))
            acc = acc + dot_nn(vt_ref[head, :, pl.ds(own_row, BRANCH)], probs(own, top))
            outs.append((acc, top))
        finish(outs)


def attend(meta, q, k, v):
    rows, width = q.shape
    keys = k.shape[0]
    pairs = width // 128
    blocks = rows // BRANCH
    return pl.pallas_call(
        fwd_kernel,
        out_shape=(
            jax.ShapeDtypeStruct((rows, width), jnp.bfloat16),
            jax.ShapeDtypeStruct((pairs, 2, rows), jnp.float32),
        ),
        grid_spec=pltpu.PrefetchScalarGridSpec(
            num_scalar_prefetch=1,
            grid=(pairs, blocks),
            in_specs=[
                pl.BlockSpec((BRANCH, 128), lambda p, i, m: (i, p)),
                pl.BlockSpec((keys, 128), lambda p, i, m: (0, p)),
                pl.BlockSpec((keys, 128), lambda p, i, m: (0, p)),
            ],
            out_specs=[
                pl.BlockSpec((BRANCH, 128), lambda p, i, m: (i, p)),
                pl.BlockSpec((1, 2, BRANCH), lambda p, i, m: (p, 0, i)),
            ],
            scratch_shapes=[pltpu.VMEM((2, 128, keys), jnp.bfloat16)],
        ),
        compiler_params=pltpu.CompilerParams(vmem_limit_bytes=40 << 20),
        name="attend_forward",
    )(meta, q, k, v)


def bwd_kernel(meta_ref, q_ref, k_ref, v_ref, o_ref, g_ref, lse_ref,
               dq_ref, dk_ref, dv_ref, kt_ref, qm_ref, gm_ref, delta_ref, dqt_ref, dkp_ref, dvp_ref):
    place = meta_ref[0]
    scale = HEAD_DIM ** (-0.5)
    rows = q_ref.shape[0]
    blocks = rows // BRANCH
    kt_ref[...] = k_ref[...].T
    queries, grads = q_ref[...], g_ref[...]
    for head in range(2):
        lanes = head_lanes(queries.shape, 1, head)
        qm_ref[head] = jnp.where(lanes, queries, jnp.zeros_like(queries))
        gm_ref[head] = jnp.where(lanes, grads, jnp.zeros_like(grads))
    product = (grads.astype(jnp.float32) * o_ref[...].astype(jnp.float32)).T
    for head in range(2):
        delta_ref[head : head + 1, :] = jnp.sum(
            product[head * HEAD_DIM : (head + 1) * HEAD_DIM], axis=0, keepdims=True
        )
    dqt_ref[...] = jnp.zeros_like(dqt_ref)

    def step(key_row, query_row, count, mask_of=None):
        kb = k_ref[pl.ds(key_row, BRANCH)]
        vb = v_ref[pl.ds(key_row, BRANCH)]
        dk = dv = None
        for head in range(2):
            at = pl.ds(query_row, count)
            qm, gm = qm_ref[head, at], gm_ref[head, at]
            scores = dot_nt(kb, qm)
            probs = jnp.exp2(scores * EXP_SCALE - lse_ref[0, head : head + 1, at])
            if mask_of is not None:
                probs = mask_of(probs)
            prob_grad = dot_nt(vb, gm)
            score_grad = (probs * (prob_grad - delta_ref[head : head + 1, at])).astype(jnp.bfloat16)
            dv_part = dot_nn(probs.astype(jnp.bfloat16), gm)
            dk_part = dot_nn(score_grad, qm)
            dv = dv_part if dv is None else dv + dv_part
            dk = dk_part if dk is None else dk + dk_part
            mine = slice(head * HEAD_DIM, (head + 1) * HEAD_DIM)
            dqt_ref[mine, at] += dot_nn(kt_ref[mine, pl.ds(key_row, BRANCH)], score_grad)
        return dk * scale, dv

    def causal(offset):
        def mask_of(probs):
            keys = lax.broadcasted_iota(jnp.int32, probs.shape, 0) + offset
            at = lax.broadcasted_iota(jnp.int32, probs.shape, 1)
            return jnp.where(keys <= at, probs, 0.0)
        return mask_of

    @pl.when(place == 0)
    def _():
        @pl.loop(0, TRUNK // BRANCH)
        def _(b):
            row = pl.multiple_of(b * BRANCH, BRANCH)
            dk, dv = step(row, 0, rows, causal(row))
            dk_ref[pl.ds(row, BRANCH)] = dk.astype(dk_ref.dtype)
            dv_ref[pl.ds(row, BRANCH)] = dv.astype(dv_ref.dtype)
        rest = (dk_ref.shape[0] - TRUNK, dk_ref.shape[1])
        dk_ref[TRUNK:] = jnp.zeros(rest, dk_ref.dtype)
        dv_ref[TRUNK:] = jnp.zeros(rest, dv_ref.dtype)

    @pl.when(place > 0)
    def _():
        @pl.loop(0, TRUNK // BRANCH)
        def _(b):
            row = pl.multiple_of(b * BRANCH, BRANCH)
            dk, dv = step(row, 0, rows)
            dk_ref[pl.ds(row, BRANCH)] = dk.astype(dk_ref.dtype)
            dv_ref[pl.ds(row, BRANCH)] = dv.astype(dv_ref.dtype)

        dkp_ref[...] = jnp.zeros_like(dkp_ref)
        dvp_ref[...] = jnp.zeros_like(dvp_ref)

        @pl.loop(0, blocks)
        def _(b):
            at = pl.multiple_of(b * BRANCH, BRANCH)
            parent = pl.multiple_of(meta_ref[1 + b] * BRANCH, BRANCH)
            dk, dv = step(TRUNK + parent, at, BRANCH, lambda probs: jnp.where(place > 1, probs, 0.0))
            dkp_ref[pl.ds(parent, BRANCH)] += dk
            dvp_ref[pl.ds(parent, BRANCH)] += dv
            own = pl.multiple_of(2 * TRUNK + at, BRANCH)
            dk, dv = step(own, at, BRANCH, causal(0))
            dk_ref[pl.ds(own, BRANCH)] = dk.astype(dk_ref.dtype)
            dv_ref[pl.ds(own, BRANCH)] = dv.astype(dv_ref.dtype)

        dk_ref[TRUNK : 2 * TRUNK] = dkp_ref[...].astype(dk_ref.dtype)
        dv_ref[TRUNK : 2 * TRUNK] = dvp_ref[...].astype(dv_ref.dtype)

    dq_ref[...] = (dqt_ref[...] * scale).T.astype(dq_ref.dtype)


def attend_back(meta, q, k, v, o, grad, lse):
    rows, width = q.shape
    keys = k.shape[0]
    pairs = width // 128
    here = pl.BlockSpec((rows, 128), lambda p, m: (0, p))
    wide = pl.BlockSpec((keys, 128), lambda p, m: (0, p))
    return pl.pallas_call(
        bwd_kernel,
        out_shape=(
            jax.ShapeDtypeStruct((rows, width), jnp.bfloat16),
            jax.ShapeDtypeStruct((keys, width), jnp.bfloat16),
            jax.ShapeDtypeStruct((keys, width), jnp.bfloat16),
        ),
        grid_spec=pltpu.PrefetchScalarGridSpec(
            num_scalar_prefetch=1,
            grid=(pairs,),
            in_specs=[here, wide, wide, here, here, pl.BlockSpec((1, 2, rows), lambda p, m: (p, 0, 0))],
            out_specs=[here, wide, wide],
            scratch_shapes=[
                pltpu.VMEM((128, keys), jnp.bfloat16),
                pltpu.VMEM((2, rows, 128), jnp.bfloat16),
                pltpu.VMEM((2, rows, 128), jnp.bfloat16),
                pltpu.VMEM((2, rows), jnp.float32),
                pltpu.VMEM((128, rows), jnp.float32),
                pltpu.VMEM((TRUNK, 128), jnp.float32),
                pltpu.VMEM((TRUNK, 128), jnp.float32),
            ],
        ),
        compiler_params=pltpu.CompilerParams(vmem_limit_bytes=48 << 20),
        name="attend_backward",
    )(meta, q, k, v, o, grad, lse)


ROWS = 256
HALF_ROOT = math.sqrt(0.5)
PDF_SCALE = 1.0 / math.sqrt(2.0 * math.pi)
CHUNK = 512


def expert_fwd_kernel(x_ref, in_ref, out_ref, active_ref, slope_ref, keep_ref, send_ref):
    step = pl.program_id(0)
    half = pl.num_programs(0) // 2
    rows = x_ref[...]
    total = None
    for first in range(0, in_ref.shape[1], CHUNK):
        cols = slice(first, first + CHUNK)
        up = dot_nn(rows, in_ref[:, cols])
        below = 0.5 * (1.0 + lax.erf(up * HALF_ROOT))
        active = (up * below).astype(jnp.bfloat16)
        slope = below + up * (jnp.exp(-0.5 * up * up) * PDF_SCALE)
        active_ref[:, cols] = active
        slope_ref[:, cols] = slope.astype(jnp.bfloat16)
        part = dot_nn(active, out_ref[cols])
        total = part if total is None else total + part

    @pl.when(step < half)
    def _():
        keep_ref[...] = total

    @pl.when(step >= half)
    def _():
        send_ref[...] = total.astype(send_ref.dtype)


def expert_bwd_kernel(grad_ref, slope_ref, in_ref, out_ref, upgrad_ref, keep_ref, send_ref):
    step = pl.program_id(0)
    half = pl.num_programs(0) // 2
    grads = grad_ref[...]
    total = None
    for first in range(0, in_ref.shape[1], CHUNK):
        cols = slice(first, first + CHUNK)
        active_grad = dot_nt(grads, out_ref[cols])
        up_grad = (active_grad * slope_ref[:, cols].astype(jnp.float32)).astype(jnp.bfloat16)
        upgrad_ref[:, cols] = up_grad
        part = dot_nt(up_grad, in_ref[:, cols])
        total = part if total is None else total + part

    @pl.when(step < half)
    def _():
        keep_ref[...] = total

    @pl.when(step >= half)
    def _():
        send_ref[...] = total.astype(send_ref.dtype)


def split_specs(count, width):
    half = count // 2
    return [
        pl.BlockSpec((ROWS, width), lambda i: (jnp.minimum(i, half - 1), 0)),
        pl.BlockSpec((ROWS, width), lambda i: (jnp.maximum(i - half, 0), 0)),
    ]


def expert_forward(x, w_in, w_out):
    rows, width = x.shape
    hidden = w_in.shape[1]
    count = rows // ROWS
    def wide(cols):
        return pl.BlockSpec((ROWS, cols), lambda i: (i, 0))
    def whole(shape):
        return pl.BlockSpec(shape, lambda i: (0, 0), pipeline_mode=pl.Buffered(1))
    return pl.pallas_call(
        expert_fwd_kernel,
        grid=(count,),
        in_specs=[wide(width), whole(w_in.shape), whole(w_out.shape)],
        out_specs=[wide(hidden), wide(hidden)] + split_specs(count, width),
        out_shape=(
            jax.ShapeDtypeStruct((rows, hidden), jnp.bfloat16),
            jax.ShapeDtypeStruct((rows, hidden), jnp.bfloat16),
            jax.ShapeDtypeStruct((rows // 2, width), jnp.float32),
            jax.ShapeDtypeStruct((rows // 2, width), jnp.bfloat16),
        ),
        cost_estimate=pl.CostEstimate(flops=4 * rows * width * hidden, bytes_accessed=24 << 20, transcendentals=2 * rows * hidden),
        compiler_params=pltpu.CompilerParams(vmem_limit_bytes=40 << 20),
        name="expert_forward",
    )(x, w_in, w_out)


def expert_back(grads, slope, w_in, w_out):
    rows, width = grads.shape
    hidden = w_in.shape[1]
    count = rows // ROWS
    def wide(cols):
        return pl.BlockSpec((ROWS, cols), lambda i: (i, 0))
    def whole(shape):
        return pl.BlockSpec(shape, lambda i: (0, 0), pipeline_mode=pl.Buffered(1))
    return pl.pallas_call(
        expert_bwd_kernel,
        grid=(count,),
        in_specs=[wide(width), wide(hidden), whole(w_in.shape), whole(w_out.shape)],
        out_specs=[wide(hidden)] + split_specs(count, width),
        out_shape=(
            jax.ShapeDtypeStruct((rows, hidden), jnp.bfloat16),
            jax.ShapeDtypeStruct((rows // 2, width), jnp.float32),
            jax.ShapeDtypeStruct((rows // 2, width), jnp.bfloat16),
        ),
        cost_estimate=pl.CostEstimate(flops=4 * rows * width * hidden, bytes_accessed=24 << 20, transcendentals=0),
        compiler_params=pltpu.CompilerParams(vmem_limit_bytes=40 << 20),
        name="expert_backward",
    )(grads, slope, w_in, w_out)


MESH = pl.DeviceIdType.MESH


def total_kernel(ways, tensor, part_ref, out_ref, land_ref, send1, recv1, send2, recv2):
    me = lax.axis_index("dp") * tensor + lax.axis_index("tensor")

    def other(step):
        peer = lax.rem(me + step, ways)
        return peer, (peer // tensor, lax.rem(peer, tensor))

    barrier = pltpu.get_barrier_semaphore()

    @pl.loop(1, ways)
    def _(step):
        pl.semaphore_signal(barrier, inc=1, device_id=other(step)[1], device_id_type=MESH)

    pl.semaphore_wait(barrier, ways - 1)

    def scatter(step):
        peer, where = other(step)
        return pltpu.make_async_remote_copy(
            src_ref=part_ref.at[peer], dst_ref=land_ref.at[me],
            send_sem=send1.at[step], recv_sem=recv1.at[me],
            device_id=where, device_id_type=MESH,
        )

    def arrival(step):
        source = lax.rem(me - step + ways, ways)
        return pltpu.make_async_remote_copy(
            src_ref=part_ref.at[source], dst_ref=land_ref.at[source],
            send_sem=send1.at[step], recv_sem=recv1.at[source],
            device_id=other(step)[1], device_id_type=MESH,
        )

    def spread(step):
        return pltpu.make_async_remote_copy(
            src_ref=out_ref.at[me], dst_ref=out_ref.at[me],
            send_sem=send2.at[step], recv_sem=recv2.at[me],
            device_id=other(step)[1], device_id_type=MESH,
        )

    def landing(step):
        source = lax.rem(me - step + ways, ways)
        return pltpu.make_async_remote_copy(
            src_ref=out_ref.at[source], dst_ref=out_ref.at[source],
            send_sem=send2.at[step], recv_sem=recv2.at[source],
            device_id=other(step)[1], device_id_type=MESH,
        )

    @pl.loop(1, ways)
    def _(step):
        scatter(step).start()

    def add(step, total):
        arrival(step).wait_recv()
        return total + land_ref[lax.rem(me - step + ways, ways)]

    out_ref[me] = lax.fori_loop(1, ways, add, part_ref[me])

    @pl.loop(1, ways)
    def _(step):
        spread(step).start()

    @pl.loop(1, ways)
    def _(step):
        landing(step).wait_recv()

    @pl.loop(1, ways)
    def _(step):
        scatter(step).wait_send()
        spread(step).wait_send()


def total_over_devices(parts):
    tensor = lax.axis_size("tensor")
    ways = lax.axis_size("dp") * tensor
    flat = jnp.concatenate([part.reshape(-1) for part in parts])
    lanes = -(-flat.shape[0] // (ways * 8 * 128)) * 128
    padded = jnp.pad(flat, (0, ways * 8 * lanes - flat.shape[0])).reshape(ways, 8, lanes)
    summed = pl.pallas_call(
        lambda *refs: total_kernel(ways, tensor, *refs),
        out_shape=jax.ShapeDtypeStruct(padded.shape, jnp.float32),
        in_specs=[pl.BlockSpec(memory_space=pltpu.VMEM)],
        out_specs=pl.BlockSpec(memory_space=pltpu.VMEM),
        scratch_shapes=[pltpu.VMEM(padded.shape, jnp.float32)]
        + [pltpu.SemaphoreType.DMA((ways,))] * 4,
        compiler_params=pltpu.CompilerParams(collective_id=1, has_side_effects=True),
        name="total_over_devices",
    )(padded).reshape(-1)
    results, first = [], 0
    for part in parts:
        results.append(summed[first : first + part.size].reshape(part.shape))
        first += part.size
    return results


PIECE = 64


def greet(peers):
    barrier = pltpu.get_barrier_semaphore()
    for peer in peers:
        pl.semaphore_signal(barrier, inc=1, device_id=peer, device_id_type=MESH)
    pl.semaphore_wait(barrier, len(peers))


def share_kernel(dp, tensor, own_ref, block_ref, seen_ref, weights_ref,
                 row_send, row_recv, copy_sem, block_sem,
                 line_send, line_recv, chip_send, chip_recv, pair_send, pair_recv):
    spot, place = lax.axis_index("dp"), lax.axis_index("tensor")
    chip, core = spot // 2, lax.rem(spot, 2)
    chips = dp // 2
    rows = own_ref.shape[0]
    pieces = rows // PIECE
    partner = (chip * 2 + 1 - core, place)

    def along(step):
        return lax.rem(place + step, tensor)

    def chip_at(step):
        return lax.rem(chip + step, chips)

    greet(
        [(spot, along(step)) for step in range(1, tensor)]
        + [(chip_at(step) * 2 + core, place) for step in range(1, chips)]
        + [partner]
    )

    def keep(part):
        return pltpu.make_async_copy(
            own_ref, seen_ref.at[pl.ds(part * rows, rows)], copy_sem.at[part]
        )

    def keep_block():
        return pltpu.make_async_copy(block_ref, weights_ref.at[place, spot], block_sem)

    def pass_on(part, piece, fresh):
        at = pl.ds(part * rows + piece * PIECE, PIECE)
        source = own_ref.at[pl.ds(piece * PIECE, PIECE)] if fresh else seen_ref.at[at]
        return pltpu.make_async_remote_copy(
            src_ref=source, dst_ref=seen_ref.at[at],
            send_sem=row_send.at[part, piece], recv_sem=row_recv.at[part, piece],
            device_id=(spot, lax.rem(place + 1, tensor)), device_id_type=MESH,
        )

    def line(step):
        return pltpu.make_async_remote_copy(
            src_ref=block_ref, dst_ref=weights_ref.at[place, spot],
            send_sem=line_send.at[step], recv_sem=line_recv.at[place],
            device_id=(spot, along(step)), device_id_type=MESH,
        )

    def line_in(step):
        source = along(tensor - step)
        return pltpu.make_async_remote_copy(
            src_ref=block_ref, dst_ref=weights_ref.at[source, spot],
            send_sem=line_send.at[step], recv_sem=line_recv.at[source],
            device_id=(spot, along(step)), device_id_type=MESH,
        )

    def plane(part, step):
        block = weights_ref.at[part, spot]
        return pltpu.make_async_remote_copy(
            src_ref=block, dst_ref=block,
            send_sem=chip_send.at[part, step], recv_sem=chip_recv.at[part, chip],
            device_id=(chip_at(step) * 2 + core, place), device_id_type=MESH,
        )

    def plane_in(part, step):
        source = chip_at(chips - step)
        block = weights_ref.at[part, source * 2 + core]
        return pltpu.make_async_remote_copy(
            src_ref=block, dst_ref=block,
            send_sem=chip_send.at[part, step], recv_sem=chip_recv.at[part, source],
            device_id=(chip_at(step) * 2 + core, place), device_id_type=MESH,
        )

    def across(part, source, source_core):
        block = weights_ref.at[part, source * 2 + source_core]
        return pltpu.make_async_remote_copy(
            src_ref=block, dst_ref=block,
            send_sem=pair_send.at[part, source], recv_sem=pair_recv.at[part, source],
            device_id=partner, device_id_type=MESH,
        )

    keep_block().start()
    keep(2).start()

    @pl.when(place < 2)
    def _():
        keep(1).start()

    @pl.when(place == 0)
    def _():
        keep(0).start()

    for step in range(1, tensor):
        line(step).start()

    def row_steps(first, last):
        @pl.loop(first, last)
        def _(piece):
            @pl.when(place == 0)
            def _():
                pass_on(0, piece, True).start()

            @pl.when(place > 0)
            def _():
                pass_on(0, piece, False).wait_recv()

            @pl.when((place > 0) & (place < tensor - 1))
            def _():
                pass_on(0, piece, False).start()

            @pl.when(place == 1)
            def _():
                pass_on(1, piece, True).start()

            @pl.when(place > 1)
            def _():
                pass_on(1, piece, False).wait_recv()

            @pl.when((place > 1) & (place < tensor - 1))
            def _():
                pass_on(1, piece, False).start()

    row_steps(0, pieces // 4)
    keep_block().wait()
    for step in range(tensor):
        part = along(tensor - step)
        if step:
            line_in(step).wait_recv()

        @pl.loop(1, chips)
        def _(hop):
            plane(part, hop).start()

        across(part, chip, core).start()
    row_steps(pieces // 4, (pieces * 5) // 8)
    for step in range(tensor):
        part = along(tensor - step)

        @pl.loop(1, chips)
        def _(hop):
            plane_in(part, hop).wait_recv()
            across(part, chip_at(chips - hop), core).start()

    row_steps((pieces * 5) // 8, pieces)
    for part in range(tensor):

        @pl.loop(0, chips)
        def _(source):
            across(part, source, 1 - core).wait_recv()
            across(part, source, core).wait_send()

        @pl.loop(1, chips)
        def _(hop):
            plane(part, hop).wait_send()

    for step in range(1, tensor):
        line(step).wait_send()

    @pl.when(place < tensor - 1)
    def _():
        @pl.loop(0, pieces)
        def _(piece):
            pass_on(0, piece, False).wait_send()

    @pl.when((place > 0) & (place < tensor - 1))
    def _():
        @pl.loop(0, pieces)
        def _(piece):
            pass_on(1, piece, False).wait_send()

    keep(2).wait()

    @pl.when(place < 2)
    def _():
        keep(1).wait()

    @pl.when(place == 0)
    def _():
        keep(0).wait()


def share_rows_and_weights(own, block):
    dp, tensor = lax.axis_size("dp"), lax.axis_size("tensor")
    rows, width = own.shape
    pieces, chips = rows // PIECE, dp // 2
    dma = pltpu.SemaphoreType.DMA
    anywhere = pl.BlockSpec(memory_space=pl.ANY)
    return pl.pallas_call(
        lambda *refs: share_kernel(dp, tensor, *refs),
        out_shape=(
            jax.ShapeDtypeStruct((3 * rows, width), own.dtype),
            jax.ShapeDtypeStruct((tensor, dp) + block.shape, block.dtype),
        ),
        in_specs=[anywhere, anywhere],
        out_specs=[anywhere, anywhere],
        scratch_shapes=[
            dma((2, pieces)), dma((2, pieces)), dma((3,)), dma,
            dma((tensor,)), dma((tensor,)),
            dma((tensor, chips)), dma((tensor, chips)),
            dma((tensor, chips)), dma((tensor, chips)),
        ],
        compiler_params=pltpu.CompilerParams(collective_id=2, has_side_effects=True),
        name="share_rows_and_weights",
    )(own, block)


def gather_grads_kernel(dp, tensor, rows_ref, grads_ref, out_ref, sum_ref,
                        land_ref, pass_ref, grad_land, grad_sum, line_out, line_land,
                        row_send, row_recv, grad_send, grad_recv, line_send, line_recv):
    spot, place = lax.axis_index("dp"), lax.axis_index("tensor")
    rows = out_ref.shape[0]
    pieces = rows // PIECE
    parts = grads_ref.shape[2] // (tensor * sum_ref.shape[1] // 4)
    share = sum_ref.shape[1] // parts

    def along(step):
        return lax.rem(place + step, tensor)

    def peer(step):
        return lax.rem(spot + step, dp)

    greet(
        [(spot, along(step)) for step in range(1, tensor)]
        + [(peer(step), place) for step in range(1, dp)]
    )

    def pass_down(piece, fresh):
        at = pl.ds(piece * PIECE, PIECE)
        source = rows_ref if fresh else pass_ref
        return pltpu.make_async_remote_copy(
            src_ref=source.at[at], dst_ref=land_ref.at[at],
            send_sem=row_send.at[piece], recv_sem=row_recv.at[piece],
            device_id=(spot, lax.rem(place + tensor - 1, tensor)), device_id_type=MESH,
        )

    def give(step):
        return pltpu.make_async_remote_copy(
            src_ref=grads_ref.at[peer(step)], dst_ref=grad_land.at[spot],
            send_sem=grad_send.at[step], recv_sem=grad_recv.at[spot],
            device_id=(peer(step), place), device_id_type=MESH,
        )

    def take(step):
        source = peer(dp - step)
        return pltpu.make_async_remote_copy(
            src_ref=grads_ref.at[source], dst_ref=grad_land.at[source],
            send_sem=grad_send.at[step], recv_sem=grad_recv.at[source],
            device_id=(peer(step), place), device_id_type=MESH,
        )

    def line(step):
        return pltpu.make_async_remote_copy(
            src_ref=line_out.at[along(step)], dst_ref=line_land.at[place],
            send_sem=line_send.at[step], recv_sem=line_recv.at[place],
            device_id=(spot, along(step)), device_id_type=MESH,
        )

    def line_in(step):
        source = along(tensor - step)
        return pltpu.make_async_remote_copy(
            src_ref=line_out.at[source], dst_ref=line_land.at[source],
            send_sem=line_send.at[step], recv_sem=line_recv.at[source],
            device_id=(spot, along(step)), device_id_type=MESH,
        )

    @pl.when(place == tensor - 1)
    def _():
        @pl.loop(0, 2 * pieces)
        def _(piece):
            pass_down(piece, True).start()

    @pl.loop(1, dp)
    def _(step):
        give(step).start()

    @pl.when(place > 1)
    def _():
        out_ref[...] = jnp.zeros_like(out_ref)

    def row_steps(first, last):
        @pl.loop(first, last)
        def _(piece):
            trunk = piece < pieces
            at = pl.ds(pl.multiple_of(piece * PIECE, PIECE), PIECE)
            takes = (place < tensor - 1) & ((place > 0) | trunk)
            sends = takes & (place > 0) & ((place > 1) | trunk)

            @pl.when(takes)
            def _():
                pass_down(piece, False).wait_recv()

            @pl.when(sends)
            def _():
                total = rows_ref[at].astype(jnp.float32) + land_ref[at].astype(jnp.float32)
                pass_ref[at] = total.astype(pass_ref.dtype)
                pass_down(piece, False).start()

            @pl.when(takes & jnp.logical_not(sends))
            def _():
                total = rows_ref[at].astype(jnp.float32) + land_ref[at].astype(jnp.float32)
                here = lax.rem(piece, pieces) * PIECE
                out_ref[pl.ds(pl.multiple_of(here, PIECE), PIECE)] = total

    row_steps(0, pieces + pieces // 2)
    grad_sum[...] = grads_ref[spot].astype(jnp.float32)

    @pl.loop(1, dp)
    def _(step):
        take(step).wait_recv()
        grad_sum[...] += grad_land[peer(dp - step)].astype(jnp.float32)

    for target in range(tensor):
        mine = jnp.concatenate(
            [
                grad_sum[:, (part * tensor + target) * share : (part * tensor + target + 1) * share]
                for part in range(parts)
            ],
            axis=1,
        )
        line_out[target] = mine.astype(line_out.dtype)

        @pl.when(place == target)
        def _():
            sum_ref[...] = mine

    for step in range(1, tensor):
        line(step).start()
    row_steps(pieces + pieces // 2, 2 * pieces)
    for step in range(1, tensor):
        line_in(step).wait_recv()
        sum_ref[...] += line_land[along(tensor - step)].astype(jnp.float32)
    for step in range(1, tensor):
        line(step).wait_send()

    @pl.loop(1, dp)
    def _(step):
        give(step).wait_send()

    @pl.loop(0, 2 * pieces)
    def _(piece):
        sends = (place > 0) & ((place > 1) | (piece < pieces))

        @pl.when(sends)
        def _():
            pass_down(piece, True).wait_send()


def collect_grads(rows, grads):
    dp, tensor = lax.axis_size("dp"), lax.axis_size("tensor")
    count, width = rows.shape[0] // 2, rows.shape[1]
    depth = grads.shape[0] // dp
    grads = grads.reshape(dp, depth, grads.shape[1])
    slab = grads.shape[2] // tensor
    pieces = count // PIECE
    dma = pltpu.SemaphoreType.DMA
    here = pl.BlockSpec(memory_space=pltpu.VMEM)
    return pl.pallas_call(
        lambda *refs: gather_grads_kernel(dp, tensor, *refs),
        out_shape=(
            jax.ShapeDtypeStruct((count, width), jnp.float32),
            jax.ShapeDtypeStruct((depth, slab), jnp.float32),
        ),
        in_specs=[here, here],
        out_specs=[here, here],
        scratch_shapes=[
            pltpu.VMEM(rows.shape, rows.dtype),
            pltpu.VMEM(rows.shape, rows.dtype),
            pltpu.VMEM(grads.shape, grads.dtype),
            pltpu.VMEM(grads.shape[1:], jnp.float32),
            pltpu.VMEM((tensor, depth, slab), grads.dtype),
            pltpu.VMEM((tensor, depth, slab), grads.dtype),
            dma((2 * pieces,)), dma((2 * pieces,)),
            dma((dp,)), dma((dp,)), dma((tensor,)), dma((tensor,)),
        ],
        compiler_params=pltpu.CompilerParams(
            collective_id=3, has_side_effects=True, vmem_limit_bytes=56 << 20
        ),
        name="collect_grads",
    )(rows, grads)


norm_eps = 1e-05
route_scale = 3.0
masked_score = -1e30
highest = lax.Precision.HIGHEST


def layer_norm(values, norm_gain):
    centred = values - jnp.mean(values, axis=-1, keepdims=True)
    spread = jnp.mean(centred * centred, axis=-1, keepdims=True)
    return centred * lax.rsqrt(spread + norm_eps) * norm_gain


def unit_rows(values):
    return values * lax.rsqrt(jnp.sum(values * values, axis=-1, keepdims=True) + 1.0)


def router_gate(normed, router_proj, expert_embed, picked):
    routed = jnp.dot(normed, router_proj, precision=highest)
    logits = route_scale * jnp.dot(unit_rows(routed), unit_rows(expert_embed).T, precision=highest)
    return jnp.sum(jax.nn.softmax(logits, axis=-1) * picked, axis=-1)


def gelu_exact(values):
    return jax.nn.gelu(values, approximate=False)


def slot_table(route_ids, order_ids, capacity):
    same_expert = route_ids[:, None] == route_ids[None, :]
    earlier = order_ids[None, :] < order_ids[:, None]
    ranking = jnp.sum(jnp.where(same_expert & earlier, 1, 0), axis=1).astype(jnp.int32)
    kept_mask = ranking < capacity
    column = route_ids * capacity + jnp.minimum(ranking, capacity - 1)
    return (column, kept_mask)


def low_dot(rows, weight):
    return jnp.dot(rows, weight, preferred_element_type=jnp.float32).astype(jnp.bfloat16)


def shards(
    tokens,
    norm1_gain,
    qkv_weight,
    attn_proj,
    norm2_gain,
    router_proj,
    expert_embed,
    expert_in,
    expert_out,
    routes,
    orders,
    leaf_parent,
    cotangent,
):
    rows_here = tokens.shape[0]
    model_width = tokens.shape[1]
    experts = expert_embed.shape[0]
    capacity = rows_here // experts
    dp_size, tensor_size = lax.axis_size("dp"), lax.axis_size("tensor")
    leaf_parents = leaf_parent[0]

    def hop(rows, chip_step, core_step):
        route = []
        for source in range(dp_size):
            chip, core = source // 2, source % 2
            route.append((source, (chip ^ chip_step) * 2 + (core ^ core_step)))
        return lax.ppermute(rows, "dp", route)

    def across_chips(rows):
        blocks = rows.reshape(experts, capacity, model_width)
        moved = [blocks[0]] + [hop(blocks[step], step, 0) for step in range(1, experts)]
        return jnp.concatenate(moved, axis=0)

    def dispatch(slot_input):
        arrived = across_chips(slot_input)
        return jnp.concatenate([arrived, hop(arrived, 0, 1)], axis=0)

    def combine(kept_rows, sent_rows):
        paired = (kept_rows + hop(sent_rows, 0, 1).astype(jnp.float32)).astype(jnp.bfloat16)
        return across_chips(paired)

    hidden = tokens.astype(jnp.float32)
    normed_in, norm1_back = jax.vjp(layer_norm, hidden, norm1_gain)
    own_in = normed_in.astype(jnp.bfloat16)
    flat_qkv = qkv_weight.reshape(qkv_weight.shape[0], -1)
    seen_in, weights = share_rows_and_weights(
        own_in, jnp.concatenate([flat_qkv, attn_proj.T], axis=1)
    )
    weights = weights.reshape(tensor_size, model_width, 4, model_width // tensor_size)
    weights = weights.transpose(2, 1, 0, 3).reshape(4, model_width, model_width)
    query_weight, key_weight, value_weight, proj_back = weights
    query_rows = low_dot(own_in, query_weight)
    key_rows = low_dot(seen_in, key_weight)
    value_rows = low_dot(seen_in, value_weight)
    place = lax.axis_index("tensor")
    leaf_blocks = rows_here // BRANCH
    first_leaf = jnp.maximum(place - 2, 0) * leaf_blocks
    parents = lax.dynamic_slice_in_dim(leaf_parents, first_leaf, leaf_blocks, 0) - 1
    meta = jnp.concatenate([place[None], parents]).astype(jnp.int32)
    attended, log_totals = attend(meta, query_rows, key_rows, value_rows)
    branch_out = jnp.einsum(
        "sc,dc->sd", attended, proj_back, preferred_element_type=jnp.float32
    )
    mid_stream = hidden + branch_out
    normed_mid, norm2_back = jax.vjp(layer_norm, mid_stream, norm2_gain)
    moe_in = normed_mid.astype(jnp.bfloat16)
    route_ids = routes[:, 0]
    near_route = route_ids ^ (lax.axis_index("dp") // 2)
    column, kept_mask = slot_table(near_route, orders[0], capacity)
    picked = (route_ids[:, None] == jnp.arange(experts)[None, :]).astype(jnp.float32)
    gate_value, gate_back = jax.vjp(
        lambda normed_rows, route_proj, embed_rows: router_gate(
            normed_rows, route_proj, embed_rows, picked
        ),
        moe_in.astype(jnp.float32),
        router_proj,
        expert_embed,
    )
    select = (
        (column[:, None] == jnp.arange(experts * capacity)[None, :]) & kept_mask[:, None]
    ).astype(jnp.bfloat16)
    def to_slots(token_rows):
        return jnp.einsum(
            "ts,td->sd", select, token_rows, preferred_element_type=jnp.float32
        ).astype(jnp.bfloat16)

    def from_slots(slot_rows):
        return jnp.dot(select, slot_rows, preferred_element_type=jnp.float32)

    upstream = cotangent.astype(jnp.float32)
    slot_rows, slot_grads = lax.optimization_barrier(
        (
            to_slots(moe_in),
            to_slots((gate_value[:, None] * upstream).astype(jnp.bfloat16)),
        )
    )
    expert_rows = dispatch(slot_rows)
    arrived_grad = dispatch(slot_grads)
    active, slope, kept_result, sent_result = expert_forward(expert_rows, expert_in, expert_out)
    expert_result = from_slots(combine(kept_result, sent_result))
    output = (mid_stream + gate_value[:, None] * expert_result).astype(jnp.bfloat16)
    out_weight_grad = jnp.einsum(
        "rf,rd->fd", active, arrived_grad, preferred_element_type=jnp.float32
    ).astype(jnp.bfloat16)
    up_grad, kept_grad, sent_grad = expert_back(arrived_grad, slope, expert_in, expert_out)
    in_weight_grad = jnp.einsum(
        "rd,rf->df", expert_rows, up_grad, preferred_element_type=jnp.float32
    ).astype(jnp.bfloat16)
    moe_grad = from_slots(combine(kept_grad, sent_grad))
    gate_grad = jnp.sum(upstream * expert_result, axis=-1)
    router_part, proj_grad, embed_grad = gate_back(gate_grad)
    mid_part, gain2_grad = norm2_back(moe_grad + router_part)
    mid_grad = upstream + mid_part
    mid_grad, in_weight_grad, out_weight_grad = lax.optimization_barrier(
        (mid_grad, in_weight_grad, out_weight_grad)
    )
    expert_in_grad, expert_out_grad = (
        lax.psum_scatter(in_weight_grad, "tensor", scatter_dimension=1, tiled=True).astype(
            jnp.float32
        ),
        lax.psum_scatter(out_weight_grad, "tensor", scatter_dimension=0, tiled=True).astype(
            jnp.float32
        ),
    )
    branch_grad = mid_grad.astype(jnp.bfloat16)
    attended_grad = jnp.einsum(
        "sd,dc->sc", branch_grad, proj_back, preferred_element_type=jnp.float32
    ).astype(jnp.bfloat16)
    query_grad, key_grad, value_grad = attend_back(
        meta, query_rows, key_rows, value_rows, attended, attended_grad, log_totals
    )

    def weight_grad(rows, row_grads):
        return jnp.einsum("sd,sc->dc", rows, row_grads, preferred_element_type=jnp.float32)

    def row_grad(row_grads, weight):
        return jnp.einsum("sc,dc->sd", row_grads, weight, preferred_element_type=jnp.float32)

    weight_grads = jnp.concatenate(
        [
            weight_grad(own_in, query_grad),
            weight_grad(seen_in, key_grad),
            weight_grad(seen_in, value_grad),
            weight_grad(branch_grad, attended),
        ],
        axis=1,
    ).astype(jnp.bfloat16)
    seen_grad = row_grad(key_grad, key_weight) + row_grad(value_grad, value_weight)
    own_grad = seen_grad[2 * TRUNK :] + row_grad(query_grad, query_weight)
    arrived_rows, grad_block = collect_grads(
        seen_grad[: 2 * TRUNK].astype(jnp.bfloat16), weight_grads
    )
    input_grad = own_grad + arrived_rows
    qkv_grad = grad_block[:, : flat_qkv.shape[1]].reshape(qkv_weight.shape)
    attn_proj_grad = grad_block[:, flat_qkv.shape[1] :].T
    token_part, gain1_grad = norm1_back(input_grad)
    token_grad = mid_grad + token_part
    gain1_sum, gain2_sum, router_sum, embed_sum = total_over_devices(
        (gain1_grad, gain2_grad, proj_grad, embed_grad)
    )
    return (
        output,
        token_grad,
        gain1_sum,
        qkv_grad,
        attn_proj_grad,
        gain2_sum,
        router_sum,
        embed_sum,
        expert_in_grad,
        expert_out_grad,
    )


def solution(mesh):
    in_specs = (
        P(("dp", "tensor"), None),
        P(),
        P("dp", None, "tensor"),
        P("tensor", "dp"),
        P(),
        P(),
        P(),
        P(None, "dp"),
        P("dp", None),
        P(("dp", "tensor"), None),
        P(("dp", "tensor"), None),
        P("dp", None),
        P(("dp", "tensor"), None),
    )
    out_specs = (
        P(("dp", "tensor"), None),
        P(("dp", "tensor"), None),
        P(),
        P("dp", None, "tensor"),
        P("tensor", "dp"),
        P(),
        P(),
        P(),
        P(None, ("dp", "tensor")),
        P(("dp", "tensor"), None),
    )
    return jax.shard_map(shards, mesh=mesh, in_specs=in_specs, out_specs=out_specs, check_vma=False)
```

```python
import math

import jax
import jax.numpy as jnp
from jax import lax
from jax.experimental import pallas as pl
from jax.experimental.pallas import tpu as pltpu
from jax.sharding import PartitionSpec as P

HEAD_DIM = 64
TRUNK = 1024
BRANCH = 256
MASKED = -1e30
LOG2E = math.log2(math.e)
EXP_SCALE = HEAD_DIM ** (-0.5) * LOG2E

NT = (((1,), (1,)), ((), ()))
NN = (((1,), (0,)), ((), ()))


def dot_nt(a, b):
    return lax.dot_general(a, b, NT, preferred_element_type=jnp.float32)


def dot_nn(a, b):
    return lax.dot_general(a, b, NN, preferred_element_type=jnp.float32)


def head_lanes(shape, dim, head):
    return lax.broadcasted_iota(jnp.int32, shape, dim) // HEAD_DIM == head


def fwd_kernel(meta_ref, q_ref, k_ref, v_ref, o_ref, lse_ref, vt_ref):
    block = pl.program_id(1)
    place = meta_ref[0]
    parent_row = pl.multiple_of(TRUNK + meta_ref[1 + block] * BRANCH, BRANCH)
    own_row = pl.multiple_of(2 * TRUNK + block * BRANCH, BRANCH)
    width = k_ref.shape[1]

    @pl.when(block == 0)
    def _():
        flipped = v_ref[...].T
        for head in range(2):
            vt_ref[head] = jnp.where(
                head_lanes(flipped.shape, 0, head), flipped, jnp.ones_like(flipped)
            )

    queries = q_ref[...]

    def finish(outs):
        rows = []
        for head, (acc, top) in enumerate(outs):
            mine, other = head * HEAD_DIM, (1 - head) * HEAD_DIM
            total = acc[other : other + 1]
            rows.append(acc[mine : mine + HEAD_DIM] / total)
            lse_ref[0, head : head + 1, :] = top * EXP_SCALE + jnp.log2(total)
        o_ref[...] = jnp.concatenate(rows, axis=0).T.astype(o_ref.dtype)

    def probs(scores, top):
        return jnp.exp2(scores * EXP_SCALE - top * EXP_SCALE).astype(jnp.bfloat16)

    def masked_queries(head):
        return jnp.where(head_lanes(queries.shape, 1, head), queries, jnp.zeros_like(queries))

    @pl.when(place == 0)
    def _():
        outs = []
        for head in range(2):
            scores = dot_nt(k_ref[0:TRUNK], masked_queries(head))
            keys = lax.broadcasted_iota(jnp.int32, scores.shape, 0)
            rows = lax.broadcasted_iota(jnp.int32, scores.shape, 1) + block * BRANCH
            scores = jnp.where(keys <= rows, scores, MASKED)
            top = jnp.max(scores, axis=0, keepdims=True)
            outs.append((dot_nn(vt_ref[head, :, 0:TRUNK], probs(scores, top)), top))
        finish(outs)

    @pl.when(place > 0)
    def _():
        outs = []
        for head in range(2):
            qm = masked_queries(head)
            trunk = dot_nt(k_ref[0:TRUNK], qm)
            parent = dot_nt(k_ref[pl.ds(parent_row, BRANCH)], qm)
            parent = jnp.where(place > 1, parent, MASKED)
            own = dot_nt(k_ref[pl.ds(own_row, BRANCH)], qm)
            keys = lax.broadcasted_iota(jnp.int32, own.shape, 0)
            rows = lax.broadcasted_iota(jnp.int32, own.shape, 1)
            own = jnp.where(keys <= rows, own, MASKED)
            top = jnp.maximum(
                jnp.maximum(
                    jnp.max(trunk, axis=0, keepdims=True), jnp.max(parent, axis=0, keepdims=True)
                ),
                jnp.max(own, axis=0, keepdims=True),
            )
            acc = dot_nn(vt_ref[head, :, 0:TRUNK], probs(trunk, top))
            acc = acc + dot_nn(vt_ref[head, :, pl.ds(parent_row, BRANCH)], probs(parent, top))
            acc = acc + dot_nn(vt_ref[head, :, pl.ds(own_row, BRANCH)], probs(own, top))
            outs.append((acc, top))
        finish(outs)


def attend(meta, q, k, v):
    rows, width = q.shape
    keys = k.shape[0]
    pairs = width // 128
    blocks = rows // BRANCH
    return pl.pallas_call(
        fwd_kernel,
        out_shape=(
            jax.ShapeDtypeStruct((rows, width), jnp.bfloat16),
            jax.ShapeDtypeStruct((pairs, 2, rows), jnp.float32),
        ),
        grid_spec=pltpu.PrefetchScalarGridSpec(
            num_scalar_prefetch=1,
            grid=(pairs, blocks),
            in_specs=[
                pl.BlockSpec((BRANCH, 128), lambda p, i, m: (i, p)),
                pl.BlockSpec((keys, 128), lambda p, i, m: (0, p)),
                pl.BlockSpec((keys, 128), lambda p, i, m: (0, p)),
            ],
            out_specs=[
                pl.BlockSpec((BRANCH, 128), lambda p, i, m: (i, p)),
                pl.BlockSpec((1, 2, BRANCH), lambda p, i, m: (p, 0, i)),
            ],
            scratch_shapes=[pltpu.VMEM((2, 128, keys), jnp.bfloat16)],
        ),
        compiler_params=pltpu.CompilerParams(vmem_limit_bytes=40 << 20),
        name="attend_forward",
    )(meta, q, k, v)


def bwd_kernel(meta_ref, q_ref, k_ref, v_ref, o_ref, g_ref, lse_ref,
               dq_ref, dk_ref, dv_ref, kt_ref, qm_ref, gm_ref, delta_ref, dqt_ref, dkp_ref, dvp_ref):
    place = meta_ref[0]
    scale = HEAD_DIM ** (-0.5)
    rows = q_ref.shape[0]
    blocks = rows // BRANCH
    kt_ref[...] = k_ref[...].T
    queries, grads = q_ref[...], g_ref[...]
    for head in range(2):
        lanes = head_lanes(queries.shape, 1, head)
        qm_ref[head] = jnp.where(lanes, queries, jnp.zeros_like(queries))
        gm_ref[head] = jnp.where(lanes, grads, jnp.zeros_like(grads))
    product = (grads.astype(jnp.float32) * o_ref[...].astype(jnp.float32)).T
    for head in range(2):
        delta_ref[head : head + 1, :] = jnp.sum(
            product[head * HEAD_DIM : (head + 1) * HEAD_DIM], axis=0, keepdims=True
        )
    dqt_ref[...] = jnp.zeros_like(dqt_ref)

    def step(key_row, query_row, count, mask_of=None):
        kb = k_ref[pl.ds(key_row, BRANCH)]
        vb = v_ref[pl.ds(key_row, BRANCH)]
        dk = dv = None
        for head in range(2):
            at = pl.ds(query_row, count)
            qm, gm = qm_ref[head, at], gm_ref[head, at]
            scores = dot_nt(kb, qm)
            probs = jnp.exp2(scores * EXP_SCALE - lse_ref[0, head : head + 1, at])
            if mask_of is not None:
                probs = mask_of(probs)
            prob_grad = dot_nt(vb, gm)
            score_grad = (probs * (prob_grad - delta_ref[head : head + 1, at])).astype(jnp.bfloat16)
            dv_part = dot_nn(probs.astype(jnp.bfloat16), gm)
            dk_part = dot_nn(score_grad, qm)
            dv = dv_part if dv is None else dv + dv_part
            dk = dk_part if dk is None else dk + dk_part
            mine = slice(head * HEAD_DIM, (head + 1) * HEAD_DIM)
            dqt_ref[mine, at] += dot_nn(kt_ref[mine, pl.ds(key_row, BRANCH)], score_grad)
        return dk * scale, dv

    def causal(offset):
        def mask_of(probs):
            keys = lax.broadcasted_iota(jnp.int32, probs.shape, 0) + offset
            at = lax.broadcasted_iota(jnp.int32, probs.shape, 1)
            return jnp.where(keys <= at, probs, 0.0)
        return mask_of

    @pl.when(place == 0)
    def _():
        @pl.loop(0, TRUNK // BRANCH)
        def _(b):
            row = pl.multiple_of(b * BRANCH, BRANCH)
            dk, dv = step(row, 0, rows, causal(row))
            dk_ref[pl.ds(row, BRANCH)] = dk.astype(dk_ref.dtype)
            dv_ref[pl.ds(row, BRANCH)] = dv.astype(dv_ref.dtype)
        rest = (dk_ref.shape[0] - TRUNK, dk_ref.shape[1])
        dk_ref[TRUNK:] = jnp.zeros(rest, dk_ref.dtype)
        dv_ref[TRUNK:] = jnp.zeros(rest, dv_ref.dtype)

    @pl.when(place > 0)
    def _():
        @pl.loop(0, TRUNK // BRANCH)
        def _(b):
            row = pl.multiple_of(b * BRANCH, BRANCH)
            dk, dv = step(row, 0, rows)
            dk_ref[pl.ds(row, BRANCH)] = dk.astype(dk_ref.dtype)
            dv_ref[pl.ds(row, BRANCH)] = dv.astype(dv_ref.dtype)

        dkp_ref[...] = jnp.zeros_like(dkp_ref)
        dvp_ref[...] = jnp.zeros_like(dvp_ref)

        @pl.loop(0, blocks)
        def _(b):
            at = pl.multiple_of(b * BRANCH, BRANCH)
            parent = pl.multiple_of(meta_ref[1 + b] * BRANCH, BRANCH)
            dk, dv = step(TRUNK + parent, at, BRANCH, lambda probs: jnp.where(place > 1, probs, 0.0))
            dkp_ref[pl.ds(parent, BRANCH)] += dk
            dvp_ref[pl.ds(parent, BRANCH)] += dv
            own = pl.multiple_of(2 * TRUNK + at, BRANCH)
            dk, dv = step(own, at, BRANCH, causal(0))
            dk_ref[pl.ds(own, BRANCH)] = dk.astype(dk_ref.dtype)
            dv_ref[pl.ds(own, BRANCH)] = dv.astype(dv_ref.dtype)

        dk_ref[TRUNK : 2 * TRUNK] = dkp_ref[...].astype(dk_ref.dtype)
        dv_ref[TRUNK : 2 * TRUNK] = dvp_ref[...].astype(dv_ref.dtype)

    dq_ref[...] = (dqt_ref[...] * scale).T.astype(dq_ref.dtype)


def attend_back(meta, q, k, v, o, grad, lse):
    rows, width = q.shape
    keys = k.shape[0]
    pairs = width // 128
    here = pl.BlockSpec((rows, 128), lambda p, m: (0, p))
    wide = pl.BlockSpec((keys, 128), lambda p, m: (0, p))
    return pl.pallas_call(
        bwd_kernel,
        out_shape=(
            jax.ShapeDtypeStruct((rows, width), jnp.bfloat16),
            jax.ShapeDtypeStruct((keys, width), jnp.bfloat16),
            jax.ShapeDtypeStruct((keys, width), jnp.bfloat16),
        ),
        grid_spec=pltpu.PrefetchScalarGridSpec(
            num_scalar_prefetch=1,
            grid=(pairs,),
            in_specs=[here, wide, wide, here, here, pl.BlockSpec((1, 2, rows), lambda p, m: (p, 0, 0))],
            out_specs=[here, wide, wide],
            scratch_shapes=[
                pltpu.VMEM((128, keys), jnp.bfloat16),
                pltpu.VMEM((2, rows, 128), jnp.bfloat16),
                pltpu.VMEM((2, rows, 128), jnp.bfloat16),
                pltpu.VMEM((2, rows), jnp.float32),
                pltpu.VMEM((128, rows), jnp.float32),
                pltpu.VMEM((TRUNK, 128), jnp.float32),
                pltpu.VMEM((TRUNK, 128), jnp.float32),
            ],
        ),
        compiler_params=pltpu.CompilerParams(vmem_limit_bytes=48 << 20),
        name="attend_backward",
    )(meta, q, k, v, o, grad, lse)


ROWS = 256
HALF_ROOT = math.sqrt(0.5)
PDF_SCALE = 1.0 / math.sqrt(2.0 * math.pi)
CHUNK = 512


def expert_fwd_kernel(x_ref, in_ref, out_ref, active_ref, slope_ref, keep_ref, send_ref):
    step = pl.program_id(0)
    half = pl.num_programs(0) // 2
    rows = x_ref[...]
    total = None
    for first in range(0, in_ref.shape[1], CHUNK):
        cols = slice(first, first + CHUNK)
        up = dot_nn(rows, in_ref[:, cols])
        below = 0.5 * (1.0 + lax.erf(up * HALF_ROOT))
        active = (up * below).astype(jnp.bfloat16)
        slope = below + up * (jnp.exp(-0.5 * up * up) * PDF_SCALE)
        active_ref[:, cols] = active
        slope_ref[:, cols] = slope.astype(jnp.bfloat16)
        part = dot_nn(active, out_ref[cols])
        total = part if total is None else total + part

    @pl.when(step < half)
    def _():
        keep_ref[...] = total

    @pl.when(step >= half)
    def _():
        send_ref[...] = total.astype(send_ref.dtype)


def expert_bwd_kernel(grad_ref, slope_ref, in_ref, out_ref, upgrad_ref, keep_ref, send_ref):
    step = pl.program_id(0)
    half = pl.num_programs(0) // 2
    grads = grad_ref[...]
    total = None
    for first in range(0, in_ref.shape[1], CHUNK):
        cols = slice(first, first + CHUNK)
        active_grad = dot_nt(grads, out_ref[cols])
        up_grad = (active_grad * slope_ref[:, cols].astype(jnp.float32)).astype(jnp.bfloat16)
        upgrad_ref[:, cols] = up_grad
        part = dot_nt(up_grad, in_ref[:, cols])
        total = part if total is None else total + part

    @pl.when(step < half)
    def _():
        keep_ref[...] = total

    @pl.when(step >= half)
    def _():
        send_ref[...] = total.astype(send_ref.dtype)


def split_specs(count, width):
    half = count // 2
    return [
        pl.BlockSpec((ROWS, width), lambda i: (jnp.minimum(i, half - 1), 0)),
        pl.BlockSpec((ROWS, width), lambda i: (jnp.maximum(i - half, 0), 0)),
    ]


def expert_forward(x, w_in, w_out):
    rows, width = x.shape
    hidden = w_in.shape[1]
    count = rows // ROWS
    def wide(cols):
        return pl.BlockSpec((ROWS, cols), lambda i: (i, 0))
    def whole(shape):
        return pl.BlockSpec(shape, lambda i: (0, 0), pipeline_mode=pl.Buffered(1))
    return pl.pallas_call(
        expert_fwd_kernel,
        grid=(count,),
        in_specs=[wide(width), whole(w_in.shape), whole(w_out.shape)],
        out_specs=[wide(hidden), wide(hidden)] + split_specs(count, width),
        out_shape=(
            jax.ShapeDtypeStruct((rows, hidden), jnp.bfloat16),
            jax.ShapeDtypeStruct((rows, hidden), jnp.bfloat16),
            jax.ShapeDtypeStruct((rows // 2, width), jnp.float32),
            jax.ShapeDtypeStruct((rows // 2, width), jnp.bfloat16),
        ),
        cost_estimate=pl.CostEstimate(flops=4 * rows * width * hidden, bytes_accessed=24 << 20, transcendentals=2 * rows * hidden),
        compiler_params=pltpu.CompilerParams(vmem_limit_bytes=40 << 20),
        name="expert_forward",
    )(x, w_in, w_out)


def expert_back(grads, slope, w_in, w_out):
    rows, width = grads.shape
    hidden = w_in.shape[1]
    count = rows // ROWS
    def wide(cols):
        return pl.BlockSpec((ROWS, cols), lambda i: (i, 0))
    def whole(shape):
        return pl.BlockSpec(shape, lambda i: (0, 0), pipeline_mode=pl.Buffered(1))
    return pl.pallas_call(
        expert_bwd_kernel,
        grid=(count,),
        in_specs=[wide(width), wide(hidden), whole(w_in.shape), whole(w_out.shape)],
        out_specs=[wide(hidden)] + split_specs(count, width),
        out_shape=(
            jax.ShapeDtypeStruct((rows, hidden), jnp.bfloat16),
            jax.ShapeDtypeStruct((rows // 2, width), jnp.float32),
            jax.ShapeDtypeStruct((rows // 2, width), jnp.bfloat16),
        ),
        cost_estimate=pl.CostEstimate(flops=4 * rows * width * hidden, bytes_accessed=24 << 20, transcendentals=0),
        compiler_params=pltpu.CompilerParams(vmem_limit_bytes=40 << 20),
        name="expert_backward",
    )(grads, slope, w_in, w_out)


MESH = pl.DeviceIdType.MESH


def total_kernel(ways, tensor, part_ref, out_ref, land_ref, send1, recv1, send2, recv2):
    me = lax.axis_index("dp") * tensor + lax.axis_index("tensor")

    def other(step):
        peer = lax.rem(me + step, ways)
        return peer, (peer // tensor, lax.rem(peer, tensor))

    barrier = pltpu.get_barrier_semaphore()

    @pl.loop(1, ways)
    def _(step):
        pl.semaphore_signal(barrier, inc=1, device_id=other(step)[1], device_id_type=MESH)

    pl.semaphore_wait(barrier, ways - 1)

    def scatter(step):
        peer, where = other(step)
        return pltpu.make_async_remote_copy(
            src_ref=part_ref.at[peer], dst_ref=land_ref.at[me],
            send_sem=send1.at[step], recv_sem=recv1.at[me],
            device_id=where, device_id_type=MESH,
        )

    def arrival(step):
        source = lax.rem(me - step + ways, ways)
        return pltpu.make_async_remote_copy(
            src_ref=part_ref.at[source], dst_ref=land_ref.at[source],
            send_sem=send1.at[step], recv_sem=recv1.at[source],
            device_id=other(step)[1], device_id_type=MESH,
        )

    def spread(step):
        return pltpu.make_async_remote_copy(
            src_ref=out_ref.at[me], dst_ref=out_ref.at[me],
            send_sem=send2.at[step], recv_sem=recv2.at[me],
            device_id=other(step)[1], device_id_type=MESH,
        )

    def landing(step):
        source = lax.rem(me - step + ways, ways)
        return pltpu.make_async_remote_copy(
            src_ref=out_ref.at[source], dst_ref=out_ref.at[source],
            send_sem=send2.at[step], recv_sem=recv2.at[source],
            device_id=other(step)[1], device_id_type=MESH,
        )

    @pl.loop(1, ways)
    def _(step):
        scatter(step).start()

    def add(step, total):
        arrival(step).wait_recv()
        return total + land_ref[lax.rem(me - step + ways, ways)]

    out_ref[me] = lax.fori_loop(1, ways, add, part_ref[me])

    @pl.loop(1, ways)
    def _(step):
        spread(step).start()

    @pl.loop(1, ways)
    def _(step):
        landing(step).wait_recv()

    @pl.loop(1, ways)
    def _(step):
        scatter(step).wait_send()
        spread(step).wait_send()


def total_over_devices(parts):
    tensor = lax.axis_size("tensor")
    ways = lax.axis_size("dp") * tensor
    flat = jnp.concatenate([part.reshape(-1) for part in parts])
    lanes = -(-flat.shape[0] // (ways * 8 * 128)) * 128
    padded = jnp.pad(flat, (0, ways * 8 * lanes - flat.shape[0])).reshape(ways, 8, lanes)
    summed = pl.pallas_call(
        lambda *refs: total_kernel(ways, tensor, *refs),
        out_shape=jax.ShapeDtypeStruct(padded.shape, jnp.float32),
        in_specs=[pl.BlockSpec(memory_space=pltpu.VMEM)],
        out_specs=pl.BlockSpec(memory_space=pltpu.VMEM),
        scratch_shapes=[pltpu.VMEM(padded.shape, jnp.float32)]
        + [pltpu.SemaphoreType.DMA((ways,))] * 4,
        compiler_params=pltpu.CompilerParams(collective_id=1, has_side_effects=True),
        name="total_over_devices",
    )(padded).reshape(-1)
    results, first = [], 0
    for part in parts:
        results.append(summed[first : first + part.size].reshape(part.shape))
        first += part.size
    return results


PIECE = 64


def greet(peers):
    barrier = pltpu.get_barrier_semaphore()
    for peer in peers:
        pl.semaphore_signal(barrier, inc=1, device_id=peer, device_id_type=MESH)
    pl.semaphore_wait(barrier, len(peers))


def share_kernel(dp, tensor, own_ref, block_ref, seen_ref, out_ref, weights_ref,
                 row_send, row_recv,
                 line_send, line_recv, chip_send, chip_recv, pair_send, pair_recv):
    spot, place = lax.axis_index("dp"), lax.axis_index("tensor")
    chip, core = spot // 2, lax.rem(spot, 2)
    chips = dp // 2
    rows = own_ref.shape[0]
    pieces = rows // PIECE
    part_width = out_ref.shape[2] // tensor
    partner = (chip * 2 + 1 - core, place)

    def along(step):
        return lax.rem(place + step, tensor)

    def chip_at(step):
        return lax.rem(chip + step, chips)

    greet(
        [(spot, along(step)) for step in range(1, tensor)]
        + [(chip_at(step) * 2 + core, place) for step in range(1, chips)]
        + [partner]
    )

    def pass_on(part, piece, fresh):
        at = pl.ds(part * rows + piece * PIECE, PIECE)
        source = own_ref.at[pl.ds(piece * PIECE, PIECE)] if fresh else seen_ref.at[at]
        return pltpu.make_async_remote_copy(
            src_ref=source, dst_ref=seen_ref.at[at],
            send_sem=row_send.at[part, piece], recv_sem=row_recv.at[part, piece],
            device_id=(spot, lax.rem(place + 1, tensor)), device_id_type=MESH,
        )

    def line(step):
        return pltpu.make_async_remote_copy(
            src_ref=block_ref, dst_ref=weights_ref.at[place, spot],
            send_sem=line_send.at[step], recv_sem=line_recv.at[place],
            device_id=(spot, along(step)), device_id_type=MESH,
        )

    def line_in(step):
        source = along(tensor - step)
        return pltpu.make_async_remote_copy(
            src_ref=block_ref, dst_ref=weights_ref.at[source, spot],
            send_sem=line_send.at[step], recv_sem=line_recv.at[source],
            device_id=(spot, along(step)), device_id_type=MESH,
        )

    def plane(part, step):
        block = weights_ref.at[part, spot]
        return pltpu.make_async_remote_copy(
            src_ref=block, dst_ref=block,
            send_sem=chip_send.at[part, step], recv_sem=chip_recv.at[part, chip],
            device_id=(chip_at(step) * 2 + core, place), device_id_type=MESH,
        )

    def plane_in(part, step):
        source = chip_at(chips - step)
        block = weights_ref.at[part, source * 2 + core]
        return pltpu.make_async_remote_copy(
            src_ref=block, dst_ref=block,
            send_sem=chip_send.at[part, step], recv_sem=chip_recv.at[part, source],
            device_id=(chip_at(step) * 2 + core, place), device_id_type=MESH,
        )

    def across(part, source, source_core):
        block = weights_ref.at[part, source * 2 + source_core]
        return pltpu.make_async_remote_copy(
            src_ref=block, dst_ref=block,
            send_sem=pair_send.at[part, source], recv_sem=pair_recv.at[part, source],
            device_id=partner, device_id_type=MESH,
        )

    for step in range(1, tensor):
        line(step).start()

    def row_steps(first, last):
        @pl.loop(first, last)
        def _(piece):
            @pl.when(place == 0)
            def _():
                pass_on(0, piece, True).start()

            @pl.when(place > 0)
            def _():
                pass_on(0, piece, False).wait_recv()

            @pl.when((place > 0) & (place < tensor - 1))
            def _():
                pass_on(0, piece, False).start()

            @pl.when(place == 1)
            def _():
                pass_on(1, piece, True).start()

            @pl.when(place > 1)
            def _():
                pass_on(1, piece, False).wait_recv()

            @pl.when((place > 1) & (place < tensor - 1))
            def _():
                pass_on(1, piece, False).start()

    weights_ref[place, spot] = block_ref[...]
    seen_ref[2 * rows :] = own_ref[...]

    @pl.when(place < 2)
    def _():
        seen_ref[rows : 2 * rows] = own_ref[...]

    @pl.when(place == 0)
    def _():
        seen_ref[0:rows] = own_ref[...]

    row_steps(0, pieces // 4)
    for step in range(tensor):
        part = along(tensor - step)
        if step:
            line_in(step).wait_recv()

        @pl.loop(1, chips)
        def _(hop):
            plane(part, hop).start()

        across(part, chip, core).start()
    row_steps(pieces // 4, (pieces * 5) // 8)
    for step in range(tensor):
        part = along(tensor - step)

        @pl.loop(1, chips)
        def _(hop):
            plane_in(part, hop).wait_recv()
            across(part, chip_at(chips - hop), core).start()

    row_steps((pieces * 5) // 8, pieces)
    for part in range(tensor):

        @pl.loop(0, chips)
        def _(source):
            across(part, source, 1 - core).wait_recv()
            across(part, source, core).wait_send()

        @pl.loop(1, chips)
        def _(hop):
            plane(part, hop).wait_send()

    for step in range(1, tensor):
        line(step).wait_send()

    @pl.when(place < tensor - 1)
    def _():
        @pl.loop(0, pieces)
        def _(piece):
            pass_on(0, piece, False).wait_send()

    @pl.when((place > 0) & (place < tensor - 1))
    def _():
        @pl.loop(0, pieces)
        def _(piece):
            pass_on(1, piece, False).wait_send()

    @pl.loop(0, dp)
    def _(source):
        depth = block_ref.shape[0]
        at = pl.ds(pl.multiple_of(source * depth, depth), depth)
        for kind in range(out_ref.shape[0]):
            cols = slice(kind * part_width, (kind + 1) * part_width)
            out_ref[kind, at] = jnp.concatenate(
                [weights_ref[part, source][:, cols] for part in range(tensor)], axis=1
            )


def share_rows_and_weights(own, block):
    dp, tensor = lax.axis_size("dp"), lax.axis_size("tensor")
    rows, width = own.shape
    depth, cols = block.shape
    pieces, chips = rows // PIECE, dp // 2
    kinds = cols * tensor // width
    padded = -(-depth // 16) * 16
    block = jnp.pad(block, ((0, padded - depth), (0, 0)))
    dma = pltpu.SemaphoreType.DMA
    here = pl.BlockSpec(memory_space=pltpu.VMEM)
    seen, weights = pl.pallas_call(
        lambda *refs: share_kernel(dp, tensor, *refs),
        out_shape=(
            jax.ShapeDtypeStruct((3 * rows, width), own.dtype),
            jax.ShapeDtypeStruct((kinds, dp * padded, width), block.dtype),
        ),
        in_specs=[here, here],
        out_specs=[here, here],
        scratch_shapes=[
            pltpu.VMEM((tensor, dp, padded, cols), block.dtype),
            dma((2, pieces)), dma((2, pieces)),
            dma((tensor,)), dma((tensor,)),
            dma((tensor, chips)), dma((tensor, chips)),
            dma((tensor, chips)), dma((tensor, chips)),
        ],
        compiler_params=pltpu.CompilerParams(
            collective_id=2, has_side_effects=True, vmem_limit_bytes=48 << 20
        ),
        name="share_rows_and_weights",
    )(own, block)
    weights = weights.reshape(kinds, dp, padded, width)[:, :, :depth]
    return seen, weights.reshape(kinds, dp * depth, width)


def gather_grads_kernel(dp, tensor, rows_ref, grads_ref, out_ref, sum_ref,
                        land_ref, pass_ref, grad_land, grad_sum, line_out, line_land,
                        row_send, row_recv, grad_send, grad_recv, line_send, line_recv):
    spot, place = lax.axis_index("dp"), lax.axis_index("tensor")
    rows = out_ref.shape[0]
    pieces = rows // PIECE
    parts = grads_ref.shape[2] // (tensor * sum_ref.shape[1] // 4)
    share = sum_ref.shape[1] // parts

    def along(step):
        return lax.rem(place + step, tensor)

    def peer(step):
        return lax.rem(spot + step, dp)

    greet(
        [(spot, along(step)) for step in range(1, tensor)]
        + [(peer(step), place) for step in range(1, dp)]
    )

    def pass_down(piece, fresh):
        at = pl.ds(piece * PIECE, PIECE)
        source = rows_ref if fresh else pass_ref
        return pltpu.make_async_remote_copy(
            src_ref=source.at[at], dst_ref=land_ref.at[at],
            send_sem=row_send.at[piece], recv_sem=row_recv.at[piece],
            device_id=(spot, lax.rem(place + tensor - 1, tensor)), device_id_type=MESH,
        )

    def give(step):
        return pltpu.make_async_remote_copy(
            src_ref=grads_ref.at[peer(step)], dst_ref=grad_land.at[spot],
            send_sem=grad_send.at[step], recv_sem=grad_recv.at[spot],
            device_id=(peer(step), place), device_id_type=MESH,
        )

    def take(step):
        source = peer(dp - step)
        return pltpu.make_async_remote_copy(
            src_ref=grads_ref.at[source], dst_ref=grad_land.at[source],
            send_sem=grad_send.at[step], recv_sem=grad_recv.at[source],
            device_id=(peer(step), place), device_id_type=MESH,
        )

    def line(step):
        return pltpu.make_async_remote_copy(
            src_ref=line_out.at[along(step)], dst_ref=line_land.at[place],
            send_sem=line_send.at[step], recv_sem=line_recv.at[place],
            device_id=(spot, along(step)), device_id_type=MESH,
        )

    def line_in(step):
        source = along(tensor - step)
        return pltpu.make_async_remote_copy(
            src_ref=line_out.at[source], dst_ref=line_land.at[source],
            send_sem=line_send.at[step], recv_sem=line_recv.at[source],
            device_id=(spot, along(step)), device_id_type=MESH,
        )

    @pl.when(place == tensor - 1)
    def _():
        @pl.loop(0, 2 * pieces)
        def _(piece):
            pass_down(piece, True).start()

    @pl.loop(1, dp)
    def _(step):
        give(step).start()

    @pl.when(place > 1)
    def _():
        out_ref[...] = jnp.zeros_like(out_ref)

    def row_steps(first, last):
        @pl.loop(first, last)
        def _(piece):
            trunk = piece < pieces
            at = pl.ds(pl.multiple_of(piece * PIECE, PIECE), PIECE)
            takes = (place < tensor - 1) & ((place > 0) | trunk)
            sends = takes & (place > 0) & ((place > 1) | trunk)

            @pl.when(takes)
            def _():
                pass_down(piece, False).wait_recv()

            @pl.when(sends)
            def _():
                total = rows_ref[at].astype(jnp.float32) + land_ref[at].astype(jnp.float32)
                pass_ref[at] = total.astype(pass_ref.dtype)
                pass_down(piece, False).start()

            @pl.when(takes & jnp.logical_not(sends))
            def _():
                total = rows_ref[at].astype(jnp.float32) + land_ref[at].astype(jnp.float32)
                here = lax.rem(piece, pieces) * PIECE
                out_ref[pl.ds(pl.multiple_of(here, PIECE), PIECE)] = total

    row_steps(0, pieces + pieces // 2)
    grad_sum[...] = grads_ref[spot].astype(jnp.float32)

    @pl.loop(1, dp)
    def _(step):
        take(step).wait_recv()
        grad_sum[...] += grad_land[peer(dp - step)].astype(jnp.float32)

    for target in range(tensor):
        mine = jnp.concatenate(
            [
                grad_sum[:, (part * tensor + target) * share : (part * tensor + target + 1) * share]
                for part in range(parts)
            ],
            axis=1,
        )
        line_out[target] = mine.astype(line_out.dtype)

        @pl.when(place == target)
        def _():
            sum_ref[...] = mine

    for step in range(1, tensor):
        line(step).start()
    row_steps(pieces + pieces // 2, 2 * pieces)
    for step in range(1, tensor):
        line_in(step).wait_recv()
        sum_ref[...] += line_land[along(tensor - step)].astype(jnp.float32)
    for step in range(1, tensor):
        line(step).wait_send()

    @pl.loop(1, dp)
    def _(step):
        give(step).wait_send()

    @pl.loop(0, 2 * pieces)
    def _(piece):
        sends = (place > 0) & ((place > 1) | (piece < pieces))

        @pl.when(sends)
        def _():
            pass_down(piece, True).wait_send()


def collect_grads(rows, grads):
    dp, tensor = lax.axis_size("dp"), lax.axis_size("tensor")
    count, width = rows.shape[0] // 2, rows.shape[1]
    depth = grads.shape[0] // dp
    grads = grads.reshape(dp, depth, grads.shape[1])
    slab = grads.shape[2] // tensor
    pieces = count // PIECE
    dma = pltpu.SemaphoreType.DMA
    here = pl.BlockSpec(memory_space=pltpu.VMEM)
    return pl.pallas_call(
        lambda *refs: gather_grads_kernel(dp, tensor, *refs),
        out_shape=(
            jax.ShapeDtypeStruct((count, width), jnp.float32),
            jax.ShapeDtypeStruct((depth, slab), jnp.float32),
        ),
        in_specs=[here, here],
        out_specs=[here, here],
        scratch_shapes=[
            pltpu.VMEM(rows.shape, rows.dtype),
            pltpu.VMEM(rows.shape, rows.dtype),
            pltpu.VMEM(grads.shape, grads.dtype),
            pltpu.VMEM(grads.shape[1:], jnp.float32),
            pltpu.VMEM((tensor, depth, slab), grads.dtype),
            pltpu.VMEM((tensor, depth, slab), grads.dtype),
            dma((2 * pieces,)), dma((2 * pieces,)),
            dma((dp,)), dma((dp,)), dma((tensor,)), dma((tensor,)),
        ],
        compiler_params=pltpu.CompilerParams(
            collective_id=3, has_side_effects=True, vmem_limit_bytes=56 << 20
        ),
        name="collect_grads",
    )(rows, grads)


norm_eps = 1e-05
route_scale = 3.0
masked_score = -1e30
highest = lax.Precision.HIGHEST


def layer_norm(values, norm_gain):
    centred = values - jnp.mean(values, axis=-1, keepdims=True)
    spread = jnp.mean(centred * centred, axis=-1, keepdims=True)
    return centred * lax.rsqrt(spread + norm_eps) * norm_gain


def unit_rows(values):
    return values * lax.rsqrt(jnp.sum(values * values, axis=-1, keepdims=True) + 1.0)


def router_gate(normed, router_proj, expert_embed, picked):
    routed = jnp.dot(normed, router_proj, precision=highest)
    logits = route_scale * jnp.dot(unit_rows(routed), unit_rows(expert_embed).T, precision=highest)
    return jnp.sum(jax.nn.softmax(logits, axis=-1) * picked, axis=-1)


def gelu_exact(values):
    return jax.nn.gelu(values, approximate=False)


def slot_table(route_ids, order_ids, capacity):
    same_expert = route_ids[:, None] == route_ids[None, :]
    earlier = order_ids[None, :] < order_ids[:, None]
    ranking = jnp.sum(jnp.where(same_expert & earlier, 1, 0), axis=1).astype(jnp.int32)
    kept_mask = ranking < capacity
    column = route_ids * capacity + jnp.minimum(ranking, capacity - 1)
    return (column, kept_mask)


def low_dot(rows, weight):
    return jnp.dot(rows, weight, preferred_element_type=jnp.float32).astype(jnp.bfloat16)


def shards(
    tokens,
    norm1_gain,
    qkv_weight,
    attn_proj,
    norm2_gain,
    router_proj,
    expert_embed,
    expert_in,
    expert_out,
    routes,
    orders,
    leaf_parent,
    cotangent,
):
    rows_here = tokens.shape[0]
    model_width = tokens.shape[1]
    experts = expert_embed.shape[0]
    capacity = rows_here // experts
    dp_size, tensor_size = lax.axis_size("dp"), lax.axis_size("tensor")
    leaf_parents = leaf_parent[0]

    def hop(rows, chip_step, core_step):
        route = []
        for source in range(dp_size):
            chip, core = source // 2, source % 2
            route.append((source, (chip ^ chip_step) * 2 + (core ^ core_step)))
        return lax.ppermute(rows, "dp", route)

    def chip_blocks(rows):
        blocks = rows.reshape(experts, capacity, model_width)
        return [blocks[0]] + [hop(blocks[step], step, 0) for step in range(1, experts)]

    def across_chips(rows):
        return jnp.concatenate(chip_blocks(rows), axis=0)

    def with_partner(blocks):
        arrived = jnp.concatenate(blocks, axis=0)
        return jnp.concatenate([arrived, hop(arrived, 0, 1)], axis=0)

    def pair_sum(kept_rows, sent_rows):
        return (kept_rows + hop(sent_rows, 0, 1).astype(jnp.float32)).astype(jnp.bfloat16)

    hidden = tokens.astype(jnp.float32)
    normed_in, norm1_back = jax.vjp(layer_norm, hidden, norm1_gain)
    own_in = normed_in.astype(jnp.bfloat16)
    flat_qkv = qkv_weight.reshape(qkv_weight.shape[0], -1)
    seen_in, weights = share_rows_and_weights(
        own_in, jnp.concatenate([flat_qkv, attn_proj.T], axis=1)
    )
    query_weight, key_weight, value_weight, proj_back = weights
    query_rows = low_dot(own_in, query_weight)
    key_rows = low_dot(seen_in, key_weight)
    value_rows = low_dot(seen_in, value_weight)
    place = lax.axis_index("tensor")
    leaf_blocks = rows_here // BRANCH
    first_leaf = jnp.maximum(place - 2, 0) * leaf_blocks
    parents = lax.dynamic_slice_in_dim(leaf_parents, first_leaf, leaf_blocks, 0) - 1
    meta = jnp.concatenate([place[None], parents]).astype(jnp.int32)
    attended, log_totals = attend(meta, query_rows, key_rows, value_rows)
    branch_out = jnp.einsum(
        "sc,dc->sd", attended, proj_back, preferred_element_type=jnp.float32
    )
    mid_stream = hidden + branch_out
    normed_mid, norm2_back = jax.vjp(layer_norm, mid_stream, norm2_gain)
    moe_in = normed_mid.astype(jnp.bfloat16)
    route_ids = routes[:, 0]
    near_route = route_ids ^ (lax.axis_index("dp") // 2)
    column, kept_mask = slot_table(near_route, orders[0], capacity)
    picked = (route_ids[:, None] == jnp.arange(experts)[None, :]).astype(jnp.float32)
    gate_value, gate_back = jax.vjp(
        lambda normed_rows, route_proj, embed_rows: router_gate(
            normed_rows, route_proj, embed_rows, picked
        ),
        moe_in.astype(jnp.float32),
        router_proj,
        expert_embed,
    )
    select = (
        (column[:, None] == jnp.arange(experts * capacity)[None, :]) & kept_mask[:, None]
    ).astype(jnp.bfloat16)
    def to_slots(token_rows):
        return jnp.einsum(
            "ts,td->sd", select, token_rows, preferred_element_type=jnp.float32
        ).astype(jnp.bfloat16)

    def from_slots(slot_rows):
        return jnp.dot(select, slot_rows, preferred_element_type=jnp.float32)

    upstream = cotangent.astype(jnp.float32)
    slot_grads = to_slots((gate_value[:, None] * upstream).astype(jnp.bfloat16))
    row_blocks, slot_grads = lax.optimization_barrier(
        (chip_blocks(to_slots(moe_in)), slot_grads)
    )
    grad_blocks = chip_blocks(slot_grads)
    expert_rows = with_partner(row_blocks)
    active, slope, kept_result, sent_result = expert_forward(expert_rows, expert_in, expert_out)
    grad_blocks, kept_result, sent_result = lax.optimization_barrier(
        (grad_blocks, kept_result, sent_result)
    )
    arrived_grad = with_partner(grad_blocks)
    result_rows, late_grad = lax.optimization_barrier(
        (pair_sum(kept_result, sent_result), arrived_grad)
    )
    expert_result = from_slots(across_chips(result_rows))
    output = (mid_stream + gate_value[:, None] * expert_result).astype(jnp.bfloat16)
    out_weight_grad = jnp.einsum(
        "rf,rd->fd", active, arrived_grad, preferred_element_type=jnp.float32
    ).astype(jnp.bfloat16)
    up_grad, kept_grad, sent_grad = expert_back(late_grad, slope, expert_in, expert_out)
    in_weight_grad = jnp.einsum(
        "rd,rf->df", expert_rows, up_grad, preferred_element_type=jnp.float32
    ).astype(jnp.bfloat16)
    moe_grad = from_slots(across_chips(pair_sum(kept_grad, sent_grad)))
    gate_grad = jnp.sum(upstream * expert_result, axis=-1)
    router_part, proj_grad, embed_grad = gate_back(gate_grad)
    mid_part, gain2_grad = norm2_back(moe_grad + router_part)
    mid_grad = upstream + mid_part
    mid_grad, in_weight_grad, out_weight_grad = lax.optimization_barrier(
        (mid_grad, in_weight_grad, out_weight_grad)
    )
    expert_in_grad, expert_out_grad = (
        lax.psum_scatter(in_weight_grad, "tensor", scatter_dimension=1, tiled=True).astype(
            jnp.float32
        ),
        lax.psum_scatter(out_weight_grad, "tensor", scatter_dimension=0, tiled=True).astype(
            jnp.float32
        ),
    )
    branch_grad = mid_grad.astype(jnp.bfloat16)
    attended_grad = jnp.einsum(
        "sd,dc->sc", branch_grad, proj_back, preferred_element_type=jnp.float32
    ).astype(jnp.bfloat16)
    query_grad, key_grad, value_grad = attend_back(
        meta, query_rows, key_rows, value_rows, attended, attended_grad, log_totals
    )

    def weight_grad(rows, row_grads):
        return jnp.einsum("sd,sc->dc", rows, row_grads, preferred_element_type=jnp.float32)

    def row_grad(row_grads, weight):
        return jnp.einsum("sc,dc->sd", row_grads, weight, preferred_element_type=jnp.float32)

    weight_grads = jnp.concatenate(
        [
            weight_grad(own_in, query_grad),
            weight_grad(seen_in, key_grad),
            weight_grad(seen_in, value_grad),
            weight_grad(branch_grad, attended),
        ],
        axis=1,
    ).astype(jnp.bfloat16)
    seen_grad = row_grad(key_grad, key_weight) + row_grad(value_grad, value_weight)
    own_grad = seen_grad[2 * TRUNK :] + row_grad(query_grad, query_weight)
    arrived_rows, grad_block = collect_grads(
        seen_grad[: 2 * TRUNK].astype(jnp.bfloat16), weight_grads
    )
    input_grad = own_grad + arrived_rows
    qkv_grad = grad_block[:, : flat_qkv.shape[1]].reshape(qkv_weight.shape)
    attn_proj_grad = grad_block[:, flat_qkv.shape[1] :].T
    token_part, gain1_grad = norm1_back(input_grad)
    token_grad = mid_grad + token_part
    gain1_sum, gain2_sum, router_sum, embed_sum = total_over_devices(
        (gain1_grad, gain2_grad, proj_grad, embed_grad)
    )
    return (
        output,
        token_grad,
        gain1_sum,
        qkv_grad,
        attn_proj_grad,
        gain2_sum,
        router_sum,
        embed_sum,
        expert_in_grad,
        expert_out_grad,
    )


def solution(mesh):
    in_specs = (
        P(("dp", "tensor"), None),
        P(),
        P("dp", None, "tensor"),
        P("tensor", "dp"),
        P(),
        P(),
        P(),
        P(None, "dp"),
        P("dp", None),
        P(("dp", "tensor"), None),
        P(("dp", "tensor"), None),
        P("dp", None),
        P(("dp", "tensor"), None),
    )
    out_specs = (
        P(("dp", "tensor"), None),
        P(("dp", "tensor"), None),
        P(),
        P("dp", None, "tensor"),
        P("tensor", "dp"),
        P(),
        P(),
        P(),
        P(None, ("dp", "tensor")),
        P(("dp", "tensor"), None),
    )
    return jax.shard_map(shards, mesh=mesh, in_specs=in_specs, out_specs=out_specs, check_vma=False)
```

```python
import math

import jax
import jax.numpy as jnp
from jax import lax
from jax.experimental import pallas as pl
from jax.experimental.pallas import tpu as pltpu
from jax.sharding import PartitionSpec as P

HEAD_DIM = 64
TRUNK = 1024
BRANCH = 256
MASKED = -1e30
LOG2E = math.log2(math.e)
EXP_SCALE = HEAD_DIM ** (-0.5) * LOG2E

NT = (((1,), (1,)), ((), ()))
NN = (((1,), (0,)), ((), ()))


def dot_nt(a, b):
    return lax.dot_general(a, b, NT, preferred_element_type=jnp.float32)


def dot_nn(a, b):
    return lax.dot_general(a, b, NN, preferred_element_type=jnp.float32)


def head_lanes(shape, dim, head):
    return lax.broadcasted_iota(jnp.int32, shape, dim) // HEAD_DIM == head


def fwd_kernel(meta_ref, q_ref, k_ref, v_ref, o_ref, lse_ref, vt_ref):
    block = pl.program_id(1)
    place = meta_ref[0]
    parent_row = pl.multiple_of(TRUNK + block * BRANCH, BRANCH)
    own_row = pl.multiple_of(2 * TRUNK + block * BRANCH, BRANCH)
    width = k_ref.shape[1]

    @pl.when(block == 0)
    def _():
        flipped = v_ref[...].T
        for head in range(2):
            vt_ref[head] = jnp.where(
                head_lanes(flipped.shape, 0, head), flipped, jnp.ones_like(flipped)
            )

    queries = q_ref[...]

    def finish(outs):
        rows = []
        for head, (acc, top) in enumerate(outs):
            mine, other = head * HEAD_DIM, (1 - head) * HEAD_DIM
            total = acc[other : other + 1]
            rows.append(acc[mine : mine + HEAD_DIM] / total)
            lse_ref[0, head : head + 1, :] = top * EXP_SCALE + jnp.log2(total)
        o_ref[...] = jnp.concatenate(rows, axis=0).T.astype(o_ref.dtype)

    def probs(scores, top):
        return jnp.exp2(scores * EXP_SCALE - top * EXP_SCALE).astype(jnp.bfloat16)

    def masked_queries(head):
        return jnp.where(head_lanes(queries.shape, 1, head), queries, jnp.zeros_like(queries))

    @pl.when(place == 0)
    def _():
        outs = []
        for head in range(2):
            scores = dot_nt(k_ref[0:TRUNK], masked_queries(head))
            keys = lax.broadcasted_iota(jnp.int32, scores.shape, 0)
            rows = lax.broadcasted_iota(jnp.int32, scores.shape, 1) + block * BRANCH
            scores = jnp.where(keys <= rows, scores, MASKED)
            top = jnp.max(scores, axis=0, keepdims=True)
            outs.append((dot_nn(vt_ref[head, :, 0:TRUNK], probs(scores, top)), top))
        finish(outs)

    @pl.when(place > 0)
    def _():
        outs = []
        for head in range(2):
            qm = masked_queries(head)
            trunk = dot_nt(k_ref[0:TRUNK], qm)
            parent = dot_nt(k_ref[pl.ds(parent_row, BRANCH)], qm)
            parent = jnp.where(place > 1, parent, MASKED)
            own = dot_nt(k_ref[pl.ds(own_row, BRANCH)], qm)
            keys = lax.broadcasted_iota(jnp.int32, own.shape, 0)
            rows = lax.broadcasted_iota(jnp.int32, own.shape, 1)
            own = jnp.where(keys <= rows, own, MASKED)
            top = jnp.maximum(
                jnp.maximum(
                    jnp.max(trunk, axis=0, keepdims=True), jnp.max(parent, axis=0, keepdims=True)
                ),
                jnp.max(own, axis=0, keepdims=True),
            )
            acc = dot_nn(vt_ref[head, :, 0:TRUNK], probs(trunk, top))
            acc = acc + dot_nn(vt_ref[head, :, pl.ds(parent_row, BRANCH)], probs(parent, top))
            acc = acc + dot_nn(vt_ref[head, :, pl.ds(own_row, BRANCH)], probs(own, top))
            outs.append((acc, top))
        finish(outs)


def attend(meta, q, k, v):
    rows, width = q.shape
    keys = k.shape[0]
    pairs = width // 128
    blocks = rows // BRANCH
    return pl.pallas_call(
        fwd_kernel,
        out_shape=(
            jax.ShapeDtypeStruct((rows, width), jnp.bfloat16),
            jax.ShapeDtypeStruct((pairs, 2, rows), jnp.float32),
        ),
        grid_spec=pltpu.PrefetchScalarGridSpec(
            num_scalar_prefetch=1,
            grid=(pairs, blocks),
            in_specs=[
                pl.BlockSpec((BRANCH, 128), lambda p, i, m: (i, p)),
                pl.BlockSpec((keys, 128), lambda p, i, m: (0, p)),
                pl.BlockSpec((keys, 128), lambda p, i, m: (0, p)),
            ],
            out_specs=[
                pl.BlockSpec((BRANCH, 128), lambda p, i, m: (i, p)),
                pl.BlockSpec((1, 2, BRANCH), lambda p, i, m: (p, 0, i)),
            ],
            scratch_shapes=[pltpu.VMEM((2, 128, keys), jnp.bfloat16)],
        ),
        compiler_params=pltpu.CompilerParams(vmem_limit_bytes=40 << 20),
        name="attend_forward",
    )(meta, q, k, v)


ROWS = 256
HALF_ROOT = math.sqrt(0.5)
PDF_SCALE = 1.0 / math.sqrt(2.0 * math.pi)
CHUNK = 512


def expert_fwd_kernel(x_ref, in_ref, out_ref, active_ref, slope_ref, keep_ref, send_ref):
    step = pl.program_id(0)
    half = pl.num_programs(0) // 2
    rows = x_ref[...]
    total = None
    for first in range(0, in_ref.shape[1], CHUNK):
        cols = slice(first, first + CHUNK)
        up = dot_nn(rows, in_ref[:, cols])
        below = 0.5 * (1.0 + lax.erf(up * HALF_ROOT))
        active = (up * below).astype(jnp.bfloat16)
        slope = below + up * (jnp.exp(-0.5 * up * up) * PDF_SCALE)
        active_ref[:, cols] = active
        slope_ref[:, cols] = slope.astype(jnp.bfloat16)
        part = dot_nn(active, out_ref[cols])
        total = part if total is None else total + part

    @pl.when(step < half)
    def _():
        keep_ref[...] = total

    @pl.when(step >= half)
    def _():
        send_ref[...] = total.astype(send_ref.dtype)


def expert_bwd_kernel(grad_ref, slope_ref, in_ref, out_ref, upgrad_ref, keep_ref, send_ref):
    step = pl.program_id(0)
    half = pl.num_programs(0) // 2
    grads = grad_ref[...]
    total = None
    for first in range(0, in_ref.shape[1], CHUNK):
        cols = slice(first, first + CHUNK)
        active_grad = dot_nt(grads, out_ref[cols])
        up_grad = (active_grad * slope_ref[:, cols].astype(jnp.float32)).astype(jnp.bfloat16)
        upgrad_ref[:, cols] = up_grad
        part = dot_nt(up_grad, in_ref[:, cols])
        total = part if total is None else total + part

    @pl.when(step < half)
    def _():
        keep_ref[...] = total

    @pl.when(step >= half)
    def _():
        send_ref[...] = total.astype(send_ref.dtype)


def split_specs(count, width):
    half = count // 2
    return [
        pl.BlockSpec((ROWS, width), lambda i: (jnp.minimum(i, half - 1), 0)),
        pl.BlockSpec((ROWS, width), lambda i: (jnp.maximum(i - half, 0), 0)),
    ]


def expert_forward(x, w_in, w_out):
    rows, width = x.shape
    hidden = w_in.shape[1]
    count = rows // ROWS
    def wide(cols):
        return pl.BlockSpec((ROWS, cols), lambda i: (i, 0))
    def whole(shape):
        return pl.BlockSpec(shape, lambda i: (0, 0), pipeline_mode=pl.Buffered(1))
    return pl.pallas_call(
        expert_fwd_kernel,
        grid=(count,),
        in_specs=[wide(width), whole(w_in.shape), whole(w_out.shape)],
        out_specs=[wide(hidden), wide(hidden)] + split_specs(count, width),
        out_shape=(
            jax.ShapeDtypeStruct((rows, hidden), jnp.bfloat16),
            jax.ShapeDtypeStruct((rows, hidden), jnp.bfloat16),
            jax.ShapeDtypeStruct((rows // 2, width), jnp.float32),
            jax.ShapeDtypeStruct((rows // 2, width), jnp.bfloat16),
        ),
        cost_estimate=pl.CostEstimate(flops=4 * rows * width * hidden, bytes_accessed=24 << 20, transcendentals=2 * rows * hidden),
        compiler_params=pltpu.CompilerParams(vmem_limit_bytes=40 << 20),
        name="expert_forward",
    )(x, w_in, w_out)


def expert_back(grads, slope, w_in, w_out):
    rows, width = grads.shape
    hidden = w_in.shape[1]
    count = rows // ROWS
    def wide(cols):
        return pl.BlockSpec((ROWS, cols), lambda i: (i, 0))
    def whole(shape):
        return pl.BlockSpec(shape, lambda i: (0, 0), pipeline_mode=pl.Buffered(1))
    return pl.pallas_call(
        expert_bwd_kernel,
        grid=(count,),
        in_specs=[wide(width), wide(hidden), whole(w_in.shape), whole(w_out.shape)],
        out_specs=[wide(hidden)] + split_specs(count, width),
        out_shape=(
            jax.ShapeDtypeStruct((rows, hidden), jnp.bfloat16),
            jax.ShapeDtypeStruct((rows // 2, width), jnp.float32),
            jax.ShapeDtypeStruct((rows // 2, width), jnp.bfloat16),
        ),
        cost_estimate=pl.CostEstimate(flops=4 * rows * width * hidden, bytes_accessed=24 << 20, transcendentals=0),
        compiler_params=pltpu.CompilerParams(vmem_limit_bytes=40 << 20),
        name="expert_backward",
    )(grads, slope, w_in, w_out)


MESH = pl.DeviceIdType.MESH


PIECE = 64


def greet(peers):
    barrier = pltpu.get_barrier_semaphore()
    for peer in peers:
        pl.semaphore_signal(barrier, inc=1, device_id=peer, device_id_type=MESH)
    pl.semaphore_wait(barrier, len(peers))


def share_kernel(dp, tensor, own_ref, block_ref, parent_ref, seen_ref, out_ref, weights_ref,
                 ordered_ref, row_send, row_recv,
                 line_send, line_recv, chip_send, chip_recv, pair_send, pair_recv):
    spot, place = lax.axis_index("dp"), lax.axis_index("tensor")
    chip, core = spot // 2, lax.rem(spot, 2)
    chips = dp // 2
    rows = own_ref.shape[0]
    pieces = rows // PIECE
    part_width = out_ref.shape[2] // tensor
    partner = (chip * 2 + 1 - core, place)

    def along(step):
        return lax.rem(place + step, tensor)

    def chip_at(step):
        return lax.rem(chip + step, chips)

    greet(
        [(spot, along(step)) for step in range(1, tensor)]
        + [(chip_at(step) * 2 + core, place) for step in range(1, chips)]
        + [partner]
    )

    def pass_on(part, piece, fresh):
        at = pl.ds(part * rows + piece * PIECE, PIECE)
        source = own_ref.at[pl.ds(piece * PIECE, PIECE)] if fresh else seen_ref.at[at]
        return pltpu.make_async_remote_copy(
            src_ref=source, dst_ref=seen_ref.at[at],
            send_sem=row_send.at[part, piece], recv_sem=row_recv.at[part, piece],
            device_id=(spot, lax.rem(place + 1, tensor)), device_id_type=MESH,
        )

    def line(step):
        return pltpu.make_async_remote_copy(
            src_ref=block_ref, dst_ref=weights_ref.at[place, spot],
            send_sem=line_send.at[step], recv_sem=line_recv.at[place],
            device_id=(spot, along(step)), device_id_type=MESH,
        )

    def line_in(step):
        source = along(tensor - step)
        return pltpu.make_async_remote_copy(
            src_ref=block_ref, dst_ref=weights_ref.at[source, spot],
            send_sem=line_send.at[step], recv_sem=line_recv.at[source],
            device_id=(spot, along(step)), device_id_type=MESH,
        )

    def plane(part, step):
        block = weights_ref.at[part, spot]
        return pltpu.make_async_remote_copy(
            src_ref=block, dst_ref=block,
            send_sem=chip_send.at[part, step], recv_sem=chip_recv.at[part, chip],
            device_id=(chip_at(step) * 2 + core, place), device_id_type=MESH,
        )

    def plane_in(part, step):
        source = chip_at(chips - step)
        block = weights_ref.at[part, source * 2 + core]
        return pltpu.make_async_remote_copy(
            src_ref=block, dst_ref=block,
            send_sem=chip_send.at[part, step], recv_sem=chip_recv.at[part, source],
            device_id=(chip_at(step) * 2 + core, place), device_id_type=MESH,
        )

    def across(part, source, source_core):
        block = weights_ref.at[part, source * 2 + source_core]
        return pltpu.make_async_remote_copy(
            src_ref=block, dst_ref=block,
            send_sem=pair_send.at[part, source], recv_sem=pair_recv.at[part, source],
            device_id=partner, device_id_type=MESH,
        )

    for step in range(1, tensor):
        line(step).start()

    def row_steps(first, last):
        @pl.loop(first, last)
        def _(piece):
            @pl.when(place == 0)
            def _():
                pass_on(0, piece, True).start()

            @pl.when(place > 0)
            def _():
                pass_on(0, piece, False).wait_recv()

            @pl.when((place > 0) & (place < tensor - 1))
            def _():
                pass_on(0, piece, False).start()

            @pl.when(place == 1)
            def _():
                pass_on(1, piece, True).start()

            @pl.when(place > 1)
            def _():
                pass_on(1, piece, False).wait_recv()

            @pl.when((place > 1) & (place < tensor - 1))
            def _():
                pass_on(1, piece, False).start()

    weights_ref[place, spot] = block_ref[...]
    seen_ref[2 * rows :] = own_ref[...]

    @pl.when(place < 2)
    def _():
        seen_ref[rows : 2 * rows] = own_ref[...]

    @pl.when(place == 0)
    def _():
        seen_ref[0:rows] = own_ref[...]

    row_steps(0, pieces // 4)
    for step in range(tensor):
        part = along(tensor - step)
        if step:
            line_in(step).wait_recv()

        @pl.loop(1, chips)
        def _(hop):
            plane(part, hop).start()

        across(part, chip, core).start()
    row_steps(pieces // 4, (pieces * 5) // 8)
    for step in range(tensor):
        part = along(tensor - step)

        @pl.loop(1, chips)
        def _(hop):
            plane_in(part, hop).wait_recv()
            across(part, chip_at(chips - hop), core).start()

    row_steps((pieces * 5) // 8, pieces)
    for part in range(tensor):

        @pl.loop(0, chips)
        def _(source):
            across(part, source, 1 - core).wait_recv()
            across(part, source, core).wait_send()

        @pl.loop(1, chips)
        def _(hop):
            plane(part, hop).wait_send()

    for step in range(1, tensor):
        line(step).wait_send()

    @pl.when(place < tensor - 1)
    def _():
        @pl.loop(0, pieces)
        def _(piece):
            pass_on(0, piece, False).wait_send()

    @pl.when((place > 0) & (place < tensor - 1))
    def _():
        @pl.loop(0, pieces)
        def _(piece):
            pass_on(1, piece, False).wait_send()

    @pl.when(place > 1)
    def _():
        blocks = rows // BRANCH
        branches = [
            seen_ref[rows + branch * BRANCH : rows + (branch + 1) * BRANCH]
            for branch in range(blocks)
        ]
        for leaf in range(blocks):
            chosen = None
            for branch in range(blocks):
                at = leaf * blocks + branch
                part = branches[branch] * parent_ref[at : at + 1].astype(own_ref.dtype)
                chosen = part if chosen is None else chosen + part
            ordered_ref[leaf * BRANCH : (leaf + 1) * BRANCH] = chosen
        seen_ref[rows : 2 * rows] = ordered_ref[...]

    @pl.loop(0, dp)
    def _(source):
        depth = block_ref.shape[0]
        at = pl.ds(pl.multiple_of(source * depth, depth), depth)
        for kind in range(out_ref.shape[0]):
            cols = slice(kind * part_width, (kind + 1) * part_width)
            out_ref[kind, at] = jnp.concatenate(
                [weights_ref[part, source][:, cols] for part in range(tensor)], axis=1
            )


def share_rows_and_weights(own, block, parents):
    dp, tensor = lax.axis_size("dp"), lax.axis_size("tensor")
    rows, width = own.shape
    depth, cols = block.shape
    pieces, chips = rows // PIECE, dp // 2
    kinds = cols * tensor // width
    padded = -(-depth // 16) * 16
    block = jnp.pad(block, ((0, padded - depth), (0, 0)))
    dma = pltpu.SemaphoreType.DMA
    here = pl.BlockSpec(memory_space=pltpu.VMEM)
    seen, weights = pl.pallas_call(
        lambda *refs: share_kernel(dp, tensor, *refs),
        out_shape=(
            jax.ShapeDtypeStruct((3 * rows, width), own.dtype),
            jax.ShapeDtypeStruct((kinds, dp * padded, width), block.dtype),
        ),
        in_specs=[here, here, here],
        out_specs=[here, here],
        scratch_shapes=[
            pltpu.VMEM((tensor, dp, padded, cols), block.dtype),
            pltpu.VMEM(own.shape, own.dtype),
            dma((2, pieces)), dma((2, pieces)),
            dma((tensor,)), dma((tensor,)),
            dma((tensor, chips)), dma((tensor, chips)),
            dma((tensor, chips)), dma((tensor, chips)),
        ],
        compiler_params=pltpu.CompilerParams(
            collective_id=2, has_side_effects=True, vmem_limit_bytes=48 << 20
        ),
        name="share_rows_and_weights",
    )(own, block, parents)
    weights = weights.reshape(kinds, dp, padded, width)[:, :, :depth]
    return seen, weights.reshape(kinds, dp * depth, width)


TN = (((0,), (0,)), ((), ()))
GROUP = 256


def dot_tn(a, b):
    return lax.dot_general(a, b, TN, preferred_element_type=jnp.float32)


def back_kernel(
    dp, tensor, depth,
    parent_ref, q_in, k_in, v_in, o_in, grad_in, seen_in, weight_in, lse_ref, small_ref,
    out_ref, sum_ref, total_ref,
    q_ref, k_ref, v_ref, o_ref, bg_ref, g_ref, seen_ref, weight_ref,
    kt_ref, qm_ref, gm_ref, delta_ref, dqt_ref,
    rows_ref, land_ref, acc_ref, gain_ref, slab_ref, slab_land, slab_sum,
    line_out, line_land, part_ref, part_land,
    load_sem, pair_sem, row_send, row_recv, slab_send, slab_recv, line_send, line_recv,
    small_send, small_recv, spread_send, spread_recv,
):
    spot, place = lax.axis_index("dp"), lax.axis_index("tensor")
    ways = dp * tensor
    me = spot * tensor + place
    scale = HEAD_DIM ** (-0.5)
    rows, width = q_ref.shape
    pairs = width // 128
    groups = width // GROUP
    blocks = rows // BRANCH
    pieces = rows // PIECE

    def device(index):
        return (index // tensor, lax.rem(index, tensor))

    def along(step):
        return lax.rem(place + step, tensor)

    def peer(step):
        return lax.rem(spot + step, dp)

    barrier = pltpu.get_barrier_semaphore()

    @pl.loop(1, ways)
    def _(step):
        pl.semaphore_signal(
            barrier, inc=1, device_id=device(lax.rem(me + step, ways)), device_id_type=MESH
        )

    def lanes(pair):
        return pl.ds(pl.multiple_of(pair * 128, 128), 128)

    plain_loads = [
        pltpu.make_async_copy(grad_in, bg_ref, load_sem.at[0]),
        pltpu.make_async_copy(weight_in, weight_ref, load_sem.at[1]),
        pltpu.make_async_copy(seen_in, seen_ref, load_sem.at[2]),
    ]

    def pair_loads(pair):
        return [
            pltpu.make_async_copy(
                source.at[:, lanes(pair)], held.at[:, lanes(pair)], pair_sem.at[which, pair]
            )
            for which, (source, held) in enumerate(
                ((q_in, q_ref), (k_in, k_ref), (v_in, v_ref), (o_in, o_ref))
            )
        ]

    plain_loads[0].start()
    plain_loads[1].start()

    @pl.loop(0, pairs)
    def _(pair):
        for load in pair_loads(pair):
            load.start()

    plain_loads[2].start()
    plain_loads[0].wait()
    plain_loads[1].wait()

    @pl.loop(0, blocks)
    def _(b):
        at = pl.ds(pl.multiple_of(b * BRANCH, BRANCH), BRANCH)
        g_ref[at] = dot_nn(bg_ref[at], weight_ref[3]).astype(g_ref.dtype)

    def mask_heads(pair):
        queries, grads = q_ref[:, lanes(pair)], g_ref[:, lanes(pair)]
        for head in range(2):
            mine = head_lanes(queries.shape, 1, head)
            qm_ref[head] = jnp.where(mine, queries, jnp.zeros_like(queries))
            gm_ref[head] = jnp.where(mine, grads, jnp.zeros_like(grads))
        return grads

    def step(pair, key_row, query_row, count, mask_of=None):
        kb = k_ref[pl.ds(key_row, BRANCH), lanes(pair)]
        vb = v_ref[pl.ds(key_row, BRANCH), lanes(pair)]
        dk = dv = None
        at = pl.ds(query_row, count)
        for head in range(2):
            qm, gm = qm_ref[head, at], gm_ref[head, at]
            probs = jnp.exp2(dot_nt(kb, qm) * EXP_SCALE - lse_ref[pair, head : head + 1, at])
            if mask_of is not None:
                probs = mask_of(probs)
            prob_grad = dot_nt(vb, gm) - delta_ref[pair, head : head + 1, at]
            score_grad = (probs * prob_grad).astype(jnp.bfloat16)
            dv_part = dot_nn(probs.astype(jnp.bfloat16), gm)
            dk_part = dot_nn(score_grad, qm)
            dv = dv_part if dv is None else dv + dv_part
            dk = dk_part if dk is None else dk + dk_part
            mine = slice(head * HEAD_DIM, (head + 1) * HEAD_DIM)
            dqt_ref[pair, mine, at] += dot_nn(kt_ref[mine, pl.ds(key_row, BRANCH)], score_grad)
        return dk * scale, dv

    def causal(offset):
        def mask_of(probs):
            keys = lax.broadcasted_iota(jnp.int32, probs.shape, 0) + offset
            at = lax.broadcasted_iota(jnp.int32, probs.shape, 1)
            return jnp.where(keys <= at, probs, 0.0)

        return mask_of

    def put(pair, row, dk, dv):
        at = pl.ds(row, BRANCH)
        k_ref[at, lanes(pair)] = dk.astype(k_ref.dtype)
        v_ref[at, lanes(pair)] = dv.astype(v_ref.dtype)

    @pl.loop(0, pairs)
    def _(pair):
        for load in pair_loads(pair):
            load.wait()
        kt_ref[:, 0:rows] = k_ref[0:rows, lanes(pair)].T
        grads = mask_heads(pair)
        product = (grads.astype(jnp.float32) * o_ref[:, lanes(pair)].astype(jnp.float32)).T
        for head in range(2):
            delta_ref[pair, head : head + 1, :] = jnp.sum(
                product[head * HEAD_DIM : (head + 1) * HEAD_DIM], axis=0, keepdims=True
            )
        dqt_ref[pair] = jnp.zeros(dqt_ref.shape[1:], dqt_ref.dtype)

        @pl.when(place == 0)
        def _():
            @pl.loop(0, blocks)
            def _(b):
                row = pl.multiple_of(b * BRANCH, BRANCH)
                put(pair, row, *step(pair, row, 0, rows, causal(row)))

        @pl.when(place > 0)
        def _():
            @pl.loop(0, blocks)
            def _(b):
                row = pl.multiple_of(b * BRANCH, BRANCH)
                put(pair, row, *step(pair, row, 0, rows))

    pl.semaphore_wait(barrier, ways - 1)

    def pass_down(piece):
        at = pl.ds(pl.multiple_of(piece * PIECE, PIECE), PIECE)
        return pltpu.make_async_remote_copy(
            src_ref=rows_ref.at[at], dst_ref=land_ref.at[at],
            send_sem=row_send.at[piece], recv_sem=row_recv.at[piece],
            device_id=(spot, lax.rem(place + tensor - 1, tensor)), device_id_type=MESH,
        )

    def row_grad(b):
        at = pl.ds(pl.multiple_of(b * BRANCH, BRANCH), BRANCH)
        return dot_nt(k_ref[at], weight_ref[1]) + dot_nt(v_ref[at], weight_ref[2])

    def hand_down(b, total):
        rows_ref[pl.ds(pl.multiple_of(b * BRANCH, BRANCH), BRANCH)] = total.astype(rows_ref.dtype)

        @pl.when(place == tensor - 1)
        def _():
            for piece in range(BRANCH // PIECE):
                pass_down(b * (BRANCH // PIECE) + piece).start()

    def joined(piece):
        at = pl.ds(pl.multiple_of(piece * PIECE, PIECE), PIECE)
        return rows_ref[at].astype(jnp.float32) + land_ref[at].astype(jnp.float32)

    middle = (place > 0) & (place < tensor - 1)
    late = 3 * jnp.maximum(tensor - 2 - place, 0)
    relayed = jnp.where(middle, jnp.where(place > 1, 2 * pieces, pieces), 0)

    def serve(first, last):
        def one(piece, carry):
            pass_down(piece).wait_recv()
            at = pl.ds(pl.multiple_of(piece * PIECE, PIECE), PIECE)
            rows_ref[at] = joined(piece).astype(rows_ref.dtype)
            pass_down(piece).start()
            return carry

        low = jnp.clip(first - late, 0, relayed)
        lax.fori_loop(low, jnp.clip(last - late, low, relayed), one, 0)

    @pl.loop(0, blocks)
    def _(b):
        hand_down(b, row_grad(b))

    @pl.loop(0, pairs)
    def _(pair):
        @pl.when(place == 0)
        def _():
            for ref in (k_ref, v_ref):
                ref[rows : 3 * rows, lanes(pair)] = jnp.zeros((2 * rows, 128), ref.dtype)

        @pl.when(place > 0)
        def _():
            kt_ref[:, rows : 2 * rows] = k_ref[rows : 2 * rows, lanes(pair)].T
            mask_heads(pair)

            @pl.loop(0, blocks)
            def _(b):
                at = pl.multiple_of(b * BRANCH, BRANCH)
                parent = pl.multiple_of(rows + at, BRANCH)
                put(
                    pair, parent,
                    *step(
                        pair, parent, at, BRANCH, lambda probs: jnp.where(place > 1, probs, 0.0)
                    ),
                )

        serve(pair, pair + 1)

    @pl.loop(0, blocks)
    def _(leaf):
        out_ref[pl.ds(pl.multiple_of(leaf * BRANCH, BRANCH), BRANCH)] = row_grad(blocks + leaf)

    for branch in range(blocks):
        total = None
        for leaf in range(blocks):
            at = leaf * blocks + branch
            part = out_ref[leaf * BRANCH : (leaf + 1) * BRANCH] * parent_ref[at : at + 1]
            total = part if total is None else total + part
        hand_down(blocks + branch, total)

    served = pairs
    serve(served, served + 1)
    served += 1
    plain_loads[2].wait()
    gain_ref[...] = jnp.zeros_like(gain_ref)

    def give(group, step):
        return pltpu.make_async_remote_copy(
            src_ref=slab_ref.at[group, peer(step)], dst_ref=slab_land.at[group, spot],
            send_sem=slab_send.at[group, step], recv_sem=slab_recv.at[group, spot],
            device_id=(peer(step), place), device_id_type=MESH,
        )

    def take(group, step):
        source = peer(dp - step)
        return pltpu.make_async_remote_copy(
            src_ref=slab_ref.at[group, source], dst_ref=slab_land.at[group, source],
            send_sem=slab_send.at[group, step], recv_sem=slab_recv.at[group, source],
            device_id=(peer(step), place), device_id_type=MESH,
        )

    @pl.loop(0, groups)
    def _(group):
        base = served + group * 4

        @pl.loop(0, 2)
        def _(half):
            pair = group * 2 + half

            @pl.when(place > 0)
            def _():
                kt_ref[:, 2 * rows : 3 * rows] = k_ref[2 * rows : 3 * rows, lanes(pair)].T
                mask_heads(pair)

                @pl.loop(0, blocks)
                def _(b):
                    at = pl.multiple_of(b * BRANCH, BRANCH)
                    own = pl.multiple_of(2 * rows + at, BRANCH)
                    put(pair, own, *step(pair, own, at, BRANCH, causal(0)))

            q_ref[:, lanes(pair)] = (dqt_ref[pair] * scale).T.astype(q_ref.dtype)
            serve(base + half, base + half + 1)

        cols = pl.ds(pl.multiple_of(group * GROUP, GROUP), GROUP)

        def keep(kind, value, weighted):
            if weighted:
                weight = weight_ref[kind, :, cols].astype(jnp.float32)
                scaled = value * weight
                gain_ref[...] += scaled[:, 0:128] + scaled[:, 128:256]
            acc_ref[...] = value

            def put_block(target, at):
                slab_ref[group, target, 0:depth, kind * GROUP : (kind + 1) * GROUP] = acc_ref[
                    at
                ].astype(slab_ref.dtype)

            if depth % 16:
                for target in range(dp):
                    put_block(target, slice(target * depth, (target + 1) * depth))
            else:

                @pl.loop(0, dp)
                def _(target):
                    put_block(target, pl.ds(pl.multiple_of(target * depth, depth), depth))

        keep(0, dot_tn(seen_ref[2 * rows : 3 * rows], q_ref[:, cols]), True)
        keep(3, dot_tn(bg_ref[...], o_ref[:, cols]), False)
        serve(base + 2, base + 3)
        for kind, ref in ((1, k_ref), (2, v_ref)):
            value = dot_tn(seen_ref[0:rows], ref[0:rows, cols])
            value = value + dot_tn(seen_ref[rows : 2 * rows], ref[rows : 2 * rows, cols])
            value = value + dot_tn(seen_ref[2 * rows : 3 * rows], ref[2 * rows : 3 * rows, cols])
            keep(kind, value, True)
        serve(base + 3, base + 4)

        @pl.loop(1, dp)
        def _(step_):
            give(group, step_).start()

    served += groups * 4

    part_ref[...] = small_ref[...]
    gains = jnp.sum(gain_ref[...].T, axis=0, keepdims=True)
    for row in range(width // 128):
        part_ref[0, row : row + 1, :] = gains[:, row * 128 : (row + 1) * 128]

    def scatter(step):
        to = lax.rem(me + step, ways)
        return pltpu.make_async_remote_copy(
            src_ref=part_ref.at[to], dst_ref=part_land.at[me],
            send_sem=small_send.at[step], recv_sem=small_recv.at[me],
            device_id=device(to), device_id_type=MESH,
        )

    def arrival(step):
        source = lax.rem(me - step + ways, ways)
        return pltpu.make_async_remote_copy(
            src_ref=part_ref.at[source], dst_ref=part_land.at[source],
            send_sem=small_send.at[step], recv_sem=small_recv.at[source],
            device_id=device(lax.rem(me + step, ways)), device_id_type=MESH,
        )

    def spread(step):
        return pltpu.make_async_remote_copy(
            src_ref=total_ref.at[me], dst_ref=total_ref.at[me],
            send_sem=spread_send.at[step], recv_sem=spread_recv.at[me],
            device_id=device(lax.rem(me + step, ways)), device_id_type=MESH,
        )

    def landing(step):
        source = lax.rem(me - step + ways, ways)
        return pltpu.make_async_remote_copy(
            src_ref=total_ref.at[source], dst_ref=total_ref.at[source],
            send_sem=spread_send.at[step], recv_sem=spread_recv.at[source],
            device_id=device(lax.rem(me + step, ways)), device_id_type=MESH,
        )

    @pl.loop(1, ways)
    def _(step_):
        scatter(step_).start()

    @pl.loop(0, blocks)
    def _(b):
        at = pl.ds(pl.multiple_of(b * BRANCH, BRANCH), BRANCH)
        out_ref[at] = row_grad(2 * blocks + b) + dot_nt(q_ref[at], weight_ref[0])
        serve(served + b, served + b + 1)

    served += blocks

    def add(step_, total):
        arrival(step_).wait_recv()
        return total + part_land[lax.rem(me - step_ + ways, ways)]

    total_ref[me] = lax.fori_loop(1, ways, add, part_ref[me])

    @pl.loop(1, ways)
    def _(step_):
        spread(step_).start()

    serve(served, 2 * pieces)

    @pl.loop(0, groups)
    def _(group):
        slab_sum[group] = slab_ref[group, spot].astype(jnp.float32)

        @pl.loop(1, dp)
        def _(step_):
            take(group, step_).wait_recv()
            slab_sum[group] += slab_land[group, peer(dp - step_)].astype(jnp.float32)

    serve(2 * pieces, 2 * pieces + late)
    share = width // tensor
    kinds = [
        jnp.concatenate(
            [slab_sum[group][:, kind * GROUP : (kind + 1) * GROUP] for group in range(groups)],
            axis=1,
        )
        for kind in range(4)
    ]
    for target in range(tensor):
        mine = jnp.concatenate(
            [kind[:, target * share : (target + 1) * share] for kind in kinds], axis=1
        )
        line_out[target] = mine.astype(line_out.dtype)

        @pl.when(place == target)
        def _():
            sum_ref[...] = mine

    def line(step):
        return pltpu.make_async_remote_copy(
            src_ref=line_out.at[along(step)], dst_ref=line_land.at[place],
            send_sem=line_send.at[step], recv_sem=line_recv.at[place],
            device_id=(spot, along(step)), device_id_type=MESH,
        )

    def line_in(step):
        source = along(tensor - step)
        return pltpu.make_async_remote_copy(
            src_ref=line_out.at[source], dst_ref=line_land.at[source],
            send_sem=line_send.at[step], recv_sem=line_recv.at[source],
            device_id=(spot, along(step)), device_id_type=MESH,
        )

    for step_ in range(1, tensor):
        line(step_).start()

    @pl.when(place < 2)
    def _():
        @pl.loop(0, pieces)
        def _(piece):
            source = place * pieces + piece
            pass_down(source).wait_recv()
            at = pl.ds(pl.multiple_of(piece * PIECE, PIECE), PIECE)
            out_ref[at] += joined(source)

    for step_ in range(1, tensor):
        line_in(step_).wait_recv()
        sum_ref[...] += line_land[along(tensor - step_)].astype(jnp.float32)

    @pl.loop(1, ways)
    def _(step_):
        landing(step_).wait_recv()

    for step_ in range(1, tensor):
        line(step_).wait_send()

    @pl.loop(1, ways)
    def _(step_):
        scatter(step_).wait_send()
        spread(step_).wait_send()

    @pl.loop(0, groups)
    def _(group):
        @pl.loop(1, dp)
        def _(step_):
            give(group, step_).wait_send()

    sent = jnp.where(place == tensor - 1, 2 * pieces, relayed)

    def sent_one(piece, carry):
        pass_down(piece).wait_send()
        return carry

    lax.fori_loop(0, sent, sent_one, 0)


def backward(parents, q, k, v, o, branch_grad, seen, weights, lse, small):
    dp, tensor = lax.axis_size("dp"), lax.axis_size("tensor")
    ways = dp * tensor
    rows, width = q.shape
    seen_rows = k.shape[0]
    depth = width // dp
    padded = -(-depth // 16) * 16
    pairs, groups, pieces = width // 128, width // GROUP, rows // PIECE
    slab = (groups, dp, padded, 4 * GROUP)
    low, full = jnp.bfloat16, jnp.float32
    dma = pltpu.SemaphoreType.DMA
    anywhere = pl.BlockSpec(memory_space=pl.ANY)
    here = pl.BlockSpec(memory_space=pltpu.VMEM)
    out, block, total = pl.pallas_call(
        lambda *refs: back_kernel(dp, tensor, depth, *refs),
        out_shape=(
            jax.ShapeDtypeStruct((rows, width), full),
            jax.ShapeDtypeStruct((padded, width), full),
            jax.ShapeDtypeStruct(small.shape, full),
        ),
        in_specs=[here] + [anywhere] * 7 + [here] * 2,
        out_specs=[here, here, here],
        scratch_shapes=[
            pltpu.VMEM((rows, width), low),
            pltpu.VMEM((seen_rows, width), low),
            pltpu.VMEM((seen_rows, width), low),
            pltpu.VMEM((rows, width), low),
            pltpu.VMEM((rows, width), low),
            pltpu.VMEM((rows, width), low),
            pltpu.VMEM((seen_rows, width), low),
            pltpu.VMEM(weights.shape, low),
            pltpu.VMEM((128, seen_rows), low),
            pltpu.VMEM((2, rows, 128), low),
            pltpu.VMEM((2, rows, 128), low),
            pltpu.VMEM((pairs, 2, rows), full),
            pltpu.VMEM((pairs, 128, rows), full),
            pltpu.VMEM((2 * rows, width), low),
            pltpu.VMEM((2 * rows, width), low),
            pltpu.VMEM((width, GROUP), full),
            pltpu.VMEM((width, 128), full),
            pltpu.VMEM(slab, low),
            pltpu.VMEM(slab, low),
            pltpu.VMEM((groups, padded, 4 * GROUP), full),
            pltpu.VMEM((tensor, padded, width), low),
            pltpu.VMEM((tensor, padded, width), low),
            pltpu.VMEM(small.shape, full),
            pltpu.VMEM(small.shape, full),
            dma((3,)), dma((4, pairs)),
            dma((2 * pieces,)), dma((2 * pieces,)),
            dma((groups, dp)), dma((groups, dp)),
            dma((tensor,)), dma((tensor,)),
            dma((ways,)), dma((ways,)), dma((ways,)), dma((ways,)),
        ],
        compiler_params=pltpu.CompilerParams(
            collective_id=3, has_side_effects=True, vmem_limit_bytes=62 << 20
        ),
        name="attend_backward",
    )(parents, q, k, v, o, branch_grad, seen, weights, lse, small)
    return out, block[:depth], total


norm_eps = 1e-05
route_scale = 3.0
masked_score = -1e30
highest = lax.Precision.HIGHEST


def layer_norm(values, norm_gain):
    centred = values - jnp.mean(values, axis=-1, keepdims=True)
    spread = jnp.mean(centred * centred, axis=-1, keepdims=True)
    return centred * lax.rsqrt(spread + norm_eps) * norm_gain


def unit_rows(values):
    return values * lax.rsqrt(jnp.sum(values * values, axis=-1, keepdims=True) + 1.0)


def router_gate(normed, router_proj, expert_embed, picked):
    routed = jnp.dot(normed, router_proj, precision=highest)
    logits = route_scale * jnp.dot(unit_rows(routed), unit_rows(expert_embed).T, precision=highest)
    return jnp.sum(jax.nn.softmax(logits, axis=-1) * picked, axis=-1)


def gelu_exact(values):
    return jax.nn.gelu(values, approximate=False)


def slot_table(route_ids, order_ids, capacity):
    same_expert = route_ids[:, None] == route_ids[None, :]
    earlier = order_ids[None, :] < order_ids[:, None]
    ranking = jnp.sum(jnp.where(same_expert & earlier, 1, 0), axis=1).astype(jnp.int32)
    kept_mask = ranking < capacity
    column = route_ids * capacity + jnp.minimum(ranking, capacity - 1)
    return (column, kept_mask)


def low_dot(rows, weight):
    return jnp.dot(rows, weight, preferred_element_type=jnp.float32).astype(jnp.bfloat16)


def shards(
    tokens,
    norm1_gain,
    qkv_weight,
    attn_proj,
    norm2_gain,
    router_proj,
    expert_embed,
    expert_in,
    expert_out,
    routes,
    orders,
    leaf_parent,
    cotangent,
):
    rows_here = tokens.shape[0]
    model_width = tokens.shape[1]
    experts = expert_embed.shape[0]
    capacity = rows_here // experts
    dp_size, tensor_size = lax.axis_size("dp"), lax.axis_size("tensor")

    def hop(rows, chip_step, core_step):
        route = []
        for source in range(dp_size):
            chip, core = source // 2, source % 2
            route.append((source, (chip ^ chip_step) * 2 + (core ^ core_step)))
        return lax.ppermute(rows, "dp", route)

    def chip_blocks(rows):
        blocks = rows.reshape(experts, capacity, model_width)
        return [blocks[0]] + [hop(blocks[step], step, 0) for step in range(1, experts)]

    def across_chips(rows):
        return jnp.concatenate(chip_blocks(rows), axis=0)

    def with_partner(blocks):
        arrived = jnp.concatenate(blocks, axis=0)
        return jnp.concatenate([arrived, hop(arrived, 0, 1)], axis=0)

    def pair_sum(kept_rows, sent_rows):
        return (kept_rows + hop(sent_rows, 0, 1).astype(jnp.float32)).astype(jnp.bfloat16)

    hidden = tokens.astype(jnp.float32)
    normed_in, norm1_back = jax.vjp(layer_norm, hidden, norm1_gain)
    own_in = normed_in.astype(jnp.bfloat16)
    flat_qkv = qkv_weight.reshape(qkv_weight.shape[0], -1)
    place = lax.axis_index("tensor")
    leaf_blocks = rows_here // BRANCH
    first_leaf = jnp.maximum(place - 2, 0) * leaf_blocks
    leaf_parents = lax.dynamic_slice_in_dim(leaf_parent[0], first_leaf, leaf_blocks, 0) - 1
    parents = (leaf_parents[:, None] == jnp.arange(leaf_blocks)[None, :]).astype(jnp.float32)
    parents = jnp.broadcast_to(parents.reshape(-1, 1), (leaf_blocks * leaf_blocks, model_width))
    seen_in, weights = share_rows_and_weights(
        own_in, jnp.concatenate([flat_qkv, attn_proj.T], axis=1), parents
    )
    query_weight, key_weight, value_weight, proj_back = weights
    query_rows = low_dot(own_in, query_weight)
    key_rows = low_dot(seen_in, key_weight)
    value_rows = low_dot(seen_in, value_weight)
    attended, log_totals = attend(place[None].astype(jnp.int32), query_rows, key_rows, value_rows)
    branch_out = jnp.einsum(
        "sc,dc->sd", attended, proj_back, preferred_element_type=jnp.float32
    )
    mid_stream = hidden + branch_out
    normed_mid, norm2_back = jax.vjp(layer_norm, mid_stream, norm2_gain)
    moe_in = normed_mid.astype(jnp.bfloat16)
    route_ids = routes[:, 0]
    near_route = route_ids ^ (lax.axis_index("dp") // 2)
    column, kept_mask = slot_table(near_route, orders[0], capacity)
    picked = (route_ids[:, None] == jnp.arange(experts)[None, :]).astype(jnp.float32)
    gate_value, gate_back = jax.vjp(
        lambda normed_rows, route_proj, embed_rows: router_gate(
            normed_rows, route_proj, embed_rows, picked
        ),
        moe_in.astype(jnp.float32),
        router_proj,
        expert_embed,
    )
    select = (
        (column[:, None] == jnp.arange(experts * capacity)[None, :]) & kept_mask[:, None]
    ).astype(jnp.bfloat16)
    def to_slots(token_rows):
        return jnp.einsum(
            "ts,td->sd", select, token_rows, preferred_element_type=jnp.float32
        ).astype(jnp.bfloat16)

    def from_slots(slot_rows):
        return jnp.dot(select, slot_rows, preferred_element_type=jnp.float32)

    upstream = cotangent.astype(jnp.float32)
    slot_grads = to_slots((gate_value[:, None] * upstream).astype(jnp.bfloat16))
    row_blocks, slot_grads = lax.optimization_barrier(
        (chip_blocks(to_slots(moe_in)), slot_grads)
    )
    grad_blocks = chip_blocks(slot_grads)
    expert_rows = with_partner(row_blocks)
    active, slope, kept_result, sent_result = expert_forward(expert_rows, expert_in, expert_out)
    grad_blocks, kept_result, sent_result = lax.optimization_barrier(
        (grad_blocks, kept_result, sent_result)
    )
    arrived_grad = with_partner(grad_blocks)
    result_rows, late_grad = lax.optimization_barrier(
        (pair_sum(kept_result, sent_result), arrived_grad)
    )
    expert_result = from_slots(across_chips(result_rows))
    output = (mid_stream + gate_value[:, None] * expert_result).astype(jnp.bfloat16)
    out_weight_grad = jnp.einsum(
        "rf,rd->fd", active, arrived_grad, preferred_element_type=jnp.float32
    ).astype(jnp.bfloat16)
    up_grad, kept_grad, sent_grad = expert_back(late_grad, slope, expert_in, expert_out)
    in_weight_grad = jnp.einsum(
        "rf,rd->fd", up_grad, expert_rows, preferred_element_type=jnp.float32
    ).astype(jnp.bfloat16)
    moe_grad = from_slots(across_chips(pair_sum(kept_grad, sent_grad)))
    gate_grad = jnp.sum(upstream * expert_result, axis=-1)
    router_part, proj_grad, embed_grad = gate_back(gate_grad)
    mid_part, gain2_grad = norm2_back(moe_grad + router_part)
    mid_grad = upstream + mid_part
    expert_grads = jnp.stack(
        [
            part.reshape(tensor_size, -1, model_width)
            for part in (in_weight_grad, out_weight_grad)
        ],
        axis=1,
    )
    mid_grad, expert_grads = lax.optimization_barrier((mid_grad, expert_grads))
    expert_grad_block = lax.psum_scatter(
        expert_grads.reshape(-1, model_width), "tensor", scatter_dimension=0, tiled=True
    ).astype(jnp.float32)
    half_block = expert_grad_block.shape[0] // 2
    expert_in_grad = expert_grad_block[:half_block].T
    expert_out_grad = expert_grad_block[half_block:]
    branch_grad = mid_grad.astype(jnp.bfloat16)
    later = [gain2_grad, proj_grad, embed_grad]
    flat = jnp.concatenate([jnp.zeros_like(norm1_gain)] + [part.reshape(-1) for part in later])
    ways = dp_size * tensor_size
    lanes = -(-flat.shape[0] // (ways * 8 * 128)) * 128
    small = jnp.pad(flat, (0, ways * 8 * lanes - flat.shape[0])).reshape(ways, 8, lanes)
    input_grad, grad_block, totals = backward(
        parents, query_rows, key_rows, value_rows, attended, branch_grad, seen_in, weights,
        log_totals, small,
    )
    qkv_grad = grad_block[:, : flat_qkv.shape[1]].reshape(qkv_weight.shape)
    attn_proj_grad = grad_block[:, flat_qkv.shape[1] :].T
    totals = totals.reshape(-1)
    gain1_sum = totals[:model_width] / norm1_gain
    gain2_sum, router_sum, embed_sum = (
        totals[first : first + part.size].reshape(part.shape)
        for first, part in zip(
            (model_width, 2 * model_width, 2 * model_width + proj_grad.size), later
        )
    )
    token_part, _ = norm1_back(input_grad)
    token_grad = mid_grad + token_part
    return (
        output,
        token_grad,
        gain1_sum,
        qkv_grad,
        attn_proj_grad,
        gain2_sum,
        router_sum,
        embed_sum,
        expert_in_grad,
        expert_out_grad,
    )


def solution(mesh):
    in_specs = (
        P(("dp", "tensor"), None),
        P(),
        P("dp", None, "tensor"),
        P("tensor", "dp"),
        P(),
        P(),
        P(),
        P(None, "dp"),
        P("dp", None),
        P(("dp", "tensor"), None),
        P(("dp", "tensor"), None),
        P("dp", None),
        P(("dp", "tensor"), None),
    )
    out_specs = (
        P(("dp", "tensor"), None),
        P(("dp", "tensor"), None),
        P(),
        P("dp", None, "tensor"),
        P("tensor", "dp"),
        P(),
        P(),
        P(),
        P(None, ("dp", "tensor")),
        P(("dp", "tensor"), None),
    )
    return jax.shard_map(shards, mesh=mesh, in_specs=in_specs, out_specs=out_specs, check_vma=False)
```

```python
import functools
import math

import jax
import jax.numpy as jnp
from jax import lax
from jax.experimental import pallas as pl
from jax.experimental.pallas import tpu as pltpu
from jax.sharding import PartitionSpec as P

HEAD_DIM = 64
TRUNK = 1024
BRANCH = 256
MASKED = -1e30
LOG2E = math.log2(math.e)
EXP_SCALE = HEAD_DIM ** (-0.5) * LOG2E

NT = (((1,), (1,)), ((), ()))
NN = (((1,), (0,)), ((), ()))


def dot_nt(a, b):
    return lax.dot_general(a, b, NT, preferred_element_type=jnp.float32)


def dot_nn(a, b):
    return lax.dot_general(a, b, NN, preferred_element_type=jnp.float32)


def head_lanes(shape, dim, head):
    return lax.broadcasted_iota(jnp.int32, shape, dim) // HEAD_DIM == head


def fwd_kernel(place_ref, q_ref, k_ref, v_ref, o_ref, lse_ref, vt_ref, acc_ref):
    place = place_ref[0]
    rows = q_ref.shape[0]
    blocks = rows // BRANCH
    flipped = v_ref[...].T
    for head in range(2):
        vt_ref[head] = jnp.where(
            head_lanes(flipped.shape, 0, head), flipped, jnp.ones_like(flipped)
        )

    def start(block, head, in_trunk):
        queries = q_ref[block * BRANCH : (block + 1) * BRANCH]
        queries = jnp.where(head_lanes(queries.shape, 1, head), queries, jnp.zeros_like(queries))
        firsts = list(range(0, TRUNK, BRANCH))
        if not in_trunk:
            firsts += [rows + block * BRANCH, 2 * rows + block * BRANCH]
        scores = [dot_nt(k_ref[first : first + BRANCH], queries) for first in firsts]

        def causal(tile, offset):
            keys = lax.broadcasted_iota(jnp.int32, tile.shape, 0) + offset
            at = lax.broadcasted_iota(jnp.int32, tile.shape, 1)
            return jnp.where(keys <= at, tile, MASKED)

        if in_trunk:
            scores = [
                causal(tile, first - block * BRANCH) for tile, first in zip(scores, firsts)
            ]
        else:
            scores[-2] = jnp.where(place > 1, scores[-2], MASKED)
            scores[-1] = causal(scores[-1], 0)
        top = jnp.max(functools.reduce(jnp.maximum, scores), axis=0, keepdims=True)
        return firsts, scores, top

    def middle(firsts, scores, top):
        shift = top * EXP_SCALE
        probs = [jnp.exp2(tile * EXP_SCALE - shift).astype(jnp.bfloat16) for tile in scores]
        return firsts, probs, top

    def finish(block, head, firsts, probs, top):
        acc = None
        for first, tile in zip(firsts, probs):
            part = dot_nn(vt_ref[head, :, first : first + BRANCH], tile)
            acc = part if acc is None else acc + part
        mine, other = head * HEAD_DIM, (1 - head) * HEAD_DIM
        total = acc[other : other + 1]
        cols = slice(block * BRANCH, (block + 1) * BRANCH)
        acc_ref[mine : mine + HEAD_DIM, cols] = acc[mine : mine + HEAD_DIM] / total
        lse_ref[0, head : head + 1, cols] = top * EXP_SCALE + jnp.log2(total)

    def run(in_trunk):
        work = [(block, head) for block in range(blocks) for head in range(2)]
        ready, held = start(*work[0], in_trunk), None
        for at, item in enumerate(work):
            now = ready
            if at + 1 < len(work):
                ready = start(*work[at + 1], in_trunk)
            done = middle(*now)
            if held is not None:
                finish(*held)
            held = (*item, *done)
        finish(*held)

    @pl.when(place == 0)
    def _():
        run(True)

    @pl.when(place > 0)
    def _():
        run(False)

    o_ref[...] = acc_ref[...].T.astype(o_ref.dtype)


def attend(place, q, k, v):
    rows, width = q.shape
    keys = k.shape[0]
    pairs = width // 128
    few = pl.BlockSpec((rows, 128), lambda p, m: (0, p))
    many = pl.BlockSpec((keys, 128), lambda p, m: (0, p))
    return pl.pallas_call(
        fwd_kernel,
        out_shape=(
            jax.ShapeDtypeStruct((rows, width), jnp.bfloat16),
            jax.ShapeDtypeStruct((pairs, 2, rows), jnp.float32),
        ),
        grid_spec=pltpu.PrefetchScalarGridSpec(
            num_scalar_prefetch=1,
            grid=(pairs,),
            in_specs=[few, many, many],
            out_specs=[few, pl.BlockSpec((1, 2, rows), lambda p, m: (p, 0, 0))],
            scratch_shapes=[
                pltpu.VMEM((2, 128, keys), jnp.bfloat16),
                pltpu.VMEM((128, rows), jnp.float32),
            ],
        ),
        compiler_params=pltpu.CompilerParams(vmem_limit_bytes=48 << 20),
        name="attend_forward",
    )(place, q, k, v)


ROWS = 256
HALF_ROOT = math.sqrt(0.5)
PDF_SCALE = 1.0 / math.sqrt(2.0 * math.pi)
CHUNK = 512


def expert_fwd_kernel(x_ref, in_ref, out_ref, active_ref, slope_ref, keep_ref, send_ref):
    step = pl.program_id(0)
    half = pl.num_programs(0) // 2
    rows = x_ref[...]
    total = None
    for first in range(0, in_ref.shape[1], CHUNK):
        cols = slice(first, first + CHUNK)
        up = dot_nn(rows, in_ref[:, cols])
        below = 0.5 * (1.0 + lax.erf(up * HALF_ROOT))
        active = (up * below).astype(jnp.bfloat16)
        slope = below + up * (jnp.exp(-0.5 * up * up) * PDF_SCALE)
        active_ref[:, cols] = active
        slope_ref[:, cols] = slope.astype(jnp.bfloat16)
        part = dot_nn(active, out_ref[cols])
        total = part if total is None else total + part

    @pl.when(step < half)
    def _():
        keep_ref[...] = total

    @pl.when(step >= half)
    def _():
        send_ref[...] = total.astype(send_ref.dtype)


def expert_bwd_kernel(grad_ref, slope_ref, in_ref, out_ref, upgrad_ref, keep_ref, send_ref):
    step = pl.program_id(0)
    half = pl.num_programs(0) // 2
    grads = grad_ref[...]
    total = None
    for first in range(0, in_ref.shape[1], CHUNK):
        cols = slice(first, first + CHUNK)
        active_grad = dot_nt(grads, out_ref[cols])
        up_grad = (active_grad * slope_ref[:, cols].astype(jnp.float32)).astype(jnp.bfloat16)
        upgrad_ref[:, cols] = up_grad
        part = dot_nt(up_grad, in_ref[:, cols])
        total = part if total is None else total + part

    @pl.when(step < half)
    def _():
        keep_ref[...] = total

    @pl.when(step >= half)
    def _():
        send_ref[...] = total.astype(send_ref.dtype)


def split_specs(count, width):
    half = count // 2
    return [
        pl.BlockSpec((ROWS, width), lambda i: (jnp.minimum(i, half - 1), 0)),
        pl.BlockSpec((ROWS, width), lambda i: (jnp.maximum(i - half, 0), 0)),
    ]


def expert_forward(x, w_in, w_out):
    rows, width = x.shape
    hidden = w_in.shape[1]
    count = rows // ROWS
    def wide(cols):
        return pl.BlockSpec((ROWS, cols), lambda i: (i, 0))
    def whole(shape):
        return pl.BlockSpec(shape, lambda i: (0, 0), pipeline_mode=pl.Buffered(1))
    return pl.pallas_call(
        expert_fwd_kernel,
        grid=(count,),
        in_specs=[wide(width), whole(w_in.shape), whole(w_out.shape)],
        out_specs=[wide(hidden), wide(hidden)] + split_specs(count, width),
        out_shape=(
            jax.ShapeDtypeStruct((rows, hidden), jnp.bfloat16),
            jax.ShapeDtypeStruct((rows, hidden), jnp.bfloat16),
            jax.ShapeDtypeStruct((rows // 2, width), jnp.float32),
            jax.ShapeDtypeStruct((rows // 2, width), jnp.bfloat16),
        ),
        cost_estimate=pl.CostEstimate(flops=4 * rows * width * hidden, bytes_accessed=24 << 20, transcendentals=2 * rows * hidden),
        compiler_params=pltpu.CompilerParams(vmem_limit_bytes=40 << 20),
        name="expert_forward",
    )(x, w_in, w_out)


def expert_back(grads, slope, w_in, w_out):
    rows, width = grads.shape
    hidden = w_in.shape[1]
    count = rows // ROWS
    def wide(cols):
        return pl.BlockSpec((ROWS, cols), lambda i: (i, 0))
    def whole(shape):
        return pl.BlockSpec(shape, lambda i: (0, 0), pipeline_mode=pl.Buffered(1))
    return pl.pallas_call(
        expert_bwd_kernel,
        grid=(count,),
        in_specs=[wide(width), wide(hidden), whole(w_in.shape), whole(w_out.shape)],
        out_specs=[wide(hidden)] + split_specs(count, width),
        out_shape=(
            jax.ShapeDtypeStruct((rows, hidden), jnp.bfloat16),
            jax.ShapeDtypeStruct((rows // 2, width), jnp.float32),
            jax.ShapeDtypeStruct((rows // 2, width), jnp.bfloat16),
        ),
        cost_estimate=pl.CostEstimate(flops=4 * rows * width * hidden, bytes_accessed=24 << 20, transcendentals=0),
        compiler_params=pltpu.CompilerParams(vmem_limit_bytes=40 << 20),
        name="expert_backward",
    )(grads, slope, w_in, w_out)


MESH = pl.DeviceIdType.MESH


PIECE = 64


def greet(peers):
    barrier = pltpu.get_barrier_semaphore()
    for peer in peers:
        pl.semaphore_signal(barrier, inc=1, device_id=peer, device_id_type=MESH)
    pl.semaphore_wait(barrier, len(peers))


def share_kernel(dp, tensor, own_ref, block_ref, parent_ref, seen_ref, out_ref, weights_ref,
                 ordered_ref, row_send, row_recv,
                 line_send, line_recv, chip_send, chip_recv, pair_send, pair_recv):
    spot, place = lax.axis_index("dp"), lax.axis_index("tensor")
    chip, core = spot // 2, lax.rem(spot, 2)
    chips = dp // 2
    rows = own_ref.shape[0]
    pieces = rows // PIECE
    part_width = out_ref.shape[2] // tensor
    partner = (chip * 2 + 1 - core, place)

    def along(step):
        return lax.rem(place + step, tensor)

    def chip_at(step):
        return lax.rem(chip + step, chips)

    greet(
        [(spot, along(step)) for step in range(1, tensor)]
        + [(chip_at(step) * 2 + core, place) for step in range(1, chips)]
        + [partner]
    )

    def pass_on(part, piece, fresh):
        at = pl.ds(part * rows + piece * PIECE, PIECE)
        source = own_ref.at[pl.ds(piece * PIECE, PIECE)] if fresh else seen_ref.at[at]
        return pltpu.make_async_remote_copy(
            src_ref=source, dst_ref=seen_ref.at[at],
            send_sem=row_send.at[part, piece], recv_sem=row_recv.at[part, piece],
            device_id=(spot, lax.rem(place + 1, tensor)), device_id_type=MESH,
        )

    def line(step):
        return pltpu.make_async_remote_copy(
            src_ref=block_ref, dst_ref=weights_ref.at[place, spot],
            send_sem=line_send.at[step], recv_sem=line_recv.at[place],
            device_id=(spot, along(step)), device_id_type=MESH,
        )

    def line_in(step):
        source = along(tensor - step)
        return pltpu.make_async_remote_copy(
            src_ref=block_ref, dst_ref=weights_ref.at[source, spot],
            send_sem=line_send.at[step], recv_sem=line_recv.at[source],
            device_id=(spot, along(step)), device_id_type=MESH,
        )

    def plane(part, step):
        block = weights_ref.at[part, spot]
        return pltpu.make_async_remote_copy(
            src_ref=block, dst_ref=block,
            send_sem=chip_send.at[part, step], recv_sem=chip_recv.at[part, chip],
            device_id=(chip_at(step) * 2 + core, place), device_id_type=MESH,
        )

    def plane_in(part, step):
        source = chip_at(chips - step)
        block = weights_ref.at[part, source * 2 + core]
        return pltpu.make_async_remote_copy(
            src_ref=block, dst_ref=block,
            send_sem=chip_send.at[part, step], recv_sem=chip_recv.at[part, source],
            device_id=(chip_at(step) * 2 + core, place), device_id_type=MESH,
        )

    def across(part, source, source_core):
        block = weights_ref.at[part, source * 2 + source_core]
        return pltpu.make_async_remote_copy(
            src_ref=block, dst_ref=block,
            send_sem=pair_send.at[part, source], recv_sem=pair_recv.at[part, source],
            device_id=partner, device_id_type=MESH,
        )

    for step in range(1, tensor):
        line(step).start()

    def row_steps(first, last):
        @pl.loop(first, last)
        def _(piece):
            @pl.when(place == 0)
            def _():
                pass_on(0, piece, True).start()

            @pl.when(place > 0)
            def _():
                pass_on(0, piece, False).wait_recv()

            @pl.when((place > 0) & (place < tensor - 1))
            def _():
                pass_on(0, piece, False).start()

            @pl.when(place == 1)
            def _():
                pass_on(1, piece, True).start()

            @pl.when(place > 1)
            def _():
                pass_on(1, piece, False).wait_recv()

            @pl.when((place > 1) & (place < tensor - 1))
            def _():
                pass_on(1, piece, False).start()

    weights_ref[place, spot] = block_ref[...]
    seen_ref[2 * rows :] = own_ref[...]

    @pl.when(place < 2)
    def _():
        seen_ref[rows : 2 * rows] = own_ref[...]

    @pl.when(place == 0)
    def _():
        seen_ref[0:rows] = own_ref[...]

    row_steps(0, pieces // 4)
    for step in range(tensor):
        part = along(tensor - step)
        if step:
            line_in(step).wait_recv()

        @pl.loop(1, chips)
        def _(hop):
            plane(part, hop).start()

        across(part, chip, core).start()
    row_steps(pieces // 4, (pieces * 5) // 8)
    for step in range(tensor):
        part = along(tensor - step)

        @pl.loop(1, chips)
        def _(hop):
            plane_in(part, hop).wait_recv()
            across(part, chip_at(chips - hop), core).start()

    row_steps((pieces * 5) // 8, pieces)
    for part in range(tensor):

        @pl.loop(0, chips)
        def _(source):
            across(part, source, 1 - core).wait_recv()
            across(part, source, core).wait_send()

        @pl.loop(1, chips)
        def _(hop):
            plane(part, hop).wait_send()

    for step in range(1, tensor):
        line(step).wait_send()

    @pl.when(place < tensor - 1)
    def _():
        @pl.loop(0, pieces)
        def _(piece):
            pass_on(0, piece, False).wait_send()

    @pl.when((place > 0) & (place < tensor - 1))
    def _():
        @pl.loop(0, pieces)
        def _(piece):
            pass_on(1, piece, False).wait_send()

    @pl.when(place > 1)
    def _():
        blocks = rows // BRANCH
        branches = [
            seen_ref[rows + branch * BRANCH : rows + (branch + 1) * BRANCH]
            for branch in range(blocks)
        ]
        for leaf in range(blocks):
            chosen = None
            for branch in range(blocks):
                at = leaf * blocks + branch
                part = branches[branch] * parent_ref[at : at + 1].astype(own_ref.dtype)
                chosen = part if chosen is None else chosen + part
            ordered_ref[leaf * BRANCH : (leaf + 1) * BRANCH] = chosen
        seen_ref[rows : 2 * rows] = ordered_ref[...]

    @pl.loop(0, dp)
    def _(source):
        depth = block_ref.shape[0]
        at = pl.ds(pl.multiple_of(source * depth, depth), depth)
        for kind in range(out_ref.shape[0]):
            cols = slice(kind * part_width, (kind + 1) * part_width)
            out_ref[kind, at] = jnp.concatenate(
                [weights_ref[part, source][:, cols] for part in range(tensor)], axis=1
            )


def share_rows_and_weights(own, block, parents):
    dp, tensor = lax.axis_size("dp"), lax.axis_size("tensor")
    rows, width = own.shape
    depth, cols = block.shape
    pieces, chips = rows // PIECE, dp // 2
    kinds = cols * tensor // width
    padded = -(-depth // 16) * 16
    block = jnp.pad(block, ((0, padded - depth), (0, 0)))
    dma = pltpu.SemaphoreType.DMA
    here = pl.BlockSpec(memory_space=pltpu.VMEM)
    seen, weights = pl.pallas_call(
        lambda *refs: share_kernel(dp, tensor, *refs),
        out_shape=(
            jax.ShapeDtypeStruct((3 * rows, width), own.dtype),
            jax.ShapeDtypeStruct((kinds, dp * padded, width), block.dtype),
        ),
        in_specs=[here, here, here],
        out_specs=[here, here],
        scratch_shapes=[
            pltpu.VMEM((tensor, dp, padded, cols), block.dtype),
            pltpu.VMEM(own.shape, own.dtype),
            dma((2, pieces)), dma((2, pieces)),
            dma((tensor,)), dma((tensor,)),
            dma((tensor, chips)), dma((tensor, chips)),
            dma((tensor, chips)), dma((tensor, chips)),
        ],
        compiler_params=pltpu.CompilerParams(
            collective_id=2, has_side_effects=True, vmem_limit_bytes=48 << 20
        ),
        name="share_rows_and_weights",
    )(own, block, parents)
    weights = weights.reshape(kinds, dp, padded, width)[:, :, :depth]
    return seen, weights.reshape(kinds, dp * depth, width)


TN = (((0,), (0,)), ((), ()))
GROUP = 256


def dot_tn(a, b):
    return lax.dot_general(a, b, TN, preferred_element_type=jnp.float32)


def back_kernel(
    dp, tensor, depth,
    parent_ref, q_in, k_in, v_in, o_in, grad_in, seen_in, weight_in, lse_ref, small_ref,
    out_ref, sum_ref, total_ref,
    q_ref, k_ref, v_ref, o_ref, bg_ref, g_ref, stage_ref, seen_ref, weight_ref,
    delta_ref, dqt_ref, rows_ref, land_ref, gain_ref,
    slab_ref, slab_land, proj_ref, proj_land, line_out, line_land, part_ref, part_land,
    load_sem, pair_sem, stage_sem, row_send, row_recv, slab_send, slab_recv,
    line_send, line_recv, small_send, small_recv, spread_send, spread_recv,
):
    spot, place = lax.axis_index("dp"), lax.axis_index("tensor")
    ways = dp * tensor
    me = spot * tensor + place
    scale = HEAD_DIM ** (-0.5)
    rows, width = q_ref.shape
    pairs = width // 128
    groups = width // GROUP
    blocks = rows // BRANCH
    pieces = rows // PIECE
    stage_rows = stage_ref.shape[1]

    def device(index):
        return (index // tensor, lax.rem(index, tensor))

    def along(step):
        return lax.rem(place + step, tensor)

    def peer(step):
        return lax.rem(spot + step, dp)

    def block_at(b):
        return pl.ds(pl.multiple_of(b * BRANCH, BRANCH), BRANCH)

    barrier = pltpu.get_barrier_semaphore()

    @pl.loop(1, ways)
    def _(step):
        pl.semaphore_signal(
            barrier, inc=1, device_id=device(lax.rem(me + step, ways)), device_id_type=MESH
        )

    def lanes(pair):
        return pl.ds(pl.multiple_of(pair * 128, 128), 128)

    grad_load = pltpu.make_async_copy(grad_in, bg_ref, load_sem.at[0])
    weight_load = pltpu.make_async_copy(weight_in, weight_ref, load_sem.at[1])
    value_load = pltpu.make_async_copy(o_in, o_ref, load_sem.at[2])

    def pair_loads(pair):
        return [
            pltpu.make_async_copy(
                source.at[:, lanes(pair)], held.at[:, lanes(pair)], pair_sem.at[which, pair]
            )
            for which, (source, held) in enumerate(((q_in, q_ref), (k_in, k_ref), (v_in, v_ref)))
        ]

    def stage(part):
        slot = lax.rem(part, 2)
        at = pl.ds(pl.multiple_of(part * stage_rows, stage_rows), stage_rows)
        return pltpu.make_async_copy(seen_in.at[at], stage_ref.at[slot], stage_sem.at[slot])

    grad_load.start()
    weight_load.start()
    value_load.start()

    @pl.loop(0, pairs)
    def _(pair):
        for load in pair_loads(pair):
            load.start()

    grad_load.wait()
    weight_load.wait()
    value_load.wait()

    def keep(held, value, kind):
        cols = slice(kind * GROUP, (kind + 1) * GROUP)
        if depth % 16:
            for target in range(dp):
                held[target, 0:depth, cols] = value[target * depth : (target + 1) * depth].astype(
                    slab_ref.dtype
                )
        else:
            held[:, :, cols] = value.reshape(dp, depth, GROUP).astype(slab_ref.dtype)

    for group in range(groups):
        cols = slice(group * GROUP, (group + 1) * GROUP)
        keep(proj_ref, dot_tn(bg_ref[...], o_ref[:, cols]), group)

    @pl.loop(0, blocks)
    def _(b):
        at = block_at(b)
        g_ref[at] = dot_nn(bg_ref[at], weight_ref[3]).astype(g_ref.dtype)

    pl.semaphore_wait(barrier, ways - 1)

    def slabs(group):
        if isinstance(group, int) and group == groups:
            return proj_ref, proj_land
        return slab_ref.at[group], slab_land.at[group]

    def give(group, step):
        source, target = slabs(group)
        return pltpu.make_async_remote_copy(
            src_ref=source.at[peer(step)], dst_ref=target.at[spot],
            send_sem=slab_send.at[group, step], recv_sem=slab_recv.at[group, spot],
            device_id=(peer(step), place), device_id_type=MESH,
        )

    def take(group, step):
        owner = peer(dp - step)
        source, target = slabs(group)
        return pltpu.make_async_remote_copy(
            src_ref=source.at[owner], dst_ref=target.at[owner],
            send_sem=slab_send.at[group, step], recv_sem=slab_recv.at[group, owner],
            device_id=(peer(step), place), device_id_type=MESH,
        )

    @pl.loop(1, dp)
    def _(step):
        give(groups, step).start()

    @pl.loop(0, pairs)
    def _(pair):
        for load in pair_loads(pair):
            load.wait()
        product = g_ref[:, lanes(pair)].astype(jnp.float32)
        product = (product * o_ref[:, lanes(pair)].astype(jnp.float32)).T
        for head in range(2):
            delta_ref[pair, head : head + 1, :] = jnp.sum(
                product[head * HEAD_DIM : (head + 1) * HEAD_DIM], axis=0, keepdims=True
            )
        dqt_ref[pair] = jnp.zeros(dqt_ref.shape[1:], dqt_ref.dtype)

    def sweep(pair, tiles):
        work = [(tile, head) for tile in range(len(tiles)) for head in range(2)]
        sums = [[None, None] for _ in tiles]
        keys, flipped = {}, {}

        def key_block(tile):
            row = tiles[tile][0]
            if id(row) not in keys:
                kb = k_ref[pl.ds(row, BRANCH), lanes(pair)]
                vb = v_ref[pl.ds(row, BRANCH), lanes(pair)]
                masked = []
                for head in range(2):
                    mine = head_lanes(kb.shape, 1, head)
                    masked.append(
                        (
                            jnp.where(mine, kb, jnp.zeros_like(kb)),
                            jnp.where(mine, vb, jnp.zeros_like(vb)),
                        )
                    )
                keys[id(row)] = masked
                flipped[id(row)] = kb.T
            return keys[id(row)], flipped[id(row)]

        def start(tile, head):
            at = pl.ds(tiles[tile][1], BRANCH)
            kb, vb = key_block(tile)[0][head]
            return dot_nt(kb, q_ref[at, lanes(pair)]), dot_nt(vb, g_ref[at, lanes(pair)])

        def middle(tile, head, scores, prob_grad):
            at = pl.ds(tiles[tile][1], BRANCH)
            probs = jnp.exp2(scores * EXP_SCALE - lse_ref[pair, head : head + 1, at])
            if tiles[tile][2] is not None:
                probs = tiles[tile][2](probs)
            score_grad = probs * (prob_grad - delta_ref[pair, head : head + 1, at])
            return probs.astype(jnp.bfloat16), score_grad.astype(jnp.bfloat16)

        def finish(tile, head, probs, score_grad):
            at = pl.ds(tiles[tile][1], BRANCH)
            parts = (
                dot_nn(score_grad, q_ref[at, lanes(pair)]),
                dot_nn(probs, g_ref[at, lanes(pair)]),
            )
            for which in range(2):
                held = sums[tile][which]
                if head == 0:
                    sums[tile][which] = parts[which]
                else:
                    first = head_lanes(held.shape, 1, 0)
                    sums[tile][which] = jnp.where(first, held, parts[which])
            mine = slice(head * HEAD_DIM, (head + 1) * HEAD_DIM)
            dqt_ref[pair, mine, at] += dot_nn(key_block(tile)[1][mine], score_grad)

        ready = start(*work[0])
        held = None
        for at, item in enumerate(work):
            now = ready
            if at + 1 < len(work):
                ready = start(*work[at + 1])
            done = middle(*item, *now)
            if held is not None:
                finish(*held)
            held = (*item, *done)
        finish(*held)
        return sums

    def causal(key_row, query_row):
        def mask_of(probs):
            keys = lax.broadcasted_iota(jnp.int32, probs.shape, 0) + key_row
            at = lax.broadcasted_iota(jnp.int32, probs.shape, 1) + query_row
            return jnp.where(keys <= at, probs, 0.0)

        return mask_of

    def put(pair, row, dk, dv):
        at = pl.ds(row, BRANCH)
        k_ref[at, lanes(pair)] = (dk * scale).astype(k_ref.dtype)
        v_ref[at, lanes(pair)] = dv.astype(v_ref.dtype)

    def pass_down(piece):
        at = pl.ds(pl.multiple_of(piece * PIECE, PIECE), PIECE)
        return pltpu.make_async_remote_copy(
            src_ref=rows_ref.at[at], dst_ref=land_ref.at[at],
            send_sem=row_send.at[piece], recv_sem=row_recv.at[piece],
            device_id=(spot, lax.rem(place + tensor - 1, tensor)), device_id_type=MESH,
        )

    def row_grad(b):
        at = block_at(b)
        return dot_nt(k_ref[at], weight_ref[1]) + dot_nt(v_ref[at], weight_ref[2])

    def hand_down(b, total):
        rows_ref[block_at(b)] = total.astype(rows_ref.dtype)

        @pl.when(place == tensor - 1)
        def _():
            for piece in range(BRANCH // PIECE):
                pass_down(b * (BRANCH // PIECE) + piece).start()

    def joined(piece):
        at = pl.ds(pl.multiple_of(piece * PIECE, PIECE), PIECE)
        return rows_ref[at].astype(jnp.float32) + land_ref[at].astype(jnp.float32)

    middle_place = (place > 0) & (place < tensor - 1)
    late = 3 * jnp.maximum(tensor - 2 - place, 0)
    relayed = jnp.where(middle_place, jnp.where(place > 1, 2 * pieces, pieces), 0)

    def serve(first, last):
        def one(piece, carry):
            pass_down(piece).wait_recv()
            at = pl.ds(pl.multiple_of(piece * PIECE, PIECE), PIECE)
            rows_ref[at] = joined(piece).astype(rows_ref.dtype)
            pass_down(piece).start()
            return carry

        low = jnp.clip(first - late, 0, relayed)
        lax.fori_loop(low, jnp.clip(last - late, low, relayed), one, 0)

    stage(0).start()

    @pl.loop(0, blocks)
    def _(b):
        row = pl.multiple_of(b * BRANCH, BRANCH)

        @pl.loop(0, pairs)
        def _(pair):
            def finish_block(masked):
                tiles = [
                    (row, first, causal(row, first) if masked else None)
                    for first in range(0, rows, BRANCH)
                ]
                sums = sweep(pair, tiles)
                put(pair, row, sum(part[0] for part in sums), sum(part[1] for part in sums))

            @pl.when(place == 0)
            def _():
                finish_block(True)

            @pl.when(place > 0)
            def _():
                finish_block(False)

            @pl.when((pair > 1) & (b > 0))
            def _():
                piece = (b - 1) * (BRANCH // PIECE) + pair - 2
                serve(piece, piece + 1)

        for _half in range(2):
            part = b * 2 + _half

            @pl.when(part < 3 * rows // stage_rows)
            def _():
                stage(part).wait()

                @pl.when(part + 1 < 3 * rows // stage_rows)
                def _():
                    stage(part + 1).start()

                at = pl.ds(pl.multiple_of(part * stage_rows, stage_rows), stage_rows)
                seen_ref[:, at] = stage_ref[lax.rem(part, 2)].T

        hand_down(b, row_grad(b))

    served = (blocks - 1) * (BRANCH // PIECE)

    @pl.loop(0, pairs)
    def _(pair):
        @pl.when(place == 0)
        def _():
            for ref in (k_ref, v_ref):
                ref[rows : 3 * rows, lanes(pair)] = jnp.zeros((2 * rows, 128), ref.dtype)

        @pl.when(place > 0)
        def _():
            def seen_parent(probs):
                return jnp.where(place > 1, probs, 0.0)

            spots = range(0, rows, BRANCH)
            sums = sweep(pair, [(rows + at, at, seen_parent) for at in spots])
            for at, part in zip(spots, sums):
                put(pair, rows + at, *part)

        serve(jnp.minimum(served + pair, pieces), jnp.minimum(served + pair + 1, pieces))

    served = pieces

    @pl.loop(0, blocks)
    def _(leaf):
        out_ref[block_at(leaf)] = row_grad(blocks + leaf)

    for branch in range(blocks):
        total = None
        for leaf in range(blocks):
            at = leaf * blocks + branch
            part = out_ref[leaf * BRANCH : (leaf + 1) * BRANCH] * parent_ref[at : at + 1]
            total = part if total is None else total + part
        hand_down(blocks + branch, total)

    gain_ref[...] = jnp.zeros_like(gain_ref)

    @pl.loop(0, groups)
    def _(group):
        base = served + group * 4

        @pl.loop(0, 2)
        def _(half):
            pair = group * 2 + half

            @pl.when(place > 0)
            def _():
                spots = range(0, rows, BRANCH)
                sums = sweep(pair, [(2 * rows + at, at, causal(0, 0)) for at in spots])
                for at, part in zip(spots, sums):
                    put(pair, 2 * rows + at, *part)

            q_ref[:, lanes(pair)] = (dqt_ref[pair] * scale).T.astype(q_ref.dtype)
            serve(base + half, base + half + 1)

        cols = pl.ds(pl.multiple_of(group * GROUP, GROUP), GROUP)
        for kind, value in (
            (0, lambda: dot_nn(seen_ref[:, 2 * rows : 3 * rows], q_ref[:, cols])),
            (1, lambda: dot_nn(seen_ref[...], k_ref[:, cols])),
            (2, lambda: dot_nn(seen_ref[...], v_ref[:, cols])),
        ):
            product = value()
            scaled = product * weight_ref[kind, :, cols].astype(jnp.float32)
            gain_ref[...] += scaled[:, 0:128] + scaled[:, 128:256]
            keep(slab_ref.at[group], product, kind)
            if kind:
                serve(base + 1 + kind, base + 2 + kind)

        @pl.loop(1, dp)
        def _(step):
            give(group, step).start()

    served += groups * 4

    part_ref[...] = small_ref[...]
    gains = jnp.sum(gain_ref[...].T, axis=0, keepdims=True)
    for row in range(width // 128):
        part_ref[0, row : row + 1, :] = gains[:, row * 128 : (row + 1) * 128]

    def scatter(step):
        to = lax.rem(me + step, ways)
        return pltpu.make_async_remote_copy(
            src_ref=part_ref.at[to], dst_ref=part_land.at[me],
            send_sem=small_send.at[step], recv_sem=small_recv.at[me],
            device_id=device(to), device_id_type=MESH,
        )

    def arrival(step):
        source = lax.rem(me - step + ways, ways)
        return pltpu.make_async_remote_copy(
            src_ref=part_ref.at[source], dst_ref=part_land.at[source],
            send_sem=small_send.at[step], recv_sem=small_recv.at[source],
            device_id=device(lax.rem(me + step, ways)), device_id_type=MESH,
        )

    def spread(step):
        return pltpu.make_async_remote_copy(
            src_ref=total_ref.at[me], dst_ref=total_ref.at[me],
            send_sem=spread_send.at[step], recv_sem=spread_recv.at[me],
            device_id=device(lax.rem(me + step, ways)), device_id_type=MESH,
        )

    def landing(step):
        source = lax.rem(me - step + ways, ways)
        return pltpu.make_async_remote_copy(
            src_ref=total_ref.at[source], dst_ref=total_ref.at[source],
            send_sem=spread_send.at[step], recv_sem=spread_recv.at[source],
            device_id=device(lax.rem(me + step, ways)), device_id_type=MESH,
        )

    @pl.loop(1, ways)
    def _(step):
        scatter(step).start()

    @pl.loop(0, blocks)
    def _(b):
        at = block_at(b)
        out_ref[at] = row_grad(2 * blocks + b) + dot_nt(q_ref[at], weight_ref[0])
        serve(served + 2 * b, served + 2 * b + 2)

    served += 2 * blocks

    def add(step, total):
        arrival(step).wait_recv()
        return total + part_land[lax.rem(me - step + ways, ways)]

    total_ref[me] = lax.fori_loop(1, ways, add, part_ref[me])

    @pl.loop(1, ways)
    def _(step):
        spread(step).start()

    serve(served, 2 * pieces)
    serve(2 * pieces, 2 * pieces + late)

    kinds = [[], [], [], []]
    for group in range(groups + 1):

        @pl.loop(1, dp)
        def _(step):
            take(group, step).wait_recv()

        own, landed = slabs(group)

        def add_slab(step, total):
            return total + landed[peer(dp - step)].astype(jnp.float32)

        total = lax.fori_loop(1, dp, add_slab, own[spot].astype(jnp.float32))
        for part in range(total.shape[1] // GROUP):
            kinds[3 if group == groups else part].append(
                total[:, part * GROUP : (part + 1) * GROUP]
            )

    share = width // tensor
    kinds = [jnp.concatenate(parts, axis=1) for parts in kinds]
    for target in range(tensor):
        mine = jnp.concatenate(
            [kind[:, target * share : (target + 1) * share] for kind in kinds], axis=1
        )
        line_out[target] = mine.astype(line_out.dtype)

        @pl.when(place == target)
        def _():
            sum_ref[...] = mine

    def line(step):
        return pltpu.make_async_remote_copy(
            src_ref=line_out.at[along(step)], dst_ref=line_land.at[place],
            send_sem=line_send.at[step], recv_sem=line_recv.at[place],
            device_id=(spot, along(step)), device_id_type=MESH,
        )

    def line_in(step):
        source = along(tensor - step)
        return pltpu.make_async_remote_copy(
            src_ref=line_out.at[source], dst_ref=line_land.at[source],
            send_sem=line_send.at[step], recv_sem=line_recv.at[source],
            device_id=(spot, along(step)), device_id_type=MESH,
        )

    for step in range(1, tensor):
        line(step).start()

    @pl.when(place < 2)
    def _():
        @pl.loop(0, pieces)
        def _(piece):
            source = place * pieces + piece
            pass_down(source).wait_recv()
            at = pl.ds(pl.multiple_of(piece * PIECE, PIECE), PIECE)
            out_ref[at] += joined(source)

    for step in range(1, tensor):
        line_in(step).wait_recv()
        sum_ref[...] += line_land[along(tensor - step)].astype(jnp.float32)

    @pl.loop(1, ways)
    def _(step):
        landing(step).wait_recv()

    for step in range(1, tensor):
        line(step).wait_send()

    @pl.loop(1, ways)
    def _(step):
        scatter(step).wait_send()
        spread(step).wait_send()

    for group in range(groups + 1):

        @pl.loop(1, dp)
        def _(step):
            give(group, step).wait_send()

    sent = jnp.where(place == tensor - 1, 2 * pieces, relayed)

    def sent_one(piece, carry):
        pass_down(piece).wait_send()
        return carry

    lax.fori_loop(0, sent, sent_one, 0)


def backward(parents, q, k, v, o, branch_grad, seen, weights, lse, small):
    dp, tensor = lax.axis_size("dp"), lax.axis_size("tensor")
    ways = dp * tensor
    rows, width = q.shape
    seen_rows = k.shape[0]
    depth = width // dp
    padded = -(-depth // 16) * 16
    pairs, groups, pieces = width // 128, width // GROUP, rows // PIECE
    slab = (groups, dp, padded, 3 * GROUP)
    proj = (dp, padded, width)
    low, full = jnp.bfloat16, jnp.float32
    dma = pltpu.SemaphoreType.DMA
    anywhere = pl.BlockSpec(memory_space=pl.ANY)
    here = pl.BlockSpec(memory_space=pltpu.VMEM)
    out, block, total = pl.pallas_call(
        lambda *refs: back_kernel(dp, tensor, depth, *refs),
        out_shape=(
            jax.ShapeDtypeStruct((rows, width), full),
            jax.ShapeDtypeStruct((padded, width), full),
            jax.ShapeDtypeStruct(small.shape, full),
        ),
        in_specs=[here] + [anywhere] * 7 + [here] * 2,
        out_specs=[here, here, here],
        scratch_shapes=[
            pltpu.VMEM((rows, width), low),
            pltpu.VMEM((seen_rows, width), low),
            pltpu.VMEM((seen_rows, width), low),
            pltpu.VMEM((rows, width), low),
            pltpu.VMEM((rows, width), low),
            pltpu.VMEM((rows, width), low),
            pltpu.VMEM((2, rows // 2, width), low),
            pltpu.VMEM((width, seen_rows), low),
            pltpu.VMEM(weights.shape, low),
            pltpu.VMEM((pairs, 2, rows), full),
            pltpu.VMEM((pairs, 128, rows), full),
            pltpu.VMEM((2 * rows, width), low),
            pltpu.VMEM((2 * rows, width), low),
            pltpu.VMEM((width, 128), full),
            pltpu.VMEM(slab, low),
            pltpu.VMEM(slab, low),
            pltpu.VMEM(proj, low),
            pltpu.VMEM(proj, low),
            pltpu.VMEM((tensor, padded, width), low),
            pltpu.VMEM((tensor, padded, width), low),
            pltpu.VMEM(small.shape, full),
            pltpu.VMEM(small.shape, full),
            dma((3,)), dma((3, pairs)), dma((2,)),
            dma((2 * pieces,)), dma((2 * pieces,)),
            dma((groups + 1, dp)), dma((groups + 1, dp)),
            dma((tensor,)), dma((tensor,)),
            dma((ways,)), dma((ways,)), dma((ways,)), dma((ways,)),
        ],
        compiler_params=pltpu.CompilerParams(
            collective_id=3, has_side_effects=True, vmem_limit_bytes=62 << 20
        ),
        name="attend_backward",
    )(parents, q, k, v, o, branch_grad, seen, weights, lse, small)
    return out, block[:depth], total


norm_eps = 1e-05
route_scale = 3.0
masked_score = -1e30
highest = lax.Precision.HIGHEST


def layer_norm(values, norm_gain):
    centred = values - jnp.mean(values, axis=-1, keepdims=True)
    spread = jnp.mean(centred * centred, axis=-1, keepdims=True)
    return centred * lax.rsqrt(spread + norm_eps) * norm_gain


def unit_rows(values):
    return values * lax.rsqrt(jnp.sum(values * values, axis=-1, keepdims=True) + 1.0)


def router_gate(normed, router_proj, expert_embed, picked):
    routed = jnp.dot(normed, router_proj, precision=highest)
    logits = route_scale * jnp.dot(unit_rows(routed), unit_rows(expert_embed).T, precision=highest)
    return jnp.sum(jax.nn.softmax(logits, axis=-1) * picked, axis=-1)


def gelu_exact(values):
    return jax.nn.gelu(values, approximate=False)


def slot_table(route_ids, order_ids, capacity):
    same_expert = route_ids[:, None] == route_ids[None, :]
    earlier = order_ids[None, :] < order_ids[:, None]
    ranking = jnp.sum(jnp.where(same_expert & earlier, 1, 0), axis=1).astype(jnp.int32)
    kept_mask = ranking < capacity
    column = route_ids * capacity + jnp.minimum(ranking, capacity - 1)
    return (column, kept_mask)


def low_dot(rows, weight):
    return jnp.dot(rows, weight, preferred_element_type=jnp.float32).astype(jnp.bfloat16)


def shards(
    tokens,
    norm1_gain,
    qkv_weight,
    attn_proj,
    norm2_gain,
    router_proj,
    expert_embed,
    expert_in,
    expert_out,
    routes,
    orders,
    leaf_parent,
    cotangent,
):
    rows_here = tokens.shape[0]
    model_width = tokens.shape[1]
    experts = expert_embed.shape[0]
    capacity = rows_here // experts
    dp_size, tensor_size = lax.axis_size("dp"), lax.axis_size("tensor")

    def hop(rows, chip_step, core_step):
        route = []
        for source in range(dp_size):
            chip, core = source // 2, source % 2
            route.append((source, (chip ^ chip_step) * 2 + (core ^ core_step)))
        return lax.ppermute(rows, "dp", route)

    def chip_blocks(rows):
        blocks = rows.reshape(experts, capacity, model_width)
        return [blocks[0]] + [hop(blocks[step], step, 0) for step in range(1, experts)]

    def across_chips(rows):
        return jnp.concatenate(chip_blocks(rows), axis=0)

    def with_partner(blocks):
        arrived = jnp.concatenate(blocks, axis=0)
        return jnp.concatenate([arrived, hop(arrived, 0, 1)], axis=0)

    def pair_sum(kept_rows, sent_rows):
        return (kept_rows + hop(sent_rows, 0, 1).astype(jnp.float32)).astype(jnp.bfloat16)

    hidden = tokens.astype(jnp.float32)
    normed_in, norm1_back = jax.vjp(layer_norm, hidden, norm1_gain)
    own_in = normed_in.astype(jnp.bfloat16)
    flat_qkv = qkv_weight.reshape(qkv_weight.shape[0], -1)
    place = lax.axis_index("tensor")
    leaf_blocks = rows_here // BRANCH
    first_leaf = jnp.maximum(place - 2, 0) * leaf_blocks
    leaf_parents = lax.dynamic_slice_in_dim(leaf_parent[0], first_leaf, leaf_blocks, 0) - 1
    parents = (leaf_parents[:, None] == jnp.arange(leaf_blocks)[None, :]).astype(jnp.float32)
    parents = jnp.broadcast_to(parents.reshape(-1, 1), (leaf_blocks * leaf_blocks, model_width))
    seen_in, weights = share_rows_and_weights(
        own_in, jnp.concatenate([flat_qkv, attn_proj.T], axis=1), parents
    )
    query_weight, key_weight, value_weight, proj_back = weights
    query_rows = low_dot(own_in, query_weight)
    key_rows = low_dot(seen_in, key_weight)
    value_rows = low_dot(seen_in, value_weight)
    attended, log_totals = attend(place[None].astype(jnp.int32), query_rows, key_rows, value_rows)
    branch_out = jnp.einsum(
        "sc,dc->sd", attended, proj_back, preferred_element_type=jnp.float32
    )
    mid_stream = hidden + branch_out
    normed_mid, norm2_back = jax.vjp(layer_norm, mid_stream, norm2_gain)
    moe_in = normed_mid.astype(jnp.bfloat16)
    route_ids = routes[:, 0]
    near_route = route_ids ^ (lax.axis_index("dp") // 2)
    column, kept_mask = slot_table(near_route, orders[0], capacity)
    picked = (route_ids[:, None] == jnp.arange(experts)[None, :]).astype(jnp.float32)
    gate_value, gate_back = jax.vjp(
        lambda normed_rows, route_proj, embed_rows: router_gate(
            normed_rows, route_proj, embed_rows, picked
        ),
        moe_in.astype(jnp.float32),
        router_proj,
        expert_embed,
    )
    select = (
        (column[:, None] == jnp.arange(experts * capacity)[None, :]) & kept_mask[:, None]
    ).astype(jnp.bfloat16)
    def to_slots(token_rows):
        return jnp.einsum(
            "ts,td->sd", select, token_rows, preferred_element_type=jnp.float32
        ).astype(jnp.bfloat16)

    def from_slots(slot_rows):
        return jnp.dot(select, slot_rows, preferred_element_type=jnp.float32)

    upstream = cotangent.astype(jnp.float32)
    slot_grads = to_slots((gate_value[:, None] * upstream).astype(jnp.bfloat16))
    row_blocks, slot_grads = lax.optimization_barrier(
        (chip_blocks(to_slots(moe_in)), slot_grads)
    )
    grad_blocks = chip_blocks(slot_grads)
    expert_rows = with_partner(row_blocks)
    active, slope, kept_result, sent_result = expert_forward(expert_rows, expert_in, expert_out)
    grad_blocks, kept_result, sent_result = lax.optimization_barrier(
        (grad_blocks, kept_result, sent_result)
    )
    arrived_grad = with_partner(grad_blocks)
    result_rows, late_grad = lax.optimization_barrier(
        (pair_sum(kept_result, sent_result), arrived_grad)
    )
    expert_result = from_slots(across_chips(result_rows))
    output = (mid_stream + gate_value[:, None] * expert_result).astype(jnp.bfloat16)
    out_weight_grad = jnp.einsum(
        "rf,rd->fd", active, arrived_grad, preferred_element_type=jnp.float32
    ).astype(jnp.bfloat16)
    up_grad, kept_grad, sent_grad = expert_back(late_grad, slope, expert_in, expert_out)
    in_weight_grad = jnp.einsum(
        "rf,rd->fd", up_grad, expert_rows, preferred_element_type=jnp.float32
    ).astype(jnp.bfloat16)
    moe_grad = from_slots(across_chips(pair_sum(kept_grad, sent_grad)))
    gate_grad = jnp.sum(upstream * expert_result, axis=-1)
    router_part, proj_grad, embed_grad = gate_back(gate_grad)
    mid_part, gain2_grad = norm2_back(moe_grad + router_part)
    mid_grad = upstream + mid_part
    expert_in_grad = (
        lax.psum_scatter(in_weight_grad, "tensor", scatter_dimension=0, tiled=True)
        .astype(jnp.float32)
        .T
    )
    expert_out_grad = lax.psum_scatter(
        out_weight_grad, "tensor", scatter_dimension=0, tiled=True
    ).astype(jnp.float32)
    branch_grad = mid_grad.astype(jnp.bfloat16)
    later = [gain2_grad, proj_grad, embed_grad]
    flat = jnp.concatenate([jnp.zeros_like(norm1_gain)] + [part.reshape(-1) for part in later])
    ways = dp_size * tensor_size
    lanes = -(-flat.shape[0] // (ways * 8 * 128)) * 128
    small = jnp.pad(flat, (0, ways * 8 * lanes - flat.shape[0])).reshape(ways, 8, lanes)
    input_grad, grad_block, totals = backward(
        parents, query_rows, key_rows, value_rows, attended, branch_grad, seen_in, weights,
        log_totals, small,
    )
    qkv_grad = grad_block[:, : flat_qkv.shape[1]].reshape(qkv_weight.shape)
    attn_proj_grad = grad_block[:, flat_qkv.shape[1] :].T
    totals = totals.reshape(-1)
    gain1_sum = totals[:model_width] / norm1_gain
    gain2_sum, router_sum, embed_sum = (
        totals[first : first + part.size].reshape(part.shape)
        for first, part in zip(
            (model_width, 2 * model_width, 2 * model_width + proj_grad.size), later
        )
    )
    token_part, _ = norm1_back(input_grad)
    token_grad = mid_grad + token_part
    return (
        output,
        token_grad,
        gain1_sum,
        qkv_grad,
        attn_proj_grad,
        gain2_sum,
        router_sum,
        embed_sum,
        expert_in_grad,
        expert_out_grad,
    )


def solution(mesh):
    in_specs = (
        P(("dp", "tensor"), None),
        P(),
        P("dp", None, "tensor"),
        P("tensor", "dp"),
        P(),
        P(),
        P(),
        P(None, "dp"),
        P("dp", None),
        P(("dp", "tensor"), None),
        P(("dp", "tensor"), None),
        P("dp", None),
        P(("dp", "tensor"), None),
    )
    out_specs = (
        P(("dp", "tensor"), None),
        P(("dp", "tensor"), None),
        P(),
        P("dp", None, "tensor"),
        P("tensor", "dp"),
        P(),
        P(),
        P(),
        P(None, ("dp", "tensor")),
        P(("dp", "tensor"), None),
    )
    return jax.shard_map(shards, mesh=mesh, in_specs=in_specs, out_specs=out_specs, check_vma=False)
```

```python
import functools
import math

import jax
import jax.numpy as jnp
from jax import lax
from jax.experimental import pallas as pl
from jax.experimental.pallas import tpu as pltpu
from jax.sharding import PartitionSpec as P

HEAD_DIM = 64
TRUNK = 1024
BRANCH = 256
MASKED = -1e30
LOG2E = math.log2(math.e)
EXP_SCALE = HEAD_DIM ** (-0.5) * LOG2E

NT = (((1,), (1,)), ((), ()))
NN = (((1,), (0,)), ((), ()))


def dot_nt(a, b):
    return lax.dot_general(a, b, NT, preferred_element_type=jnp.float32)


def dot_nn(a, b):
    return lax.dot_general(a, b, NN, preferred_element_type=jnp.float32)


def head_lanes(shape, dim, head):
    return lax.broadcasted_iota(jnp.int32, shape, dim) // HEAD_DIM == head


def fwd_kernel(place_ref, q_ref, k_ref, v_ref, o_ref, lse_ref, vt_ref, acc_ref):
    place = place_ref[0]
    rows = q_ref.shape[0]
    blocks = rows // BRANCH
    flipped = v_ref[...].T
    for head in range(2):
        vt_ref[head] = jnp.where(
            head_lanes(flipped.shape, 0, head), flipped, jnp.ones_like(flipped)
        )

    def start(block, head, in_trunk):
        queries = q_ref[block * BRANCH : (block + 1) * BRANCH]
        queries = jnp.where(head_lanes(queries.shape, 1, head), queries, jnp.zeros_like(queries))
        firsts = list(range(0, TRUNK, BRANCH))
        if not in_trunk:
            firsts += [rows + block * BRANCH, 2 * rows + block * BRANCH]
        scores = [dot_nt(k_ref[first : first + BRANCH], queries) for first in firsts]

        def causal(tile, offset):
            keys = lax.broadcasted_iota(jnp.int32, tile.shape, 0) + offset
            at = lax.broadcasted_iota(jnp.int32, tile.shape, 1)
            return jnp.where(keys <= at, tile, MASKED)

        if in_trunk:
            scores = [
                causal(tile, first - block * BRANCH) for tile, first in zip(scores, firsts)
            ]
        else:
            scores[-2] = jnp.where(place > 1, scores[-2], MASKED)
            scores[-1] = causal(scores[-1], 0)
        top = jnp.max(functools.reduce(jnp.maximum, scores), axis=0, keepdims=True)
        return firsts, scores, top

    def middle(firsts, scores, top):
        shift = top * EXP_SCALE
        probs = [jnp.exp2(tile * EXP_SCALE - shift).astype(jnp.bfloat16) for tile in scores]
        return firsts, probs, top

    def finish(block, head, firsts, probs, top):
        acc = None
        for first, tile in zip(firsts, probs):
            part = dot_nn(vt_ref[head, :, first : first + BRANCH], tile)
            acc = part if acc is None else acc + part
        mine, other = head * HEAD_DIM, (1 - head) * HEAD_DIM
        total = acc[other : other + 1]
        cols = slice(block * BRANCH, (block + 1) * BRANCH)
        acc_ref[mine : mine + HEAD_DIM, cols] = acc[mine : mine + HEAD_DIM] / total
        lse_ref[0, head : head + 1, cols] = top * EXP_SCALE + jnp.log2(total)

    def run(in_trunk):
        work = [(block, head) for block in range(blocks) for head in range(2)]
        ready, held = start(*work[0], in_trunk), None
        for at, item in enumerate(work):
            now = ready
            if at + 1 < len(work):
                ready = start(*work[at + 1], in_trunk)
            done = middle(*now)
            if held is not None:
                finish(*held)
            held = (*item, *done)
        finish(*held)

    @pl.when(place == 0)
    def _():
        run(True)

    @pl.when(place > 0)
    def _():
        run(False)

    o_ref[...] = acc_ref[...].T.astype(o_ref.dtype)


def attend(place, q, k, v):
    rows, width = q.shape
    keys = k.shape[0]
    pairs = width // 128
    few = pl.BlockSpec((rows, 128), lambda p, m: (0, p))
    many = pl.BlockSpec((keys, 128), lambda p, m: (0, p))
    return pl.pallas_call(
        fwd_kernel,
        out_shape=(
            jax.ShapeDtypeStruct((rows, width), jnp.bfloat16),
            jax.ShapeDtypeStruct((pairs, 2, rows), jnp.float32),
        ),
        grid_spec=pltpu.PrefetchScalarGridSpec(
            num_scalar_prefetch=1,
            grid=(pairs,),
            in_specs=[few, many, many],
            out_specs=[few, pl.BlockSpec((1, 2, rows), lambda p, m: (p, 0, 0))],
            scratch_shapes=[
                pltpu.VMEM((2, 128, keys), jnp.bfloat16),
                pltpu.VMEM((128, rows), jnp.float32),
            ],
        ),
        compiler_params=pltpu.CompilerParams(vmem_limit_bytes=48 << 20),
        name="attend_forward",
    )(place, q, k, v)


ROWS = 256
HALF_ROOT = math.sqrt(0.5)
PDF_SCALE = 1.0 / math.sqrt(2.0 * math.pi)
CHUNK = 512


def expert_fwd_kernel(x_ref, in_ref, out_ref, active_ref, slope_ref, keep_ref, send_ref):
    step = pl.program_id(0)
    half = pl.num_programs(0) // 2
    rows = x_ref[...]
    total = None
    for first in range(0, in_ref.shape[1], CHUNK):
        cols = slice(first, first + CHUNK)
        up = dot_nn(rows, in_ref[:, cols])
        below = 0.5 * (1.0 + lax.erf(up * HALF_ROOT))
        active = (up * below).astype(jnp.bfloat16)
        slope = below + up * (jnp.exp(-0.5 * up * up) * PDF_SCALE)
        active_ref[:, cols] = active
        slope_ref[:, cols] = slope.astype(jnp.bfloat16)
        part = dot_nn(active, out_ref[cols])
        total = part if total is None else total + part

    @pl.when(step < half)
    def _():
        keep_ref[...] = total

    @pl.when(step >= half)
    def _():
        send_ref[...] = total.astype(send_ref.dtype)


def expert_bwd_kernel(grad_ref, slope_ref, in_ref, out_ref, upgrad_ref, keep_ref, send_ref):
    step = pl.program_id(0)
    half = pl.num_programs(0) // 2
    grads = grad_ref[...]
    total = None
    for first in range(0, in_ref.shape[1], CHUNK):
        cols = slice(first, first + CHUNK)
        active_grad = dot_nt(grads, out_ref[cols])
        up_grad = (active_grad * slope_ref[:, cols].astype(jnp.float32)).astype(jnp.bfloat16)
        upgrad_ref[:, cols] = up_grad
        part = dot_nt(up_grad, in_ref[:, cols])
        total = part if total is None else total + part

    @pl.when(step < half)
    def _():
        keep_ref[...] = total

    @pl.when(step >= half)
    def _():
        send_ref[...] = total.astype(send_ref.dtype)


def split_specs(count, width):
    half = count // 2
    return [
        pl.BlockSpec((ROWS, width), lambda i: (jnp.minimum(i, half - 1), 0)),
        pl.BlockSpec((ROWS, width), lambda i: (jnp.maximum(i - half, 0), 0)),
    ]


def expert_forward(x, w_in, w_out):
    rows, width = x.shape
    hidden = w_in.shape[1]
    count = rows // ROWS
    def wide(cols):
        return pl.BlockSpec((ROWS, cols), lambda i: (i, 0))
    def whole(shape):
        return pl.BlockSpec(shape, lambda i: (0, 0), pipeline_mode=pl.Buffered(1))
    return pl.pallas_call(
        expert_fwd_kernel,
        grid=(count,),
        in_specs=[wide(width), whole(w_in.shape), whole(w_out.shape)],
        out_specs=[wide(hidden), wide(hidden)] + split_specs(count, width),
        out_shape=(
            jax.ShapeDtypeStruct((rows, hidden), jnp.bfloat16),
            jax.ShapeDtypeStruct((rows, hidden), jnp.bfloat16),
            jax.ShapeDtypeStruct((rows // 2, width), jnp.float32),
            jax.ShapeDtypeStruct((rows // 2, width), jnp.bfloat16),
        ),
        cost_estimate=pl.CostEstimate(flops=4 * rows * width * hidden, bytes_accessed=24 << 20, transcendentals=2 * rows * hidden),
        compiler_params=pltpu.CompilerParams(vmem_limit_bytes=40 << 20),
        name="expert_forward",
    )(x, w_in, w_out)


def expert_back(grads, slope, w_in, w_out):
    rows, width = grads.shape
    hidden = w_in.shape[1]
    count = rows // ROWS
    def wide(cols):
        return pl.BlockSpec((ROWS, cols), lambda i: (i, 0))
    def whole(shape):
        return pl.BlockSpec(shape, lambda i: (0, 0), pipeline_mode=pl.Buffered(1))
    return pl.pallas_call(
        expert_bwd_kernel,
        grid=(count,),
        in_specs=[wide(width), wide(hidden), whole(w_in.shape), whole(w_out.shape)],
        out_specs=[wide(hidden)] + split_specs(count, width),
        out_shape=(
            jax.ShapeDtypeStruct((rows, hidden), jnp.bfloat16),
            jax.ShapeDtypeStruct((rows // 2, width), jnp.float32),
            jax.ShapeDtypeStruct((rows // 2, width), jnp.bfloat16),
        ),
        cost_estimate=pl.CostEstimate(flops=4 * rows * width * hidden, bytes_accessed=24 << 20, transcendentals=0),
        compiler_params=pltpu.CompilerParams(vmem_limit_bytes=40 << 20),
        name="expert_backward",
    )(grads, slope, w_in, w_out)


MESH = pl.DeviceIdType.MESH


PIECE = 64


def greet(peers):
    barrier = pltpu.get_barrier_semaphore()
    for peer in peers:
        pl.semaphore_signal(barrier, inc=1, device_id=peer, device_id_type=MESH)
    pl.semaphore_wait(barrier, len(peers))


def share_kernel(dp, tensor, own_ref, block_ref, parent_ref, seen_ref, out_ref, weights_ref,
                 ordered_ref, row_send, row_recv,
                 line_send, line_recv, chip_send, chip_recv, pair_send, pair_recv):
    spot, place = lax.axis_index("dp"), lax.axis_index("tensor")
    chip, core = spot // 2, lax.rem(spot, 2)
    chips = dp // 2
    rows = own_ref.shape[0]
    pieces = rows // PIECE
    part_width = out_ref.shape[2] // tensor
    partner = (chip * 2 + 1 - core, place)

    def along(step):
        return lax.rem(place + step, tensor)

    def chip_at(step):
        return lax.rem(chip + step, chips)

    greet(
        [(spot, along(step)) for step in range(1, tensor)]
        + [(chip_at(step) * 2 + core, place) for step in range(1, chips)]
        + [partner]
    )

    def pass_on(part, piece, fresh):
        at = pl.ds(part * rows + piece * PIECE, PIECE)
        source = own_ref.at[pl.ds(piece * PIECE, PIECE)] if fresh else seen_ref.at[at]
        return pltpu.make_async_remote_copy(
            src_ref=source, dst_ref=seen_ref.at[at],
            send_sem=row_send.at[part, piece], recv_sem=row_recv.at[part, piece],
            device_id=(spot, lax.rem(place + 1, tensor)), device_id_type=MESH,
        )

    def line(step):
        return pltpu.make_async_remote_copy(
            src_ref=block_ref, dst_ref=weights_ref.at[place, spot],
            send_sem=line_send.at[step], recv_sem=line_recv.at[place],
            device_id=(spot, along(step)), device_id_type=MESH,
        )

    def line_in(step):
        source = along(tensor - step)
        return pltpu.make_async_remote_copy(
            src_ref=block_ref, dst_ref=weights_ref.at[source, spot],
            send_sem=line_send.at[step], recv_sem=line_recv.at[source],
            device_id=(spot, along(step)), device_id_type=MESH,
        )

    def plane(part, step):
        block = weights_ref.at[part, spot]
        return pltpu.make_async_remote_copy(
            src_ref=block, dst_ref=block,
            send_sem=chip_send.at[part, step], recv_sem=chip_recv.at[part, chip],
            device_id=(chip_at(step) * 2 + core, place), device_id_type=MESH,
        )

    def plane_in(part, step):
        source = chip_at(chips - step)
        block = weights_ref.at[part, source * 2 + core]
        return pltpu.make_async_remote_copy(
            src_ref=block, dst_ref=block,
            send_sem=chip_send.at[part, step], recv_sem=chip_recv.at[part, source],
            device_id=(chip_at(step) * 2 + core, place), device_id_type=MESH,
        )

    def across(part, source, source_core):
        block = weights_ref.at[part, source * 2 + source_core]
        return pltpu.make_async_remote_copy(
            src_ref=block, dst_ref=block,
            send_sem=pair_send.at[part, source], recv_sem=pair_recv.at[part, source],
            device_id=partner, device_id_type=MESH,
        )

    for step in range(1, tensor):
        line(step).start()

    def row_steps(first, last):
        @pl.loop(first, last)
        def _(piece):
            @pl.when(place == 0)
            def _():
                pass_on(0, piece, True).start()

            @pl.when(place > 0)
            def _():
                pass_on(0, piece, False).wait_recv()

            @pl.when((place > 0) & (place < tensor - 1))
            def _():
                pass_on(0, piece, False).start()

            @pl.when(place == 1)
            def _():
                pass_on(1, piece, True).start()

            @pl.when(place > 1)
            def _():
                pass_on(1, piece, False).wait_recv()

            @pl.when((place > 1) & (place < tensor - 1))
            def _():
                pass_on(1, piece, False).start()

    weights_ref[place, spot] = block_ref[...]
    seen_ref[2 * rows :] = own_ref[...]

    @pl.when(place < 2)
    def _():
        seen_ref[rows : 2 * rows] = own_ref[...]

    @pl.when(place == 0)
    def _():
        seen_ref[0:rows] = own_ref[...]

    row_steps(0, pieces // 4)
    for step in range(tensor):
        part = along(tensor - step)
        if step:
            line_in(step).wait_recv()

        @pl.loop(1, chips)
        def _(hop):
            plane(part, hop).start()

        across(part, chip, core).start()
    row_steps(pieces // 4, (pieces * 5) // 8)
    for step in range(tensor):
        part = along(tensor - step)

        @pl.loop(1, chips)
        def _(hop):
            plane_in(part, hop).wait_recv()
            across(part, chip_at(chips - hop), core).start()

    row_steps((pieces * 5) // 8, pieces)
    for part in range(tensor):

        @pl.loop(0, chips)
        def _(source):
            across(part, source, 1 - core).wait_recv()
            across(part, source, core).wait_send()

        @pl.loop(1, chips)
        def _(hop):
            plane(part, hop).wait_send()

    for step in range(1, tensor):
        line(step).wait_send()

    @pl.when(place < tensor - 1)
    def _():
        @pl.loop(0, pieces)
        def _(piece):
            pass_on(0, piece, False).wait_send()

    @pl.when((place > 0) & (place < tensor - 1))
    def _():
        @pl.loop(0, pieces)
        def _(piece):
            pass_on(1, piece, False).wait_send()

    @pl.when(place > 1)
    def _():
        blocks = rows // BRANCH
        branches = [
            seen_ref[rows + branch * BRANCH : rows + (branch + 1) * BRANCH]
            for branch in range(blocks)
        ]
        for leaf in range(blocks):
            chosen = None
            for branch in range(blocks):
                at = leaf * blocks + branch
                part = branches[branch] * parent_ref[at : at + 1].astype(own_ref.dtype)
                chosen = part if chosen is None else chosen + part
            ordered_ref[leaf * BRANCH : (leaf + 1) * BRANCH] = chosen
        seen_ref[rows : 2 * rows] = ordered_ref[...]

    @pl.loop(0, dp)
    def _(source):
        depth = block_ref.shape[0]
        at = pl.ds(pl.multiple_of(source * depth, depth), depth)
        for kind in range(out_ref.shape[0]):
            cols = slice(kind * part_width, (kind + 1) * part_width)
            out_ref[kind, at] = jnp.concatenate(
                [weights_ref[part, source][:, cols] for part in range(tensor)], axis=1
            )


def share_rows_and_weights(own, block, parents):
    dp, tensor = lax.axis_size("dp"), lax.axis_size("tensor")
    rows, width = own.shape
    depth, cols = block.shape
    pieces, chips = rows // PIECE, dp // 2
    kinds = cols * tensor // width
    padded = -(-depth // 16) * 16
    block = jnp.pad(block, ((0, padded - depth), (0, 0)))
    dma = pltpu.SemaphoreType.DMA
    here = pl.BlockSpec(memory_space=pltpu.VMEM)
    seen, weights = pl.pallas_call(
        lambda *refs: share_kernel(dp, tensor, *refs),
        out_shape=(
            jax.ShapeDtypeStruct((3 * rows, width), own.dtype),
            jax.ShapeDtypeStruct((kinds, dp * padded, width), block.dtype),
        ),
        in_specs=[here, here, here],
        out_specs=[here, here],
        scratch_shapes=[
            pltpu.VMEM((tensor, dp, padded, cols), block.dtype),
            pltpu.VMEM(own.shape, own.dtype),
            dma((2, pieces)), dma((2, pieces)),
            dma((tensor,)), dma((tensor,)),
            dma((tensor, chips)), dma((tensor, chips)),
            dma((tensor, chips)), dma((tensor, chips)),
        ],
        compiler_params=pltpu.CompilerParams(
            collective_id=2, has_side_effects=True, vmem_limit_bytes=48 << 20
        ),
        name="share_rows_and_weights",
    )(own, block, parents)
    weights = weights.reshape(kinds, dp, padded, width)[:, :, :depth]
    return seen, weights.reshape(kinds, dp * depth, width)


TN = (((0,), (0,)), ((), ()))
GROUP = 256


def dot_tn(a, b):
    return lax.dot_general(a, b, TN, preferred_element_type=jnp.float32)


def back_kernel(
    dp, tensor, depth,
    parent_ref, q_in, k_in, v_in, o_in, grad_in, seen_in, weight_in, lse_ref, small_ref,
    out_ref, sum_ref, total_ref,
    q_ref, k_ref, v_ref, o_ref, bg_ref, g_ref, stage_ref, seen_ref, weight_ref,
    delta_ref, dqt_ref, rows_ref, land_ref, gain_ref,
    slab_ref, pair_land, chip_land, line_out, line_land, part_ref, part_land,
    load_sem, pair_sem, stage_sem, row_send, row_recv,
    pair_send, pair_recv, chip_send, chip_recv,
    line_send, line_recv, small_send, small_recv, spread_send, spread_recv,
):
    spot, place = lax.axis_index("dp"), lax.axis_index("tensor")
    ways = dp * tensor
    me = spot * tensor + place
    scale = HEAD_DIM ** (-0.5)
    rows, width = q_ref.shape
    pairs = width // 128
    groups = width // GROUP
    blocks = rows // BRANCH
    pieces = rows // PIECE
    stage_rows = stage_ref.shape[1]

    def device(index):
        return (index // tensor, lax.rem(index, tensor))

    def along(step):
        return lax.rem(place + step, tensor)

    chips = dp // 2
    chip, core = spot // 2, lax.rem(spot, 2)

    def chip_at(step):
        return lax.rem(chip + step, chips)

    def block_at(b):
        return pl.ds(pl.multiple_of(b * BRANCH, BRANCH), BRANCH)

    barrier = pltpu.get_barrier_semaphore()

    @pl.loop(1, ways)
    def _(step):
        pl.semaphore_signal(
            barrier, inc=1, device_id=device(lax.rem(me + step, ways)), device_id_type=MESH
        )

    def lanes(pair):
        return pl.ds(pl.multiple_of(pair * 128, 128), 128)

    grad_load = pltpu.make_async_copy(grad_in, bg_ref, load_sem.at[0])
    weight_load = pltpu.make_async_copy(weight_in, weight_ref, load_sem.at[1])
    value_load = pltpu.make_async_copy(o_in, o_ref, load_sem.at[2])

    def pair_loads(pair):
        return [
            pltpu.make_async_copy(
                source.at[:, lanes(pair)], held.at[:, lanes(pair)], pair_sem.at[which, pair]
            )
            for which, (source, held) in enumerate(((q_in, q_ref), (k_in, k_ref), (v_in, v_ref)))
        ]

    def stage(part):
        slot = lax.rem(part, 2)
        at = pl.ds(pl.multiple_of(part * stage_rows, stage_rows), stage_rows)
        return pltpu.make_async_copy(seen_in.at[at], stage_ref.at[slot], stage_sem.at[slot])

    grad_load.start()
    weight_load.start()
    value_load.start()

    @pl.loop(0, pairs)
    def _(pair):
        for load in pair_loads(pair):
            load.start()

    grad_load.wait()
    weight_load.wait()
    value_load.wait()

    def keep(held, value, kind):
        cols = slice(kind * GROUP, (kind + 1) * GROUP)
        if depth % 16:
            for target in range(dp):
                held[target, 0:depth, cols] = value[target * depth : (target + 1) * depth].astype(
                    slab_ref.dtype
                )
        else:
            held[:, :, cols] = value.reshape(dp, depth, GROUP).astype(slab_ref.dtype)

    for group in range(groups):
        cols = slice(group * GROUP, (group + 1) * GROUP)
        keep(slab_ref.at[groups], dot_tn(bg_ref[...], o_ref[:, cols]), group)

    @pl.loop(0, blocks)
    def _(b):
        at = block_at(b)
        g_ref[at] = dot_nn(bg_ref[at], weight_ref[3]).astype(g_ref.dtype)

    pl.semaphore_wait(barrier, ways - 1)

    def halve(group, source):
        return pltpu.make_async_remote_copy(
            src_ref=slab_ref.at[group, source * 2 + 1 - core],
            dst_ref=pair_land.at[group, source],
            send_sem=pair_send.at[group, source], recv_sem=pair_recv.at[group, source],
            device_id=(chip * 2 + 1 - core, place), device_id_type=MESH,
        )

    def give(group, step):
        to = chip_at(step) * 2 + core
        return pltpu.make_async_remote_copy(
            src_ref=slab_ref.at[group, to], dst_ref=chip_land.at[group, chip],
            send_sem=chip_send.at[group, step], recv_sem=chip_recv.at[group, chip],
            device_id=(to, place), device_id_type=MESH,
        )

    def take(group, step):
        source = chip_at(chips - step)
        return pltpu.make_async_remote_copy(
            src_ref=slab_ref.at[group, source * 2 + core], dst_ref=chip_land.at[group, source],
            send_sem=chip_send.at[group, step], recv_sem=chip_recv.at[group, source],
            device_id=(chip_at(step) * 2 + core, place), device_id_type=MESH,
        )

    def share_slabs(group):
        @pl.loop(0, chips)
        def _(source):
            halve(group, source).start()

    def send_slabs(group):
        @pl.loop(0, chips)
        def _(step):
            to = chip_at(step)
            halve(group, to).wait_recv()
            mine = slab_ref[group, to * 2 + core].astype(jnp.float32)
            mine = mine + pair_land[group, to].astype(jnp.float32)
            slab_ref[group, to * 2 + core] = mine.astype(slab_ref.dtype)

            @pl.when(step > 0)
            def _():
                give(group, step).start()

    share_slabs(groups)

    @pl.loop(0, pairs)
    def _(pair):
        for load in pair_loads(pair):
            load.wait()
        product = g_ref[:, lanes(pair)].astype(jnp.float32)
        product = (product * o_ref[:, lanes(pair)].astype(jnp.float32)).T
        for head in range(2):
            delta_ref[pair, head : head + 1, :] = jnp.sum(
                product[head * HEAD_DIM : (head + 1) * HEAD_DIM], axis=0, keepdims=True
            )
        dqt_ref[pair] = jnp.zeros(dqt_ref.shape[1:], dqt_ref.dtype)

    def sweep(pair, tiles):
        work = [(tile, head) for tile in range(len(tiles)) for head in range(2)]
        sums = [[None, None] for _ in tiles]
        keys, flipped = {}, {}

        def key_block(tile):
            row = tiles[tile][0]
            if id(row) not in keys:
                kb = k_ref[pl.ds(row, BRANCH), lanes(pair)]
                vb = v_ref[pl.ds(row, BRANCH), lanes(pair)]
                masked = []
                for head in range(2):
                    mine = head_lanes(kb.shape, 1, head)
                    masked.append(
                        (
                            jnp.where(mine, kb, jnp.zeros_like(kb)),
                            jnp.where(mine, vb, jnp.zeros_like(vb)),
                        )
                    )
                keys[id(row)] = masked
                flipped[id(row)] = kb.T
            return keys[id(row)], flipped[id(row)]

        def start(tile, head):
            at = pl.ds(tiles[tile][1], BRANCH)
            kb, vb = key_block(tile)[0][head]
            return dot_nt(kb, q_ref[at, lanes(pair)]), dot_nt(vb, g_ref[at, lanes(pair)])

        def middle(tile, head, scores, prob_grad):
            at = pl.ds(tiles[tile][1], BRANCH)
            probs = jnp.exp2(scores * EXP_SCALE - lse_ref[pair, head : head + 1, at])
            if tiles[tile][2] is not None:
                probs = tiles[tile][2](probs)
            score_grad = probs * (prob_grad - delta_ref[pair, head : head + 1, at])
            return probs.astype(jnp.bfloat16), score_grad.astype(jnp.bfloat16)

        def finish(tile, head, probs, score_grad):
            at = pl.ds(tiles[tile][1], BRANCH)
            parts = (
                dot_nn(score_grad, q_ref[at, lanes(pair)]),
                dot_nn(probs, g_ref[at, lanes(pair)]),
            )
            for which in range(2):
                held = sums[tile][which]
                if head == 0:
                    sums[tile][which] = parts[which]
                else:
                    first = head_lanes(held.shape, 1, 0)
                    sums[tile][which] = jnp.where(first, held, parts[which])
            mine = slice(head * HEAD_DIM, (head + 1) * HEAD_DIM)
            dqt_ref[pair, mine, at] += dot_nn(key_block(tile)[1][mine], score_grad)

        ready = start(*work[0])
        held = None
        for at, item in enumerate(work):
            now = ready
            if at + 1 < len(work):
                ready = start(*work[at + 1])
            done = middle(*item, *now)
            if held is not None:
                finish(*held)
            held = (*item, *done)
        finish(*held)
        return sums

    def causal(key_row, query_row):
        def mask_of(probs):
            keys = lax.broadcasted_iota(jnp.int32, probs.shape, 0) + key_row
            at = lax.broadcasted_iota(jnp.int32, probs.shape, 1) + query_row
            return jnp.where(keys <= at, probs, 0.0)

        return mask_of

    def put(pair, row, dk, dv):
        at = pl.ds(row, BRANCH)
        k_ref[at, lanes(pair)] = (dk * scale).astype(k_ref.dtype)
        v_ref[at, lanes(pair)] = dv.astype(v_ref.dtype)

    def pass_down(piece):
        at = pl.ds(pl.multiple_of(piece * PIECE, PIECE), PIECE)
        return pltpu.make_async_remote_copy(
            src_ref=rows_ref.at[at], dst_ref=land_ref.at[at],
            send_sem=row_send.at[piece], recv_sem=row_recv.at[piece],
            device_id=(spot, lax.rem(place + tensor - 1, tensor)), device_id_type=MESH,
        )

    def row_grad(b):
        at = block_at(b)
        return dot_nt(k_ref[at], weight_ref[1]) + dot_nt(v_ref[at], weight_ref[2])

    def hand_down(b, total):
        rows_ref[block_at(b)] = total.astype(rows_ref.dtype)

        @pl.when(place == tensor - 1)
        def _():
            for piece in range(BRANCH // PIECE):
                pass_down(b * (BRANCH // PIECE) + piece).start()

    def joined(piece):
        at = pl.ds(pl.multiple_of(piece * PIECE, PIECE), PIECE)
        return rows_ref[at].astype(jnp.float32) + land_ref[at].astype(jnp.float32)

    middle_place = (place > 0) & (place < tensor - 1)
    late = 3 * jnp.maximum(tensor - 2 - place, 0)
    first_relay = jnp.where(place > 1, 0, pieces)
    last_relay = jnp.where(middle_place, 2 * pieces, first_relay)

    def piece_of(order):
        return lax.rem(order + pieces, 2 * pieces)

    def serve(first, last):
        def one(order, carry):
            piece = piece_of(order)
            pass_down(piece).wait_recv()
            at = pl.ds(pl.multiple_of(piece * PIECE, PIECE), PIECE)
            rows_ref[at] = joined(piece).astype(rows_ref.dtype)
            pass_down(piece).start()
            return carry

        low = jnp.clip(first - late, first_relay, last_relay)
        lax.fori_loop(low, jnp.clip(last - late, low, last_relay), one, 0)

    @pl.loop(0, pairs)
    def _(pair):
        @pl.when(place == 0)
        def _():
            for ref in (k_ref, v_ref):
                ref[rows : 3 * rows, lanes(pair)] = jnp.zeros((2 * rows, 128), ref.dtype)

        @pl.when(place > 0)
        def _():
            def seen_parent(probs):
                return jnp.where(place > 1, probs, 0.0)

            spots = range(0, rows, BRANCH)
            sums = sweep(pair, [(rows + at, at, seen_parent) for at in spots])
            for at, part in zip(spots, sums):
                put(pair, rows + at, *part)

    send_slabs(groups)

    @pl.loop(0, blocks)
    def _(leaf):
        out_ref[block_at(leaf)] = row_grad(blocks + leaf)

    for branch in range(blocks):
        total = None
        for leaf in range(blocks):
            at = leaf * blocks + branch
            part = out_ref[leaf * BRANCH : (leaf + 1) * BRANCH] * parent_ref[at : at + 1]
            total = part if total is None else total + part
        hand_down(blocks + branch, total)

    stage(0).start()

    @pl.loop(0, blocks)
    def _(b):
        row = pl.multiple_of(b * BRANCH, BRANCH)

        @pl.loop(0, pairs)
        def _(pair):
            def finish_block(masked):
                tiles = [
                    (row, first, causal(row, first) if masked else None)
                    for first in range(0, rows, BRANCH)
                ]
                sums = sweep(pair, tiles)
                put(pair, row, sum(part[0] for part in sums), sum(part[1] for part in sums))

            @pl.when(place == 0)
            def _():
                finish_block(True)

            @pl.when(place > 0)
            def _():
                finish_block(False)

            slot = b * pairs + pair
            serve(slot - 1, slot)

        for _half in range(2):
            part = b * 2 + _half

            @pl.when(part < 3 * rows // stage_rows)
            def _():
                stage(part).wait()

                @pl.when(part + 1 < 3 * rows // stage_rows)
                def _():
                    stage(part + 1).start()

                at = pl.ds(pl.multiple_of(part * stage_rows, stage_rows), stage_rows)
                seen_ref[:, at] = stage_ref[lax.rem(part, 2)].T

        hand_down(b, row_grad(b))

    served = blocks * pairs - 1

    gain_ref[...] = jnp.zeros_like(gain_ref)

    @pl.loop(0, groups)
    def _(group):
        base = served + group * 4

        @pl.loop(0, 2)
        def _(half):
            pair = group * 2 + half

            @pl.when(place > 0)
            def _():
                spots = range(0, rows, BRANCH)
                sums = sweep(pair, [(2 * rows + at, at, causal(0, 0)) for at in spots])
                for at, part in zip(spots, sums):
                    put(pair, 2 * rows + at, *part)

            q_ref[:, lanes(pair)] = (dqt_ref[pair] * scale).T.astype(q_ref.dtype)
            serve(base + half, base + half + 1)

        cols = pl.ds(pl.multiple_of(group * GROUP, GROUP), GROUP)
        for kind, value in (
            (0, lambda: dot_nn(seen_ref[:, 2 * rows : 3 * rows], q_ref[:, cols])),
            (1, lambda: dot_nn(seen_ref[...], k_ref[:, cols])),
            (2, lambda: dot_nn(seen_ref[...], v_ref[:, cols])),
        ):
            product = value()
            scaled = product * weight_ref[kind, :, cols].astype(jnp.float32)
            gain_ref[...] += scaled[:, 0:128] + scaled[:, 128:256]
            keep(slab_ref.at[group], product, kind)
            if kind:
                serve(base + 1 + kind, base + 2 + kind)

        share_slabs(group)

        @pl.when(group > 0)
        def _():
            send_slabs(group - 1)

    served += groups * 4

    part_ref[...] = small_ref[...]
    gains = jnp.sum(gain_ref[...].T, axis=0, keepdims=True)
    for row in range(width // 128):
        part_ref[0, row : row + 1, :] = gains[:, row * 128 : (row + 1) * 128]

    def scatter(step):
        to = lax.rem(me + step, ways)
        return pltpu.make_async_remote_copy(
            src_ref=part_ref.at[to], dst_ref=part_land.at[me],
            send_sem=small_send.at[step], recv_sem=small_recv.at[me],
            device_id=device(to), device_id_type=MESH,
        )

    def arrival(step):
        source = lax.rem(me - step + ways, ways)
        return pltpu.make_async_remote_copy(
            src_ref=part_ref.at[source], dst_ref=part_land.at[source],
            send_sem=small_send.at[step], recv_sem=small_recv.at[source],
            device_id=device(lax.rem(me + step, ways)), device_id_type=MESH,
        )

    def spread(step):
        return pltpu.make_async_remote_copy(
            src_ref=total_ref.at[me], dst_ref=total_ref.at[me],
            send_sem=spread_send.at[step], recv_sem=spread_recv.at[me],
            device_id=device(lax.rem(me + step, ways)), device_id_type=MESH,
        )

    def landing(step):
        source = lax.rem(me - step + ways, ways)
        return pltpu.make_async_remote_copy(
            src_ref=total_ref.at[source], dst_ref=total_ref.at[source],
            send_sem=spread_send.at[step], recv_sem=spread_recv.at[source],
            device_id=device(lax.rem(me + step, ways)), device_id_type=MESH,
        )

    @pl.loop(1, ways)
    def _(step):
        scatter(step).start()

    send_slabs(groups - 1)

    @pl.loop(0, blocks)
    def _(b):
        at = block_at(b)
        out_ref[at] = row_grad(2 * blocks + b) + dot_nt(q_ref[at], weight_ref[0])
        serve(served + 2 * b, served + 2 * b + 2)

    served += 2 * blocks

    def add(step, total):
        arrival(step).wait_recv()
        return total + part_land[lax.rem(me - step + ways, ways)]

    total_ref[me] = lax.fori_loop(1, ways, add, part_ref[me])

    @pl.loop(1, ways)
    def _(step):
        spread(step).start()

    serve(served, jnp.maximum(served, 2 * pieces) + late)

    kinds = [[], [], [], []]
    for group in range(groups + 1):

        def add_slab(step, total):
            take(group, step).wait_recv()
            return total + chip_land[group, chip_at(chips - step)].astype(jnp.float32)

        total = lax.fori_loop(1, chips, add_slab, slab_ref[group, spot].astype(jnp.float32))
        for part in range(total.shape[1] // GROUP):
            kinds[3 if group == groups else part].append(
                total[:, part * GROUP : (part + 1) * GROUP]
            )

    share = width // tensor
    kinds = [jnp.concatenate(parts, axis=1) for parts in kinds]
    for target in range(tensor):
        mine = jnp.concatenate(
            [kind[:, target * share : (target + 1) * share] for kind in kinds], axis=1
        )
        line_out[target] = mine.astype(line_out.dtype)

        @pl.when(place == target)
        def _():
            sum_ref[...] = mine

    def line(step):
        return pltpu.make_async_remote_copy(
            src_ref=line_out.at[along(step)], dst_ref=line_land.at[place],
            send_sem=line_send.at[step], recv_sem=line_recv.at[place],
            device_id=(spot, along(step)), device_id_type=MESH,
        )

    def line_in(step):
        source = along(tensor - step)
        return pltpu.make_async_remote_copy(
            src_ref=line_out.at[source], dst_ref=line_land.at[source],
            send_sem=line_send.at[step], recv_sem=line_recv.at[source],
            device_id=(spot, along(step)), device_id_type=MESH,
        )

    for step in range(1, tensor):
        line(step).start()

    @pl.when(place < 2)
    def _():
        @pl.loop(0, pieces)
        def _(piece):
            source = place * pieces + piece
            pass_down(source).wait_recv()
            at = pl.ds(pl.multiple_of(piece * PIECE, PIECE), PIECE)
            out_ref[at] += joined(source)

    for step in range(1, tensor):
        line_in(step).wait_recv()
        sum_ref[...] += line_land[along(tensor - step)].astype(jnp.float32)

    @pl.loop(1, ways)
    def _(step):
        landing(step).wait_recv()

    for step in range(1, tensor):
        line(step).wait_send()

    @pl.loop(1, ways)
    def _(step):
        scatter(step).wait_send()
        spread(step).wait_send()

    for group in range(groups + 1):

        @pl.loop(0, chips)
        def _(step):
            halve(group, step).wait_send()

            @pl.when(step > 0)
            def _():
                give(group, step).wait_send()

    sent = jnp.where(place == tensor - 1, 2 * pieces, last_relay)
    first_sent = jnp.where(place == tensor - 1, 0, first_relay)

    def sent_one(order, carry):
        pass_down(piece_of(order)).wait_send()
        return carry

    lax.fori_loop(first_sent, sent, sent_one, 0)


def backward(parents, q, k, v, o, branch_grad, seen, weights, lse, small):
    dp, tensor = lax.axis_size("dp"), lax.axis_size("tensor")
    ways = dp * tensor
    rows, width = q.shape
    seen_rows = k.shape[0]
    depth = width // dp
    padded = -(-depth // 16) * 16
    pairs, groups, pieces = width // 128, width // GROUP, rows // PIECE
    slab = (padded, width)
    low, full = jnp.bfloat16, jnp.float32
    dma = pltpu.SemaphoreType.DMA
    anywhere = pl.BlockSpec(memory_space=pl.ANY)
    here = pl.BlockSpec(memory_space=pltpu.VMEM)
    out, block, total = pl.pallas_call(
        lambda *refs: back_kernel(dp, tensor, depth, *refs),
        out_shape=(
            jax.ShapeDtypeStruct((rows, width), full),
            jax.ShapeDtypeStruct((padded, width), full),
            jax.ShapeDtypeStruct(small.shape, full),
        ),
        in_specs=[here] + [anywhere] * 7 + [here] * 2,
        out_specs=[here, here, here],
        scratch_shapes=[
            pltpu.VMEM((rows, width), low),
            pltpu.VMEM((seen_rows, width), low),
            pltpu.VMEM((seen_rows, width), low),
            pltpu.VMEM((rows, width), low),
            pltpu.VMEM((rows, width), low),
            pltpu.VMEM((rows, width), low),
            pltpu.VMEM((2, rows // 2, width), low),
            pltpu.VMEM((width, seen_rows), low),
            pltpu.VMEM(weights.shape, low),
            pltpu.VMEM((pairs, 2, rows), full),
            pltpu.VMEM((pairs, 128, rows), full),
            pltpu.VMEM((2 * rows, width), low),
            pltpu.VMEM((2 * rows, width), low),
            pltpu.VMEM((width, 128), full),
            pltpu.VMEM((groups + 1, dp) + slab, low),
            pltpu.VMEM((groups + 1, dp // 2) + slab, low),
            pltpu.VMEM((groups + 1, dp // 2) + slab, low),
            pltpu.VMEM((tensor, padded, width), low),
            pltpu.VMEM((tensor, padded, width), low),
            pltpu.VMEM(small.shape, full),
            pltpu.VMEM(small.shape, full),
            dma((3,)), dma((3, pairs)), dma((2,)),
            dma((2 * pieces,)), dma((2 * pieces,)),
            dma((groups + 1, dp // 2)), dma((groups + 1, dp // 2)),
            dma((groups + 1, dp // 2)), dma((groups + 1, dp // 2)),
            dma((tensor,)), dma((tensor,)),
            dma((ways,)), dma((ways,)), dma((ways,)), dma((ways,)),
        ],
        compiler_params=pltpu.CompilerParams(
            collective_id=3, has_side_effects=True, vmem_limit_bytes=62 << 20
        ),
        name="attend_backward",
    )(parents, q, k, v, o, branch_grad, seen, weights, lse, small)
    return out, block[:depth], total


norm_eps = 1e-05
route_scale = 3.0
masked_score = -1e30
highest = lax.Precision.HIGHEST


def layer_norm(values, norm_gain):
    centred = values - jnp.mean(values, axis=-1, keepdims=True)
    spread = jnp.mean(centred * centred, axis=-1, keepdims=True)
    return centred * lax.rsqrt(spread + norm_eps) * norm_gain


def unit_rows(values):
    return values * lax.rsqrt(jnp.sum(values * values, axis=-1, keepdims=True) + 1.0)


def router_gate(normed, router_proj, expert_embed, picked):
    routed = jnp.dot(normed, router_proj, precision=highest)
    logits = route_scale * jnp.dot(unit_rows(routed), unit_rows(expert_embed).T, precision=highest)
    return jnp.sum(jax.nn.softmax(logits, axis=-1) * picked, axis=-1)


def gelu_exact(values):
    return jax.nn.gelu(values, approximate=False)


def slot_table(route_ids, order_ids, capacity):
    same_expert = route_ids[:, None] == route_ids[None, :]
    earlier = order_ids[None, :] < order_ids[:, None]
    ranking = jnp.sum(jnp.where(same_expert & earlier, 1, 0), axis=1).astype(jnp.int32)
    kept_mask = ranking < capacity
    column = route_ids * capacity + jnp.minimum(ranking, capacity - 1)
    return (column, kept_mask)


def low_dot(rows, weight):
    return jnp.dot(rows, weight, preferred_element_type=jnp.float32).astype(jnp.bfloat16)


def shards(
    tokens,
    norm1_gain,
    qkv_weight,
    attn_proj,
    norm2_gain,
    router_proj,
    expert_embed,
    expert_in,
    expert_out,
    routes,
    orders,
    leaf_parent,
    cotangent,
):
    rows_here = tokens.shape[0]
    model_width = tokens.shape[1]
    experts = expert_embed.shape[0]
    capacity = rows_here // experts
    dp_size, tensor_size = lax.axis_size("dp"), lax.axis_size("tensor")

    def hop(rows, chip_step, core_step):
        route = []
        for source in range(dp_size):
            chip, core = source // 2, source % 2
            route.append((source, (chip ^ chip_step) * 2 + (core ^ core_step)))
        return lax.ppermute(rows, "dp", route)

    def chip_blocks(rows):
        blocks = rows.reshape(experts, capacity, model_width)
        return [blocks[0]] + [hop(blocks[step], step, 0) for step in range(1, experts)]

    def across_chips(rows):
        return jnp.concatenate(chip_blocks(rows), axis=0)

    def with_partner(blocks):
        arrived = jnp.concatenate(blocks, axis=0)
        return jnp.concatenate([arrived, hop(arrived, 0, 1)], axis=0)

    def pair_sum(kept_rows, sent_rows):
        return (kept_rows + hop(sent_rows, 0, 1).astype(jnp.float32)).astype(jnp.bfloat16)

    hidden = tokens.astype(jnp.float32)
    normed_in, norm1_back = jax.vjp(layer_norm, hidden, norm1_gain)
    own_in = normed_in.astype(jnp.bfloat16)
    flat_qkv = qkv_weight.reshape(qkv_weight.shape[0], -1)
    place = lax.axis_index("tensor")
    leaf_blocks = rows_here // BRANCH
    first_leaf = jnp.maximum(place - 2, 0) * leaf_blocks
    leaf_parents = lax.dynamic_slice_in_dim(leaf_parent[0], first_leaf, leaf_blocks, 0) - 1
    parents = (leaf_parents[:, None] == jnp.arange(leaf_blocks)[None, :]).astype(jnp.float32)
    parents = jnp.broadcast_to(parents.reshape(-1, 1), (leaf_blocks * leaf_blocks, model_width))
    seen_in, weights = share_rows_and_weights(
        own_in, jnp.concatenate([flat_qkv, attn_proj.T], axis=1), parents
    )
    query_weight, key_weight, value_weight, proj_back = weights
    query_rows = low_dot(own_in, query_weight)
    key_rows = low_dot(seen_in, key_weight)
    value_rows = low_dot(seen_in, value_weight)
    attended, log_totals = attend(place[None].astype(jnp.int32), query_rows, key_rows, value_rows)
    branch_out = jnp.einsum(
        "sc,dc->sd", attended, proj_back, preferred_element_type=jnp.float32
    )
    mid_stream = hidden + branch_out
    normed_mid, norm2_back = jax.vjp(layer_norm, mid_stream, norm2_gain)
    moe_in = normed_mid.astype(jnp.bfloat16)
    route_ids = routes[:, 0]
    near_route = route_ids ^ (lax.axis_index("dp") // 2)
    column, kept_mask = slot_table(near_route, orders[0], capacity)
    picked = (route_ids[:, None] == jnp.arange(experts)[None, :]).astype(jnp.float32)
    gate_value, gate_back = jax.vjp(
        lambda normed_rows, route_proj, embed_rows: router_gate(
            normed_rows, route_proj, embed_rows, picked
        ),
        moe_in.astype(jnp.float32),
        router_proj,
        expert_embed,
    )
    select = (
        (column[:, None] == jnp.arange(experts * capacity)[None, :]) & kept_mask[:, None]
    ).astype(jnp.bfloat16)
    def to_slots(token_rows):
        return jnp.einsum(
            "ts,td->sd", select, token_rows, preferred_element_type=jnp.float32
        ).astype(jnp.bfloat16)

    def from_slots(slot_rows):
        return jnp.dot(select, slot_rows, preferred_element_type=jnp.float32)

    upstream = cotangent.astype(jnp.float32)
    slot_grads = to_slots((gate_value[:, None] * upstream).astype(jnp.bfloat16))
    row_blocks, slot_grads = lax.optimization_barrier(
        (chip_blocks(to_slots(moe_in)), slot_grads)
    )
    grad_blocks = chip_blocks(slot_grads)
    expert_rows = with_partner(row_blocks)
    active, slope, kept_result, sent_result = expert_forward(expert_rows, expert_in, expert_out)
    grad_blocks, kept_result, sent_result = lax.optimization_barrier(
        (grad_blocks, kept_result, sent_result)
    )
    arrived_grad = with_partner(grad_blocks)
    result_rows, late_grad = lax.optimization_barrier(
        (pair_sum(kept_result, sent_result), arrived_grad)
    )
    expert_result = from_slots(across_chips(result_rows))
    output = (mid_stream + gate_value[:, None] * expert_result).astype(jnp.bfloat16)
    out_weight_grad = jnp.einsum(
        "rf,rd->fd", active, arrived_grad, preferred_element_type=jnp.float32
    ).astype(jnp.bfloat16)
    up_grad, kept_grad, sent_grad = expert_back(late_grad, slope, expert_in, expert_out)
    in_weight_grad = jnp.einsum(
        "rf,rd->fd", up_grad, expert_rows, preferred_element_type=jnp.float32
    ).astype(jnp.bfloat16)
    moe_grad = from_slots(across_chips(pair_sum(kept_grad, sent_grad)))
    gate_grad = jnp.sum(upstream * expert_result, axis=-1)
    router_part, proj_grad, embed_grad = gate_back(gate_grad)
    mid_part, gain2_grad = norm2_back(moe_grad + router_part)
    mid_grad = upstream + mid_part
    expert_in_grad = (
        lax.psum_scatter(in_weight_grad, "tensor", scatter_dimension=0, tiled=True)
        .astype(jnp.float32)
        .T
    )
    expert_out_grad = lax.psum_scatter(
        out_weight_grad, "tensor", scatter_dimension=0, tiled=True
    ).astype(jnp.float32)
    branch_grad = mid_grad.astype(jnp.bfloat16)
    later = [gain2_grad, proj_grad, embed_grad]
    flat = jnp.concatenate([jnp.zeros_like(norm1_gain)] + [part.reshape(-1) for part in later])
    ways = dp_size * tensor_size
    lanes = -(-flat.shape[0] // (ways * 8 * 128)) * 128
    small = jnp.pad(flat, (0, ways * 8 * lanes - flat.shape[0])).reshape(ways, 8, lanes)
    input_grad, grad_block, totals = backward(
        parents, query_rows, key_rows, value_rows, attended, branch_grad, seen_in, weights,
        log_totals, small,
    )
    qkv_grad = grad_block[:, : flat_qkv.shape[1]].reshape(qkv_weight.shape)
    attn_proj_grad = grad_block[:, flat_qkv.shape[1] :].T
    totals = totals.reshape(-1)
    gain1_sum = totals[:model_width] / norm1_gain
    gain2_sum, router_sum, embed_sum = (
        totals[first : first + part.size].reshape(part.shape)
        for first, part in zip(
            (model_width, 2 * model_width, 2 * model_width + proj_grad.size), later
        )
    )
    token_part, _ = norm1_back(input_grad)
    token_grad = mid_grad + token_part
    return (
        output,
        token_grad,
        gain1_sum,
        qkv_grad,
        attn_proj_grad,
        gain2_sum,
        router_sum,
        embed_sum,
        expert_in_grad,
        expert_out_grad,
    )


def solution(mesh):
    in_specs = (
        P(("dp", "tensor"), None),
        P(),
        P("dp", None, "tensor"),
        P("tensor", "dp"),
        P(),
        P(),
        P(),
        P(None, "dp"),
        P("dp", None),
        P(("dp", "tensor"), None),
        P(("dp", "tensor"), None),
        P("dp", None),
        P(("dp", "tensor"), None),
    )
    out_specs = (
        P(("dp", "tensor"), None),
        P(("dp", "tensor"), None),
        P(),
        P("dp", None, "tensor"),
        P("tensor", "dp"),
        P(),
        P(),
        P(),
        P(None, ("dp", "tensor")),
        P(("dp", "tensor"), None),
    )
    return jax.shard_map(shards, mesh=mesh, in_specs=in_specs, out_specs=out_specs, check_vma=False)
```

```python
import functools
import math

import jax
import jax.numpy as jnp
from jax import lax
from jax.experimental import pallas as pl
from jax.experimental.pallas import tpu as pltpu
from jax.sharding import PartitionSpec as P

HEAD_DIM = 64
TRUNK = 1024
BRANCH = 256
MASKED = -1e30
LOG2E = math.log2(math.e)
EXP_SCALE = HEAD_DIM ** (-0.5) * LOG2E

NT = (((1,), (1,)), ((), ()))
NN = (((1,), (0,)), ((), ()))


def dot_nt(a, b):
    return lax.dot_general(a, b, NT, preferred_element_type=jnp.float32)


def dot_nn(a, b):
    return lax.dot_general(a, b, NN, preferred_element_type=jnp.float32)


def head_lanes(shape, dim, head):
    return lax.broadcasted_iota(jnp.int32, shape, dim) // HEAD_DIM == head


def fwd_kernel(place_ref, q_ref, k_ref, v_ref, o_ref, lse_ref, vt_ref, acc_ref):
    place = place_ref[0]
    rows = q_ref.shape[0]
    blocks = rows // BRANCH
    flipped = v_ref[...].T
    for head in range(2):
        vt_ref[head] = jnp.where(
            head_lanes(flipped.shape, 0, head), flipped, jnp.ones_like(flipped)
        )

    def start(block, head, in_trunk):
        queries = q_ref[block * BRANCH : (block + 1) * BRANCH]
        queries = jnp.where(head_lanes(queries.shape, 1, head), queries, jnp.zeros_like(queries))
        firsts = list(range(0, TRUNK, BRANCH))
        if not in_trunk:
            firsts += [rows + block * BRANCH, 2 * rows + block * BRANCH]
        scores = [dot_nt(k_ref[first : first + BRANCH], queries) for first in firsts]

        def causal(tile, offset):
            keys = lax.broadcasted_iota(jnp.int32, tile.shape, 0) + offset
            at = lax.broadcasted_iota(jnp.int32, tile.shape, 1)
            return jnp.where(keys <= at, tile, MASKED)

        if in_trunk:
            scores = [
                causal(tile, first - block * BRANCH) for tile, first in zip(scores, firsts)
            ]
        else:
            scores[-2] = jnp.where(place > 1, scores[-2], MASKED)
            scores[-1] = causal(scores[-1], 0)
        top = jnp.max(functools.reduce(jnp.maximum, scores), axis=0, keepdims=True)
        return firsts, scores, top

    def middle(firsts, scores, top):
        shift = top * EXP_SCALE
        probs = [jnp.exp2(tile * EXP_SCALE - shift).astype(jnp.bfloat16) for tile in scores]
        return firsts, probs, top

    def finish(block, head, firsts, probs, top):
        acc = None
        for first, tile in zip(firsts, probs):
            part = dot_nn(vt_ref[head, :, first : first + BRANCH], tile)
            acc = part if acc is None else acc + part
        mine, other = head * HEAD_DIM, (1 - head) * HEAD_DIM
        total = acc[other : other + 1]
        cols = slice(block * BRANCH, (block + 1) * BRANCH)
        acc_ref[mine : mine + HEAD_DIM, cols] = acc[mine : mine + HEAD_DIM] / total
        lse_ref[0, head : head + 1, cols] = top * EXP_SCALE + jnp.log2(total)

    def run(in_trunk):
        work = [(block, head) for block in range(blocks) for head in range(2)]
        ready, held = start(*work[0], in_trunk), None
        for at, item in enumerate(work):
            now = ready
            if at + 1 < len(work):
                ready = start(*work[at + 1], in_trunk)
            done = middle(*now)
            if held is not None:
                finish(*held)
            held = (*item, *done)
        finish(*held)

    @pl.when(place == 0)
    def _():
        run(True)

    @pl.when(place > 0)
    def _():
        run(False)

    o_ref[...] = acc_ref[...].T.astype(o_ref.dtype)


def attend(place, q, k, v):
    rows, width = q.shape
    keys = k.shape[0]
    pairs = width // 128
    few = pl.BlockSpec((rows, 128), lambda p, m: (0, p))
    many = pl.BlockSpec((keys, 128), lambda p, m: (0, p))
    return pl.pallas_call(
        fwd_kernel,
        out_shape=(
            jax.ShapeDtypeStruct((rows, width), jnp.bfloat16),
            jax.ShapeDtypeStruct((pairs, 2, rows), jnp.float32),
        ),
        grid_spec=pltpu.PrefetchScalarGridSpec(
            num_scalar_prefetch=1,
            grid=(pairs,),
            in_specs=[few, many, many],
            out_specs=[few, pl.BlockSpec((1, 2, rows), lambda p, m: (p, 0, 0))],
            scratch_shapes=[
                pltpu.VMEM((2, 128, keys), jnp.bfloat16),
                pltpu.VMEM((128, rows), jnp.float32),
            ],
        ),
        compiler_params=pltpu.CompilerParams(vmem_limit_bytes=48 << 20),
        name="attend_forward",
    )(place, q, k, v)


MESH = pl.DeviceIdType.MESH
PIECE = 64


def greet(peers):
    barrier = pltpu.get_barrier_semaphore()
    for peer in peers:
        pl.semaphore_signal(barrier, inc=1, device_id=peer, device_id_type=MESH)
    pl.semaphore_wait(barrier, len(peers))


def share_kernel(dp, tensor, own_ref, block_ref, parent_ref, seen_ref, out_ref, weights_ref,
                 ordered_ref, row_send, row_recv,
                 line_send, line_recv, chip_send, chip_recv, pair_send, pair_recv):
    spot, place = lax.axis_index("dp"), lax.axis_index("tensor")
    chip, core = spot // 2, lax.rem(spot, 2)
    chips = dp // 2
    rows = own_ref.shape[0]
    pieces = rows // PIECE
    part_width = out_ref.shape[2] // tensor
    partner = (chip * 2 + 1 - core, place)

    def along(step):
        return lax.rem(place + step, tensor)

    def chip_at(step):
        return lax.rem(chip + step, chips)

    greet(
        [(spot, along(step)) for step in range(1, tensor)]
        + [(chip_at(step) * 2 + core, place) for step in range(1, chips)]
        + [partner]
    )

    def pass_on(part, piece, fresh):
        at = pl.ds(part * rows + piece * PIECE, PIECE)
        source = own_ref.at[pl.ds(piece * PIECE, PIECE)] if fresh else seen_ref.at[at]
        return pltpu.make_async_remote_copy(
            src_ref=source, dst_ref=seen_ref.at[at],
            send_sem=row_send.at[part, piece], recv_sem=row_recv.at[part, piece],
            device_id=(spot, lax.rem(place + 1, tensor)), device_id_type=MESH,
        )

    def line(step):
        return pltpu.make_async_remote_copy(
            src_ref=block_ref, dst_ref=weights_ref.at[place, spot],
            send_sem=line_send.at[step], recv_sem=line_recv.at[place],
            device_id=(spot, along(step)), device_id_type=MESH,
        )

    def line_in(step):
        source = along(tensor - step)
        return pltpu.make_async_remote_copy(
            src_ref=block_ref, dst_ref=weights_ref.at[source, spot],
            send_sem=line_send.at[step], recv_sem=line_recv.at[source],
            device_id=(spot, along(step)), device_id_type=MESH,
        )

    def plane(part, step):
        block = weights_ref.at[part, spot]
        return pltpu.make_async_remote_copy(
            src_ref=block, dst_ref=block,
            send_sem=chip_send.at[part, step], recv_sem=chip_recv.at[part, chip],
            device_id=(chip_at(step) * 2 + core, place), device_id_type=MESH,
        )

    def plane_in(part, step):
        source = chip_at(chips - step)
        block = weights_ref.at[part, source * 2 + core]
        return pltpu.make_async_remote_copy(
            src_ref=block, dst_ref=block,
            send_sem=chip_send.at[part, step], recv_sem=chip_recv.at[part, source],
            device_id=(chip_at(step) * 2 + core, place), device_id_type=MESH,
        )

    def across(part, source, source_core):
        block = weights_ref.at[part, source * 2 + source_core]
        return pltpu.make_async_remote_copy(
            src_ref=block, dst_ref=block,
            send_sem=pair_send.at[part, source], recv_sem=pair_recv.at[part, source],
            device_id=partner, device_id_type=MESH,
        )

    for step in range(1, tensor):
        line(step).start()

    def row_steps(first, last):
        @pl.loop(first, last)
        def _(piece):
            @pl.when(place == 0)
            def _():
                pass_on(0, piece, True).start()

            @pl.when(place > 0)
            def _():
                pass_on(0, piece, False).wait_recv()

            @pl.when((place > 0) & (place < tensor - 1))
            def _():
                pass_on(0, piece, False).start()

            @pl.when(place == 1)
            def _():
                pass_on(1, piece, True).start()

            @pl.when(place > 1)
            def _():
                pass_on(1, piece, False).wait_recv()

            @pl.when((place > 1) & (place < tensor - 1))
            def _():
                pass_on(1, piece, False).start()

    weights_ref[place, spot] = block_ref[...]
    seen_ref[2 * rows :] = own_ref[...]

    @pl.when(place < 2)
    def _():
        seen_ref[rows : 2 * rows] = own_ref[...]

    @pl.when(place == 0)
    def _():
        seen_ref[0:rows] = own_ref[...]

    row_steps(0, pieces // 4)
    for step in range(tensor):
        part = along(tensor - step)
        if step:
            line_in(step).wait_recv()

        @pl.loop(1, chips)
        def _(hop):
            plane(part, hop).start()

        across(part, chip, core).start()
    row_steps(pieces // 4, (pieces * 5) // 8)
    for step in range(tensor):
        part = along(tensor - step)

        @pl.loop(1, chips)
        def _(hop):
            plane_in(part, hop).wait_recv()
            across(part, chip_at(chips - hop), core).start()

    row_steps((pieces * 5) // 8, pieces)
    for part in range(tensor):

        @pl.loop(0, chips)
        def _(source):
            across(part, source, 1 - core).wait_recv()
            across(part, source, core).wait_send()

        @pl.loop(1, chips)
        def _(hop):
            plane(part, hop).wait_send()

    for step in range(1, tensor):
        line(step).wait_send()

    @pl.when(place < tensor - 1)
    def _():
        @pl.loop(0, pieces)
        def _(piece):
            pass_on(0, piece, False).wait_send()

    @pl.when((place > 0) & (place < tensor - 1))
    def _():
        @pl.loop(0, pieces)
        def _(piece):
            pass_on(1, piece, False).wait_send()

    @pl.when(place > 1)
    def _():
        blocks = rows // BRANCH
        branches = [
            seen_ref[rows + branch * BRANCH : rows + (branch + 1) * BRANCH]
            for branch in range(blocks)
        ]
        for leaf in range(blocks):
            chosen = None
            for branch in range(blocks):
                at = leaf * blocks + branch
                part = branches[branch] * parent_ref[at : at + 1].astype(own_ref.dtype)
                chosen = part if chosen is None else chosen + part
            ordered_ref[leaf * BRANCH : (leaf + 1) * BRANCH] = chosen
        seen_ref[rows : 2 * rows] = ordered_ref[...]

    @pl.loop(0, dp)
    def _(source):
        depth = block_ref.shape[0]
        at = pl.ds(pl.multiple_of(source * depth, depth), depth)
        for kind in range(out_ref.shape[0]):
            cols = slice(kind * part_width, (kind + 1) * part_width)
            out_ref[kind, at] = jnp.concatenate(
                [weights_ref[part, source][:, cols] for part in range(tensor)], axis=1
            )


def share_rows_and_weights(own, block, parents):
    dp, tensor = lax.axis_size("dp"), lax.axis_size("tensor")
    rows, width = own.shape
    depth, cols = block.shape
    pieces, chips = rows // PIECE, dp // 2
    kinds = cols * tensor // width
    padded = -(-depth // 16) * 16
    block = jnp.pad(block, ((0, padded - depth), (0, 0)))
    dma = pltpu.SemaphoreType.DMA
    here = pl.BlockSpec(memory_space=pltpu.VMEM)
    seen, weights = pl.pallas_call(
        lambda *refs: share_kernel(dp, tensor, *refs),
        out_shape=(
            jax.ShapeDtypeStruct((3 * rows, width), own.dtype),
            jax.ShapeDtypeStruct((kinds, dp * padded, width), block.dtype),
        ),
        in_specs=[here, here, here],
        out_specs=[here, here],
        scratch_shapes=[
            pltpu.VMEM((tensor, dp, padded, cols), block.dtype),
            pltpu.VMEM(own.shape, own.dtype),
            dma((2, pieces)), dma((2, pieces)),
            dma((tensor,)), dma((tensor,)),
            dma((tensor, chips)), dma((tensor, chips)),
            dma((tensor, chips)), dma((tensor, chips)),
        ],
        compiler_params=pltpu.CompilerParams(
            collective_id=2, has_side_effects=True, vmem_limit_bytes=48 << 20
        ),
        name="share_rows_and_weights",
    )(own, block, parents)
    weights = weights.reshape(kinds, dp, padded, width)[:, :, :depth]
    return seen, weights.reshape(kinds, dp * depth, width)


TN = (((0,), (0,)), ((), ()))
GROUP = 256


def dot_tn(a, b):
    return lax.dot_general(a, b, TN, preferred_element_type=jnp.float32)


def back_kernel(
    dp, tensor, depth,
    parent_ref, q_in, k_in, v_in, o_in, grad_in, seen_in, weight_in, lse_ref, small_ref,
    out_ref, sum_ref, total_ref,
    q_ref, k_ref, v_ref, o_ref, bg_ref, g_ref, stage_ref, seen_ref, weight_ref,
    delta_ref, dqt_ref, rows_ref, land_ref, gain_ref,
    slab_ref, pair_land, chip_land, line_out, line_land, part_ref, part_land,
    load_sem, pair_sem, stage_sem, row_send, row_recv,
    pair_send, pair_recv, chip_send, chip_recv,
    line_send, line_recv, small_send, small_recv, spread_send, spread_recv,
):
    spot, place = lax.axis_index("dp"), lax.axis_index("tensor")
    ways = dp * tensor
    me = spot * tensor + place
    scale = HEAD_DIM ** (-0.5)
    rows, width = q_ref.shape
    pairs = width // 128
    groups = width // GROUP
    blocks = rows // BRANCH
    pieces = rows // PIECE
    stage_rows = stage_ref.shape[1]

    def device(index):
        return (index // tensor, lax.rem(index, tensor))

    def along(step):
        return lax.rem(place + step, tensor)

    chips = dp // 2
    chip, core = spot // 2, lax.rem(spot, 2)

    def chip_at(step):
        return lax.rem(chip + step, chips)

    def block_at(b):
        return pl.ds(pl.multiple_of(b * BRANCH, BRANCH), BRANCH)

    barrier = pltpu.get_barrier_semaphore()

    @pl.loop(1, ways)
    def _(step):
        pl.semaphore_signal(
            barrier, inc=1, device_id=device(lax.rem(me + step, ways)), device_id_type=MESH
        )

    def lanes(pair):
        return pl.ds(pl.multiple_of(pair * 128, 128), 128)

    grad_load = pltpu.make_async_copy(grad_in, bg_ref, load_sem.at[0])
    weight_load = pltpu.make_async_copy(weight_in, weight_ref, load_sem.at[1])
    value_load = pltpu.make_async_copy(o_in, o_ref, load_sem.at[2])

    def pair_loads(pair):
        return [
            pltpu.make_async_copy(
                source.at[:, lanes(pair)], held.at[:, lanes(pair)], pair_sem.at[which, pair]
            )
            for which, (source, held) in enumerate(((q_in, q_ref), (k_in, k_ref), (v_in, v_ref)))
        ]

    def stage(part):
        slot = lax.rem(part, 2)
        at = pl.ds(pl.multiple_of(part * stage_rows, stage_rows), stage_rows)
        return pltpu.make_async_copy(seen_in.at[at], stage_ref.at[slot], stage_sem.at[slot])

    grad_load.start()
    weight_load.start()
    value_load.start()

    @pl.loop(0, pairs)
    def _(pair):
        for load in pair_loads(pair):
            load.start()

    grad_load.wait()
    weight_load.wait()
    value_load.wait()

    def keep(held, value, kind):
        cols = slice(kind * GROUP, (kind + 1) * GROUP)
        if depth % 16:
            for target in range(dp):
                held[target, 0:depth, cols] = value[target * depth : (target + 1) * depth].astype(
                    slab_ref.dtype
                )
        else:
            held[:, :, cols] = value.reshape(dp, depth, GROUP).astype(slab_ref.dtype)

    for group in range(groups):
        cols = slice(group * GROUP, (group + 1) * GROUP)
        keep(slab_ref.at[groups], dot_tn(bg_ref[...], o_ref[:, cols]), group)

    @pl.loop(0, blocks)
    def _(b):
        at = block_at(b)
        g_ref[at] = dot_nn(bg_ref[at], weight_ref[3]).astype(g_ref.dtype)

    pl.semaphore_wait(barrier, ways - 1)

    def halve(group, source):
        return pltpu.make_async_remote_copy(
            src_ref=slab_ref.at[group, source * 2 + 1 - core],
            dst_ref=pair_land.at[group, source],
            send_sem=pair_send.at[group, source], recv_sem=pair_recv.at[group, source],
            device_id=(chip * 2 + 1 - core, place), device_id_type=MESH,
        )

    def give(group, step):
        to = chip_at(step) * 2 + core
        return pltpu.make_async_remote_copy(
            src_ref=slab_ref.at[group, to], dst_ref=chip_land.at[group, chip],
            send_sem=chip_send.at[group, step], recv_sem=chip_recv.at[group, chip],
            device_id=(to, place), device_id_type=MESH,
        )

    def take(group, step):
        source = chip_at(chips - step)
        return pltpu.make_async_remote_copy(
            src_ref=slab_ref.at[group, source * 2 + core], dst_ref=chip_land.at[group, source],
            send_sem=chip_send.at[group, step], recv_sem=chip_recv.at[group, source],
            device_id=(chip_at(step) * 2 + core, place), device_id_type=MESH,
        )

    def share_slabs(group):
        @pl.loop(0, chips)
        def _(source):
            halve(group, source).start()

    def send_slabs(group):
        @pl.loop(0, chips)
        def _(step):
            to = chip_at(step)
            halve(group, to).wait_recv()
            mine = slab_ref[group, to * 2 + core].astype(jnp.float32)
            mine = mine + pair_land[group, to].astype(jnp.float32)
            slab_ref[group, to * 2 + core] = mine.astype(slab_ref.dtype)

            @pl.when(step > 0)
            def _():
                give(group, step).start()

    share_slabs(groups)

    @pl.loop(0, pairs)
    def _(pair):
        for load in pair_loads(pair):
            load.wait()
        product = g_ref[:, lanes(pair)].astype(jnp.float32)
        product = (product * o_ref[:, lanes(pair)].astype(jnp.float32)).T
        for head in range(2):
            delta_ref[pair, head : head + 1, :] = jnp.sum(
                product[head * HEAD_DIM : (head + 1) * HEAD_DIM], axis=0, keepdims=True
            )
        dqt_ref[pair] = jnp.zeros(dqt_ref.shape[1:], dqt_ref.dtype)

    def sweep(pair, tiles):
        work = [(tile, head) for tile in range(len(tiles)) for head in range(2)]
        sums = [[None, None] for _ in tiles]
        keys, flipped = {}, {}

        def key_block(tile):
            row = tiles[tile][0]
            if id(row) not in keys:
                kb = k_ref[pl.ds(row, BRANCH), lanes(pair)]
                vb = v_ref[pl.ds(row, BRANCH), lanes(pair)]
                masked = []
                for head in range(2):
                    mine = head_lanes(kb.shape, 1, head)
                    masked.append(
                        (
                            jnp.where(mine, kb, jnp.zeros_like(kb)),
                            jnp.where(mine, vb, jnp.zeros_like(vb)),
                        )
                    )
                keys[id(row)] = masked
                flipped[id(row)] = kb.T
            return keys[id(row)], flipped[id(row)]

        def start(tile, head):
            at = pl.ds(tiles[tile][1], BRANCH)
            kb, vb = key_block(tile)[0][head]
            return dot_nt(kb, q_ref[at, lanes(pair)]), dot_nt(vb, g_ref[at, lanes(pair)])

        def middle(tile, head, scores, prob_grad):
            at = pl.ds(tiles[tile][1], BRANCH)
            probs = jnp.exp2(scores * EXP_SCALE - lse_ref[pair, head : head + 1, at])
            if tiles[tile][2] is not None:
                probs = tiles[tile][2](probs)
            score_grad = probs * (prob_grad - delta_ref[pair, head : head + 1, at])
            return probs.astype(jnp.bfloat16), score_grad.astype(jnp.bfloat16)

        def finish(tile, head, probs, score_grad):
            at = pl.ds(tiles[tile][1], BRANCH)
            parts = (
                dot_nn(score_grad, q_ref[at, lanes(pair)]),
                dot_nn(probs, g_ref[at, lanes(pair)]),
            )
            for which in range(2):
                held = sums[tile][which]
                if head == 0:
                    sums[tile][which] = parts[which]
                else:
                    first = head_lanes(held.shape, 1, 0)
                    sums[tile][which] = jnp.where(first, held, parts[which])
            mine = slice(head * HEAD_DIM, (head + 1) * HEAD_DIM)
            dqt_ref[pair, mine, at] += dot_nn(key_block(tile)[1][mine], score_grad)

        ready = start(*work[0])
        held = None
        for at, item in enumerate(work):
            now = ready
            if at + 1 < len(work):
                ready = start(*work[at + 1])
            done = middle(*item, *now)
            if held is not None:
                finish(*held)
            held = (*item, *done)
        finish(*held)
        return sums

    def causal(key_row, query_row):
        def mask_of(probs):
            keys = lax.broadcasted_iota(jnp.int32, probs.shape, 0) + key_row
            at = lax.broadcasted_iota(jnp.int32, probs.shape, 1) + query_row
            return jnp.where(keys <= at, probs, 0.0)

        return mask_of

    def put(pair, row, dk, dv):
        at = pl.ds(row, BRANCH)
        k_ref[at, lanes(pair)] = (dk * scale).astype(k_ref.dtype)
        v_ref[at, lanes(pair)] = dv.astype(v_ref.dtype)

    def pass_down(piece):
        at = pl.ds(pl.multiple_of(piece * PIECE, PIECE), PIECE)
        return pltpu.make_async_remote_copy(
            src_ref=rows_ref.at[at], dst_ref=land_ref.at[at],
            send_sem=row_send.at[piece], recv_sem=row_recv.at[piece],
            device_id=(spot, lax.rem(place + tensor - 1, tensor)), device_id_type=MESH,
        )

    def row_grad(b):
        at = block_at(b)
        return dot_nt(k_ref[at], weight_ref[1]) + dot_nt(v_ref[at], weight_ref[2])

    def hand_down(b, total):
        rows_ref[block_at(b)] = total.astype(rows_ref.dtype)

        @pl.when(place == tensor - 1)
        def _():
            for piece in range(BRANCH // PIECE):
                pass_down(b * (BRANCH // PIECE) + piece).start()

    def joined(piece):
        at = pl.ds(pl.multiple_of(piece * PIECE, PIECE), PIECE)
        return rows_ref[at].astype(jnp.float32) + land_ref[at].astype(jnp.float32)

    middle_place = (place > 0) & (place < tensor - 1)
    late = 3 * jnp.maximum(tensor - 2 - place, 0)
    first_relay = jnp.where(place > 1, 0, pieces)
    last_relay = jnp.where(middle_place, 2 * pieces, first_relay)

    def piece_of(order):
        return lax.rem(order + pieces, 2 * pieces)

    def serve(first, last):
        def one(order, carry):
            piece = piece_of(order)
            pass_down(piece).wait_recv()
            at = pl.ds(pl.multiple_of(piece * PIECE, PIECE), PIECE)
            rows_ref[at] = joined(piece).astype(rows_ref.dtype)
            pass_down(piece).start()
            return carry

        low = jnp.clip(first - late, first_relay, last_relay)
        lax.fori_loop(low, jnp.clip(last - late, low, last_relay), one, 0)

    @pl.loop(0, pairs)
    def _(pair):
        @pl.when(place == 0)
        def _():
            for ref in (k_ref, v_ref):
                ref[rows : 3 * rows, lanes(pair)] = jnp.zeros((2 * rows, 128), ref.dtype)

        @pl.when(place > 0)
        def _():
            def seen_parent(probs):
                return jnp.where(place > 1, probs, 0.0)

            spots = range(0, rows, BRANCH)
            sums = sweep(pair, [(rows + at, at, seen_parent) for at in spots])
            for at, part in zip(spots, sums):
                put(pair, rows + at, *part)

    send_slabs(groups)

    @pl.loop(0, blocks)
    def _(leaf):
        out_ref[block_at(leaf)] = row_grad(blocks + leaf)

    for branch in range(blocks):
        total = None
        for leaf in range(blocks):
            at = leaf * blocks + branch
            part = out_ref[leaf * BRANCH : (leaf + 1) * BRANCH] * parent_ref[at : at + 1]
            total = part if total is None else total + part
        hand_down(blocks + branch, total)

    stage(0).start()

    @pl.loop(0, blocks)
    def _(b):
        row = pl.multiple_of(b * BRANCH, BRANCH)

        @pl.loop(0, pairs)
        def _(pair):
            def finish_block(masked):
                tiles = [
                    (row, first, causal(row, first) if masked else None)
                    for first in range(0, rows, BRANCH)
                ]
                sums = sweep(pair, tiles)
                put(pair, row, sum(part[0] for part in sums), sum(part[1] for part in sums))

            @pl.when(place == 0)
            def _():
                finish_block(True)

            @pl.when(place > 0)
            def _():
                finish_block(False)

            slot = b * pairs + pair
            serve(slot - 1, slot)

        for _half in range(2):
            part = b * 2 + _half

            @pl.when(part < 3 * rows // stage_rows)
            def _():
                stage(part).wait()

                @pl.when(part + 1 < 3 * rows // stage_rows)
                def _():
                    stage(part + 1).start()

                at = pl.ds(pl.multiple_of(part * stage_rows, stage_rows), stage_rows)
                seen_ref[:, at] = stage_ref[lax.rem(part, 2)].T

        hand_down(b, row_grad(b))

    served = blocks * pairs - 1

    gain_ref[...] = jnp.zeros_like(gain_ref)

    @pl.loop(0, groups)
    def _(group):
        base = served + group * 4

        @pl.loop(0, 2)
        def _(half):
            pair = group * 2 + half

            @pl.when(place > 0)
            def _():
                spots = range(0, rows, BRANCH)
                sums = sweep(pair, [(2 * rows + at, at, causal(0, 0)) for at in spots])
                for at, part in zip(spots, sums):
                    put(pair, 2 * rows + at, *part)

            q_ref[:, lanes(pair)] = (dqt_ref[pair] * scale).T.astype(q_ref.dtype)
            serve(base + half, base + half + 1)

        cols = pl.ds(pl.multiple_of(group * GROUP, GROUP), GROUP)
        for kind, value in (
            (0, lambda: dot_nn(seen_ref[:, 2 * rows : 3 * rows], q_ref[:, cols])),
            (1, lambda: dot_nn(seen_ref[...], k_ref[:, cols])),
            (2, lambda: dot_nn(seen_ref[...], v_ref[:, cols])),
        ):
            product = value()
            scaled = product * weight_ref[kind, :, cols].astype(jnp.float32)
            gain_ref[...] += scaled[:, 0:128] + scaled[:, 128:256]
            keep(slab_ref.at[group], product, kind)
            if kind:
                serve(base + 1 + kind, base + 2 + kind)

        share_slabs(group)

        @pl.when(group > 0)
        def _():
            send_slabs(group - 1)

    served += groups * 4

    part_ref[...] = small_ref[...]
    gains = jnp.sum(gain_ref[...].T, axis=0, keepdims=True)
    for row in range(width // 128):
        part_ref[0, row : row + 1, :] = gains[:, row * 128 : (row + 1) * 128]

    def scatter(step):
        to = lax.rem(me + step, ways)
        return pltpu.make_async_remote_copy(
            src_ref=part_ref.at[to], dst_ref=part_land.at[me],
            send_sem=small_send.at[step], recv_sem=small_recv.at[me],
            device_id=device(to), device_id_type=MESH,
        )

    def arrival(step):
        source = lax.rem(me - step + ways, ways)
        return pltpu.make_async_remote_copy(
            src_ref=part_ref.at[source], dst_ref=part_land.at[source],
            send_sem=small_send.at[step], recv_sem=small_recv.at[source],
            device_id=device(lax.rem(me + step, ways)), device_id_type=MESH,
        )

    def spread(step):
        return pltpu.make_async_remote_copy(
            src_ref=total_ref.at[me], dst_ref=total_ref.at[me],
            send_sem=spread_send.at[step], recv_sem=spread_recv.at[me],
            device_id=device(lax.rem(me + step, ways)), device_id_type=MESH,
        )

    def landing(step):
        source = lax.rem(me - step + ways, ways)
        return pltpu.make_async_remote_copy(
            src_ref=total_ref.at[source], dst_ref=total_ref.at[source],
            send_sem=spread_send.at[step], recv_sem=spread_recv.at[source],
            device_id=device(lax.rem(me + step, ways)), device_id_type=MESH,
        )

    @pl.loop(1, ways)
    def _(step):
        scatter(step).start()

    send_slabs(groups - 1)

    @pl.loop(0, blocks)
    def _(b):
        at = block_at(b)
        out_ref[at] = row_grad(2 * blocks + b) + dot_nt(q_ref[at], weight_ref[0])
        serve(served + 2 * b, served + 2 * b + 2)

    served += 2 * blocks

    def add(step, total):
        arrival(step).wait_recv()
        return total + part_land[lax.rem(me - step + ways, ways)]

    total_ref[me] = lax.fori_loop(1, ways, add, part_ref[me])

    @pl.loop(1, ways)
    def _(step):
        spread(step).start()

    serve(served, jnp.maximum(served, 2 * pieces) + late)

    kinds = [[], [], [], []]
    for group in range(groups + 1):

        def add_slab(step, total):
            take(group, step).wait_recv()
            return total + chip_land[group, chip_at(chips - step)].astype(jnp.float32)

        total = lax.fori_loop(1, chips, add_slab, slab_ref[group, spot].astype(jnp.float32))
        for part in range(total.shape[1] // GROUP):
            kinds[3 if group == groups else part].append(
                total[:, part * GROUP : (part + 1) * GROUP]
            )

    share = width // tensor
    kinds = [jnp.concatenate(parts, axis=1) for parts in kinds]
    for target in range(tensor):
        mine = jnp.concatenate(
            [kind[:, target * share : (target + 1) * share] for kind in kinds], axis=1
        )
        line_out[target] = mine.astype(line_out.dtype)

        @pl.when(place == target)
        def _():
            sum_ref[...] = mine

    def line(step):
        return pltpu.make_async_remote_copy(
            src_ref=line_out.at[along(step)], dst_ref=line_land.at[place],
            send_sem=line_send.at[step], recv_sem=line_recv.at[place],
            device_id=(spot, along(step)), device_id_type=MESH,
        )

    def line_in(step):
        source = along(tensor - step)
        return pltpu.make_async_remote_copy(
            src_ref=line_out.at[source], dst_ref=line_land.at[source],
            send_sem=line_send.at[step], recv_sem=line_recv.at[source],
            device_id=(spot, along(step)), device_id_type=MESH,
        )

    for step in range(1, tensor):
        line(step).start()

    @pl.when(place < 2)
    def _():
        @pl.loop(0, pieces)
        def _(piece):
            source = place * pieces + piece
            pass_down(source).wait_recv()
            at = pl.ds(pl.multiple_of(piece * PIECE, PIECE), PIECE)
            out_ref[at] += joined(source)

    for step in range(1, tensor):
        line_in(step).wait_recv()
        sum_ref[...] += line_land[along(tensor - step)].astype(jnp.float32)

    @pl.loop(1, ways)
    def _(step):
        landing(step).wait_recv()

    for step in range(1, tensor):
        line(step).wait_send()

    @pl.loop(1, ways)
    def _(step):
        scatter(step).wait_send()
        spread(step).wait_send()

    for group in range(groups + 1):

        @pl.loop(0, chips)
        def _(step):
            halve(group, step).wait_send()

            @pl.when(step > 0)
            def _():
                give(group, step).wait_send()

    sent = jnp.where(place == tensor - 1, 2 * pieces, last_relay)
    first_sent = jnp.where(place == tensor - 1, 0, first_relay)

    def sent_one(order, carry):
        pass_down(piece_of(order)).wait_send()
        return carry

    lax.fori_loop(first_sent, sent, sent_one, 0)


def backward(parents, q, k, v, o, branch_grad, seen, weights, lse, small):
    dp, tensor = lax.axis_size("dp"), lax.axis_size("tensor")
    ways = dp * tensor
    rows, width = q.shape
    seen_rows = k.shape[0]
    depth = width // dp
    padded = -(-depth // 16) * 16
    pairs, groups, pieces = width // 128, width // GROUP, rows // PIECE
    slab = (padded, width)
    low, full = jnp.bfloat16, jnp.float32
    dma = pltpu.SemaphoreType.DMA
    anywhere = pl.BlockSpec(memory_space=pl.ANY)
    here = pl.BlockSpec(memory_space=pltpu.VMEM)
    out, block, total = pl.pallas_call(
        lambda *refs: back_kernel(dp, tensor, depth, *refs),
        out_shape=(
            jax.ShapeDtypeStruct((rows, width), full),
            jax.ShapeDtypeStruct((padded, width), full),
            jax.ShapeDtypeStruct(small.shape, full),
        ),
        in_specs=[here] + [anywhere] * 7 + [here] * 2,
        out_specs=[here, here, here],
        scratch_shapes=[
            pltpu.VMEM((rows, width), low),
            pltpu.VMEM((seen_rows, width), low),
            pltpu.VMEM((seen_rows, width), low),
            pltpu.VMEM((rows, width), low),
            pltpu.VMEM((rows, width), low),
            pltpu.VMEM((rows, width), low),
            pltpu.VMEM((2, rows // 2, width), low),
            pltpu.VMEM((width, seen_rows), low),
            pltpu.VMEM(weights.shape, low),
            pltpu.VMEM((pairs, 2, rows), full),
            pltpu.VMEM((pairs, 128, rows), full),
            pltpu.VMEM((2 * rows, width), low),
            pltpu.VMEM((2 * rows, width), low),
            pltpu.VMEM((width, 128), full),
            pltpu.VMEM((groups + 1, dp) + slab, low),
            pltpu.VMEM((groups + 1, dp // 2) + slab, low),
            pltpu.VMEM((groups + 1, dp // 2) + slab, low),
            pltpu.VMEM((tensor, padded, width), low),
            pltpu.VMEM((tensor, padded, width), low),
            pltpu.VMEM(small.shape, full),
            pltpu.VMEM(small.shape, full),
            dma((3,)), dma((3, pairs)), dma((2,)),
            dma((2 * pieces,)), dma((2 * pieces,)),
            dma((groups + 1, dp // 2)), dma((groups + 1, dp // 2)),
            dma((groups + 1, dp // 2)), dma((groups + 1, dp // 2)),
            dma((tensor,)), dma((tensor,)),
            dma((ways,)), dma((ways,)), dma((ways,)), dma((ways,)),
        ],
        compiler_params=pltpu.CompilerParams(
            collective_id=3, has_side_effects=True, vmem_limit_bytes=62 << 20
        ),
        name="attend_backward",
    )(parents, q, k, v, o, branch_grad, seen, weights, lse, small)
    return out, block[:depth], total


HALF_ROOT = math.sqrt(0.5)
PDF_SCALE = 1.0 / math.sqrt(2.0 * math.pi)
CHUNK = 512
BAND = 256


def expert_kernel(
    dp, x_in, g_in, w_in, w_out, result_ref, back_ref, in_grad_ref, out_grad_ref,
    x_ref, g_ref, active_ref, slope_ref, keep_ref, part_ref, land_ref, home_ref,
    back_part, back_land, back_home,
    x_send, x_recv, x_pair_send, x_pair_recv, g_send, g_recv, g_pair_send, g_pair_recv,
    y_pair_send, y_pair_recv, y_send, y_recv, d_pair_send, d_pair_recv, d_send, d_recv,
):
    spot, place = lax.axis_index("dp"), lax.axis_index("tensor")
    chips = dp // 2
    chip, core = spot // 2, lax.rem(spot, 2)
    partner = (chip * 2 + 1 - core, place)
    capacity = x_in.shape[0] // chips

    def ahead(step):
        return (lax.rem(chip + step, chips) * 2 + core, place)

    def behind(step):
        return (lax.rem(chip - step + chips, chips) * 2 + core, place)

    def at(side, step):
        return pl.ds(pl.multiple_of((side * chips + step) * capacity, capacity), capacity)

    greet([ahead(step) for step in range(1, chips)] + [partner])

    def copy(source, target, send, recv, step, where):
        return pltpu.make_async_remote_copy(
            src_ref=source, dst_ref=target, send_sem=send.at[step], recv_sem=recv.at[step],
            device_id=where, device_id_type=MESH,
        )

    def go_x(step):
        return copy(x_in.at[at(0, step)], x_ref.at[at(0, step)], x_send, x_recv, step, ahead(step))

    def go_g(step):
        return copy(g_in.at[at(0, step)], g_ref.at[at(0, step)], g_send, g_recv, step, ahead(step))

    def pair_x(step):
        return copy(
            x_ref.at[at(0, step)], x_ref.at[at(1, step)], x_pair_send, x_pair_recv, step, partner
        )

    def pair_g(step):
        return copy(
            g_ref.at[at(0, step)], g_ref.at[at(1, step)], g_pair_send, g_pair_recv, step, partner
        )

    def pair_y(step):
        here = at(0, step)
        return copy(part_ref.at[here], land_ref.at[here], y_pair_send, y_pair_recv, step, partner)

    def pair_d(step):
        here = at(0, step)
        return copy(back_part.at[here], back_land.at[here], d_pair_send, d_pair_recv, step, partner)

    def home_y(step):
        here = at(0, step)
        return copy(home_ref.at[here], result_ref.at[here], y_send, y_recv, step, behind(step))

    def home_d(step):
        here = at(0, step)
        return copy(back_home.at[here], back_ref.at[here], d_send, d_recv, step, behind(step))

    @pl.loop(1, chips)
    def _(step):
        go_x(step).start()

    x_ref[at(0, 0)] = x_in[at(0, 0)]
    pair_x(0).start()

    @pl.loop(1, chips)
    def _(step):
        go_g(step).start()

    g_ref[at(0, 0)] = g_in[at(0, 0)]

    def ahead_pass(side, step):
        rows = x_ref[at(side, step)]
        total = None
        for first in range(0, w_in.shape[1], CHUNK):
            cols = slice(first, first + CHUNK)
            up = dot_nn(rows, w_in[:, cols])
            below = 0.5 * (1.0 + lax.erf(up * HALF_ROOT))
            active = (up * below).astype(jnp.bfloat16)
            slope = below + up * (jnp.exp(-0.5 * up * up) * PDF_SCALE)
            active_ref[at(side, step), cols] = active
            slope_ref[at(side, step), cols] = slope.astype(jnp.bfloat16)
            part = dot_nn(active, w_out[cols])
            total = part if total is None else total + part
        return total

    def back_pass(side, step):
        grads = g_ref[at(side, step)]
        total = None
        for first in range(0, w_in.shape[1], CHUNK):
            cols = slice(first, first + CHUNK)
            active_grad = dot_nt(grads, w_out[cols])
            up_grad = active_grad * slope_ref[at(side, step), cols].astype(jnp.float32)
            up_grad = up_grad.astype(jnp.bfloat16)
            slope_ref[at(side, step), cols] = up_grad
            part = dot_nt(up_grad, w_in[:, cols])
            total = part if total is None else total + part
        return total

    keep_ref[at(0, 0)] = ahead_pass(0, 0)

    @pl.loop(1, chips)
    def _(step):
        go_x(step).wait_recv()
        pair_x(step).start()
        keep_ref[at(0, step)] = ahead_pass(0, step)

    pair_g(0).start()

    @pl.loop(0, chips)
    def _(step):
        pair_x(step).wait_recv()
        part_ref[at(0, step)] = ahead_pass(1, step).astype(part_ref.dtype)
        pair_y(step).start()

    @pl.loop(1, chips)
    def _(step):
        go_g(step).wait_recv()
        pair_g(step).start()

    @pl.loop(0, chips)
    def _(step):
        pair_y(step).wait_recv()
        here = at(0, step)
        total = keep_ref[here] + land_ref[here].astype(jnp.float32)
        home_ref[here] = total.astype(home_ref.dtype)

        @pl.when(step > 0)
        def _():
            home_y(step).start()

        @pl.when(step == 0)
        def _():
            result_ref[here] = total.astype(result_ref.dtype)

    @pl.loop(0, chips)
    def _(step):
        pair_g(step).wait_recv()
        back_part[at(0, step)] = back_pass(1, step).astype(back_part.dtype)
        pair_d(step).start()

    @pl.loop(0, chips)
    def _(turn):
        step = chips - 1 - turn
        here = at(0, step)
        total = back_pass(0, step)
        pair_d(step).wait_recv()
        total = (total + back_land[here].astype(jnp.float32)).astype(back_home.dtype)
        back_home[here] = total

        @pl.when(step > 0)
        def _():
            home_d(step).start()

        @pl.when(step == 0)
        def _():
            back_ref[here] = total

    @pl.loop(0, w_in.shape[1] // BAND)
    def _(band):
        cols = pl.ds(pl.multiple_of(band * BAND, BAND), BAND)
        out_grad_ref[cols] = dot_tn(active_ref[:, cols], g_ref[...]).astype(out_grad_ref.dtype)
        in_grad_ref[cols] = dot_tn(slope_ref[:, cols], x_ref[...]).astype(in_grad_ref.dtype)

    @pl.loop(1, chips)
    def _(step):
        home_y(step).wait_recv()
        home_d(step).wait_recv()

    @pl.loop(0, chips)
    def _(step):
        pair_x(step).wait_send()
        pair_g(step).wait_send()
        pair_y(step).wait_send()
        pair_d(step).wait_send()

    @pl.loop(1, chips)
    def _(step):
        go_x(step).wait_send()
        go_g(step).wait_send()
        home_y(step).wait_send()
        home_d(step).wait_send()


def run_experts(slot_rows, slot_grads, w_in, w_out):
    dp = lax.axis_size("dp")
    rows, width = slot_rows.shape
    hidden = w_in.shape[1]
    low = jnp.bfloat16
    here = pl.BlockSpec(memory_space=pltpu.VMEM)
    near = pltpu.VMEM((rows, width), low)
    both = pltpu.VMEM((2 * rows, width), low)
    middle = pltpu.VMEM((2 * rows, hidden), low)
    return pl.pallas_call(
        lambda *refs: expert_kernel(dp, *refs),
        out_shape=(
            jax.ShapeDtypeStruct((rows, width), low),
            jax.ShapeDtypeStruct((rows, width), low),
            jax.ShapeDtypeStruct((hidden, width), low),
            jax.ShapeDtypeStruct((hidden, width), low),
        ),
        in_specs=[here] * 4,
        out_specs=[here] * 4,
        scratch_shapes=[
            both, both, middle, middle, pltpu.VMEM((rows, width), jnp.float32),
            near, near, near, near, near, near,
        ]
        + [pltpu.SemaphoreType.DMA((dp // 2,))] * 16,
        compiler_params=pltpu.CompilerParams(
            collective_id=4, has_side_effects=True, vmem_limit_bytes=60 << 20
        ),
        name="run_experts",
    )(slot_rows, slot_grads, w_in, w_out)


norm_eps = 1e-05
route_scale = 3.0
masked_score = -1e30
highest = lax.Precision.HIGHEST


def layer_norm(values, norm_gain):
    centred = values - jnp.mean(values, axis=-1, keepdims=True)
    spread = jnp.mean(centred * centred, axis=-1, keepdims=True)
    return centred * lax.rsqrt(spread + norm_eps) * norm_gain


def unit_rows(values):
    return values * lax.rsqrt(jnp.sum(values * values, axis=-1, keepdims=True) + 1.0)


def router_gate(normed, router_proj, expert_embed, picked):
    routed = jnp.dot(normed, router_proj, precision=highest)
    logits = route_scale * jnp.dot(unit_rows(routed), unit_rows(expert_embed).T, precision=highest)
    return jnp.sum(jax.nn.softmax(logits, axis=-1) * picked, axis=-1)


def gelu_exact(values):
    return jax.nn.gelu(values, approximate=False)


def slot_table(route_ids, order_ids, capacity):
    same_expert = route_ids[:, None] == route_ids[None, :]
    earlier = order_ids[None, :] < order_ids[:, None]
    ranking = jnp.sum(jnp.where(same_expert & earlier, 1, 0), axis=1).astype(jnp.int32)
    kept_mask = ranking < capacity
    column = route_ids * capacity + jnp.minimum(ranking, capacity - 1)
    return (column, kept_mask)


def low_dot(rows, weight):
    return jnp.dot(rows, weight, preferred_element_type=jnp.float32).astype(jnp.bfloat16)


def shards(
    tokens,
    norm1_gain,
    qkv_weight,
    attn_proj,
    norm2_gain,
    router_proj,
    expert_embed,
    expert_in,
    expert_out,
    routes,
    orders,
    leaf_parent,
    cotangent,
):
    rows_here = tokens.shape[0]
    model_width = tokens.shape[1]
    experts = expert_embed.shape[0]
    capacity = rows_here // experts
    dp_size, tensor_size = lax.axis_size("dp"), lax.axis_size("tensor")

    hidden = tokens.astype(jnp.float32)
    normed_in, norm1_back = jax.vjp(layer_norm, hidden, norm1_gain)
    own_in = normed_in.astype(jnp.bfloat16)
    flat_qkv = qkv_weight.reshape(qkv_weight.shape[0], -1)
    place = lax.axis_index("tensor")
    leaf_blocks = rows_here // BRANCH
    first_leaf = jnp.maximum(place - 2, 0) * leaf_blocks
    leaf_parents = lax.dynamic_slice_in_dim(leaf_parent[0], first_leaf, leaf_blocks, 0) - 1
    parents = (leaf_parents[:, None] == jnp.arange(leaf_blocks)[None, :]).astype(jnp.float32)
    parents = jnp.broadcast_to(parents.reshape(-1, 1), (leaf_blocks * leaf_blocks, model_width))
    seen_in, weights = share_rows_and_weights(
        own_in, jnp.concatenate([flat_qkv, attn_proj.T], axis=1), parents
    )
    query_weight, key_weight, value_weight, proj_back = weights
    query_rows = low_dot(own_in, query_weight)
    key_rows = low_dot(seen_in, key_weight)
    value_rows = low_dot(seen_in, value_weight)
    attended, log_totals = attend(place[None].astype(jnp.int32), query_rows, key_rows, value_rows)
    branch_out = jnp.einsum(
        "sc,dc->sd", attended, proj_back, preferred_element_type=jnp.float32
    )
    mid_stream = hidden + branch_out
    normed_mid, norm2_back = jax.vjp(layer_norm, mid_stream, norm2_gain)
    moe_in = normed_mid.astype(jnp.bfloat16)
    route_ids = routes[:, 0]
    near_route = (route_ids - lax.axis_index("dp") // 2) % experts
    column, kept_mask = slot_table(near_route, orders[0], capacity)
    picked = (route_ids[:, None] == jnp.arange(experts)[None, :]).astype(jnp.float32)
    gate_value, gate_back = jax.vjp(
        lambda normed_rows, route_proj, embed_rows: router_gate(
            normed_rows, route_proj, embed_rows, picked
        ),
        moe_in.astype(jnp.float32),
        router_proj,
        expert_embed,
    )
    select = (
        (column[:, None] == jnp.arange(experts * capacity)[None, :]) & kept_mask[:, None]
    ).astype(jnp.bfloat16)
    def to_slots(token_rows):
        return jnp.einsum(
            "ts,td->sd", select, token_rows, preferred_element_type=jnp.float32
        ).astype(jnp.bfloat16)

    def from_slots(slot_rows):
        return jnp.dot(select, slot_rows, preferred_element_type=jnp.float32)

    upstream = cotangent.astype(jnp.float32)
    slot_grads = to_slots((gate_value[:, None] * upstream).astype(jnp.bfloat16))
    result_rows, grad_rows, in_weight_grad, out_weight_grad = run_experts(
        to_slots(moe_in), slot_grads, expert_in, expert_out
    )
    expert_result = from_slots(result_rows)
    output = (mid_stream + gate_value[:, None] * expert_result).astype(jnp.bfloat16)
    moe_grad = from_slots(grad_rows)
    gate_grad = jnp.sum(upstream * expert_result, axis=-1)
    router_part, proj_grad, embed_grad = gate_back(gate_grad)
    mid_part, gain2_grad = norm2_back(moe_grad + router_part)
    mid_grad = upstream + mid_part
    expert_in_grad = (
        lax.psum_scatter(in_weight_grad, "tensor", scatter_dimension=0, tiled=True)
        .astype(jnp.float32)
        .T
    )
    expert_out_grad = lax.psum_scatter(
        out_weight_grad, "tensor", scatter_dimension=0, tiled=True
    ).astype(jnp.float32)
    branch_grad = mid_grad.astype(jnp.bfloat16)
    later = [gain2_grad, proj_grad, embed_grad]
    flat = jnp.concatenate([jnp.zeros_like(norm1_gain)] + [part.reshape(-1) for part in later])
    ways = dp_size * tensor_size
    lanes = -(-flat.shape[0] // (ways * 8 * 128)) * 128
    small = jnp.pad(flat, (0, ways * 8 * lanes - flat.shape[0])).reshape(ways, 8, lanes)
    input_grad, grad_block, totals = backward(
        parents, query_rows, key_rows, value_rows, attended, branch_grad, seen_in, weights,
        log_totals, small,
    )
    qkv_grad = grad_block[:, : flat_qkv.shape[1]].reshape(qkv_weight.shape)
    attn_proj_grad = grad_block[:, flat_qkv.shape[1] :].T
    totals = totals.reshape(-1)
    gain1_sum = totals[:model_width] / norm1_gain
    gain2_sum, router_sum, embed_sum = (
        totals[first : first + part.size].reshape(part.shape)
        for first, part in zip(
            (model_width, 2 * model_width, 2 * model_width + proj_grad.size), later
        )
    )
    token_part, _ = norm1_back(input_grad)
    token_grad = mid_grad + token_part
    return (
        output,
        token_grad,
        gain1_sum,
        qkv_grad,
        attn_proj_grad,
        gain2_sum,
        router_sum,
        embed_sum,
        expert_in_grad,
        expert_out_grad,
    )


def solution(mesh):
    in_specs = (
        P(("dp", "tensor"), None),
        P(),
        P("dp", None, "tensor"),
        P("tensor", "dp"),
        P(),
        P(),
        P(),
        P(None, "dp"),
        P("dp", None),
        P(("dp", "tensor"), None),
        P(("dp", "tensor"), None),
        P("dp", None),
        P(("dp", "tensor"), None),
    )
    out_specs = (
        P(("dp", "tensor"), None),
        P(("dp", "tensor"), None),
        P(),
        P("dp", None, "tensor"),
        P("tensor", "dp"),
        P(),
        P(),
        P(),
        P(None, ("dp", "tensor")),
        P(("dp", "tensor"), None),
    )
    return jax.shard_map(shards, mesh=mesh, in_specs=in_specs, out_specs=out_specs, check_vma=False)
```

```python
import functools
import math

import jax
import jax.numpy as jnp
from jax import lax
from jax.experimental import pallas as pl
from jax.experimental.pallas import tpu as pltpu
from jax.sharding import PartitionSpec as P

HEAD_DIM = 64
TRUNK = 1024
BRANCH = 256
MASKED = -1e30
LOG2E = math.log2(math.e)
EXP_SCALE = HEAD_DIM ** (-0.5) * LOG2E

NT = (((1,), (1,)), ((), ()))
NN = (((1,), (0,)), ((), ()))


def dot_nt(a, b):
    return lax.dot_general(a, b, NT, preferred_element_type=jnp.float32)


def dot_nn(a, b):
    return lax.dot_general(a, b, NN, preferred_element_type=jnp.float32)


def head_lanes(shape, dim, head):
    return lax.broadcasted_iota(jnp.int32, shape, dim) // HEAD_DIM == head


def fwd_kernel(place_ref, q_ref, k_ref, v_ref, o_ref, lse_ref, vt_ref, acc_ref):
    place = place_ref[0]
    rows = q_ref.shape[0]
    blocks = rows // BRANCH
    flipped = v_ref[...].T
    for head in range(2):
        vt_ref[head] = jnp.where(
            head_lanes(flipped.shape, 0, head), flipped, jnp.ones_like(flipped)
        )

    def start(block, head, in_trunk):
        queries = q_ref[block * BRANCH : (block + 1) * BRANCH]
        queries = jnp.where(head_lanes(queries.shape, 1, head), queries, jnp.zeros_like(queries))
        firsts = list(range(0, TRUNK, BRANCH))
        if not in_trunk:
            firsts += [rows + block * BRANCH, 2 * rows + block * BRANCH]
        scores = [dot_nt(k_ref[first : first + BRANCH], queries) for first in firsts]

        def causal(tile, offset):
            keys = lax.broadcasted_iota(jnp.int32, tile.shape, 0) + offset
            at = lax.broadcasted_iota(jnp.int32, tile.shape, 1)
            return jnp.where(keys <= at, tile, MASKED)

        if in_trunk:
            scores = [
                causal(tile, first - block * BRANCH) for tile, first in zip(scores, firsts)
            ]
        else:
            scores[-2] = jnp.where(place > 1, scores[-2], MASKED)
            scores[-1] = causal(scores[-1], 0)
        top = jnp.max(functools.reduce(jnp.maximum, scores), axis=0, keepdims=True)
        return firsts, scores, top

    def middle(firsts, scores, top):
        shift = top * EXP_SCALE
        probs = [jnp.exp2(tile * EXP_SCALE - shift).astype(jnp.bfloat16) for tile in scores]
        return firsts, probs, top

    def finish(block, head, firsts, probs, top):
        acc = None
        for first, tile in zip(firsts, probs):
            part = dot_nn(vt_ref[head, :, first : first + BRANCH], tile)
            acc = part if acc is None else acc + part
        mine, other = head * HEAD_DIM, (1 - head) * HEAD_DIM
        total = acc[other : other + 1]
        cols = slice(block * BRANCH, (block + 1) * BRANCH)
        acc_ref[mine : mine + HEAD_DIM, cols] = acc[mine : mine + HEAD_DIM] / total
        lse_ref[0, head : head + 1, cols] = top * EXP_SCALE + jnp.log2(total)

    def run(in_trunk):
        work = [(block, head) for block in range(blocks) for head in range(2)]
        ready, held = start(*work[0], in_trunk), None
        for at, item in enumerate(work):
            now = ready
            if at + 1 < len(work):
                ready = start(*work[at + 1], in_trunk)
            done = middle(*now)
            if held is not None:
                finish(*held)
            held = (*item, *done)
        finish(*held)

    @pl.when(place == 0)
    def _():
        run(True)

    @pl.when(place > 0)
    def _():
        run(False)

    o_ref[...] = acc_ref[...].T.astype(o_ref.dtype)


def attend(place, q, k, v):
    rows, width = q.shape
    keys = k.shape[0]
    pairs = width // 128
    few = pl.BlockSpec((rows, 128), lambda p, m: (0, p))
    many = pl.BlockSpec((keys, 128), lambda p, m: (0, p))
    return pl.pallas_call(
        fwd_kernel,
        out_shape=(
            jax.ShapeDtypeStruct((rows, width), jnp.bfloat16),
            jax.ShapeDtypeStruct((pairs, 2, rows), jnp.float32),
        ),
        grid_spec=pltpu.PrefetchScalarGridSpec(
            num_scalar_prefetch=1,
            grid=(pairs,),
            in_specs=[few, many, many],
            out_specs=[few, pl.BlockSpec((1, 2, rows), lambda p, m: (p, 0, 0))],
            scratch_shapes=[
                pltpu.VMEM((2, 128, keys), jnp.bfloat16),
                pltpu.VMEM((128, rows), jnp.float32),
            ],
        ),
        compiler_params=pltpu.CompilerParams(vmem_limit_bytes=48 << 20),
        name="attend_forward",
    )(place, q, k, v)


MESH = pl.DeviceIdType.MESH
PIECE = 64


def greet(peers):
    barrier = pltpu.get_barrier_semaphore()
    for peer in peers:
        pl.semaphore_signal(barrier, inc=1, device_id=peer, device_id_type=MESH)
    pl.semaphore_wait(barrier, len(peers))


def share_kernel(dp, tensor, own_ref, block_ref, parent_ref, seen_ref, out_ref, weights_ref,
                 ordered_ref, row_send, row_recv,
                 line_send, line_recv, chip_send, chip_recv, pair_send, pair_recv):
    spot, place = lax.axis_index("dp"), lax.axis_index("tensor")
    chip, core = spot // 2, lax.rem(spot, 2)
    chips = dp // 2
    rows = own_ref.shape[0]
    pieces = rows // PIECE
    part_width = out_ref.shape[2] // tensor
    partner = (chip * 2 + 1 - core, place)

    def along(step):
        return lax.rem(place + step, tensor)

    def chip_at(step):
        return lax.rem(chip + step, chips)

    greet(
        [(spot, along(step)) for step in range(1, tensor)]
        + [(chip_at(step) * 2 + core, place) for step in range(1, chips)]
        + [partner]
    )

    def pass_on(part, piece, fresh):
        at = pl.ds(part * rows + piece * PIECE, PIECE)
        source = own_ref.at[pl.ds(piece * PIECE, PIECE)] if fresh else seen_ref.at[at]
        return pltpu.make_async_remote_copy(
            src_ref=source, dst_ref=seen_ref.at[at],
            send_sem=row_send.at[part, piece], recv_sem=row_recv.at[part, piece],
            device_id=(spot, lax.rem(place + 1, tensor)), device_id_type=MESH,
        )

    def line(step):
        return pltpu.make_async_remote_copy(
            src_ref=block_ref, dst_ref=weights_ref.at[place, spot],
            send_sem=line_send.at[step], recv_sem=line_recv.at[place],
            device_id=(spot, along(step)), device_id_type=MESH,
        )

    def line_in(step):
        source = along(tensor - step)
        return pltpu.make_async_remote_copy(
            src_ref=block_ref, dst_ref=weights_ref.at[source, spot],
            send_sem=line_send.at[step], recv_sem=line_recv.at[source],
            device_id=(spot, along(step)), device_id_type=MESH,
        )

    def plane(part, step):
        block = weights_ref.at[part, spot]
        return pltpu.make_async_remote_copy(
            src_ref=block, dst_ref=block,
            send_sem=chip_send.at[part, step], recv_sem=chip_recv.at[part, chip],
            device_id=(chip_at(step) * 2 + core, place), device_id_type=MESH,
        )

    def plane_in(part, step):
        source = chip_at(chips - step)
        block = weights_ref.at[part, source * 2 + core]
        return pltpu.make_async_remote_copy(
            src_ref=block, dst_ref=block,
            send_sem=chip_send.at[part, step], recv_sem=chip_recv.at[part, source],
            device_id=(chip_at(step) * 2 + core, place), device_id_type=MESH,
        )

    def across(part, source, source_core):
        block = weights_ref.at[part, source * 2 + source_core]
        return pltpu.make_async_remote_copy(
            src_ref=block, dst_ref=block,
            send_sem=pair_send.at[part, source], recv_sem=pair_recv.at[part, source],
            device_id=partner, device_id_type=MESH,
        )

    for step in range(1, tensor):
        line(step).start()

    def row_steps(first, last):
        @pl.loop(first, last)
        def _(piece):
            @pl.when(place == 0)
            def _():
                pass_on(0, piece, True).start()

            @pl.when(place > 0)
            def _():
                pass_on(0, piece, False).wait_recv()

            @pl.when((place > 0) & (place < tensor - 1))
            def _():
                pass_on(0, piece, False).start()

            @pl.when(place == 1)
            def _():
                pass_on(1, piece, True).start()

            @pl.when(place > 1)
            def _():
                pass_on(1, piece, False).wait_recv()

            @pl.when((place > 1) & (place < tensor - 1))
            def _():
                pass_on(1, piece, False).start()

    weights_ref[place, spot] = block_ref[...]
    seen_ref[2 * rows :] = own_ref[...]

    @pl.when(place < 2)
    def _():
        seen_ref[rows : 2 * rows] = own_ref[...]

    @pl.when(place == 0)
    def _():
        seen_ref[0:rows] = own_ref[...]

    row_steps(0, pieces // 4)
    for step in range(tensor):
        part = along(tensor - step)
        if step:
            line_in(step).wait_recv()

        @pl.loop(1, chips)
        def _(hop):
            plane(part, hop).start()

        across(part, chip, core).start()
    row_steps(pieces // 4, (pieces * 5) // 8)
    for step in range(tensor):
        part = along(tensor - step)

        @pl.loop(1, chips)
        def _(hop):
            plane_in(part, hop).wait_recv()
            across(part, chip_at(chips - hop), core).start()

    row_steps((pieces * 5) // 8, pieces)
    for part in range(tensor):

        @pl.loop(0, chips)
        def _(source):
            across(part, source, 1 - core).wait_recv()
            across(part, source, core).wait_send()

        @pl.loop(1, chips)
        def _(hop):
            plane(part, hop).wait_send()

    for step in range(1, tensor):
        line(step).wait_send()

    @pl.when(place < tensor - 1)
    def _():
        @pl.loop(0, pieces)
        def _(piece):
            pass_on(0, piece, False).wait_send()

    @pl.when((place > 0) & (place < tensor - 1))
    def _():
        @pl.loop(0, pieces)
        def _(piece):
            pass_on(1, piece, False).wait_send()

    @pl.when(place > 1)
    def _():
        blocks = rows // BRANCH
        branches = [
            seen_ref[rows + branch * BRANCH : rows + (branch + 1) * BRANCH]
            for branch in range(blocks)
        ]
        for leaf in range(blocks):
            chosen = None
            for branch in range(blocks):
                at = leaf * blocks + branch
                part = branches[branch] * parent_ref[at : at + 1].astype(own_ref.dtype)
                chosen = part if chosen is None else chosen + part
            ordered_ref[leaf * BRANCH : (leaf + 1) * BRANCH] = chosen
        seen_ref[rows : 2 * rows] = ordered_ref[...]

    @pl.loop(0, dp)
    def _(source):
        depth = block_ref.shape[0]
        at = pl.ds(pl.multiple_of(source * depth, depth), depth)
        for kind in range(out_ref.shape[0]):
            cols = slice(kind * part_width, (kind + 1) * part_width)
            out_ref[kind, at] = jnp.concatenate(
                [weights_ref[part, source][:, cols] for part in range(tensor)], axis=1
            )


def share_rows_and_weights(own, block, parents):
    dp, tensor = lax.axis_size("dp"), lax.axis_size("tensor")
    rows, width = own.shape
    depth, cols = block.shape
    pieces, chips = rows // PIECE, dp // 2
    kinds = cols * tensor // width
    padded = -(-depth // 16) * 16
    block = jnp.pad(block, ((0, padded - depth), (0, 0)))
    dma = pltpu.SemaphoreType.DMA
    here = pl.BlockSpec(memory_space=pltpu.VMEM)
    seen, weights = pl.pallas_call(
        lambda *refs: share_kernel(dp, tensor, *refs),
        out_shape=(
            jax.ShapeDtypeStruct((3 * rows, width), own.dtype),
            jax.ShapeDtypeStruct((kinds, dp * padded, width), block.dtype),
        ),
        in_specs=[here, here, here],
        out_specs=[here, here],
        scratch_shapes=[
            pltpu.VMEM((tensor, dp, padded, cols), block.dtype),
            pltpu.VMEM(own.shape, own.dtype),
            dma((2, pieces)), dma((2, pieces)),
            dma((tensor,)), dma((tensor,)),
            dma((tensor, chips)), dma((tensor, chips)),
            dma((tensor, chips)), dma((tensor, chips)),
        ],
        compiler_params=pltpu.CompilerParams(
            collective_id=2, has_side_effects=True, vmem_limit_bytes=48 << 20
        ),
        name="share_rows_and_weights",
    )(own, block, parents)
    weights = weights.reshape(kinds, dp, padded, width)[:, :, :depth]
    return seen, weights.reshape(kinds, dp * depth, width)


TN = (((0,), (0,)), ((), ()))
GROUP = 256


def dot_tn(a, b):
    return lax.dot_general(a, b, TN, preferred_element_type=jnp.float32)


def back_kernel(
    dp, tensor, depth,
    parent_ref, q_in, k_in, v_in, o_in, grad_in, seen_in, weight_in, lse_ref, small_ref,
    out_ref, sum_ref, total_ref,
    q_ref, k_ref, v_ref, o_ref, bg_ref, g_ref, stage_ref, seen_ref, weight_ref,
    delta_ref, dqt_ref, rows_ref, land_ref, gain_ref,
    slab_ref, pair_land, chip_land, line_out, line_land, part_ref, part_land,
    load_sem, pair_sem, stage_sem, row_send, row_recv,
    pair_send, pair_recv, chip_send, chip_recv,
    line_send, line_recv, small_send, small_recv, spread_send, spread_recv,
):
    spot, place = lax.axis_index("dp"), lax.axis_index("tensor")
    ways = dp * tensor
    me = spot * tensor + place
    scale = HEAD_DIM ** (-0.5)
    rows, width = q_ref.shape
    pairs = width // 128
    groups = width // GROUP
    blocks = rows // BRANCH
    pieces = rows // PIECE
    stage_rows = stage_ref.shape[1]

    def device(index):
        return (index // tensor, lax.rem(index, tensor))

    def along(step):
        return lax.rem(place + step, tensor)

    chips = dp // 2
    chip, core = spot // 2, lax.rem(spot, 2)

    def chip_at(step):
        return lax.rem(chip + step, chips)

    def block_at(b):
        return pl.ds(pl.multiple_of(b * BRANCH, BRANCH), BRANCH)

    barrier = pltpu.get_barrier_semaphore()

    @pl.loop(1, ways)
    def _(step):
        pl.semaphore_signal(
            barrier, inc=1, device_id=device(lax.rem(me + step, ways)), device_id_type=MESH
        )

    def lanes(pair):
        return pl.ds(pl.multiple_of(pair * 128, 128), 128)

    grad_load = pltpu.make_async_copy(grad_in, bg_ref, load_sem.at[0])
    weight_load = pltpu.make_async_copy(weight_in, weight_ref, load_sem.at[1])
    value_load = pltpu.make_async_copy(o_in, o_ref, load_sem.at[2])

    def pair_loads(pair):
        return [
            pltpu.make_async_copy(
                source.at[:, lanes(pair)], held.at[:, lanes(pair)], pair_sem.at[which, pair]
            )
            for which, (source, held) in enumerate(((q_in, q_ref), (k_in, k_ref), (v_in, v_ref)))
        ]

    def stage(part):
        slot = lax.rem(part, 2)
        at = pl.ds(pl.multiple_of(part * stage_rows, stage_rows), stage_rows)
        return pltpu.make_async_copy(seen_in.at[at], stage_ref.at[slot], stage_sem.at[slot])

    grad_load.start()
    weight_load.start()
    value_load.start()

    @pl.loop(0, pairs)
    def _(pair):
        for load in pair_loads(pair):
            load.start()

    grad_load.wait()
    weight_load.wait()
    value_load.wait()

    def keep(held, value, kind):
        cols = slice(kind * GROUP, (kind + 1) * GROUP)
        if depth % 16:
            for target in range(dp):
                held[target, 0:depth, cols] = value[target * depth : (target + 1) * depth].astype(
                    slab_ref.dtype
                )
        else:
            held[:, :, cols] = value.reshape(dp, depth, GROUP).astype(slab_ref.dtype)

    for group in range(groups):
        cols = slice(group * GROUP, (group + 1) * GROUP)
        keep(slab_ref.at[groups], dot_tn(bg_ref[...], o_ref[:, cols]), group)

    @pl.loop(0, blocks)
    def _(b):
        at = block_at(b)
        g_ref[at] = dot_nn(bg_ref[at], weight_ref[3]).astype(g_ref.dtype)

    pl.semaphore_wait(barrier, ways - 1)

    def halve(group, source):
        return pltpu.make_async_remote_copy(
            src_ref=slab_ref.at[group, source * 2 + 1 - core],
            dst_ref=pair_land.at[group, source],
            send_sem=pair_send.at[group, source], recv_sem=pair_recv.at[group, source],
            device_id=(chip * 2 + 1 - core, place), device_id_type=MESH,
        )

    def give(group, step):
        to = chip_at(step) * 2 + core
        return pltpu.make_async_remote_copy(
            src_ref=slab_ref.at[group, to], dst_ref=chip_land.at[group, chip],
            send_sem=chip_send.at[group, step], recv_sem=chip_recv.at[group, chip],
            device_id=(to, place), device_id_type=MESH,
        )

    def take(group, step):
        source = chip_at(chips - step)
        return pltpu.make_async_remote_copy(
            src_ref=slab_ref.at[group, source * 2 + core], dst_ref=chip_land.at[group, source],
            send_sem=chip_send.at[group, step], recv_sem=chip_recv.at[group, source],
            device_id=(chip_at(step) * 2 + core, place), device_id_type=MESH,
        )

    def share_slabs(group):
        @pl.loop(0, chips)
        def _(source):
            halve(group, source).start()

    def send_slabs(group):
        @pl.loop(0, chips)
        def _(step):
            to = chip_at(step)
            halve(group, to).wait_recv()
            mine = slab_ref[group, to * 2 + core].astype(jnp.float32)
            mine = mine + pair_land[group, to].astype(jnp.float32)
            slab_ref[group, to * 2 + core] = mine.astype(slab_ref.dtype)

            @pl.when(step > 0)
            def _():
                give(group, step).start()

    share_slabs(groups)

    @pl.loop(0, pairs)
    def _(pair):
        for load in pair_loads(pair):
            load.wait()
        product = g_ref[:, lanes(pair)].astype(jnp.float32)
        product = (product * o_ref[:, lanes(pair)].astype(jnp.float32)).T
        for head in range(2):
            delta_ref[pair, head : head + 1, :] = jnp.sum(
                product[head * HEAD_DIM : (head + 1) * HEAD_DIM], axis=0, keepdims=True
            )
        dqt_ref[pair] = jnp.zeros(dqt_ref.shape[1:], dqt_ref.dtype)

    def sweep(pair, tiles):
        work = [(tile, head) for tile in range(len(tiles)) for head in range(2)]
        sums = [[None, None] for _ in tiles]
        keys, flipped = {}, {}

        def key_block(tile):
            row = tiles[tile][0]
            if id(row) not in keys:
                kb = k_ref[pl.ds(row, BRANCH), lanes(pair)]
                vb = v_ref[pl.ds(row, BRANCH), lanes(pair)]
                masked = []
                for head in range(2):
                    mine = head_lanes(kb.shape, 1, head)
                    masked.append(
                        (
                            jnp.where(mine, kb, jnp.zeros_like(kb)),
                            jnp.where(mine, vb, jnp.zeros_like(vb)),
                        )
                    )
                keys[id(row)] = masked
                flipped[id(row)] = kb.T
            return keys[id(row)], flipped[id(row)]

        def start(tile, head):
            at = pl.ds(tiles[tile][1], BRANCH)
            kb, vb = key_block(tile)[0][head]
            return dot_nt(kb, q_ref[at, lanes(pair)]), dot_nt(vb, g_ref[at, lanes(pair)])

        def middle(tile, head, scores, prob_grad):
            at = pl.ds(tiles[tile][1], BRANCH)
            probs = jnp.exp2(scores * EXP_SCALE - lse_ref[pair, head : head + 1, at])
            if tiles[tile][2] is not None:
                probs = tiles[tile][2](probs)
            score_grad = probs * (prob_grad - delta_ref[pair, head : head + 1, at])
            return probs.astype(jnp.bfloat16), score_grad.astype(jnp.bfloat16)

        def finish(tile, head, probs, score_grad):
            at = pl.ds(tiles[tile][1], BRANCH)
            parts = (
                dot_nn(score_grad, q_ref[at, lanes(pair)]),
                dot_nn(probs, g_ref[at, lanes(pair)]),
            )
            for which in range(2):
                held = sums[tile][which]
                if head == 0:
                    sums[tile][which] = parts[which]
                else:
                    first = head_lanes(held.shape, 1, 0)
                    sums[tile][which] = jnp.where(first, held, parts[which])
            mine = slice(head * HEAD_DIM, (head + 1) * HEAD_DIM)
            dqt_ref[pair, mine, at] += dot_nn(key_block(tile)[1][mine], score_grad)

        ready = start(*work[0])
        held = None
        for at, item in enumerate(work):
            now = ready
            if at + 1 < len(work):
                ready = start(*work[at + 1])
            done = middle(*item, *now)
            if held is not None:
                finish(*held)
            held = (*item, *done)
        finish(*held)
        return sums

    def causal(key_row, query_row):
        def mask_of(probs):
            keys = lax.broadcasted_iota(jnp.int32, probs.shape, 0) + key_row
            at = lax.broadcasted_iota(jnp.int32, probs.shape, 1) + query_row
            return jnp.where(keys <= at, probs, 0.0)

        return mask_of

    def put(pair, row, dk, dv):
        at = pl.ds(row, BRANCH)
        k_ref[at, lanes(pair)] = (dk * scale).astype(k_ref.dtype)
        v_ref[at, lanes(pair)] = dv.astype(v_ref.dtype)

    def pass_down(piece):
        at = pl.ds(pl.multiple_of(piece * PIECE, PIECE), PIECE)
        return pltpu.make_async_remote_copy(
            src_ref=rows_ref.at[at], dst_ref=land_ref.at[at],
            send_sem=row_send.at[piece], recv_sem=row_recv.at[piece],
            device_id=(spot, lax.rem(place + tensor - 1, tensor)), device_id_type=MESH,
        )

    def row_grad(b):
        at = block_at(b)
        return dot_nt(k_ref[at], weight_ref[1]) + dot_nt(v_ref[at], weight_ref[2])

    def hand_down(b, total):
        rows_ref[block_at(b)] = total.astype(rows_ref.dtype)

        @pl.when(place == tensor - 1)
        def _():
            for piece in range(BRANCH // PIECE):
                pass_down(b * (BRANCH // PIECE) + piece).start()

    def joined(piece):
        at = pl.ds(pl.multiple_of(piece * PIECE, PIECE), PIECE)
        return rows_ref[at].astype(jnp.float32) + land_ref[at].astype(jnp.float32)

    middle_place = (place > 0) & (place < tensor - 1)
    late = 3 * jnp.maximum(tensor - 2 - place, 0)
    first_relay = jnp.where(place > 1, 0, pieces)
    last_relay = jnp.where(middle_place, 2 * pieces, first_relay)

    def piece_of(order):
        return lax.rem(order + pieces, 2 * pieces)

    def serve(first, last):
        def one(order, carry):
            piece = piece_of(order)
            pass_down(piece).wait_recv()
            at = pl.ds(pl.multiple_of(piece * PIECE, PIECE), PIECE)
            rows_ref[at] = joined(piece).astype(rows_ref.dtype)
            pass_down(piece).start()
            return carry

        low = jnp.clip(first - late, first_relay, last_relay)
        lax.fori_loop(low, jnp.clip(last - late, low, last_relay), one, 0)

    @pl.loop(0, pairs)
    def _(pair):
        @pl.when(place == 0)
        def _():
            for ref in (k_ref, v_ref):
                ref[rows : 3 * rows, lanes(pair)] = jnp.zeros((2 * rows, 128), ref.dtype)

        @pl.when(place > 0)
        def _():
            def seen_parent(probs):
                return jnp.where(place > 1, probs, 0.0)

            spots = range(0, rows, BRANCH)
            sums = sweep(pair, [(rows + at, at, seen_parent) for at in spots])
            for at, part in zip(spots, sums):
                put(pair, rows + at, *part)

    send_slabs(groups)

    @pl.loop(0, blocks)
    def _(leaf):
        out_ref[block_at(leaf)] = row_grad(blocks + leaf)

    for branch in range(blocks):
        total = None
        for leaf in range(blocks):
            at = leaf * blocks + branch
            part = out_ref[leaf * BRANCH : (leaf + 1) * BRANCH] * parent_ref[at : at + 1]
            total = part if total is None else total + part
        hand_down(blocks + branch, total)

    stage(0).start()

    @pl.loop(0, blocks)
    def _(b):
        row = pl.multiple_of(b * BRANCH, BRANCH)

        @pl.loop(0, pairs)
        def _(pair):
            def finish_block(masked):
                tiles = [
                    (row, first, causal(row, first) if masked else None)
                    for first in range(0, rows, BRANCH)
                ]
                sums = sweep(pair, tiles)
                put(pair, row, sum(part[0] for part in sums), sum(part[1] for part in sums))

            @pl.when(place == 0)
            def _():
                finish_block(True)

            @pl.when(place > 0)
            def _():
                finish_block(False)

            slot = b * pairs + pair
            serve(slot - 1, slot)

        for _half in range(2):
            part = b * 2 + _half

            @pl.when(part < 3 * rows // stage_rows)
            def _():
                stage(part).wait()

                @pl.when(part + 1 < 3 * rows // stage_rows)
                def _():
                    stage(part + 1).start()

                at = pl.ds(pl.multiple_of(part * stage_rows, stage_rows), stage_rows)
                seen_ref[:, at] = stage_ref[lax.rem(part, 2)].T

        hand_down(b, row_grad(b))

    served = blocks * pairs - 1

    gain_ref[...] = jnp.zeros_like(gain_ref)

    @pl.loop(0, groups)
    def _(group):
        base = served + group * 4

        @pl.loop(0, 2)
        def _(half):
            pair = group * 2 + half

            @pl.when(place > 0)
            def _():
                spots = range(0, rows, BRANCH)
                sums = sweep(pair, [(2 * rows + at, at, causal(0, 0)) for at in spots])
                for at, part in zip(spots, sums):
                    put(pair, 2 * rows + at, *part)

            q_ref[:, lanes(pair)] = (dqt_ref[pair] * scale).T.astype(q_ref.dtype)
            serve(base + half, base + half + 1)

        cols = pl.ds(pl.multiple_of(group * GROUP, GROUP), GROUP)
        for kind, value in (
            (0, lambda: dot_nn(seen_ref[:, 2 * rows : 3 * rows], q_ref[:, cols])),
            (1, lambda: dot_nn(seen_ref[...], k_ref[:, cols])),
            (2, lambda: dot_nn(seen_ref[...], v_ref[:, cols])),
        ):
            product = value()
            scaled = product * weight_ref[kind, :, cols].astype(jnp.float32)
            gain_ref[...] += scaled[:, 0:128] + scaled[:, 128:256]
            keep(slab_ref.at[group], product, kind)
            if kind:
                serve(base + 1 + kind, base + 2 + kind)

        share_slabs(group)

        @pl.when(group > 0)
        def _():
            send_slabs(group - 1)

    served += groups * 4

    part_ref[...] = small_ref[...]
    gains = jnp.sum(gain_ref[...].T, axis=0, keepdims=True)
    for row in range(width // 128):
        part_ref[0, row : row + 1, :] = gains[:, row * 128 : (row + 1) * 128]

    def scatter(step):
        to = lax.rem(me + step, ways)
        return pltpu.make_async_remote_copy(
            src_ref=part_ref.at[to], dst_ref=part_land.at[me],
            send_sem=small_send.at[step], recv_sem=small_recv.at[me],
            device_id=device(to), device_id_type=MESH,
        )

    def arrival(step):
        source = lax.rem(me - step + ways, ways)
        return pltpu.make_async_remote_copy(
            src_ref=part_ref.at[source], dst_ref=part_land.at[source],
            send_sem=small_send.at[step], recv_sem=small_recv.at[source],
            device_id=device(lax.rem(me + step, ways)), device_id_type=MESH,
        )

    def spread(step):
        return pltpu.make_async_remote_copy(
            src_ref=total_ref.at[me], dst_ref=total_ref.at[me],
            send_sem=spread_send.at[step], recv_sem=spread_recv.at[me],
            device_id=device(lax.rem(me + step, ways)), device_id_type=MESH,
        )

    def landing(step):
        source = lax.rem(me - step + ways, ways)
        return pltpu.make_async_remote_copy(
            src_ref=total_ref.at[source], dst_ref=total_ref.at[source],
            send_sem=spread_send.at[step], recv_sem=spread_recv.at[source],
            device_id=device(lax.rem(me + step, ways)), device_id_type=MESH,
        )

    @pl.loop(1, ways)
    def _(step):
        scatter(step).start()

    send_slabs(groups - 1)

    @pl.loop(0, blocks)
    def _(b):
        at = block_at(b)
        out_ref[at] = row_grad(2 * blocks + b) + dot_nt(q_ref[at], weight_ref[0])
        serve(served + 2 * b, served + 2 * b + 2)

    served += 2 * blocks

    def add(step, total):
        arrival(step).wait_recv()
        return total + part_land[lax.rem(me - step + ways, ways)]

    total_ref[me] = lax.fori_loop(1, ways, add, part_ref[me])

    @pl.loop(1, ways)
    def _(step):
        spread(step).start()

    serve(served, jnp.maximum(served, 2 * pieces) + late)

    kinds = [[], [], [], []]
    for group in range(groups + 1):

        def add_slab(step, total):
            take(group, step).wait_recv()
            return total + chip_land[group, chip_at(chips - step)].astype(jnp.float32)

        total = lax.fori_loop(1, chips, add_slab, slab_ref[group, spot].astype(jnp.float32))
        for part in range(total.shape[1] // GROUP):
            kinds[3 if group == groups else part].append(
                total[:, part * GROUP : (part + 1) * GROUP]
            )

    share = width // tensor
    kinds = [jnp.concatenate(parts, axis=1) for parts in kinds]
    for target in range(tensor):
        mine = jnp.concatenate(
            [kind[:, target * share : (target + 1) * share] for kind in kinds], axis=1
        )
        line_out[target] = mine.astype(line_out.dtype)

        @pl.when(place == target)
        def _():
            sum_ref[...] = mine

    def line(step):
        return pltpu.make_async_remote_copy(
            src_ref=line_out.at[along(step)], dst_ref=line_land.at[place],
            send_sem=line_send.at[step], recv_sem=line_recv.at[place],
            device_id=(spot, along(step)), device_id_type=MESH,
        )

    def line_in(step):
        source = along(tensor - step)
        return pltpu.make_async_remote_copy(
            src_ref=line_out.at[source], dst_ref=line_land.at[source],
            send_sem=line_send.at[step], recv_sem=line_recv.at[source],
            device_id=(spot, along(step)), device_id_type=MESH,
        )

    for step in range(1, tensor):
        line(step).start()

    @pl.when(place < 2)
    def _():
        @pl.loop(0, pieces)
        def _(piece):
            source = place * pieces + piece
            pass_down(source).wait_recv()
            at = pl.ds(pl.multiple_of(piece * PIECE, PIECE), PIECE)
            out_ref[at] += joined(source)

    for step in range(1, tensor):
        line_in(step).wait_recv()
        sum_ref[...] += line_land[along(tensor - step)].astype(jnp.float32)

    @pl.loop(1, ways)
    def _(step):
        landing(step).wait_recv()

    for step in range(1, tensor):
        line(step).wait_send()

    @pl.loop(1, ways)
    def _(step):
        scatter(step).wait_send()
        spread(step).wait_send()

    for group in range(groups + 1):

        @pl.loop(0, chips)
        def _(step):
            halve(group, step).wait_send()

            @pl.when(step > 0)
            def _():
                give(group, step).wait_send()

    sent = jnp.where(place == tensor - 1, 2 * pieces, last_relay)
    first_sent = jnp.where(place == tensor - 1, 0, first_relay)

    def sent_one(order, carry):
        pass_down(piece_of(order)).wait_send()
        return carry

    lax.fori_loop(first_sent, sent, sent_one, 0)


def backward(parents, q, k, v, o, branch_grad, seen, weights, lse, small):
    dp, tensor = lax.axis_size("dp"), lax.axis_size("tensor")
    ways = dp * tensor
    rows, width = q.shape
    seen_rows = k.shape[0]
    depth = width // dp
    padded = -(-depth // 16) * 16
    pairs, groups, pieces = width // 128, width // GROUP, rows // PIECE
    slab = (padded, width)
    low, full = jnp.bfloat16, jnp.float32
    dma = pltpu.SemaphoreType.DMA
    anywhere = pl.BlockSpec(memory_space=pl.ANY)
    here = pl.BlockSpec(memory_space=pltpu.VMEM)
    out, block, total = pl.pallas_call(
        lambda *refs: back_kernel(dp, tensor, depth, *refs),
        out_shape=(
            jax.ShapeDtypeStruct((rows, width), full),
            jax.ShapeDtypeStruct((padded, width), full),
            jax.ShapeDtypeStruct(small.shape, full),
        ),
        in_specs=[here] + [anywhere] * 7 + [here] * 2,
        out_specs=[here, here, here],
        scratch_shapes=[
            pltpu.VMEM((rows, width), low),
            pltpu.VMEM((seen_rows, width), low),
            pltpu.VMEM((seen_rows, width), low),
            pltpu.VMEM((rows, width), low),
            pltpu.VMEM((rows, width), low),
            pltpu.VMEM((rows, width), low),
            pltpu.VMEM((2, rows // 2, width), low),
            pltpu.VMEM((width, seen_rows), low),
            pltpu.VMEM(weights.shape, low),
            pltpu.VMEM((pairs, 2, rows), full),
            pltpu.VMEM((pairs, 128, rows), full),
            pltpu.VMEM((2 * rows, width), low),
            pltpu.VMEM((2 * rows, width), low),
            pltpu.VMEM((width, 128), full),
            pltpu.VMEM((groups + 1, dp) + slab, low),
            pltpu.VMEM((groups + 1, dp // 2) + slab, low),
            pltpu.VMEM((groups + 1, dp // 2) + slab, low),
            pltpu.VMEM((tensor, padded, width), low),
            pltpu.VMEM((tensor, padded, width), low),
            pltpu.VMEM(small.shape, full),
            pltpu.VMEM(small.shape, full),
            dma((3,)), dma((3, pairs)), dma((2,)),
            dma((2 * pieces,)), dma((2 * pieces,)),
            dma((groups + 1, dp // 2)), dma((groups + 1, dp // 2)),
            dma((groups + 1, dp // 2)), dma((groups + 1, dp // 2)),
            dma((tensor,)), dma((tensor,)),
            dma((ways,)), dma((ways,)), dma((ways,)), dma((ways,)),
        ],
        compiler_params=pltpu.CompilerParams(
            collective_id=3, has_side_effects=True, vmem_limit_bytes=62 << 20
        ),
        name="attend_backward",
    )(parents, q, k, v, o, branch_grad, seen, weights, lse, small)
    return out, block[:depth], total


HALF_ROOT = math.sqrt(0.5)
PDF_SCALE = 1.0 / math.sqrt(2.0 * math.pi)
CHUNK = 512
BAND = 256


def expert_kernel(
    dp, tensor, x_in, g_in, w_in, w_out, result_ref, back_ref, in_grad_ref, out_grad_ref,
    x_ref, g_ref, active_ref, slope_ref, keep_ref, part_ref, land_ref, home_ref,
    back_part, back_land, back_home, grad_ref, grad_land,
    x_send, x_recv, x_pair_send, x_pair_recv, g_send, g_recv, g_pair_send, g_pair_recv,
    y_pair_send, y_pair_recv, y_send, y_recv, d_pair_send, d_pair_recv, d_send, d_recv,
    line_send, line_recv,
):
    spot, place = lax.axis_index("dp"), lax.axis_index("tensor")
    chips = dp // 2
    chip, core = spot // 2, lax.rem(spot, 2)
    partner = (chip * 2 + 1 - core, place)
    capacity = x_in.shape[0] // chips

    def ahead(step):
        return (lax.rem(chip + step, chips) * 2 + core, place)

    def behind(step):
        return (lax.rem(chip - step + chips, chips) * 2 + core, place)

    def at(side, step):
        return pl.ds(pl.multiple_of((side * chips + step) * capacity, capacity), capacity)

    def along(step):
        return lax.rem(place + step, tensor)

    greet(
        [ahead(step) for step in range(1, chips)]
        + [partner]
        + [(spot, along(step)) for step in range(1, tensor)]
    )
    share = out_grad_ref.shape[0]

    def line(step):
        return pltpu.make_async_remote_copy(
            src_ref=grad_ref.at[along(step)], dst_ref=grad_land.at[place],
            send_sem=line_send.at[step], recv_sem=line_recv.at[place],
            device_id=(spot, along(step)), device_id_type=MESH,
        )

    def line_in(step):
        source = along(tensor - step)
        return pltpu.make_async_remote_copy(
            src_ref=grad_ref.at[source], dst_ref=grad_land.at[source],
            send_sem=line_send.at[step], recv_sem=line_recv.at[source],
            device_id=(spot, along(step)), device_id_type=MESH,
        )

    def copy(source, target, send, recv, step, where):
        return pltpu.make_async_remote_copy(
            src_ref=source, dst_ref=target, send_sem=send.at[step], recv_sem=recv.at[step],
            device_id=where, device_id_type=MESH,
        )

    def go_x(step):
        return copy(x_in.at[at(0, step)], x_ref.at[at(0, step)], x_send, x_recv, step, ahead(step))

    def go_g(step):
        return copy(g_in.at[at(0, step)], g_ref.at[at(0, step)], g_send, g_recv, step, ahead(step))

    def pair_x(step):
        return copy(
            x_ref.at[at(0, step)], x_ref.at[at(1, step)], x_pair_send, x_pair_recv, step, partner
        )

    def pair_g(step):
        return copy(
            g_ref.at[at(0, step)], g_ref.at[at(1, step)], g_pair_send, g_pair_recv, step, partner
        )

    def pair_y(step):
        here = at(0, step)
        return copy(part_ref.at[here], land_ref.at[here], y_pair_send, y_pair_recv, step, partner)

    def pair_d(step):
        here = at(0, step)
        return copy(back_part.at[here], back_land.at[here], d_pair_send, d_pair_recv, step, partner)

    def home_y(step):
        here = at(0, step)
        return copy(home_ref.at[here], result_ref.at[here], y_send, y_recv, step, behind(step))

    def home_d(step):
        here = at(0, step)
        return copy(back_home.at[here], back_ref.at[here], d_send, d_recv, step, behind(step))

    @pl.loop(1, chips)
    def _(step):
        go_x(step).start()

    x_ref[at(0, 0)] = x_in[at(0, 0)]
    pair_x(0).start()

    @pl.loop(1, chips)
    def _(step):
        go_g(step).start()

    g_ref[at(0, 0)] = g_in[at(0, 0)]

    def ahead_pass(side, step):
        rows = x_ref[at(side, step)]
        total = None
        for first in range(0, w_in.shape[1], CHUNK):
            cols = slice(first, first + CHUNK)
            up = dot_nn(rows, w_in[:, cols])
            below = 0.5 * (1.0 + lax.erf(up * HALF_ROOT))
            active = (up * below).astype(jnp.bfloat16)
            slope = below + up * (jnp.exp(-0.5 * up * up) * PDF_SCALE)
            active_ref[at(side, step), cols] = active
            slope_ref[at(side, step), cols] = slope.astype(jnp.bfloat16)
            part = dot_nn(active, w_out[cols])
            total = part if total is None else total + part
        return total

    def back_pass(side, step):
        grads = g_ref[at(side, step)]
        total = None
        for first in range(0, w_in.shape[1], CHUNK):
            cols = slice(first, first + CHUNK)
            active_grad = dot_nt(grads, w_out[cols])
            up_grad = active_grad * slope_ref[at(side, step), cols].astype(jnp.float32)
            up_grad = up_grad.astype(jnp.bfloat16)
            slope_ref[at(side, step), cols] = up_grad
            part = dot_nt(up_grad, w_in[:, cols])
            total = part if total is None else total + part
        return total

    keep_ref[at(0, 0)] = ahead_pass(0, 0)

    @pl.loop(1, chips)
    def _(step):
        go_x(step).wait_recv()
        pair_x(step).start()
        keep_ref[at(0, step)] = ahead_pass(0, step)

    pair_g(0).start()

    @pl.loop(0, chips)
    def _(step):
        pair_x(step).wait_recv()
        part_ref[at(0, step)] = ahead_pass(1, step).astype(part_ref.dtype)
        pair_y(step).start()

    @pl.loop(1, chips)
    def _(step):
        go_g(step).wait_recv()
        pair_g(step).start()

    @pl.loop(0, chips)
    def _(step):
        pair_y(step).wait_recv()
        here = at(0, step)
        total = keep_ref[here] + land_ref[here].astype(jnp.float32)
        home_ref[here] = total.astype(home_ref.dtype)

        @pl.when(step > 0)
        def _():
            home_y(step).start()

        @pl.when(step == 0)
        def _():
            result_ref[here] = total.astype(result_ref.dtype)

    @pl.loop(0, chips)
    def _(step):
        pair_g(step).wait_recv()

    @pl.loop(0, tensor)
    def _(part):
        for first in range(0, share, 128):
            cols = pl.ds(pl.multiple_of(part * share + first, 128), 128)
            grad_ref[part, first : first + 128] = dot_tn(active_ref[:, cols], g_ref[...]).astype(
                grad_ref.dtype
            )

    for step in range(1, tensor):
        line(step).start()

    @pl.loop(0, chips)
    def _(step):
        back_part[at(0, step)] = back_pass(1, step).astype(back_part.dtype)
        pair_d(step).start()

    @pl.loop(0, chips)
    def _(turn):
        step = chips - 1 - turn
        here = at(0, step)
        total = back_pass(0, step)
        pair_d(step).wait_recv()
        total = (total + back_land[here].astype(jnp.float32)).astype(back_home.dtype)
        back_home[here] = total

        @pl.when(step > 0)
        def _():
            home_d(step).start()

        @pl.when(step == 0)
        def _():
            back_ref[here] = total

    @pl.loop(0, w_in.shape[1] // BAND)
    def _(band):
        cols = pl.ds(pl.multiple_of(band * BAND, BAND), BAND)
        in_grad_ref[cols] = dot_tn(slope_ref[:, cols], x_ref[...]).astype(in_grad_ref.dtype)

    out_grad_ref[...] = grad_ref[place].astype(jnp.float32)
    for step in range(1, tensor):
        line_in(step).wait_recv()
        out_grad_ref[...] += grad_land[along(tensor - step)].astype(jnp.float32)
    for step in range(1, tensor):
        line(step).wait_send()

    @pl.loop(1, chips)
    def _(step):
        home_y(step).wait_recv()
        home_d(step).wait_recv()

    @pl.loop(0, chips)
    def _(step):
        pair_x(step).wait_send()
        pair_g(step).wait_send()
        pair_y(step).wait_send()
        pair_d(step).wait_send()

    @pl.loop(1, chips)
    def _(step):
        go_x(step).wait_send()
        go_g(step).wait_send()
        home_y(step).wait_send()
        home_d(step).wait_send()


def run_experts(slot_rows, slot_grads, w_in, w_out):
    dp, tensor = lax.axis_size("dp"), lax.axis_size("tensor")
    rows, width = slot_rows.shape
    hidden = w_in.shape[1]
    low = jnp.bfloat16
    here = pl.BlockSpec(memory_space=pltpu.VMEM)
    near = pltpu.VMEM((rows, width), low)
    both = pltpu.VMEM((2 * rows, width), low)
    middle = pltpu.VMEM((2 * rows, hidden), low)
    return pl.pallas_call(
        lambda *refs: expert_kernel(dp, tensor, *refs),
        out_shape=(
            jax.ShapeDtypeStruct((rows, width), low),
            jax.ShapeDtypeStruct((rows, width), low),
            jax.ShapeDtypeStruct((hidden, width), low),
            jax.ShapeDtypeStruct((hidden // tensor, width), jnp.float32),
        ),
        in_specs=[here] * 4,
        out_specs=[here] * 4,
        scratch_shapes=[
            both, both, middle, middle, pltpu.VMEM((rows, width), jnp.float32),
            near, near, near, near, near, near,
            pltpu.VMEM((tensor, hidden // tensor, width), low),
            pltpu.VMEM((tensor, hidden // tensor, width), low),
        ]
        + [pltpu.SemaphoreType.DMA((dp // 2,))] * 16
        + [pltpu.SemaphoreType.DMA((tensor,))] * 2,
        compiler_params=pltpu.CompilerParams(
            collective_id=4, has_side_effects=True, vmem_limit_bytes=60 << 20
        ),
        name="run_experts",
    )(slot_rows, slot_grads, w_in, w_out)


norm_eps = 1e-05
route_scale = 3.0
masked_score = -1e30
highest = lax.Precision.HIGHEST


def layer_norm(values, norm_gain):
    centred = values - jnp.mean(values, axis=-1, keepdims=True)
    spread = jnp.mean(centred * centred, axis=-1, keepdims=True)
    return centred * lax.rsqrt(spread + norm_eps) * norm_gain


def unit_rows(values):
    return values * lax.rsqrt(jnp.sum(values * values, axis=-1, keepdims=True) + 1.0)


def router_gate(normed, router_proj, expert_embed, picked):
    routed = jnp.dot(normed, router_proj, precision=highest)
    logits = route_scale * jnp.dot(unit_rows(routed), unit_rows(expert_embed).T, precision=highest)
    return jnp.sum(jax.nn.softmax(logits, axis=-1) * picked, axis=-1)


def gelu_exact(values):
    return jax.nn.gelu(values, approximate=False)


def slot_table(route_ids, order_ids, capacity):
    same_expert = route_ids[:, None] == route_ids[None, :]
    earlier = order_ids[None, :] < order_ids[:, None]
    ranking = jnp.sum(jnp.where(same_expert & earlier, 1, 0), axis=1).astype(jnp.int32)
    kept_mask = ranking < capacity
    column = route_ids * capacity + jnp.minimum(ranking, capacity - 1)
    return (column, kept_mask)


def low_dot(rows, weight):
    return jnp.dot(rows, weight, preferred_element_type=jnp.float32).astype(jnp.bfloat16)


def shards(
    tokens,
    norm1_gain,
    qkv_weight,
    attn_proj,
    norm2_gain,
    router_proj,
    expert_embed,
    expert_in,
    expert_out,
    routes,
    orders,
    leaf_parent,
    cotangent,
):
    rows_here = tokens.shape[0]
    model_width = tokens.shape[1]
    experts = expert_embed.shape[0]
    capacity = rows_here // experts
    dp_size, tensor_size = lax.axis_size("dp"), lax.axis_size("tensor")

    hidden = tokens.astype(jnp.float32)
    normed_in, norm1_back = jax.vjp(layer_norm, hidden, norm1_gain)
    own_in = normed_in.astype(jnp.bfloat16)
    flat_qkv = qkv_weight.reshape(qkv_weight.shape[0], -1)
    place = lax.axis_index("tensor")
    leaf_blocks = rows_here // BRANCH
    first_leaf = jnp.maximum(place - 2, 0) * leaf_blocks
    leaf_parents = lax.dynamic_slice_in_dim(leaf_parent[0], first_leaf, leaf_blocks, 0) - 1
    parents = (leaf_parents[:, None] == jnp.arange(leaf_blocks)[None, :]).astype(jnp.float32)
    parents = jnp.broadcast_to(parents.reshape(-1, 1), (leaf_blocks * leaf_blocks, model_width))
    seen_in, weights = share_rows_and_weights(
        own_in, jnp.concatenate([flat_qkv, attn_proj.T], axis=1), parents
    )
    query_weight, key_weight, value_weight, proj_back = weights
    query_rows = low_dot(own_in, query_weight)
    key_rows = low_dot(seen_in, key_weight)
    value_rows = low_dot(seen_in, value_weight)
    attended, log_totals = attend(place[None].astype(jnp.int32), query_rows, key_rows, value_rows)
    branch_out = jnp.einsum(
        "sc,dc->sd", attended, proj_back, preferred_element_type=jnp.float32
    )
    mid_stream = hidden + branch_out
    normed_mid, norm2_back = jax.vjp(layer_norm, mid_stream, norm2_gain)
    moe_in = normed_mid.astype(jnp.bfloat16)
    route_ids = routes[:, 0]
    near_route = (route_ids - lax.axis_index("dp") // 2) % experts
    column, kept_mask = slot_table(near_route, orders[0], capacity)
    picked = (route_ids[:, None] == jnp.arange(experts)[None, :]).astype(jnp.float32)
    gate_value, gate_back = jax.vjp(
        lambda normed_rows, route_proj, embed_rows: router_gate(
            normed_rows, route_proj, embed_rows, picked
        ),
        moe_in.astype(jnp.float32),
        router_proj,
        expert_embed,
    )
    select = (
        (column[:, None] == jnp.arange(experts * capacity)[None, :]) & kept_mask[:, None]
    ).astype(jnp.bfloat16)
    def to_slots(token_rows):
        return jnp.einsum(
            "ts,td->sd", select, token_rows, preferred_element_type=jnp.float32
        ).astype(jnp.bfloat16)

    def from_slots(slot_rows):
        return jnp.dot(select, slot_rows, preferred_element_type=jnp.float32)

    upstream = cotangent.astype(jnp.float32)
    slot_grads = to_slots((gate_value[:, None] * upstream).astype(jnp.bfloat16))
    result_rows, grad_rows, in_weight_grad, expert_out_grad = run_experts(
        to_slots(moe_in), slot_grads, expert_in, expert_out
    )
    expert_result = from_slots(result_rows)
    output = (mid_stream + gate_value[:, None] * expert_result).astype(jnp.bfloat16)
    moe_grad = from_slots(grad_rows)
    gate_grad = jnp.sum(upstream * expert_result, axis=-1)
    router_part, proj_grad, embed_grad = gate_back(gate_grad)
    mid_part, gain2_grad = norm2_back(moe_grad + router_part)
    mid_grad = upstream + mid_part
    expert_in_grad = (
        lax.psum_scatter(in_weight_grad, "tensor", scatter_dimension=0, tiled=True)
        .astype(jnp.float32)
        .T
    )
    branch_grad = mid_grad.astype(jnp.bfloat16)
    later = [gain2_grad, proj_grad, embed_grad]
    flat = jnp.concatenate([jnp.zeros_like(norm1_gain)] + [part.reshape(-1) for part in later])
    ways = dp_size * tensor_size
    lanes = -(-flat.shape[0] // (ways * 8 * 128)) * 128
    small = jnp.pad(flat, (0, ways * 8 * lanes - flat.shape[0])).reshape(ways, 8, lanes)
    input_grad, grad_block, totals = backward(
        parents, query_rows, key_rows, value_rows, attended, branch_grad, seen_in, weights,
        log_totals, small,
    )
    qkv_grad = grad_block[:, : flat_qkv.shape[1]].reshape(qkv_weight.shape)
    attn_proj_grad = grad_block[:, flat_qkv.shape[1] :].T
    totals = totals.reshape(-1)
    gain1_sum = totals[:model_width] / norm1_gain
    gain2_sum, router_sum, embed_sum = (
        totals[first : first + part.size].reshape(part.shape)
        for first, part in zip(
            (model_width, 2 * model_width, 2 * model_width + proj_grad.size), later
        )
    )
    token_part, _ = norm1_back(input_grad)
    token_grad = mid_grad + token_part
    return (
        output,
        token_grad,
        gain1_sum,
        qkv_grad,
        attn_proj_grad,
        gain2_sum,
        router_sum,
        embed_sum,
        expert_in_grad,
        expert_out_grad,
    )


def solution(mesh):
    in_specs = (
        P(("dp", "tensor"), None),
        P(),
        P("dp", None, "tensor"),
        P("tensor", "dp"),
        P(),
        P(),
        P(),
        P(None, "dp"),
        P("dp", None),
        P(("dp", "tensor"), None),
        P(("dp", "tensor"), None),
        P("dp", None),
        P(("dp", "tensor"), None),
    )
    out_specs = (
        P(("dp", "tensor"), None),
        P(("dp", "tensor"), None),
        P(),
        P("dp", None, "tensor"),
        P("tensor", "dp"),
        P(),
        P(),
        P(),
        P(None, ("dp", "tensor")),
        P(("dp", "tensor"), None),
    )
    return jax.shard_map(shards, mesh=mesh, in_specs=in_specs, out_specs=out_specs, check_vma=False)
```

```python
import functools
import math

import jax
import jax.numpy as jnp
from jax import lax
from jax.experimental import pallas as pl
from jax.experimental.pallas import tpu as pltpu
from jax.sharding import PartitionSpec as P

HEAD_DIM = 64
TRUNK = 1024
BRANCH = 256
MASKED = -1e30
LOG2E = math.log2(math.e)
EXP_SCALE = HEAD_DIM ** (-0.5) * LOG2E

NT = (((1,), (1,)), ((), ()))
NN = (((1,), (0,)), ((), ()))


def dot_nt(a, b):
    return lax.dot_general(a, b, NT, preferred_element_type=jnp.float32)


def dot_nn(a, b):
    return lax.dot_general(a, b, NN, preferred_element_type=jnp.float32)


def head_lanes(shape, dim, head):
    return lax.broadcasted_iota(jnp.int32, shape, dim) // HEAD_DIM == head


MESH = pl.DeviceIdType.MESH
PIECE = 64


def greet(peers):
    barrier = pltpu.get_barrier_semaphore()
    for peer in peers:
        pl.semaphore_signal(barrier, inc=1, device_id=peer, device_id_type=MESH)
    pl.semaphore_wait(barrier, len(peers))


def front_kernel(
    dp, tensor, depth, own_ref, block_ref, parent_ref,
    seen_out, weight_out, q_out, k_out, v_out, o_out, lse_ref,
    seen_ref, land_ref, weight_ref, q_ref, k_ref, v_ref, o_ref, acc_ref, top_ref, spare_ref,
    row_send, row_recv, line_send, line_recv, chip_send, chip_recv, pair_send, pair_recv, save_sem,
):
    spot, place = lax.axis_index("dp"), lax.axis_index("tensor")
    chip, core = spot // 2, lax.rem(spot, 2)
    chips = dp // 2
    rows, width = own_ref.shape
    pieces = rows // PIECE
    pairs = width // 128
    blocks = rows // BRANCH
    share = width // tensor
    partner = (chip * 2 + 1 - core, place)

    def along(step):
        return lax.rem(place + step, tensor)

    def chip_at(step):
        return lax.rem(chip + step, chips)

    greet(
        [(spot, along(step)) for step in range(1, tensor)]
        + [(chip_at(step) * 2 + core, place) for step in range(1, chips)]
        + [partner]
    )

    def pass_on(piece, fresh):
        at = pl.ds(pl.multiple_of(piece * PIECE, PIECE), PIECE)
        source = seen_ref.at[at]
        if fresh:
            here = lax.rem(piece, pieces) * PIECE
            source = own_ref.at[pl.ds(pl.multiple_of(here, PIECE), PIECE)]
        return pltpu.make_async_remote_copy(
            src_ref=source, dst_ref=seen_ref.at[at],
            send_sem=row_send.at[piece], recv_sem=row_recv.at[piece],
            device_id=(spot, lax.rem(place + 1, tensor)), device_id_type=MESH,
        )

    def line(step):
        return pltpu.make_async_remote_copy(
            src_ref=block_ref, dst_ref=land_ref.at[place, spot],
            send_sem=line_send.at[step], recv_sem=line_recv.at[place],
            device_id=(spot, along(step)), device_id_type=MESH,
        )

    def line_in(step):
        source = along(tensor - step)
        return pltpu.make_async_remote_copy(
            src_ref=block_ref, dst_ref=land_ref.at[source, spot],
            send_sem=line_send.at[step], recv_sem=line_recv.at[source],
            device_id=(spot, along(step)), device_id_type=MESH,
        )

    def plane(part, step):
        block = land_ref.at[part, spot]
        return pltpu.make_async_remote_copy(
            src_ref=block, dst_ref=block,
            send_sem=chip_send.at[part, step], recv_sem=chip_recv.at[part, chip],
            device_id=(chip_at(step) * 2 + core, place), device_id_type=MESH,
        )

    def plane_in(part, step):
        source = chip_at(chips - step)
        block = land_ref.at[part, source * 2 + core]
        return pltpu.make_async_remote_copy(
            src_ref=block, dst_ref=block,
            send_sem=chip_send.at[part, step], recv_sem=chip_recv.at[part, source],
            device_id=(chip_at(step) * 2 + core, place), device_id_type=MESH,
        )

    def across(part, source, source_core):
        block = land_ref.at[part, source * 2 + source_core]
        return pltpu.make_async_remote_copy(
            src_ref=block, dst_ref=block,
            send_sem=pair_send.at[part, source], recv_sem=pair_recv.at[part, source],
            device_id=partner, device_id_type=MESH,
        )

    for step in range(1, tensor):
        line(step).start()

    @pl.when(place == 0)
    def _():
        @pl.loop(0, pieces)
        def _(piece):
            pass_on(piece, True).start()

    land_ref[place, spot] = block_ref[...]
    seen_ref[2 * rows :] = own_ref[...]

    @pl.when(place < 2)
    def _():
        seen_ref[rows : 2 * rows] = own_ref[...]

    @pl.when(place == 0)
    def _():
        seen_ref[0:rows] = own_ref[...]

    def serve(first, last):
        @pl.loop(first, last)
        def _(piece):
            trunk = piece < pieces
            takes = (place > 1) | ((place > 0) & trunk)

            @pl.when(takes)
            def _():
                pass_on(piece, False).wait_recv()

                @pl.when(place < tensor - 1)
                def _():
                    pass_on(piece, False).start()

            @pl.when((place == 1) & jnp.logical_not(trunk))
            def _():
                pass_on(piece, True).start()

    def part_of(index):
        return pl.ds(index * rows, rows)

    saves = [
        pltpu.make_async_copy(source, target, save_sem.at[index])
        for index, (source, target) in enumerate(
            [(weight_ref, weight_out), (q_ref, q_out), (o_ref, o_out)]
            + [
                (held.at[part_of(part)], target.at[part_of(part)])
                for part in (2, 0, 1)
                for held, target in ((seen_ref, seen_out), (k_ref, k_out), (v_ref, v_out))
            ]
        )
    ]

    serve(0, pieces // 4)
    for step in range(tensor):
        part = along(tensor - step)
        if step:
            line_in(step).wait_recv()

        @pl.loop(1, chips)
        def _(hop):
            plane(part, hop).start()

        across(part, chip, core).start()
    serve(pieces // 4, pieces // 2)
    for step in range(tensor):
        part = along(tensor - step)

        @pl.loop(1, chips)
        def _(hop):
            plane_in(part, hop).wait_recv()
            across(part, chip_at(chips - hop), core).start()

    for part in range(tensor):

        @pl.loop(0, chips)
        def _(source):
            across(part, source, 1 - core).wait_recv()

    def ordered(source, kind):
        cols = slice(kind * share, (kind + 1) * share)
        return jnp.concatenate(
            [land_ref[part, source][:, cols] for part in range(tensor)], axis=1
        )

    if depth % 16:
        for kind in range(4):
            for source in range(dp):
                spare_ref[source * depth : (source + 1) * depth] = ordered(source, kind)[
                    0:depth
                ].astype(jnp.float32)
            weight_ref[kind] = spare_ref[...].astype(weight_ref.dtype)
    else:

        @pl.loop(0, dp)
        def _(source):
            at = pl.ds(pl.multiple_of(source * depth, depth), depth)
            for kind in range(4):
                weight_ref[kind, at] = ordered(source, kind)

    saves[0].start()

    def lanes(pair):
        return pl.ds(pl.multiple_of(pair * 128, 128), 128)

    def project(first, also_queries=False):
        @pl.loop(0, blocks)
        def _(b):
            at = pl.ds(pl.multiple_of(first + b * BRANCH, BRANCH), BRANCH)
            normed = seen_ref[at]
            k_ref[at] = dot_nn(normed, weight_ref[1]).astype(k_ref.dtype)
            v_ref[at] = dot_nn(normed, weight_ref[2]).astype(v_ref.dtype)
            if also_queries:
                here = pl.ds(pl.multiple_of(b * BRANCH, BRANCH), BRANCH)
                q_ref[here] = dot_nn(normed, weight_ref[0]).astype(q_ref.dtype)

    def attend_tiles(pair, tiles_of, opening):
        values, work = {}, [(block, head) for block in range(blocks) for head in range(2)]

        def value_tile(first, head):
            if (first, head) not in values:
                flipped = v_ref[first : first + BRANCH, lanes(pair)].T
                for side in range(2):
                    values[first, side] = jnp.where(
                        head_lanes(flipped.shape, 0, side), flipped, jnp.ones_like(flipped)
                    )
            return values[first, head]

        def start(block, head):
            queries = q_ref[block * BRANCH : (block + 1) * BRANCH, lanes(pair)]
            queries = jnp.where(
                head_lanes(queries.shape, 1, head), queries, jnp.zeros_like(queries)
            )
            scores = []
            for first, masked in tiles_of(block):
                tile = dot_nt(k_ref[first : first + BRANCH, lanes(pair)], queries)
                if masked:
                    keys = lax.broadcasted_iota(jnp.int32, tile.shape, 0)
                    at = lax.broadcasted_iota(jnp.int32, tile.shape, 1)
                    tile = jnp.where(keys <= at, tile, MASKED)
                scores.append(tile)
            top = jnp.max(functools.reduce(jnp.maximum, scores), axis=0, keepdims=True)
            return scores, top

        def middle(block, head, scores, top):
            cols = slice(block * BRANCH, (block + 1) * BRANCH)
            fade = None
            if not opening:
                before = top_ref[pair, head : head + 1, cols]
                top = jnp.maximum(before, top)
                fade = jnp.exp2((before - top) * EXP_SCALE)
            top_ref[pair, head : head + 1, cols] = top
            shift = top * EXP_SCALE
            return [
                jnp.exp2(tile * EXP_SCALE - shift).astype(jnp.bfloat16) for tile in scores
            ], fade

        def finish(block, head, probs, fade):
            cols = slice(block * BRANCH, (block + 1) * BRANCH)
            acc = None if opening else acc_ref[pair, head, :, cols] * fade
            for (first, _), tile in zip(tiles_of(block), probs):
                part = dot_nn(value_tile(first, head), tile)
                acc = part if acc is None else acc + part
            acc_ref[pair, head, :, cols] = acc

        ready, held = start(*work[0]), None
        for at, item in enumerate(work):
            now = ready
            if at + 1 < len(work):
                ready = start(*work[at + 1])
            done = middle(*item, *now)
            if held is not None:
                finish(*held)
            held = (*item, *done)
        finish(*held)

    project(2 * rows, True)
    for index in (1, 3, 4, 5):
        saves[index].start()
    serve(pieces // 2, (3 * pieces) // 4)

    @pl.loop(0, pairs)
    def _(pair):
        @pl.when(place == 0)
        def _():
            attend_tiles(
                pair,
                lambda block: [
                    (2 * rows + j * BRANCH, j == block) for j in range(block + 1)
                ],
                True,
            )

        @pl.when(place > 0)
        def _():
            attend_tiles(pair, lambda block: [(2 * rows + block * BRANCH, True)], True)

    serve((3 * pieces) // 4, pieces)
    project(0)
    for index in (6, 7, 8):
        saves[index].start()
    per_pair = -(-pieces // pairs)

    @pl.loop(0, pairs)
    def _(pair):
        @pl.when(place > 0)
        def _():
            attend_tiles(pair, lambda block: [(j * BRANCH, False) for j in range(blocks)], False)

        first = pieces + pair * per_pair
        serve(jnp.minimum(first, 2 * pieces), jnp.minimum(first + per_pair, 2 * pieces))

    @pl.when((place > 0) & (place < tensor - 1))
    def _():
        @pl.loop(0, 2 * pieces)
        def _(piece):
            pass_on(piece, False).wait_send()

    @pl.when(place > 1)
    def _():
        branches = [
            seen_ref[rows + branch * BRANCH : rows + (branch + 1) * BRANCH]
            for branch in range(blocks)
        ]
        for leaf in range(blocks):
            chosen = None
            for branch in range(blocks):
                at = leaf * blocks + branch
                part = branches[branch] * parent_ref[at : at + 1].astype(own_ref.dtype)
                chosen = part if chosen is None else chosen + part
            o_ref[leaf * BRANCH : (leaf + 1) * BRANCH] = chosen
        seen_ref[rows : 2 * rows] = o_ref[...]

    project(rows)
    for index in (9, 10, 11):
        saves[index].start()

    @pl.loop(0, pairs)
    def _(pair):
        @pl.when(place > 1)
        def _():
            attend_tiles(pair, lambda block: [(rows + block * BRANCH, False)], False)

        outs = []
        for head in range(2):
            mine, other = head * HEAD_DIM, (1 - head) * HEAD_DIM
            total = acc_ref[pair, head, other : other + 1]
            outs.append(acc_ref[pair, head, mine : mine + HEAD_DIM] / total)
            lse_ref[pair, head : head + 1] = (
                top_ref[pair, head : head + 1] * EXP_SCALE + jnp.log2(total)
            )
        o_ref[:, lanes(pair)] = jnp.concatenate(outs, axis=0).T.astype(o_ref.dtype)

    saves[2].start()
    for part in range(tensor):

        @pl.loop(0, chips)
        def _(source):
            across(part, source, core).wait_send()

        @pl.loop(1, chips)
        def _(hop):
            plane(part, hop).wait_send()

    for step in range(1, tensor):
        line(step).wait_send()

    @pl.when(place == 0)
    def _():
        @pl.loop(0, pieces)
        def _(piece):
            pass_on(piece, True).wait_send()

    for save in saves:
        save.wait()


def front(own, block, parents):
    dp, tensor = lax.axis_size("dp"), lax.axis_size("tensor")
    rows, width = own.shape
    depth, cols = block.shape
    pieces, chips, pairs = rows // PIECE, dp // 2, width // 128
    padded = -(-depth // 16) * 16
    block = jnp.pad(block, ((0, padded - depth), (0, 0)))
    low, full = jnp.bfloat16, jnp.float32
    few, many = (rows, width), (3 * rows, width)
    weights = (4, width, width)
    dma = pltpu.SemaphoreType.DMA
    here = pl.BlockSpec(memory_space=pltpu.VMEM)
    anywhere = pl.BlockSpec(memory_space=pl.ANY)
    return pl.pallas_call(
        lambda *refs: front_kernel(dp, tensor, depth, *refs),
        out_shape=tuple(
            jax.ShapeDtypeStruct(shape, low) for shape in (many, weights, few, many, many, few)
        )
        + (jax.ShapeDtypeStruct((pairs, 2, rows), full),),
        in_specs=[here, here, here],
        out_specs=[anywhere] * 6 + [here],
        scratch_shapes=[
            pltpu.VMEM(many, low),
            pltpu.VMEM((tensor, dp, padded, cols), low),
            pltpu.VMEM(weights, low),
            pltpu.VMEM(few, low),
            pltpu.VMEM(many, low),
            pltpu.VMEM(many, low),
            pltpu.VMEM(few, low),
            pltpu.VMEM((pairs, 2, 128, rows), full),
            pltpu.VMEM((pairs, 2, rows), full),
            pltpu.VMEM((width, width) if depth % 16 else (8, 128), full),
            dma((2 * pieces,)), dma((2 * pieces,)),
            dma((tensor,)), dma((tensor,)),
            dma((tensor, chips)), dma((tensor, chips)),
            dma((tensor, chips)), dma((tensor, chips)),
            dma((12,)),
        ],
        compiler_params=pltpu.CompilerParams(
            collective_id=2, has_side_effects=True, vmem_limit_bytes=58 << 20
        ),
        name="front",
    )(own, block, parents)


TN = (((0,), (0,)), ((), ()))
GROUP = 256


def dot_tn(a, b):
    return lax.dot_general(a, b, TN, preferred_element_type=jnp.float32)


def back_kernel(
    dp, tensor, depth,
    parent_ref, q_in, k_in, v_in, o_in, grad_in, seen_in, weight_in, lse_ref, small_ref,
    out_ref, sum_ref, total_ref,
    q_ref, k_ref, v_ref, o_ref, bg_ref, g_ref, stage_ref, seen_ref, weight_ref,
    delta_ref, dqt_ref, rows_ref, land_ref, gain_ref,
    slab_ref, pair_land, chip_land, line_out, line_land, part_ref, part_land,
    load_sem, pair_sem, stage_sem, row_send, row_recv,
    pair_send, pair_recv, chip_send, chip_recv,
    line_send, line_recv, small_send, small_recv, spread_send, spread_recv,
):
    spot, place = lax.axis_index("dp"), lax.axis_index("tensor")
    ways = dp * tensor
    me = spot * tensor + place
    scale = HEAD_DIM ** (-0.5)
    rows, width = q_ref.shape
    pairs = width // 128
    groups = width // GROUP
    blocks = rows // BRANCH
    pieces = rows // PIECE
    stage_rows = stage_ref.shape[1]

    def device(index):
        return (index // tensor, lax.rem(index, tensor))

    def along(step):
        return lax.rem(place + step, tensor)

    chips = dp // 2
    chip, core = spot // 2, lax.rem(spot, 2)

    def chip_at(step):
        return lax.rem(chip + step, chips)

    def block_at(b):
        return pl.ds(pl.multiple_of(b * BRANCH, BRANCH), BRANCH)

    barrier = pltpu.get_barrier_semaphore()

    @pl.loop(1, ways)
    def _(step):
        pl.semaphore_signal(
            barrier, inc=1, device_id=device(lax.rem(me + step, ways)), device_id_type=MESH
        )

    def lanes(pair):
        return pl.ds(pl.multiple_of(pair * 128, 128), 128)

    grad_load = pltpu.make_async_copy(grad_in, bg_ref, load_sem.at[0])
    weight_load = pltpu.make_async_copy(weight_in, weight_ref, load_sem.at[1])
    value_load = pltpu.make_async_copy(o_in, o_ref, load_sem.at[2])

    def pair_loads(pair):
        return [
            pltpu.make_async_copy(
                source.at[:, lanes(pair)], held.at[:, lanes(pair)], pair_sem.at[which, pair]
            )
            for which, (source, held) in enumerate(((q_in, q_ref), (k_in, k_ref), (v_in, v_ref)))
        ]

    def stage(part):
        slot = lax.rem(part, 2)
        at = pl.ds(pl.multiple_of(part * stage_rows, stage_rows), stage_rows)
        return pltpu.make_async_copy(seen_in.at[at], stage_ref.at[slot], stage_sem.at[slot])

    grad_load.start()
    weight_load.start()
    value_load.start()

    @pl.loop(0, pairs)
    def _(pair):
        for load in pair_loads(pair):
            load.start()

    grad_load.wait()
    weight_load.wait()
    value_load.wait()

    def keep(held, value, kind):
        cols = slice(kind * GROUP, (kind + 1) * GROUP)
        if depth % 16:
            for target in range(dp):
                held[target, 0:depth, cols] = value[target * depth : (target + 1) * depth].astype(
                    slab_ref.dtype
                )
        else:
            held[:, :, cols] = value.reshape(dp, depth, GROUP).astype(slab_ref.dtype)

    for group in range(groups):
        cols = slice(group * GROUP, (group + 1) * GROUP)
        keep(slab_ref.at[groups], dot_tn(bg_ref[...], o_ref[:, cols]), group)

    @pl.loop(0, blocks)
    def _(b):
        at = block_at(b)
        g_ref[at] = dot_nn(bg_ref[at], weight_ref[3]).astype(g_ref.dtype)

    pl.semaphore_wait(barrier, ways - 1)

    def halve(group, source):
        return pltpu.make_async_remote_copy(
            src_ref=slab_ref.at[group, source * 2 + 1 - core],
            dst_ref=pair_land.at[group, source],
            send_sem=pair_send.at[group, source], recv_sem=pair_recv.at[group, source],
            device_id=(chip * 2 + 1 - core, place), device_id_type=MESH,
        )

    def give(group, step):
        to = chip_at(step) * 2 + core
        return pltpu.make_async_remote_copy(
            src_ref=slab_ref.at[group, to], dst_ref=chip_land.at[group, chip],
            send_sem=chip_send.at[group, step], recv_sem=chip_recv.at[group, chip],
            device_id=(to, place), device_id_type=MESH,
        )

    def take(group, step):
        source = chip_at(chips - step)
        return pltpu.make_async_remote_copy(
            src_ref=slab_ref.at[group, source * 2 + core], dst_ref=chip_land.at[group, source],
            send_sem=chip_send.at[group, step], recv_sem=chip_recv.at[group, source],
            device_id=(chip_at(step) * 2 + core, place), device_id_type=MESH,
        )

    def share_slabs(group):
        @pl.loop(0, chips)
        def _(source):
            halve(group, source).start()

    def send_slabs(group):
        @pl.loop(0, chips)
        def _(step):
            to = chip_at(step)
            halve(group, to).wait_recv()
            mine = slab_ref[group, to * 2 + core].astype(jnp.float32)
            mine = mine + pair_land[group, to].astype(jnp.float32)
            slab_ref[group, to * 2 + core] = mine.astype(slab_ref.dtype)

            @pl.when(step > 0)
            def _():
                give(group, step).start()

    share_slabs(groups)

    @pl.loop(0, pairs)
    def _(pair):
        for load in pair_loads(pair):
            load.wait()
        product = g_ref[:, lanes(pair)].astype(jnp.float32)
        product = (product * o_ref[:, lanes(pair)].astype(jnp.float32)).T
        for head in range(2):
            delta_ref[pair, head : head + 1, :] = jnp.sum(
                product[head * HEAD_DIM : (head + 1) * HEAD_DIM], axis=0, keepdims=True
            )
        dqt_ref[pair] = jnp.zeros(dqt_ref.shape[1:], dqt_ref.dtype)

    def sweep(pair, tiles):
        work = [(tile, head) for tile in range(len(tiles)) for head in range(2)]
        sums = [[None, None] for _ in tiles]
        keys, flipped = {}, {}

        def key_block(tile):
            row = tiles[tile][0]
            if id(row) not in keys:
                kb = k_ref[pl.ds(row, BRANCH), lanes(pair)]
                vb = v_ref[pl.ds(row, BRANCH), lanes(pair)]
                masked = []
                for head in range(2):
                    mine = head_lanes(kb.shape, 1, head)
                    masked.append(
                        (
                            jnp.where(mine, kb, jnp.zeros_like(kb)),
                            jnp.where(mine, vb, jnp.zeros_like(vb)),
                        )
                    )
                keys[id(row)] = masked
                flipped[id(row)] = kb.T
            return keys[id(row)], flipped[id(row)]

        def start(tile, head):
            at = pl.ds(tiles[tile][1], BRANCH)
            kb, vb = key_block(tile)[0][head]
            return dot_nt(kb, q_ref[at, lanes(pair)]), dot_nt(vb, g_ref[at, lanes(pair)])

        def middle(tile, head, scores, prob_grad):
            at = pl.ds(tiles[tile][1], BRANCH)
            probs = jnp.exp2(scores * EXP_SCALE - lse_ref[pair, head : head + 1, at])
            if tiles[tile][2] is not None:
                probs = tiles[tile][2](probs)
            score_grad = probs * (prob_grad - delta_ref[pair, head : head + 1, at])
            return probs.astype(jnp.bfloat16), score_grad.astype(jnp.bfloat16)

        def finish(tile, head, probs, score_grad):
            at = pl.ds(tiles[tile][1], BRANCH)
            parts = (
                dot_nn(score_grad, q_ref[at, lanes(pair)]),
                dot_nn(probs, g_ref[at, lanes(pair)]),
            )
            for which in range(2):
                held = sums[tile][which]
                if head == 0:
                    sums[tile][which] = parts[which]
                else:
                    first = head_lanes(held.shape, 1, 0)
                    sums[tile][which] = jnp.where(first, held, parts[which])
            mine = slice(head * HEAD_DIM, (head + 1) * HEAD_DIM)
            dqt_ref[pair, mine, at] += dot_nn(key_block(tile)[1][mine], score_grad)

        ready = start(*work[0])
        held = None
        for at, item in enumerate(work):
            now = ready
            if at + 1 < len(work):
                ready = start(*work[at + 1])
            done = middle(*item, *now)
            if held is not None:
                finish(*held)
            held = (*item, *done)
        finish(*held)
        return sums

    def causal(key_row, query_row):
        def mask_of(probs):
            keys = lax.broadcasted_iota(jnp.int32, probs.shape, 0) + key_row
            at = lax.broadcasted_iota(jnp.int32, probs.shape, 1) + query_row
            return jnp.where(keys <= at, probs, 0.0)

        return mask_of

    def put(pair, row, dk, dv):
        at = pl.ds(row, BRANCH)
        k_ref[at, lanes(pair)] = (dk * scale).astype(k_ref.dtype)
        v_ref[at, lanes(pair)] = dv.astype(v_ref.dtype)

    def pass_down(piece):
        at = pl.ds(pl.multiple_of(piece * PIECE, PIECE), PIECE)
        return pltpu.make_async_remote_copy(
            src_ref=rows_ref.at[at], dst_ref=land_ref.at[at],
            send_sem=row_send.at[piece], recv_sem=row_recv.at[piece],
            device_id=(spot, lax.rem(place + tensor - 1, tensor)), device_id_type=MESH,
        )

    def row_grad(b):
        at = block_at(b)
        return dot_nt(k_ref[at], weight_ref[1]) + dot_nt(v_ref[at], weight_ref[2])

    def hand_down(b, total):
        rows_ref[block_at(b)] = total.astype(rows_ref.dtype)

        @pl.when(place == tensor - 1)
        def _():
            for piece in range(BRANCH // PIECE):
                pass_down(b * (BRANCH // PIECE) + piece).start()

    def joined(piece):
        at = pl.ds(pl.multiple_of(piece * PIECE, PIECE), PIECE)
        return rows_ref[at].astype(jnp.float32) + land_ref[at].astype(jnp.float32)

    middle_place = (place > 0) & (place < tensor - 1)
    late = 3 * jnp.maximum(tensor - 2 - place, 0)
    first_relay = jnp.where(place > 1, 0, pieces)
    last_relay = jnp.where(middle_place, 2 * pieces, first_relay)

    def piece_of(order):
        return lax.rem(order + pieces, 2 * pieces)

    def serve(first, last):
        def one(order, carry):
            piece = piece_of(order)
            pass_down(piece).wait_recv()
            at = pl.ds(pl.multiple_of(piece * PIECE, PIECE), PIECE)
            rows_ref[at] = joined(piece).astype(rows_ref.dtype)
            pass_down(piece).start()
            return carry

        low = jnp.clip(first - late, first_relay, last_relay)
        lax.fori_loop(low, jnp.clip(last - late, low, last_relay), one, 0)

    @pl.loop(0, pairs)
    def _(pair):
        @pl.when(place == 0)
        def _():
            for ref in (k_ref, v_ref):
                ref[rows : 3 * rows, lanes(pair)] = jnp.zeros((2 * rows, 128), ref.dtype)

        @pl.when(place > 0)
        def _():
            def seen_parent(probs):
                return jnp.where(place > 1, probs, 0.0)

            spots = range(0, rows, BRANCH)
            sums = sweep(pair, [(rows + at, at, seen_parent) for at in spots])
            for at, part in zip(spots, sums):
                put(pair, rows + at, *part)

    send_slabs(groups)

    @pl.loop(0, blocks)
    def _(leaf):
        out_ref[block_at(leaf)] = row_grad(blocks + leaf)

    for branch in range(blocks):
        total = None
        for leaf in range(blocks):
            at = leaf * blocks + branch
            part = out_ref[leaf * BRANCH : (leaf + 1) * BRANCH] * parent_ref[at : at + 1]
            total = part if total is None else total + part
        hand_down(blocks + branch, total)

    stage(0).start()

    @pl.loop(0, blocks)
    def _(b):
        row = pl.multiple_of(b * BRANCH, BRANCH)

        @pl.loop(0, pairs)
        def _(pair):
            def finish_block(masked):
                tiles = [
                    (row, first, causal(row, first) if masked else None)
                    for first in range(0, rows, BRANCH)
                ]
                sums = sweep(pair, tiles)
                put(pair, row, sum(part[0] for part in sums), sum(part[1] for part in sums))

            @pl.when(place == 0)
            def _():
                finish_block(True)

            @pl.when(place > 0)
            def _():
                finish_block(False)

            slot = b * pairs + pair
            serve(slot - 1, slot)

        for _half in range(2):
            part = b * 2 + _half

            @pl.when(part < 3 * rows // stage_rows)
            def _():
                stage(part).wait()

                @pl.when(part + 1 < 3 * rows // stage_rows)
                def _():
                    stage(part + 1).start()

                at = pl.ds(pl.multiple_of(part * stage_rows, stage_rows), stage_rows)
                seen_ref[:, at] = stage_ref[lax.rem(part, 2)].T

        hand_down(b, row_grad(b))

    served = blocks * pairs - 1

    gain_ref[...] = jnp.zeros_like(gain_ref)

    @pl.loop(0, groups)
    def _(group):
        base = served + group * 4

        @pl.loop(0, 2)
        def _(half):
            pair = group * 2 + half

            @pl.when(place > 0)
            def _():
                spots = range(0, rows, BRANCH)
                sums = sweep(pair, [(2 * rows + at, at, causal(0, 0)) for at in spots])
                for at, part in zip(spots, sums):
                    put(pair, 2 * rows + at, *part)

            q_ref[:, lanes(pair)] = (dqt_ref[pair] * scale).T.astype(q_ref.dtype)
            serve(base + half, base + half + 1)

        cols = pl.ds(pl.multiple_of(group * GROUP, GROUP), GROUP)
        for kind, value in (
            (0, lambda: dot_nn(seen_ref[:, 2 * rows : 3 * rows], q_ref[:, cols])),
            (1, lambda: dot_nn(seen_ref[...], k_ref[:, cols])),
            (2, lambda: dot_nn(seen_ref[...], v_ref[:, cols])),
        ):
            product = value()
            scaled = product * weight_ref[kind, :, cols].astype(jnp.float32)
            gain_ref[...] += scaled[:, 0:128] + scaled[:, 128:256]
            keep(slab_ref.at[group], product, kind)
            if kind:
                serve(base + 1 + kind, base + 2 + kind)

        share_slabs(group)

        @pl.when(group > 0)
        def _():
            send_slabs(group - 1)

    served += groups * 4

    part_ref[...] = small_ref[...]
    gains = jnp.sum(gain_ref[...].T, axis=0, keepdims=True)
    for row in range(width // 128):
        part_ref[0, row : row + 1, :] = gains[:, row * 128 : (row + 1) * 128]

    def scatter(step):
        to = lax.rem(me + step, ways)
        return pltpu.make_async_remote_copy(
            src_ref=part_ref.at[to], dst_ref=part_land.at[me],
            send_sem=small_send.at[step], recv_sem=small_recv.at[me],
            device_id=device(to), device_id_type=MESH,
        )

    def arrival(step):
        source = lax.rem(me - step + ways, ways)
        return pltpu.make_async_remote_copy(
            src_ref=part_ref.at[source], dst_ref=part_land.at[source],
            send_sem=small_send.at[step], recv_sem=small_recv.at[source],
            device_id=device(lax.rem(me + step, ways)), device_id_type=MESH,
        )

    def spread(step):
        return pltpu.make_async_remote_copy(
            src_ref=total_ref.at[me], dst_ref=total_ref.at[me],
            send_sem=spread_send.at[step], recv_sem=spread_recv.at[me],
            device_id=device(lax.rem(me + step, ways)), device_id_type=MESH,
        )

    def landing(step):
        source = lax.rem(me - step + ways, ways)
        return pltpu.make_async_remote_copy(
            src_ref=total_ref.at[source], dst_ref=total_ref.at[source],
            send_sem=spread_send.at[step], recv_sem=spread_recv.at[source],
            device_id=device(lax.rem(me + step, ways)), device_id_type=MESH,
        )

    @pl.loop(1, ways)
    def _(step):
        scatter(step).start()

    send_slabs(groups - 1)

    @pl.loop(0, blocks)
    def _(b):
        at = block_at(b)
        out_ref[at] = row_grad(2 * blocks + b) + dot_nt(q_ref[at], weight_ref[0])
        serve(served + 2 * b, served + 2 * b + 2)

    served += 2 * blocks

    def add(step, total):
        arrival(step).wait_recv()
        return total + part_land[lax.rem(me - step + ways, ways)]

    total_ref[me] = lax.fori_loop(1, ways, add, part_ref[me])

    @pl.loop(1, ways)
    def _(step):
        spread(step).start()

    serve(served, jnp.maximum(served, 2 * pieces) + late)

    kinds = [[], [], [], []]
    for group in range(groups + 1):

        def add_slab(step, total):
            take(group, step).wait_recv()
            return total + chip_land[group, chip_at(chips - step)].astype(jnp.float32)

        total = lax.fori_loop(1, chips, add_slab, slab_ref[group, spot].astype(jnp.float32))
        for part in range(total.shape[1] // GROUP):
            kinds[3 if group == groups else part].append(
                total[:, part * GROUP : (part + 1) * GROUP]
            )

    share = width // tensor
    kinds = [jnp.concatenate(parts, axis=1) for parts in kinds]
    for target in range(tensor):
        mine = jnp.concatenate(
            [kind[:, target * share : (target + 1) * share] for kind in kinds], axis=1
        )
        line_out[target] = mine.astype(line_out.dtype)

        @pl.when(place == target)
        def _():
            sum_ref[...] = mine

    def line(step):
        return pltpu.make_async_remote_copy(
            src_ref=line_out.at[along(step)], dst_ref=line_land.at[place],
            send_sem=line_send.at[step], recv_sem=line_recv.at[place],
            device_id=(spot, along(step)), device_id_type=MESH,
        )

    def line_in(step):
        source = along(tensor - step)
        return pltpu.make_async_remote_copy(
            src_ref=line_out.at[source], dst_ref=line_land.at[source],
            send_sem=line_send.at[step], recv_sem=line_recv.at[source],
            device_id=(spot, along(step)), device_id_type=MESH,
        )

    for step in range(1, tensor):
        line(step).start()

    @pl.when(place < 2)
    def _():
        @pl.loop(0, pieces)
        def _(piece):
            source = place * pieces + piece
            pass_down(source).wait_recv()
            at = pl.ds(pl.multiple_of(piece * PIECE, PIECE), PIECE)
            out_ref[at] += joined(source)

    for step in range(1, tensor):
        line_in(step).wait_recv()
        sum_ref[...] += line_land[along(tensor - step)].astype(jnp.float32)

    @pl.loop(1, ways)
    def _(step):
        landing(step).wait_recv()

    for step in range(1, tensor):
        line(step).wait_send()

    @pl.loop(1, ways)
    def _(step):
        scatter(step).wait_send()
        spread(step).wait_send()

    for group in range(groups + 1):

        @pl.loop(0, chips)
        def _(step):
            halve(group, step).wait_send()

            @pl.when(step > 0)
            def _():
                give(group, step).wait_send()

    sent = jnp.where(place == tensor - 1, 2 * pieces, last_relay)
    first_sent = jnp.where(place == tensor - 1, 0, first_relay)

    def sent_one(order, carry):
        pass_down(piece_of(order)).wait_send()
        return carry

    lax.fori_loop(first_sent, sent, sent_one, 0)


def backward(parents, q, k, v, o, branch_grad, seen, weights, lse, small):
    dp, tensor = lax.axis_size("dp"), lax.axis_size("tensor")
    ways = dp * tensor
    rows, width = q.shape
    seen_rows = k.shape[0]
    depth = width // dp
    padded = -(-depth // 16) * 16
    pairs, groups, pieces = width // 128, width // GROUP, rows // PIECE
    slab = (padded, width)
    low, full = jnp.bfloat16, jnp.float32
    dma = pltpu.SemaphoreType.DMA
    anywhere = pl.BlockSpec(memory_space=pl.ANY)
    here = pl.BlockSpec(memory_space=pltpu.VMEM)
    out, block, total = pl.pallas_call(
        lambda *refs: back_kernel(dp, tensor, depth, *refs),
        out_shape=(
            jax.ShapeDtypeStruct((rows, width), full),
            jax.ShapeDtypeStruct((padded, width), full),
            jax.ShapeDtypeStruct(small.shape, full),
        ),
        in_specs=[here] + [anywhere] * 7 + [here] * 2,
        out_specs=[here, here, here],
        scratch_shapes=[
            pltpu.VMEM((rows, width), low),
            pltpu.VMEM((seen_rows, width), low),
            pltpu.VMEM((seen_rows, width), low),
            pltpu.VMEM((rows, width), low),
            pltpu.VMEM((rows, width), low),
            pltpu.VMEM((rows, width), low),
            pltpu.VMEM((2, rows // 2, width), low),
            pltpu.VMEM((width, seen_rows), low),
            pltpu.VMEM(weights.shape, low),
            pltpu.VMEM((pairs, 2, rows), full),
            pltpu.VMEM((pairs, 128, rows), full),
            pltpu.VMEM((2 * rows, width), low),
            pltpu.VMEM((2 * rows, width), low),
            pltpu.VMEM((width, 128), full),
            pltpu.VMEM((groups + 1, dp) + slab, low),
            pltpu.VMEM((groups + 1, dp // 2) + slab, low),
            pltpu.VMEM((groups + 1, dp // 2) + slab, low),
            pltpu.VMEM((tensor, padded, width), low),
            pltpu.VMEM((tensor, padded, width), low),
            pltpu.VMEM(small.shape, full),
            pltpu.VMEM(small.shape, full),
            dma((3,)), dma((3, pairs)), dma((2,)),
            dma((2 * pieces,)), dma((2 * pieces,)),
            dma((groups + 1, dp // 2)), dma((groups + 1, dp // 2)),
            dma((groups + 1, dp // 2)), dma((groups + 1, dp // 2)),
            dma((tensor,)), dma((tensor,)),
            dma((ways,)), dma((ways,)), dma((ways,)), dma((ways,)),
        ],
        compiler_params=pltpu.CompilerParams(
            collective_id=3, has_side_effects=True, vmem_limit_bytes=62 << 20
        ),
        name="attend_backward",
    )(parents, q, k, v, o, branch_grad, seen, weights, lse, small)
    return out, block[:depth], total


HALF_ROOT = math.sqrt(0.5)
PDF_SCALE = 1.0 / math.sqrt(2.0 * math.pi)
CHUNK = 512
BAND = 256


def expert_kernel(
    dp, tensor, x_in, g_in, w_in, w_out, result_ref, back_ref, in_grad_ref, out_grad_ref,
    x_ref, g_ref, active_ref, slope_ref, keep_ref, part_ref, land_ref, home_ref,
    back_part, back_land, back_home, grad_ref, grad_land,
    x_send, x_recv, x_pair_send, x_pair_recv, g_send, g_recv, g_pair_send, g_pair_recv,
    y_pair_send, y_pair_recv, y_send, y_recv, d_pair_send, d_pair_recv, d_send, d_recv,
    line_send, line_recv,
):
    spot, place = lax.axis_index("dp"), lax.axis_index("tensor")
    chips = dp // 2
    chip, core = spot // 2, lax.rem(spot, 2)
    partner = (chip * 2 + 1 - core, place)
    capacity = x_in.shape[0] // chips

    def ahead(step):
        return (lax.rem(chip + step, chips) * 2 + core, place)

    def behind(step):
        return (lax.rem(chip - step + chips, chips) * 2 + core, place)

    def at(side, step):
        return pl.ds(pl.multiple_of((side * chips + step) * capacity, capacity), capacity)

    def along(step):
        return lax.rem(place + step, tensor)

    greet(
        [ahead(step) for step in range(1, chips)]
        + [partner]
        + [(spot, along(step)) for step in range(1, tensor)]
    )
    share = out_grad_ref.shape[0]

    def line(step):
        return pltpu.make_async_remote_copy(
            src_ref=grad_ref.at[along(step)], dst_ref=grad_land.at[place],
            send_sem=line_send.at[step], recv_sem=line_recv.at[place],
            device_id=(spot, along(step)), device_id_type=MESH,
        )

    def line_in(step):
        source = along(tensor - step)
        return pltpu.make_async_remote_copy(
            src_ref=grad_ref.at[source], dst_ref=grad_land.at[source],
            send_sem=line_send.at[step], recv_sem=line_recv.at[source],
            device_id=(spot, along(step)), device_id_type=MESH,
        )

    def copy(source, target, send, recv, step, where):
        return pltpu.make_async_remote_copy(
            src_ref=source, dst_ref=target, send_sem=send.at[step], recv_sem=recv.at[step],
            device_id=where, device_id_type=MESH,
        )

    def go_x(step):
        return copy(x_in.at[at(0, step)], x_ref.at[at(0, step)], x_send, x_recv, step, ahead(step))

    def go_g(step):
        return copy(g_in.at[at(0, step)], g_ref.at[at(0, step)], g_send, g_recv, step, ahead(step))

    def pair_x(step):
        return copy(
            x_ref.at[at(0, step)], x_ref.at[at(1, step)], x_pair_send, x_pair_recv, step, partner
        )

    def pair_g(step):
        return copy(
            g_ref.at[at(0, step)], g_ref.at[at(1, step)], g_pair_send, g_pair_recv, step, partner
        )

    def pair_y(step):
        here = at(0, step)
        return copy(part_ref.at[here], land_ref.at[here], y_pair_send, y_pair_recv, step, partner)

    def pair_d(step):
        here = at(0, step)
        return copy(back_part.at[here], back_land.at[here], d_pair_send, d_pair_recv, step, partner)

    def home_y(step):
        here = at(0, step)
        return copy(home_ref.at[here], result_ref.at[here], y_send, y_recv, step, behind(step))

    def home_d(step):
        here = at(0, step)
        return copy(back_home.at[here], back_ref.at[here], d_send, d_recv, step, behind(step))

    @pl.loop(1, chips)
    def _(step):
        go_x(step).start()

    x_ref[at(0, 0)] = x_in[at(0, 0)]
    pair_x(0).start()

    @pl.loop(1, chips)
    def _(step):
        go_g(step).start()

    g_ref[at(0, 0)] = g_in[at(0, 0)]

    def ahead_pass(side, step):
        rows = x_ref[at(side, step)]
        total = None
        for first in range(0, w_in.shape[1], CHUNK):
            cols = slice(first, first + CHUNK)
            up = dot_nn(rows, w_in[:, cols])
            below = 0.5 * (1.0 + lax.erf(up * HALF_ROOT))
            active = (up * below).astype(jnp.bfloat16)
            slope = below + up * (jnp.exp(-0.5 * up * up) * PDF_SCALE)
            active_ref[at(side, step), cols] = active
            slope_ref[at(side, step), cols] = slope.astype(jnp.bfloat16)
            part = dot_nn(active, w_out[cols])
            total = part if total is None else total + part
        return total

    def back_pass(side, step):
        grads = g_ref[at(side, step)]
        total = None
        for first in range(0, w_in.shape[1], CHUNK):
            cols = slice(first, first + CHUNK)
            active_grad = dot_nt(grads, w_out[cols])
            up_grad = active_grad * slope_ref[at(side, step), cols].astype(jnp.float32)
            up_grad = up_grad.astype(jnp.bfloat16)
            slope_ref[at(side, step), cols] = up_grad
            part = dot_nt(up_grad, w_in[:, cols])
            total = part if total is None else total + part
        return total

    keep_ref[at(0, 0)] = ahead_pass(0, 0)

    @pl.loop(1, chips)
    def _(step):
        go_x(step).wait_recv()
        pair_x(step).start()
        keep_ref[at(0, step)] = ahead_pass(0, step)

    pair_g(0).start()

    @pl.loop(0, chips)
    def _(step):
        pair_x(step).wait_recv()
        part_ref[at(0, step)] = ahead_pass(1, step).astype(part_ref.dtype)
        pair_y(step).start()

    @pl.loop(1, chips)
    def _(step):
        go_g(step).wait_recv()
        pair_g(step).start()

    @pl.loop(0, chips)
    def _(step):
        pair_y(step).wait_recv()
        here = at(0, step)
        total = keep_ref[here] + land_ref[here].astype(jnp.float32)
        home_ref[here] = total.astype(home_ref.dtype)

        @pl.when(step > 0)
        def _():
            home_y(step).start()

        @pl.when(step == 0)
        def _():
            result_ref[here] = total.astype(result_ref.dtype)

    @pl.loop(0, chips)
    def _(step):
        pair_g(step).wait_recv()

    @pl.loop(0, tensor)
    def _(part):
        for first in range(0, share, 128):
            cols = pl.ds(pl.multiple_of(part * share + first, 128), 128)
            grad_ref[part, first : first + 128] = dot_tn(active_ref[:, cols], g_ref[...]).astype(
                grad_ref.dtype
            )

    for step in range(1, tensor):
        line(step).start()

    @pl.loop(0, chips)
    def _(step):
        back_part[at(0, step)] = back_pass(1, step).astype(back_part.dtype)
        pair_d(step).start()

    @pl.loop(0, chips)
    def _(turn):
        step = chips - 1 - turn
        here = at(0, step)
        total = back_pass(0, step)
        pair_d(step).wait_recv()
        total = (total + back_land[here].astype(jnp.float32)).astype(back_home.dtype)
        back_home[here] = total

        @pl.when(step > 0)
        def _():
            home_d(step).start()

        @pl.when(step == 0)
        def _():
            back_ref[here] = total

    @pl.loop(0, w_in.shape[1] // BAND)
    def _(band):
        cols = pl.ds(pl.multiple_of(band * BAND, BAND), BAND)
        in_grad_ref[cols] = dot_tn(slope_ref[:, cols], x_ref[...]).astype(in_grad_ref.dtype)

    out_grad_ref[...] = grad_ref[place].astype(jnp.float32)
    for step in range(1, tensor):
        line_in(step).wait_recv()
        out_grad_ref[...] += grad_land[along(tensor - step)].astype(jnp.float32)
    for step in range(1, tensor):
        line(step).wait_send()

    @pl.loop(1, chips)
    def _(step):
        home_y(step).wait_recv()
        home_d(step).wait_recv()

    @pl.loop(0, chips)
    def _(step):
        pair_x(step).wait_send()
        pair_g(step).wait_send()
        pair_y(step).wait_send()
        pair_d(step).wait_send()

    @pl.loop(1, chips)
    def _(step):
        go_x(step).wait_send()
        go_g(step).wait_send()
        home_y(step).wait_send()
        home_d(step).wait_send()


def run_experts(slot_rows, slot_grads, w_in, w_out):
    dp, tensor = lax.axis_size("dp"), lax.axis_size("tensor")
    rows, width = slot_rows.shape
    hidden = w_in.shape[1]
    low = jnp.bfloat16
    here = pl.BlockSpec(memory_space=pltpu.VMEM)
    near = pltpu.VMEM((rows, width), low)
    both = pltpu.VMEM((2 * rows, width), low)
    middle = pltpu.VMEM((2 * rows, hidden), low)
    return pl.pallas_call(
        lambda *refs: expert_kernel(dp, tensor, *refs),
        out_shape=(
            jax.ShapeDtypeStruct((rows, width), low),
            jax.ShapeDtypeStruct((rows, width), low),
            jax.ShapeDtypeStruct((hidden, width), low),
            jax.ShapeDtypeStruct((hidden // tensor, width), jnp.float32),
        ),
        in_specs=[here] * 4,
        out_specs=[here] * 4,
        scratch_shapes=[
            both, both, middle, middle, pltpu.VMEM((rows, width), jnp.float32),
            near, near, near, near, near, near,
            pltpu.VMEM((tensor, hidden // tensor, width), low),
            pltpu.VMEM((tensor, hidden // tensor, width), low),
        ]
        + [pltpu.SemaphoreType.DMA((dp // 2,))] * 16
        + [pltpu.SemaphoreType.DMA((tensor,))] * 2,
        compiler_params=pltpu.CompilerParams(
            collective_id=4, has_side_effects=True, vmem_limit_bytes=60 << 20
        ),
        name="run_experts",
    )(slot_rows, slot_grads, w_in, w_out)


norm_eps = 1e-05
route_scale = 3.0
masked_score = -1e30
highest = lax.Precision.HIGHEST


def layer_norm(values, norm_gain):
    centred = values - jnp.mean(values, axis=-1, keepdims=True)
    spread = jnp.mean(centred * centred, axis=-1, keepdims=True)
    return centred * lax.rsqrt(spread + norm_eps) * norm_gain


def unit_rows(values):
    return values * lax.rsqrt(jnp.sum(values * values, axis=-1, keepdims=True) + 1.0)


def router_gate(normed, router_proj, expert_embed, picked):
    routed = jnp.dot(normed, router_proj, precision=highest)
    logits = route_scale * jnp.dot(unit_rows(routed), unit_rows(expert_embed).T, precision=highest)
    return jnp.sum(jax.nn.softmax(logits, axis=-1) * picked, axis=-1)


def gelu_exact(values):
    return jax.nn.gelu(values, approximate=False)


def slot_table(route_ids, order_ids, capacity):
    same_expert = route_ids[:, None] == route_ids[None, :]
    earlier = order_ids[None, :] < order_ids[:, None]
    ranking = jnp.sum(jnp.where(same_expert & earlier, 1, 0), axis=1).astype(jnp.int32)
    kept_mask = ranking < capacity
    column = route_ids * capacity + jnp.minimum(ranking, capacity - 1)
    return (column, kept_mask)


def low_dot(rows, weight):
    return jnp.dot(rows, weight, preferred_element_type=jnp.float32).astype(jnp.bfloat16)


def shards(
    tokens,
    norm1_gain,
    qkv_weight,
    attn_proj,
    norm2_gain,
    router_proj,
    expert_embed,
    expert_in,
    expert_out,
    routes,
    orders,
    leaf_parent,
    cotangent,
):
    rows_here = tokens.shape[0]
    model_width = tokens.shape[1]
    experts = expert_embed.shape[0]
    capacity = rows_here // experts
    dp_size, tensor_size = lax.axis_size("dp"), lax.axis_size("tensor")

    hidden = tokens.astype(jnp.float32)
    normed_in, norm1_back = jax.vjp(layer_norm, hidden, norm1_gain)
    own_in = normed_in.astype(jnp.bfloat16)
    flat_qkv = qkv_weight.reshape(qkv_weight.shape[0], -1)
    place = lax.axis_index("tensor")
    leaf_blocks = rows_here // BRANCH
    first_leaf = jnp.maximum(place - 2, 0) * leaf_blocks
    leaf_parents = lax.dynamic_slice_in_dim(leaf_parent[0], first_leaf, leaf_blocks, 0) - 1
    parents = (leaf_parents[:, None] == jnp.arange(leaf_blocks)[None, :]).astype(jnp.float32)
    parents = jnp.broadcast_to(parents.reshape(-1, 1), (leaf_blocks * leaf_blocks, model_width))
    seen_in, weights, query_rows, key_rows, value_rows, attended, log_totals = front(
        own_in, jnp.concatenate([flat_qkv, attn_proj.T], axis=1), parents
    )
    proj_back = weights[3]
    branch_out = jnp.einsum(
        "sc,dc->sd", attended, proj_back, preferred_element_type=jnp.float32
    )
    mid_stream = hidden + branch_out
    normed_mid, norm2_back = jax.vjp(layer_norm, mid_stream, norm2_gain)
    moe_in = normed_mid.astype(jnp.bfloat16)
    route_ids = routes[:, 0]
    near_route = (route_ids - lax.axis_index("dp") // 2) % experts
    column, kept_mask = slot_table(near_route, orders[0], capacity)
    picked = (route_ids[:, None] == jnp.arange(experts)[None, :]).astype(jnp.float32)
    gate_value, gate_back = jax.vjp(
        lambda normed_rows, route_proj, embed_rows: router_gate(
            normed_rows, route_proj, embed_rows, picked
        ),
        moe_in.astype(jnp.float32),
        router_proj,
        expert_embed,
    )
    select = (
        (column[:, None] == jnp.arange(experts * capacity)[None, :]) & kept_mask[:, None]
    ).astype(jnp.bfloat16)
    def to_slots(token_rows):
        return jnp.einsum(
            "ts,td->sd", select, token_rows, preferred_element_type=jnp.float32
        ).astype(jnp.bfloat16)

    def from_slots(slot_rows):
        return jnp.dot(select, slot_rows, preferred_element_type=jnp.float32)

    upstream = cotangent.astype(jnp.float32)
    slot_grads = to_slots((gate_value[:, None] * upstream).astype(jnp.bfloat16))
    result_rows, grad_rows, in_weight_grad, expert_out_grad = run_experts(
        to_slots(moe_in), slot_grads, expert_in, expert_out
    )
    expert_result = from_slots(result_rows)
    output = (mid_stream + gate_value[:, None] * expert_result).astype(jnp.bfloat16)
    moe_grad = from_slots(grad_rows)
    gate_grad = jnp.sum(upstream * expert_result, axis=-1)
    router_part, proj_grad, embed_grad = gate_back(gate_grad)
    mid_part, gain2_grad = norm2_back(moe_grad + router_part)
    mid_grad = upstream + mid_part
    expert_in_grad = (
        lax.psum_scatter(in_weight_grad, "tensor", scatter_dimension=0, tiled=True)
        .astype(jnp.float32)
        .T
    )
    branch_grad = mid_grad.astype(jnp.bfloat16)
    later = [gain2_grad, proj_grad, embed_grad]
    flat = jnp.concatenate([jnp.zeros_like(norm1_gain)] + [part.reshape(-1) for part in later])
    ways = dp_size * tensor_size
    lanes = -(-flat.shape[0] // (ways * 8 * 128)) * 128
    small = jnp.pad(flat, (0, ways * 8 * lanes - flat.shape[0])).reshape(ways, 8, lanes)
    input_grad, grad_block, totals = backward(
        parents, query_rows, key_rows, value_rows, attended, branch_grad, seen_in, weights,
        log_totals, small,
    )
    qkv_grad = grad_block[:, : flat_qkv.shape[1]].reshape(qkv_weight.shape)
    attn_proj_grad = grad_block[:, flat_qkv.shape[1] :].T
    totals = totals.reshape(-1)
    gain1_sum = totals[:model_width] / norm1_gain
    gain2_sum, router_sum, embed_sum = (
        totals[first : first + part.size].reshape(part.shape)
        for first, part in zip(
            (model_width, 2 * model_width, 2 * model_width + proj_grad.size), later
        )
    )
    token_part, _ = norm1_back(input_grad)
    token_grad = mid_grad + token_part
    return (
        output,
        token_grad,
        gain1_sum,
        qkv_grad,
        attn_proj_grad,
        gain2_sum,
        router_sum,
        embed_sum,
        expert_in_grad,
        expert_out_grad,
    )


def solution(mesh):
    in_specs = (
        P(("dp", "tensor"), None),
        P(),
        P("dp", None, "tensor"),
        P("tensor", "dp"),
        P(),
        P(),
        P(),
        P(None, "dp"),
        P("dp", None),
        P(("dp", "tensor"), None),
        P(("dp", "tensor"), None),
        P("dp", None),
        P(("dp", "tensor"), None),
    )
    out_specs = (
        P(("dp", "tensor"), None),
        P(("dp", "tensor"), None),
        P(),
        P("dp", None, "tensor"),
        P("tensor", "dp"),
        P(),
        P(),
        P(),
        P(None, ("dp", "tensor")),
        P(("dp", "tensor"), None),
    )
    return jax.shard_map(shards, mesh=mesh, in_specs=in_specs, out_specs=out_specs, check_vma=False)
```

```python
import functools
import math

import jax
import jax.numpy as jnp
from jax import lax
from jax.experimental import pallas as pl
from jax.experimental.pallas import tpu as pltpu
from jax.sharding import PartitionSpec as P

HEAD_DIM = 64
TRUNK = 1024
BRANCH = 256
MASKED = -1e30
LOG2E = math.log2(math.e)
EXP_SCALE = HEAD_DIM ** (-0.5) * LOG2E

NT = (((1,), (1,)), ((), ()))
NN = (((1,), (0,)), ((), ()))


def dot_nt(a, b):
    return lax.dot_general(a, b, NT, preferred_element_type=jnp.float32)


def dot_nn(a, b):
    return lax.dot_general(a, b, NN, preferred_element_type=jnp.float32)


def head_lanes(shape, dim, head):
    return lax.broadcasted_iota(jnp.int32, shape, dim) // HEAD_DIM == head


MESH = pl.DeviceIdType.MESH
PIECE = 64


def greet(peers):
    barrier = pltpu.get_barrier_semaphore()
    for peer in peers:
        pl.semaphore_signal(barrier, inc=1, device_id=peer, device_id_type=MESH)
    pl.semaphore_wait(barrier, len(peers))


def front_kernel(
    dp, tensor, depth, own_ref, block_ref, parent_ref,
    seen_out, weight_out, q_out, k_out, v_out, o_out, lse_ref,
    seen_ref, land_ref, weight_ref, q_ref, k_ref, v_ref, o_ref, acc_ref, top_ref, spare_ref,
    row_send, row_recv, line_send, line_recv, chip_send, chip_recv, pair_send, pair_recv, save_sem,
):
    spot, place = lax.axis_index("dp"), lax.axis_index("tensor")
    chip, core = spot // 2, lax.rem(spot, 2)
    chips = dp // 2
    rows, width = own_ref.shape
    pieces = rows // PIECE
    pairs = width // 128
    blocks = rows // BRANCH
    share = width // tensor
    partner = (chip * 2 + 1 - core, place)

    def along(step):
        return lax.rem(place + step, tensor)

    def chip_at(step):
        return lax.rem(chip + step, chips)

    greet(
        [(spot, along(step)) for step in range(1, tensor)]
        + [(chip_at(step) * 2 + core, place) for step in range(1, chips)]
        + [partner]
    )

    def pass_on(piece, fresh):
        at = pl.ds(pl.multiple_of(piece * PIECE, PIECE), PIECE)
        source = seen_ref.at[at]
        if fresh:
            here = lax.rem(piece, pieces) * PIECE
            source = own_ref.at[pl.ds(pl.multiple_of(here, PIECE), PIECE)]
        return pltpu.make_async_remote_copy(
            src_ref=source, dst_ref=seen_ref.at[at],
            send_sem=row_send.at[piece], recv_sem=row_recv.at[piece],
            device_id=(spot, lax.rem(place + 1, tensor)), device_id_type=MESH,
        )

    def line(step):
        return pltpu.make_async_remote_copy(
            src_ref=block_ref, dst_ref=land_ref.at[place, spot],
            send_sem=line_send.at[step], recv_sem=line_recv.at[place],
            device_id=(spot, along(step)), device_id_type=MESH,
        )

    def line_in(step):
        source = along(tensor - step)
        return pltpu.make_async_remote_copy(
            src_ref=block_ref, dst_ref=land_ref.at[source, spot],
            send_sem=line_send.at[step], recv_sem=line_recv.at[source],
            device_id=(spot, along(step)), device_id_type=MESH,
        )

    def plane(part, step):
        block = land_ref.at[part, spot]
        return pltpu.make_async_remote_copy(
            src_ref=block, dst_ref=block,
            send_sem=chip_send.at[part, step], recv_sem=chip_recv.at[part, chip],
            device_id=(chip_at(step) * 2 + core, place), device_id_type=MESH,
        )

    def plane_in(part, step):
        source = chip_at(chips - step)
        block = land_ref.at[part, source * 2 + core]
        return pltpu.make_async_remote_copy(
            src_ref=block, dst_ref=block,
            send_sem=chip_send.at[part, step], recv_sem=chip_recv.at[part, source],
            device_id=(chip_at(step) * 2 + core, place), device_id_type=MESH,
        )

    def across(part, source, source_core):
        block = land_ref.at[part, source * 2 + source_core]
        return pltpu.make_async_remote_copy(
            src_ref=block, dst_ref=block,
            send_sem=pair_send.at[part, source], recv_sem=pair_recv.at[part, source],
            device_id=partner, device_id_type=MESH,
        )

    for step in range(1, tensor):
        line(step).start()

    @pl.when(place == 0)
    def _():
        @pl.loop(0, pieces)
        def _(piece):
            pass_on(piece, True).start()

    land_ref[place, spot] = block_ref[...]
    seen_ref[2 * rows :] = own_ref[...]

    @pl.when(place < 2)
    def _():
        seen_ref[rows : 2 * rows] = own_ref[...]

    @pl.when(place == 0)
    def _():
        seen_ref[0:rows] = own_ref[...]

    def serve(first, last):
        @pl.loop(first, last)
        def _(piece):
            takes = (place > 1) | ((place > 0) & (piece < pieces))

            @pl.when(takes)
            def _():
                pass_on(piece, False).wait_recv()

                @pl.when(place < tensor - 1)
                def _():
                    pass_on(piece, False).start()

    def part_of(index):
        return pl.ds(index * rows, rows)

    saves = [
        pltpu.make_async_copy(source, target, save_sem.at[index])
        for index, (source, target) in enumerate(
            [(weight_ref, weight_out), (q_ref, q_out), (o_ref, o_out)]
            + [
                (held.at[part_of(part)], target.at[part_of(part)])
                for part in (2, 0, 1)
                for held, target in ((seen_ref, seen_out), (k_ref, k_out), (v_ref, v_out))
            ]
        )
    ]

    serve(0, pieces // 8)
    for step in range(tensor):
        part = along(tensor - step)
        if step:
            line_in(step).wait_recv()

        @pl.loop(1, chips)
        def _(hop):
            plane(part, hop).start()

        across(part, chip, core).start()
    serve(pieces // 8, (5 * pieces) // 8)
    for step in range(tensor):
        part = along(tensor - step)

        @pl.loop(1, chips)
        def _(hop):
            plane_in(part, hop).wait_recv()
            across(part, chip_at(chips - hop), core).start()

    serve((5 * pieces) // 8, pieces)

    @pl.when(place == 1)
    def _():
        @pl.loop(pieces, 2 * pieces)
        def _(piece):
            pass_on(piece, True).start()

    for part in range(tensor):

        @pl.loop(0, chips)
        def _(source):
            across(part, source, 1 - core).wait_recv()

    def ordered(source, kind):
        cols = slice(kind * share, (kind + 1) * share)
        return jnp.concatenate(
            [land_ref[part, source][:, cols] for part in range(tensor)], axis=1
        )

    if depth % 16:
        for kind in range(4):
            for source in range(dp):
                spare_ref[source * depth : (source + 1) * depth] = ordered(source, kind)[
                    0:depth
                ].astype(jnp.float32)
            weight_ref[kind] = spare_ref[...].astype(weight_ref.dtype)
    else:

        @pl.loop(0, dp)
        def _(source):
            at = pl.ds(pl.multiple_of(source * depth, depth), depth)
            for kind in range(4):
                weight_ref[kind, at] = ordered(source, kind)

    saves[0].start()

    def lanes(pair):
        return pl.ds(pl.multiple_of(pair * 128, 128), 128)

    def project(first, also_queries=False):
        @pl.loop(0, blocks)
        def _(b):
            at = pl.ds(pl.multiple_of(first + b * BRANCH, BRANCH), BRANCH)
            normed = seen_ref[at]
            k_ref[at] = dot_nn(normed, weight_ref[1]).astype(k_ref.dtype)
            v_ref[at] = dot_nn(normed, weight_ref[2]).astype(v_ref.dtype)
            if also_queries:
                here = pl.ds(pl.multiple_of(b * BRANCH, BRANCH), BRANCH)
                q_ref[here] = dot_nn(normed, weight_ref[0]).astype(q_ref.dtype)

    def attend_tiles(pair, tiles_of, opening):
        values, work = {}, [(block, head) for block in range(blocks) for head in range(2)]

        def value_tile(first, head):
            if (first, head) not in values:
                flipped = v_ref[first : first + BRANCH, lanes(pair)].T
                for side in range(2):
                    values[first, side] = jnp.where(
                        head_lanes(flipped.shape, 0, side), flipped, jnp.ones_like(flipped)
                    )
            return values[first, head]

        def start(block, head):
            queries = q_ref[block * BRANCH : (block + 1) * BRANCH, lanes(pair)]
            queries = jnp.where(
                head_lanes(queries.shape, 1, head), queries, jnp.zeros_like(queries)
            )
            scores = []
            for first, masked in tiles_of(block):
                tile = dot_nt(k_ref[first : first + BRANCH, lanes(pair)], queries)
                if masked:
                    keys = lax.broadcasted_iota(jnp.int32, tile.shape, 0)
                    at = lax.broadcasted_iota(jnp.int32, tile.shape, 1)
                    tile = jnp.where(keys <= at, tile, MASKED)
                scores.append(tile)
            top = jnp.max(functools.reduce(jnp.maximum, scores), axis=0, keepdims=True)
            return scores, top

        def middle(block, head, scores, top):
            cols = slice(block * BRANCH, (block + 1) * BRANCH)
            fade = None
            if not opening:
                before = top_ref[pair, head : head + 1, cols]
                top = jnp.maximum(before, top)
                fade = jnp.exp2((before - top) * EXP_SCALE)
            top_ref[pair, head : head + 1, cols] = top
            shift = top * EXP_SCALE
            return [
                jnp.exp2(tile * EXP_SCALE - shift).astype(jnp.bfloat16) for tile in scores
            ], fade

        def finish(block, head, probs, fade):
            cols = slice(block * BRANCH, (block + 1) * BRANCH)
            acc = None if opening else acc_ref[pair, head, :, cols] * fade
            for (first, _), tile in zip(tiles_of(block), probs):
                part = dot_nn(value_tile(first, head), tile)
                acc = part if acc is None else acc + part
            acc_ref[pair, head, :, cols] = acc

        ready, held = start(*work[0]), None
        for at, item in enumerate(work):
            now = ready
            if at + 1 < len(work):
                ready = start(*work[at + 1])
            done = middle(*item, *now)
            if held is not None:
                finish(*held)
            held = (*item, *done)
        finish(*held)

    project(2 * rows, True)
    for index in (1, 3, 4, 5):
        saves[index].start()
    serve(pieces, pieces + 2)

    @pl.loop(0, pairs)
    def _(pair):
        @pl.when(place == 0)
        def _():
            attend_tiles(
                pair,
                lambda block: [
                    (2 * rows + j * BRANCH, j == block) for j in range(block + 1)
                ],
                True,
            )

        @pl.when(place > 0)
        def _():
            attend_tiles(pair, lambda block: [(2 * rows + block * BRANCH, True)], True)

        @pl.when(lax.rem(pair, 2) == 1)
        def _():
            piece = pieces + 2 + pair // 2
            serve(piece, piece + 1)

    project(0)
    for index in (6, 7, 8):
        saves[index].start()
    served = pieces + 2 + pairs // 2
    per_pair = -(-(2 * pieces - served) // pairs)

    @pl.loop(0, pairs)
    def _(pair):
        @pl.when(place > 0)
        def _():
            attend_tiles(pair, lambda block: [(j * BRANCH, False) for j in range(blocks)], False)

        first = served + pair * per_pair
        serve(jnp.minimum(first, 2 * pieces), jnp.minimum(first + per_pair, 2 * pieces))

    @pl.when((place > 0) & (place < tensor - 1))
    def _():
        @pl.loop(0, 2 * pieces)
        def _(piece):
            pass_on(piece, False).wait_send()

    @pl.when(place > 1)
    def _():
        branches = [
            seen_ref[rows + branch * BRANCH : rows + (branch + 1) * BRANCH]
            for branch in range(blocks)
        ]
        for leaf in range(blocks):
            chosen = None
            for branch in range(blocks):
                at = leaf * blocks + branch
                part = branches[branch] * parent_ref[at : at + 1].astype(own_ref.dtype)
                chosen = part if chosen is None else chosen + part
            o_ref[leaf * BRANCH : (leaf + 1) * BRANCH] = chosen
        seen_ref[rows : 2 * rows] = o_ref[...]

    project(rows)
    for index in (9, 10, 11):
        saves[index].start()

    @pl.loop(0, pairs)
    def _(pair):
        @pl.when(place > 1)
        def _():
            attend_tiles(pair, lambda block: [(rows + block * BRANCH, False)], False)

        outs = []
        for head in range(2):
            mine, other = head * HEAD_DIM, (1 - head) * HEAD_DIM
            total = acc_ref[pair, head, other : other + 1]
            outs.append(acc_ref[pair, head, mine : mine + HEAD_DIM] / total)
            lse_ref[pair, head : head + 1] = (
                top_ref[pair, head : head + 1] * EXP_SCALE + jnp.log2(total)
            )
        o_ref[:, lanes(pair)] = jnp.concatenate(outs, axis=0).T.astype(o_ref.dtype)

    saves[2].start()
    for part in range(tensor):

        @pl.loop(0, chips)
        def _(source):
            across(part, source, core).wait_send()

        @pl.loop(1, chips)
        def _(hop):
            plane(part, hop).wait_send()

    for step in range(1, tensor):
        line(step).wait_send()

    @pl.when(place == 0)
    def _():
        @pl.loop(0, pieces)
        def _(piece):
            pass_on(piece, True).wait_send()

    for save in saves:
        save.wait()


def front(own, block, parents):
    dp, tensor = lax.axis_size("dp"), lax.axis_size("tensor")
    rows, width = own.shape
    depth, cols = block.shape
    pieces, chips, pairs = rows // PIECE, dp // 2, width // 128
    padded = -(-depth // 16) * 16
    block = jnp.pad(block, ((0, padded - depth), (0, 0)))
    low, full = jnp.bfloat16, jnp.float32
    few, many = (rows, width), (3 * rows, width)
    weights = (4, width, width)
    dma = pltpu.SemaphoreType.DMA
    here = pl.BlockSpec(memory_space=pltpu.VMEM)
    anywhere = pl.BlockSpec(memory_space=pl.ANY)
    return pl.pallas_call(
        lambda *refs: front_kernel(dp, tensor, depth, *refs),
        out_shape=tuple(
            jax.ShapeDtypeStruct(shape, low) for shape in (many, weights, few, many, many, few)
        )
        + (jax.ShapeDtypeStruct((pairs, 2, rows), full),),
        in_specs=[here, here, here],
        out_specs=[anywhere] * 6 + [here],
        scratch_shapes=[
            pltpu.VMEM(many, low),
            pltpu.VMEM((tensor, dp, padded, cols), low),
            pltpu.VMEM(weights, low),
            pltpu.VMEM(few, low),
            pltpu.VMEM(many, low),
            pltpu.VMEM(many, low),
            pltpu.VMEM(few, low),
            pltpu.VMEM((pairs, 2, 128, rows), full),
            pltpu.VMEM((pairs, 2, rows), full),
            pltpu.VMEM((width, width) if depth % 16 else (8, 128), full),
            dma((2 * pieces,)), dma((2 * pieces,)),
            dma((tensor,)), dma((tensor,)),
            dma((tensor, chips)), dma((tensor, chips)),
            dma((tensor, chips)), dma((tensor, chips)),
            dma((12,)),
        ],
        compiler_params=pltpu.CompilerParams(
            collective_id=2, has_side_effects=True, vmem_limit_bytes=58 << 20
        ),
        name="front",
    )(own, block, parents)


TN = (((0,), (0,)), ((), ()))
GROUP = 256


def dot_tn(a, b):
    return lax.dot_general(a, b, TN, preferred_element_type=jnp.float32)


def back_kernel(
    dp, tensor, depth,
    parent_ref, q_in, k_in, v_in, o_in, grad_in, seen_in, weight_in, lse_ref, small_ref,
    out_ref, sum_ref, total_ref,
    q_ref, k_ref, v_ref, o_ref, bg_ref, g_ref, stage_ref, seen_ref, weight_ref,
    delta_ref, dqt_ref, rows_ref, land_ref, gain_ref,
    slab_ref, pair_land, chip_land, line_out, line_land, part_ref, part_land,
    load_sem, pair_sem, stage_sem, row_send, row_recv,
    pair_send, pair_recv, chip_send, chip_recv,
    line_send, line_recv, small_send, small_recv, spread_send, spread_recv,
):
    spot, place = lax.axis_index("dp"), lax.axis_index("tensor")
    ways = dp * tensor
    me = spot * tensor + place
    scale = HEAD_DIM ** (-0.5)
    rows, width = q_ref.shape
    pairs = width // 128
    groups = width // GROUP
    blocks = rows // BRANCH
    pieces = rows // PIECE
    stage_rows = stage_ref.shape[1]

    def device(index):
        return (index // tensor, lax.rem(index, tensor))

    def along(step):
        return lax.rem(place + step, tensor)

    chips = dp // 2
    chip, core = spot // 2, lax.rem(spot, 2)

    def chip_at(step):
        return lax.rem(chip + step, chips)

    def block_at(b):
        return pl.ds(pl.multiple_of(b * BRANCH, BRANCH), BRANCH)

    barrier = pltpu.get_barrier_semaphore()

    @pl.loop(1, ways)
    def _(step):
        pl.semaphore_signal(
            barrier, inc=1, device_id=device(lax.rem(me + step, ways)), device_id_type=MESH
        )

    def lanes(pair):
        return pl.ds(pl.multiple_of(pair * 128, 128), 128)

    grad_load = pltpu.make_async_copy(grad_in, bg_ref, load_sem.at[0])
    weight_load = pltpu.make_async_copy(weight_in, weight_ref, load_sem.at[1])
    value_load = pltpu.make_async_copy(o_in, o_ref, load_sem.at[2])

    def pair_loads(pair):
        return [
            pltpu.make_async_copy(
                source.at[:, lanes(pair)], held.at[:, lanes(pair)], pair_sem.at[which, pair]
            )
            for which, (source, held) in enumerate(((q_in, q_ref), (k_in, k_ref), (v_in, v_ref)))
        ]

    def stage(part):
        slot = lax.rem(part, 2)
        at = pl.ds(pl.multiple_of(part * stage_rows, stage_rows), stage_rows)
        return pltpu.make_async_copy(seen_in.at[at], stage_ref.at[slot], stage_sem.at[slot])

    grad_load.start()
    weight_load.start()
    value_load.start()

    @pl.loop(0, pairs)
    def _(pair):
        for load in pair_loads(pair):
            load.start()

    grad_load.wait()
    weight_load.wait()
    value_load.wait()

    def keep(held, value, kind):
        cols = slice(kind * GROUP, (kind + 1) * GROUP)
        if depth % 16:
            for target in range(dp):
                held[target, 0:depth, cols] = value[target * depth : (target + 1) * depth].astype(
                    slab_ref.dtype
                )
        else:
            held[:, :, cols] = value.reshape(dp, depth, GROUP).astype(slab_ref.dtype)

    for group in range(groups):
        cols = slice(group * GROUP, (group + 1) * GROUP)
        keep(slab_ref.at[groups], dot_tn(bg_ref[...], o_ref[:, cols]), group)

    @pl.loop(0, blocks)
    def _(b):
        at = block_at(b)
        g_ref[at] = dot_nn(bg_ref[at], weight_ref[3]).astype(g_ref.dtype)

    pl.semaphore_wait(barrier, ways - 1)

    def halve(group, source):
        return pltpu.make_async_remote_copy(
            src_ref=slab_ref.at[group, source * 2 + 1 - core],
            dst_ref=pair_land.at[group, source],
            send_sem=pair_send.at[group, source], recv_sem=pair_recv.at[group, source],
            device_id=(chip * 2 + 1 - core, place), device_id_type=MESH,
        )

    def give(group, step):
        to = chip_at(step) * 2 + core
        return pltpu.make_async_remote_copy(
            src_ref=slab_ref.at[group, to], dst_ref=chip_land.at[group, chip],
            send_sem=chip_send.at[group, step], recv_sem=chip_recv.at[group, chip],
            device_id=(to, place), device_id_type=MESH,
        )

    def take(group, step):
        source = chip_at(chips - step)
        return pltpu.make_async_remote_copy(
            src_ref=slab_ref.at[group, source * 2 + core], dst_ref=chip_land.at[group, source],
            send_sem=chip_send.at[group, step], recv_sem=chip_recv.at[group, source],
            device_id=(chip_at(step) * 2 + core, place), device_id_type=MESH,
        )

    def share_slabs(group):
        @pl.loop(0, chips)
        def _(source):
            halve(group, source).start()

    def send_slabs(group):
        @pl.loop(0, chips)
        def _(step):
            to = chip_at(step)
            halve(group, to).wait_recv()
            mine = slab_ref[group, to * 2 + core].astype(jnp.float32)
            mine = mine + pair_land[group, to].astype(jnp.float32)
            slab_ref[group, to * 2 + core] = mine.astype(slab_ref.dtype)

            @pl.when(step > 0)
            def _():
                give(group, step).start()

    share_slabs(groups)

    @pl.loop(0, pairs)
    def _(pair):
        for load in pair_loads(pair):
            load.wait()
        product = g_ref[:, lanes(pair)].astype(jnp.float32)
        product = (product * o_ref[:, lanes(pair)].astype(jnp.float32)).T
        for head in range(2):
            delta_ref[pair, head : head + 1, :] = jnp.sum(
                product[head * HEAD_DIM : (head + 1) * HEAD_DIM], axis=0, keepdims=True
            )
        dqt_ref[pair] = jnp.zeros(dqt_ref.shape[1:], dqt_ref.dtype)

    def sweep(pair, tiles):
        work = [(tile, head) for tile in range(len(tiles)) for head in range(2)]
        sums = [[None, None] for _ in tiles]
        keys, flipped = {}, {}

        def key_block(tile):
            row = tiles[tile][0]
            if id(row) not in keys:
                kb = k_ref[pl.ds(row, BRANCH), lanes(pair)]
                vb = v_ref[pl.ds(row, BRANCH), lanes(pair)]
                masked = []
                for head in range(2):
                    mine = head_lanes(kb.shape, 1, head)
                    masked.append(
                        (
                            jnp.where(mine, kb, jnp.zeros_like(kb)),
                            jnp.where(mine, vb, jnp.zeros_like(vb)),
                        )
                    )
                keys[id(row)] = masked
                flipped[id(row)] = kb.T
            return keys[id(row)], flipped[id(row)]

        def start(tile, head):
            at = pl.ds(tiles[tile][1], BRANCH)
            kb, vb = key_block(tile)[0][head]
            return dot_nt(kb, q_ref[at, lanes(pair)]), dot_nt(vb, g_ref[at, lanes(pair)])

        def middle(tile, head, scores, prob_grad):
            at = pl.ds(tiles[tile][1], BRANCH)
            probs = jnp.exp2(scores * EXP_SCALE - lse_ref[pair, head : head + 1, at])
            if tiles[tile][2] is not None:
                probs = tiles[tile][2](probs)
            score_grad = probs * (prob_grad - delta_ref[pair, head : head + 1, at])
            return probs.astype(jnp.bfloat16), score_grad.astype(jnp.bfloat16)

        def finish(tile, head, probs, score_grad):
            at = pl.ds(tiles[tile][1], BRANCH)
            parts = (
                dot_nn(score_grad, q_ref[at, lanes(pair)]),
                dot_nn(probs, g_ref[at, lanes(pair)]),
            )
            for which in range(2):
                held = sums[tile][which]
                if head == 0:
                    sums[tile][which] = parts[which]
                else:
                    first = head_lanes(held.shape, 1, 0)
                    sums[tile][which] = jnp.where(first, held, parts[which])
            mine = slice(head * HEAD_DIM, (head + 1) * HEAD_DIM)
            dqt_ref[pair, mine, at] += dot_nn(key_block(tile)[1][mine], score_grad)

        ready = start(*work[0])
        held = None
        for at, item in enumerate(work):
            now = ready
            if at + 1 < len(work):
                ready = start(*work[at + 1])
            done = middle(*item, *now)
            if held is not None:
                finish(*held)
            held = (*item, *done)
        finish(*held)
        return sums

    def causal(key_row, query_row):
        def mask_of(probs):
            keys = lax.broadcasted_iota(jnp.int32, probs.shape, 0) + key_row
            at = lax.broadcasted_iota(jnp.int32, probs.shape, 1) + query_row
            return jnp.where(keys <= at, probs, 0.0)

        return mask_of

    def put(pair, row, dk, dv):
        at = pl.ds(row, BRANCH)
        k_ref[at, lanes(pair)] = (dk * scale).astype(k_ref.dtype)
        v_ref[at, lanes(pair)] = dv.astype(v_ref.dtype)

    def pass_down(piece):
        at = pl.ds(pl.multiple_of(piece * PIECE, PIECE), PIECE)
        return pltpu.make_async_remote_copy(
            src_ref=rows_ref.at[at], dst_ref=land_ref.at[at],
            send_sem=row_send.at[piece], recv_sem=row_recv.at[piece],
            device_id=(spot, lax.rem(place + tensor - 1, tensor)), device_id_type=MESH,
        )

    def row_grad(b):
        at = block_at(b)
        return dot_nt(k_ref[at], weight_ref[1]) + dot_nt(v_ref[at], weight_ref[2])

    def hand_down(b, total):
        rows_ref[block_at(b)] = total.astype(rows_ref.dtype)

        @pl.when(place == tensor - 1)
        def _():
            for piece in range(BRANCH // PIECE):
                pass_down(b * (BRANCH // PIECE) + piece).start()

    def joined(piece):
        at = pl.ds(pl.multiple_of(piece * PIECE, PIECE), PIECE)
        return rows_ref[at].astype(jnp.float32) + land_ref[at].astype(jnp.float32)

    middle_place = (place > 0) & (place < tensor - 1)
    late = 3 * jnp.maximum(tensor - 2 - place, 0)
    first_relay = jnp.where(place > 1, 0, pieces)
    last_relay = jnp.where(middle_place, 2 * pieces, first_relay)

    def piece_of(order):
        return lax.rem(order + pieces, 2 * pieces)

    def serve(first, last):
        def one(order, carry):
            piece = piece_of(order)
            pass_down(piece).wait_recv()
            at = pl.ds(pl.multiple_of(piece * PIECE, PIECE), PIECE)
            rows_ref[at] = joined(piece).astype(rows_ref.dtype)
            pass_down(piece).start()
            return carry

        low = jnp.clip(first - late, first_relay, last_relay)
        lax.fori_loop(low, jnp.clip(last - late, low, last_relay), one, 0)

    @pl.loop(0, pairs)
    def _(pair):
        @pl.when(place == 0)
        def _():
            for ref in (k_ref, v_ref):
                ref[rows : 3 * rows, lanes(pair)] = jnp.zeros((2 * rows, 128), ref.dtype)

        @pl.when(place > 0)
        def _():
            def seen_parent(probs):
                return jnp.where(place > 1, probs, 0.0)

            spots = range(0, rows, BRANCH)
            sums = sweep(pair, [(rows + at, at, seen_parent) for at in spots])
            for at, part in zip(spots, sums):
                put(pair, rows + at, *part)

    send_slabs(groups)

    @pl.loop(0, blocks)
    def _(leaf):
        out_ref[block_at(leaf)] = row_grad(blocks + leaf)

    for branch in range(blocks):
        total = None
        for leaf in range(blocks):
            at = leaf * blocks + branch
            part = out_ref[leaf * BRANCH : (leaf + 1) * BRANCH] * parent_ref[at : at + 1]
            total = part if total is None else total + part
        hand_down(blocks + branch, total)

    stage(0).start()

    @pl.loop(0, blocks)
    def _(b):
        row = pl.multiple_of(b * BRANCH, BRANCH)

        @pl.loop(0, pairs)
        def _(pair):
            def finish_block(masked):
                tiles = [
                    (row, first, causal(row, first) if masked else None)
                    for first in range(0, rows, BRANCH)
                ]
                sums = sweep(pair, tiles)
                put(pair, row, sum(part[0] for part in sums), sum(part[1] for part in sums))

            @pl.when(place == 0)
            def _():
                finish_block(True)

            @pl.when(place > 0)
            def _():
                finish_block(False)

            slot = b * pairs + pair
            serve(slot - 1, slot)

        for _half in range(2):
            part = b * 2 + _half

            @pl.when(part < 3 * rows // stage_rows)
            def _():
                stage(part).wait()

                @pl.when(part + 1 < 3 * rows // stage_rows)
                def _():
                    stage(part + 1).start()

                at = pl.ds(pl.multiple_of(part * stage_rows, stage_rows), stage_rows)
                seen_ref[:, at] = stage_ref[lax.rem(part, 2)].T

        hand_down(b, row_grad(b))

    served = blocks * pairs - 1

    gain_ref[...] = jnp.zeros_like(gain_ref)

    @pl.loop(0, groups)
    def _(group):
        base = served + group * 4

        @pl.loop(0, 2)
        def _(half):
            pair = group * 2 + half

            @pl.when(place > 0)
            def _():
                spots = range(0, rows, BRANCH)
                sums = sweep(pair, [(2 * rows + at, at, causal(0, 0)) for at in spots])
                for at, part in zip(spots, sums):
                    put(pair, 2 * rows + at, *part)

            q_ref[:, lanes(pair)] = (dqt_ref[pair] * scale).T.astype(q_ref.dtype)
            serve(base + half, base + half + 1)

        cols = pl.ds(pl.multiple_of(group * GROUP, GROUP), GROUP)
        for kind, value in (
            (0, lambda: dot_nn(seen_ref[:, 2 * rows : 3 * rows], q_ref[:, cols])),
            (1, lambda: dot_nn(seen_ref[...], k_ref[:, cols])),
            (2, lambda: dot_nn(seen_ref[...], v_ref[:, cols])),
        ):
            product = value()
            scaled = product * weight_ref[kind, :, cols].astype(jnp.float32)
            gain_ref[...] += scaled[:, 0:128] + scaled[:, 128:256]
            keep(slab_ref.at[group], product, kind)
            if kind:
                serve(base + 1 + kind, base + 2 + kind)

        share_slabs(group)

        @pl.when(group > 0)
        def _():
            send_slabs(group - 1)

    served += groups * 4

    part_ref[...] = small_ref[...]
    gains = jnp.sum(gain_ref[...].T, axis=0, keepdims=True)
    for row in range(width // 128):
        part_ref[0, row : row + 1, :] = gains[:, row * 128 : (row + 1) * 128]

    def scatter(step):
        to = lax.rem(me + step, ways)
        return pltpu.make_async_remote_copy(
            src_ref=part_ref.at[to], dst_ref=part_land.at[me],
            send_sem=small_send.at[step], recv_sem=small_recv.at[me],
            device_id=device(to), device_id_type=MESH,
        )

    def arrival(step):
        source = lax.rem(me - step + ways, ways)
        return pltpu.make_async_remote_copy(
            src_ref=part_ref.at[source], dst_ref=part_land.at[source],
            send_sem=small_send.at[step], recv_sem=small_recv.at[source],
            device_id=device(lax.rem(me + step, ways)), device_id_type=MESH,
        )

    def spread(step):
        return pltpu.make_async_remote_copy(
            src_ref=total_ref.at[me], dst_ref=total_ref.at[me],
            send_sem=spread_send.at[step], recv_sem=spread_recv.at[me],
            device_id=device(lax.rem(me + step, ways)), device_id_type=MESH,
        )

    def landing(step):
        source = lax.rem(me - step + ways, ways)
        return pltpu.make_async_remote_copy(
            src_ref=total_ref.at[source], dst_ref=total_ref.at[source],
            send_sem=spread_send.at[step], recv_sem=spread_recv.at[source],
            device_id=device(lax.rem(me + step, ways)), device_id_type=MESH,
        )

    @pl.loop(1, ways)
    def _(step):
        scatter(step).start()

    send_slabs(groups - 1)

    @pl.loop(0, blocks)
    def _(b):
        at = block_at(b)
        out_ref[at] = row_grad(2 * blocks + b) + dot_nt(q_ref[at], weight_ref[0])
        serve(served + 2 * b, served + 2 * b + 2)

    served += 2 * blocks

    def add(step, total):
        arrival(step).wait_recv()
        return total + part_land[lax.rem(me - step + ways, ways)]

    total_ref[me] = lax.fori_loop(1, ways, add, part_ref[me])

    @pl.loop(1, ways)
    def _(step):
        spread(step).start()

    serve(served, jnp.maximum(served, 2 * pieces) + late)

    kinds = [[], [], [], []]
    for group in range(groups + 1):

        def add_slab(step, total):
            take(group, step).wait_recv()
            return total + chip_land[group, chip_at(chips - step)].astype(jnp.float32)

        total = lax.fori_loop(1, chips, add_slab, slab_ref[group, spot].astype(jnp.float32))
        for part in range(total.shape[1] // GROUP):
            kinds[3 if group == groups else part].append(
                total[:, part * GROUP : (part + 1) * GROUP]
            )

    share = width // tensor
    kinds = [jnp.concatenate(parts, axis=1) for parts in kinds]
    for target in range(tensor):
        mine = jnp.concatenate(
            [kind[:, target * share : (target + 1) * share] for kind in kinds], axis=1
        )
        line_out[target] = mine.astype(line_out.dtype)

        @pl.when(place == target)
        def _():
            sum_ref[...] = mine

    def line(step):
        return pltpu.make_async_remote_copy(
            src_ref=line_out.at[along(step)], dst_ref=line_land.at[place],
            send_sem=line_send.at[step], recv_sem=line_recv.at[place],
            device_id=(spot, along(step)), device_id_type=MESH,
        )

    def line_in(step):
        source = along(tensor - step)
        return pltpu.make_async_remote_copy(
            src_ref=line_out.at[source], dst_ref=line_land.at[source],
            send_sem=line_send.at[step], recv_sem=line_recv.at[source],
            device_id=(spot, along(step)), device_id_type=MESH,
        )

    for step in range(1, tensor):
        line(step).start()

    @pl.when(place < 2)
    def _():
        @pl.loop(0, pieces)
        def _(piece):
            source = place * pieces + piece
            pass_down(source).wait_recv()
            at = pl.ds(pl.multiple_of(piece * PIECE, PIECE), PIECE)
            out_ref[at] += joined(source)

    for step in range(1, tensor):
        line_in(step).wait_recv()
        sum_ref[...] += line_land[along(tensor - step)].astype(jnp.float32)

    @pl.loop(1, ways)
    def _(step):
        landing(step).wait_recv()

    for step in range(1, tensor):
        line(step).wait_send()

    @pl.loop(1, ways)
    def _(step):
        scatter(step).wait_send()
        spread(step).wait_send()

    for group in range(groups + 1):

        @pl.loop(0, chips)
        def _(step):
            halve(group, step).wait_send()

            @pl.when(step > 0)
            def _():
                give(group, step).wait_send()

    sent = jnp.where(place == tensor - 1, 2 * pieces, last_relay)
    first_sent = jnp.where(place == tensor - 1, 0, first_relay)

    def sent_one(order, carry):
        pass_down(piece_of(order)).wait_send()
        return carry

    lax.fori_loop(first_sent, sent, sent_one, 0)


def backward(parents, q, k, v, o, branch_grad, seen, weights, lse, small):
    dp, tensor = lax.axis_size("dp"), lax.axis_size("tensor")
    ways = dp * tensor
    rows, width = q.shape
    seen_rows = k.shape[0]
    depth = width // dp
    padded = -(-depth // 16) * 16
    pairs, groups, pieces = width // 128, width // GROUP, rows // PIECE
    slab = (padded, width)
    low, full = jnp.bfloat16, jnp.float32
    dma = pltpu.SemaphoreType.DMA
    anywhere = pl.BlockSpec(memory_space=pl.ANY)
    here = pl.BlockSpec(memory_space=pltpu.VMEM)
    out, block, total = pl.pallas_call(
        lambda *refs: back_kernel(dp, tensor, depth, *refs),
        out_shape=(
            jax.ShapeDtypeStruct((rows, width), full),
            jax.ShapeDtypeStruct((padded, width), full),
            jax.ShapeDtypeStruct(small.shape, full),
        ),
        in_specs=[here] + [anywhere] * 7 + [here] * 2,
        out_specs=[here, here, here],
        scratch_shapes=[
            pltpu.VMEM((rows, width), low),
            pltpu.VMEM((seen_rows, width), low),
            pltpu.VMEM((seen_rows, width), low),
            pltpu.VMEM((rows, width), low),
            pltpu.VMEM((rows, width), low),
            pltpu.VMEM((rows, width), low),
            pltpu.VMEM((2, rows // 2, width), low),
            pltpu.VMEM((width, seen_rows), low),
            pltpu.VMEM(weights.shape, low),
            pltpu.VMEM((pairs, 2, rows), full),
            pltpu.VMEM((pairs, 128, rows), full),
            pltpu.VMEM((2 * rows, width), low),
            pltpu.VMEM((2 * rows, width), low),
            pltpu.VMEM((width, 128), full),
            pltpu.VMEM((groups + 1, dp) + slab, low),
            pltpu.VMEM((groups + 1, dp // 2) + slab, low),
            pltpu.VMEM((groups + 1, dp // 2) + slab, low),
            pltpu.VMEM((tensor, padded, width), low),
            pltpu.VMEM((tensor, padded, width), low),
            pltpu.VMEM(small.shape, full),
            pltpu.VMEM(small.shape, full),
            dma((3,)), dma((3, pairs)), dma((2,)),
            dma((2 * pieces,)), dma((2 * pieces,)),
            dma((groups + 1, dp // 2)), dma((groups + 1, dp // 2)),
            dma((groups + 1, dp // 2)), dma((groups + 1, dp // 2)),
            dma((tensor,)), dma((tensor,)),
            dma((ways,)), dma((ways,)), dma((ways,)), dma((ways,)),
        ],
        compiler_params=pltpu.CompilerParams(
            collective_id=3, has_side_effects=True, vmem_limit_bytes=62 << 20
        ),
        name="attend_backward",
    )(parents, q, k, v, o, branch_grad, seen, weights, lse, small)
    return out, block[:depth], total


HALF_ROOT = math.sqrt(0.5)
PDF_SCALE = 1.0 / math.sqrt(2.0 * math.pi)
CHUNK = 512
BAND = 256


def expert_kernel(
    dp, tensor, x_in, g_in, w_in, w_out, result_ref, back_ref, in_grad_ref, out_grad_ref,
    x_ref, g_ref, active_ref, slope_ref, keep_ref, part_ref, land_ref, home_ref,
    back_part, back_land, back_home, grad_ref, grad_land,
    x_send, x_recv, x_pair_send, x_pair_recv, g_send, g_recv, g_pair_send, g_pair_recv,
    y_pair_send, y_pair_recv, y_send, y_recv, d_pair_send, d_pair_recv, d_send, d_recv,
    line_send, line_recv,
):
    spot, place = lax.axis_index("dp"), lax.axis_index("tensor")
    chips = dp // 2
    chip, core = spot // 2, lax.rem(spot, 2)
    partner = (chip * 2 + 1 - core, place)
    capacity = x_in.shape[0] // chips

    def ahead(step):
        return (lax.rem(chip + step, chips) * 2 + core, place)

    def behind(step):
        return (lax.rem(chip - step + chips, chips) * 2 + core, place)

    def at(side, step):
        return pl.ds(pl.multiple_of((side * chips + step) * capacity, capacity), capacity)

    def along(step):
        return lax.rem(place + step, tensor)

    greet(
        [ahead(step) for step in range(1, chips)]
        + [partner]
        + [(spot, along(step)) for step in range(1, tensor)]
    )
    share = out_grad_ref.shape[0]

    def line(step):
        return pltpu.make_async_remote_copy(
            src_ref=grad_ref.at[along(step)], dst_ref=grad_land.at[place],
            send_sem=line_send.at[step], recv_sem=line_recv.at[place],
            device_id=(spot, along(step)), device_id_type=MESH,
        )

    def line_in(step):
        source = along(tensor - step)
        return pltpu.make_async_remote_copy(
            src_ref=grad_ref.at[source], dst_ref=grad_land.at[source],
            send_sem=line_send.at[step], recv_sem=line_recv.at[source],
            device_id=(spot, along(step)), device_id_type=MESH,
        )

    def copy(source, target, send, recv, step, where):
        return pltpu.make_async_remote_copy(
            src_ref=source, dst_ref=target, send_sem=send.at[step], recv_sem=recv.at[step],
            device_id=where, device_id_type=MESH,
        )

    def go_x(step):
        return copy(x_in.at[at(0, step)], x_ref.at[at(0, step)], x_send, x_recv, step, ahead(step))

    def go_g(step):
        return copy(g_in.at[at(0, step)], g_ref.at[at(0, step)], g_send, g_recv, step, ahead(step))

    def pair_x(step):
        return copy(
            x_ref.at[at(0, step)], x_ref.at[at(1, step)], x_pair_send, x_pair_recv, step, partner
        )

    def pair_g(step):
        return copy(
            g_ref.at[at(0, step)], g_ref.at[at(1, step)], g_pair_send, g_pair_recv, step, partner
        )

    def pair_y(step):
        here = at(0, step)
        return copy(part_ref.at[here], land_ref.at[here], y_pair_send, y_pair_recv, step, partner)

    def pair_d(step):
        here = at(0, step)
        return copy(back_part.at[here], back_land.at[here], d_pair_send, d_pair_recv, step, partner)

    def home_y(step):
        here = at(0, step)
        return copy(home_ref.at[here], result_ref.at[here], y_send, y_recv, step, behind(step))

    def home_d(step):
        here = at(0, step)
        return copy(back_home.at[here], back_ref.at[here], d_send, d_recv, step, behind(step))

    @pl.loop(1, chips)
    def _(step):
        go_x(step).start()

    x_ref[at(0, 0)] = x_in[at(0, 0)]
    pair_x(0).start()
    g_ref[at(0, 0)] = g_in[at(0, 0)]

    def ahead_pass(side, step):
        rows = x_ref[at(side, step)]
        total = None
        for first in range(0, w_in.shape[1], CHUNK):
            cols = slice(first, first + CHUNK)
            up = dot_nn(rows, w_in[:, cols])
            below = 0.5 * (1.0 + lax.erf(up * HALF_ROOT))
            active = (up * below).astype(jnp.bfloat16)
            slope = below + up * (jnp.exp(-0.5 * up * up) * PDF_SCALE)
            active_ref[at(side, step), cols] = active
            slope_ref[at(side, step), cols] = slope.astype(jnp.bfloat16)
            part = dot_nn(active, w_out[cols])
            total = part if total is None else total + part
        return total

    def back_pass(side, step):
        grads = g_ref[at(side, step)]
        total = None
        for first in range(0, w_in.shape[1], CHUNK):
            cols = slice(first, first + CHUNK)
            active_grad = dot_nt(grads, w_out[cols])
            up_grad = active_grad * slope_ref[at(side, step), cols].astype(jnp.float32)
            up_grad = up_grad.astype(jnp.bfloat16)
            slope_ref[at(side, step), cols] = up_grad
            part = dot_nt(up_grad, w_in[:, cols])
            total = part if total is None else total + part
        return total

    keep_ref[at(0, 0)] = ahead_pass(0, 0)

    @pl.loop(1, chips)
    def _(step):
        go_x(step).wait_recv()
        pair_x(step).start()
        go_g(step).start()
        keep_ref[at(0, step)] = ahead_pass(0, step)

    pair_g(0).start()

    @pl.loop(0, chips)
    def _(step):
        pair_x(step).wait_recv()
        part_ref[at(0, step)] = ahead_pass(1, step).astype(part_ref.dtype)
        pair_y(step).start()

    @pl.loop(1, chips)
    def _(step):
        go_g(step).wait_recv()
        pair_g(step).start()

    @pl.loop(0, chips)
    def _(step):
        pair_y(step).wait_recv()
        here = at(0, step)
        total = keep_ref[here] + land_ref[here].astype(jnp.float32)
        home_ref[here] = total.astype(home_ref.dtype)

        @pl.when(step > 0)
        def _():
            home_y(step).start()

        @pl.when(step == 0)
        def _():
            result_ref[here] = total.astype(result_ref.dtype)

    @pl.loop(0, chips)
    def _(step):
        pair_g(step).wait_recv()

    @pl.loop(1, tensor + 1)
    def _(turn):
        step = lax.rem(turn, tensor)
        part = along(step)
        for first in range(0, share, 128):
            cols = pl.ds(pl.multiple_of(part * share + first, 128), 128)
            grad_ref[part, first : first + 128] = dot_tn(active_ref[:, cols], g_ref[...]).astype(
                grad_ref.dtype
            )

        @pl.when(step > 0)
        def _():
            line(step).start()

    @pl.loop(0, chips)
    def _(step):
        back_part[at(0, step)] = back_pass(1, step).astype(back_part.dtype)
        pair_d(step).start()

    @pl.loop(0, chips)
    def _(turn):
        step = chips - 1 - turn
        here = at(0, step)
        total = back_pass(0, step)
        pair_d(step).wait_recv()
        total = (total + back_land[here].astype(jnp.float32)).astype(back_home.dtype)
        back_home[here] = total

        @pl.when(step > 0)
        def _():
            home_d(step).start()

        @pl.when(step == 0)
        def _():
            back_ref[here] = total

    @pl.loop(0, w_in.shape[1] // BAND)
    def _(band):
        cols = pl.ds(pl.multiple_of(band * BAND, BAND), BAND)
        in_grad_ref[cols] = dot_tn(slope_ref[:, cols], x_ref[...]).astype(in_grad_ref.dtype)

    out_grad_ref[...] = grad_ref[place].astype(jnp.float32)
    for step in range(1, tensor):
        line_in(step).wait_recv()
        out_grad_ref[...] += grad_land[along(tensor - step)].astype(jnp.float32)
    for step in range(1, tensor):
        line(step).wait_send()

    @pl.loop(1, chips)
    def _(step):
        home_y(step).wait_recv()
        home_d(step).wait_recv()

    @pl.loop(0, chips)
    def _(step):
        pair_x(step).wait_send()
        pair_g(step).wait_send()
        pair_y(step).wait_send()
        pair_d(step).wait_send()

    @pl.loop(1, chips)
    def _(step):
        go_x(step).wait_send()
        go_g(step).wait_send()
        home_y(step).wait_send()
        home_d(step).wait_send()


def run_experts(slot_rows, slot_grads, w_in, w_out):
    dp, tensor = lax.axis_size("dp"), lax.axis_size("tensor")
    rows, width = slot_rows.shape
    hidden = w_in.shape[1]
    low = jnp.bfloat16
    here = pl.BlockSpec(memory_space=pltpu.VMEM)
    near = pltpu.VMEM((rows, width), low)
    both = pltpu.VMEM((2 * rows, width), low)
    middle = pltpu.VMEM((2 * rows, hidden), low)
    return pl.pallas_call(
        lambda *refs: expert_kernel(dp, tensor, *refs),
        out_shape=(
            jax.ShapeDtypeStruct((rows, width), low),
            jax.ShapeDtypeStruct((rows, width), low),
            jax.ShapeDtypeStruct((hidden, width), low),
            jax.ShapeDtypeStruct((hidden // tensor, width), jnp.float32),
        ),
        in_specs=[here] * 4,
        out_specs=[here] * 4,
        scratch_shapes=[
            both, both, middle, middle, pltpu.VMEM((rows, width), jnp.float32),
            near, near, near, near, near, near,
            pltpu.VMEM((tensor, hidden // tensor, width), low),
            pltpu.VMEM((tensor, hidden // tensor, width), low),
        ]
        + [pltpu.SemaphoreType.DMA((dp // 2,))] * 16
        + [pltpu.SemaphoreType.DMA((tensor,))] * 2,
        compiler_params=pltpu.CompilerParams(
            collective_id=4, has_side_effects=True, vmem_limit_bytes=60 << 20
        ),
        name="run_experts",
    )(slot_rows, slot_grads, w_in, w_out)


norm_eps = 1e-05
route_scale = 3.0
masked_score = -1e30
highest = lax.Precision.HIGHEST


def layer_norm(values, norm_gain):
    centred = values - jnp.mean(values, axis=-1, keepdims=True)
    spread = jnp.mean(centred * centred, axis=-1, keepdims=True)
    return centred * lax.rsqrt(spread + norm_eps) * norm_gain


def unit_rows(values):
    return values * lax.rsqrt(jnp.sum(values * values, axis=-1, keepdims=True) + 1.0)


def router_gate(normed, router_proj, expert_embed, picked):
    routed = jnp.dot(normed, router_proj, precision=highest)
    logits = route_scale * jnp.dot(unit_rows(routed), unit_rows(expert_embed).T, precision=highest)
    return jnp.sum(jax.nn.softmax(logits, axis=-1) * picked, axis=-1)


def gelu_exact(values):
    return jax.nn.gelu(values, approximate=False)


def slot_table(route_ids, order_ids, capacity):
    same_expert = route_ids[:, None] == route_ids[None, :]
    earlier = order_ids[None, :] < order_ids[:, None]
    ranking = jnp.sum(jnp.where(same_expert & earlier, 1, 0), axis=1).astype(jnp.int32)
    kept_mask = ranking < capacity
    column = route_ids * capacity + jnp.minimum(ranking, capacity - 1)
    return (column, kept_mask)


def low_dot(rows, weight):
    return jnp.dot(rows, weight, preferred_element_type=jnp.float32).astype(jnp.bfloat16)


def shards(
    tokens,
    norm1_gain,
    qkv_weight,
    attn_proj,
    norm2_gain,
    router_proj,
    expert_embed,
    expert_in,
    expert_out,
    routes,
    orders,
    leaf_parent,
    cotangent,
):
    rows_here = tokens.shape[0]
    model_width = tokens.shape[1]
    experts = expert_embed.shape[0]
    capacity = rows_here // experts
    dp_size, tensor_size = lax.axis_size("dp"), lax.axis_size("tensor")

    hidden = tokens.astype(jnp.float32)
    normed_in, norm1_back = jax.vjp(layer_norm, hidden, norm1_gain)
    own_in = normed_in.astype(jnp.bfloat16)
    flat_qkv = qkv_weight.reshape(qkv_weight.shape[0], -1)
    place = lax.axis_index("tensor")
    leaf_blocks = rows_here // BRANCH
    first_leaf = jnp.maximum(place - 2, 0) * leaf_blocks
    leaf_parents = lax.dynamic_slice_in_dim(leaf_parent[0], first_leaf, leaf_blocks, 0) - 1
    parents = (leaf_parents[:, None] == jnp.arange(leaf_blocks)[None, :]).astype(jnp.float32)
    parents = jnp.broadcast_to(parents.reshape(-1, 1), (leaf_blocks * leaf_blocks, model_width))
    seen_in, weights, query_rows, key_rows, value_rows, attended, log_totals = front(
        own_in, jnp.concatenate([flat_qkv, attn_proj.T], axis=1), parents
    )
    proj_back = weights[3]
    branch_out = jnp.einsum(
        "sc,dc->sd", attended, proj_back, preferred_element_type=jnp.float32
    )
    mid_stream = hidden + branch_out
    normed_mid, norm2_back = jax.vjp(layer_norm, mid_stream, norm2_gain)
    moe_in = normed_mid.astype(jnp.bfloat16)
    route_ids = routes[:, 0]
    near_route = (route_ids - lax.axis_index("dp") // 2) % experts
    column, kept_mask = slot_table(near_route, orders[0], capacity)
    picked = (route_ids[:, None] == jnp.arange(experts)[None, :]).astype(jnp.float32)
    gate_value, gate_back = jax.vjp(
        lambda normed_rows, route_proj, embed_rows: router_gate(
            normed_rows, route_proj, embed_rows, picked
        ),
        moe_in.astype(jnp.float32),
        router_proj,
        expert_embed,
    )
    select = (
        (column[:, None] == jnp.arange(experts * capacity)[None, :]) & kept_mask[:, None]
    ).astype(jnp.bfloat16)
    def to_slots(token_rows):
        return jnp.einsum(
            "ts,td->sd", select, token_rows, preferred_element_type=jnp.float32
        ).astype(jnp.bfloat16)

    def from_slots(slot_rows):
        return jnp.dot(select, slot_rows, preferred_element_type=jnp.float32)

    upstream = cotangent.astype(jnp.float32)
    slot_grads = to_slots((gate_value[:, None] * upstream).astype(jnp.bfloat16))
    result_rows, grad_rows, in_weight_grad, expert_out_grad = run_experts(
        to_slots(moe_in), slot_grads, expert_in, expert_out
    )
    expert_result = from_slots(result_rows)
    output = (mid_stream + gate_value[:, None] * expert_result).astype(jnp.bfloat16)
    moe_grad = from_slots(grad_rows)
    gate_grad = jnp.sum(upstream * expert_result, axis=-1)
    router_part, proj_grad, embed_grad = gate_back(gate_grad)
    mid_part, gain2_grad = norm2_back(moe_grad + router_part)
    mid_grad = upstream + mid_part
    expert_in_grad = (
        lax.psum_scatter(in_weight_grad, "tensor", scatter_dimension=0, tiled=True)
        .astype(jnp.float32)
        .T
    )
    branch_grad = mid_grad.astype(jnp.bfloat16)
    later = [gain2_grad, proj_grad, embed_grad]
    flat = jnp.concatenate([jnp.zeros_like(norm1_gain)] + [part.reshape(-1) for part in later])
    ways = dp_size * tensor_size
    lanes = -(-flat.shape[0] // (ways * 8 * 128)) * 128
    small = jnp.pad(flat, (0, ways * 8 * lanes - flat.shape[0])).reshape(ways, 8, lanes)
    input_grad, grad_block, totals = backward(
        parents, query_rows, key_rows, value_rows, attended, branch_grad, seen_in, weights,
        log_totals, small,
    )
    qkv_grad = grad_block[:, : flat_qkv.shape[1]].reshape(qkv_weight.shape)
    attn_proj_grad = grad_block[:, flat_qkv.shape[1] :].T
    totals = totals.reshape(-1)
    gain1_sum = totals[:model_width] / norm1_gain
    gain2_sum, router_sum, embed_sum = (
        totals[first : first + part.size].reshape(part.shape)
        for first, part in zip(
            (model_width, 2 * model_width, 2 * model_width + proj_grad.size), later
        )
    )
    token_part, _ = norm1_back(input_grad)
    token_grad = mid_grad + token_part
    return (
        output,
        token_grad,
        gain1_sum,
        qkv_grad,
        attn_proj_grad,
        gain2_sum,
        router_sum,
        embed_sum,
        expert_in_grad,
        expert_out_grad,
    )


def solution(mesh):
    in_specs = (
        P(("dp", "tensor"), None),
        P(),
        P("dp", None, "tensor"),
        P("tensor", "dp"),
        P(),
        P(),
        P(),
        P(None, "dp"),
        P("dp", None),
        P(("dp", "tensor"), None),
        P(("dp", "tensor"), None),
        P("dp", None),
        P(("dp", "tensor"), None),
    )
    out_specs = (
        P(("dp", "tensor"), None),
        P(("dp", "tensor"), None),
        P(),
        P("dp", None, "tensor"),
        P("tensor", "dp"),
        P(),
        P(),
        P(),
        P(None, ("dp", "tensor")),
        P(("dp", "tensor"), None),
    )
    return jax.shard_map(shards, mesh=mesh, in_specs=in_specs, out_specs=out_specs, check_vma=False)
```

```python
import functools
import math

import jax
import jax.numpy as jnp
from jax import lax
from jax.experimental import pallas as pl
from jax.experimental.pallas import tpu as pltpu
from jax.sharding import PartitionSpec as P

HEAD_DIM = 64
TRUNK = 1024
BRANCH = 256
MASKED = -1e30
LOG2E = math.log2(math.e)
EXP_SCALE = HEAD_DIM ** (-0.5) * LOG2E

NT = (((1,), (1,)), ((), ()))
NN = (((1,), (0,)), ((), ()))


def dot_nt(a, b):
    return lax.dot_general(a, b, NT, preferred_element_type=jnp.float32)


def dot_nn(a, b):
    return lax.dot_general(a, b, NN, preferred_element_type=jnp.float32)


def head_lanes(shape, dim, head):
    return lax.broadcasted_iota(jnp.int32, shape, dim) // HEAD_DIM == head


MESH = pl.DeviceIdType.MESH
PIECE = 64


def greet(peers):
    barrier = pltpu.get_barrier_semaphore()
    for peer in peers:
        pl.semaphore_signal(barrier, inc=1, device_id=peer, device_id_type=MESH)
    pl.semaphore_wait(barrier, len(peers))


def front_kernel(
    dp, tensor, depth, token_ref, scale_ref, block_ref, parent_ref,
    seen_out, weight_out, q_out, k_out, v_out, o_out, lse_ref,
    own_ref, seen_ref, land_ref, weight_ref, q_ref, k_ref, v_ref, o_ref, acc_ref, top_ref, spare_ref,
    row_send, row_recv, line_send, line_recv, chip_send, chip_recv, pair_send, pair_recv, save_sem,
):
    spot, place = lax.axis_index("dp"), lax.axis_index("tensor")
    chip, core = spot // 2, lax.rem(spot, 2)
    chips = dp // 2
    rows, width = own_ref.shape
    pieces = rows // PIECE
    pairs = width // 128
    blocks = rows // BRANCH
    share = width // tensor

    @pl.loop(0, blocks)
    def _(b):
        at = pl.ds(pl.multiple_of(b * BRANCH, BRANCH), BRANCH)
        normed = layer_norm(token_ref[at].astype(jnp.float32), scale_ref[...])
        own_ref[at] = normed.astype(own_ref.dtype)

    partner = (chip * 2 + 1 - core, place)

    def along(step):
        return lax.rem(place + step, tensor)

    def chip_at(step):
        return lax.rem(chip + step, chips)

    greet(
        [(spot, along(step)) for step in range(1, tensor)]
        + [(chip_at(step) * 2 + core, place) for step in range(1, chips)]
        + [partner]
    )

    def pass_on(piece, fresh):
        at = pl.ds(pl.multiple_of(piece * PIECE, PIECE), PIECE)
        source = seen_ref.at[at]
        if fresh:
            here = lax.rem(piece, pieces) * PIECE
            source = own_ref.at[pl.ds(pl.multiple_of(here, PIECE), PIECE)]
        return pltpu.make_async_remote_copy(
            src_ref=source, dst_ref=seen_ref.at[at],
            send_sem=row_send.at[piece], recv_sem=row_recv.at[piece],
            device_id=(spot, lax.rem(place + 1, tensor)), device_id_type=MESH,
        )

    def line(step):
        return pltpu.make_async_remote_copy(
            src_ref=block_ref, dst_ref=land_ref.at[place, spot],
            send_sem=line_send.at[step], recv_sem=line_recv.at[place],
            device_id=(spot, along(step)), device_id_type=MESH,
        )

    def line_in(step):
        source = along(tensor - step)
        return pltpu.make_async_remote_copy(
            src_ref=block_ref, dst_ref=land_ref.at[source, spot],
            send_sem=line_send.at[step], recv_sem=line_recv.at[source],
            device_id=(spot, along(step)), device_id_type=MESH,
        )

    def plane(part, step):
        block = land_ref.at[part, spot]
        return pltpu.make_async_remote_copy(
            src_ref=block, dst_ref=block,
            send_sem=chip_send.at[part, step], recv_sem=chip_recv.at[part, chip],
            device_id=(chip_at(step) * 2 + core, place), device_id_type=MESH,
        )

    def plane_in(part, step):
        source = chip_at(chips - step)
        block = land_ref.at[part, source * 2 + core]
        return pltpu.make_async_remote_copy(
            src_ref=block, dst_ref=block,
            send_sem=chip_send.at[part, step], recv_sem=chip_recv.at[part, source],
            device_id=(chip_at(step) * 2 + core, place), device_id_type=MESH,
        )

    def across(part, source, source_core):
        block = land_ref.at[part, source * 2 + source_core]
        return pltpu.make_async_remote_copy(
            src_ref=block, dst_ref=block,
            send_sem=pair_send.at[part, source], recv_sem=pair_recv.at[part, source],
            device_id=partner, device_id_type=MESH,
        )

    for step in range(1, tensor):
        line(step).start()

    @pl.when(place == 0)
    def _():
        @pl.loop(0, pieces)
        def _(piece):
            pass_on(piece, True).start()

    land_ref[place, spot] = block_ref[...]
    seen_ref[2 * rows :] = own_ref[...]

    @pl.when(place < 2)
    def _():
        seen_ref[rows : 2 * rows] = own_ref[...]

    @pl.when(place == 0)
    def _():
        seen_ref[0:rows] = own_ref[...]

    def serve(first, last):
        @pl.loop(first, last)
        def _(piece):
            takes = (place > 1) | ((place > 0) & (piece < pieces))

            @pl.when(takes)
            def _():
                pass_on(piece, False).wait_recv()

                @pl.when(place < tensor - 1)
                def _():
                    pass_on(piece, False).start()

    def part_of(index):
        return pl.ds(index * rows, rows)

    saves = [
        pltpu.make_async_copy(source, target, save_sem.at[index])
        for index, (source, target) in enumerate(
            [(weight_ref, weight_out), (q_ref, q_out), (o_ref, o_out)]
            + [
                (held.at[part_of(part)], target.at[part_of(part)])
                for part in (2, 0, 1)
                for held, target in ((seen_ref, seen_out), (k_ref, k_out), (v_ref, v_out))
            ]
        )
    ]

    serve(0, pieces // 8)
    for step in range(tensor):
        part = along(tensor - step)
        if step:
            line_in(step).wait_recv()

        @pl.loop(1, chips)
        def _(hop):
            plane(part, hop).start()

        across(part, chip, core).start()
    serve(pieces // 8, (5 * pieces) // 8)
    for step in range(tensor):
        part = along(tensor - step)

        @pl.loop(1, chips)
        def _(hop):
            plane_in(part, hop).wait_recv()
            across(part, chip_at(chips - hop), core).start()

    serve((5 * pieces) // 8, pieces)

    @pl.when(place == 1)
    def _():
        @pl.loop(pieces, 2 * pieces)
        def _(piece):
            pass_on(piece, True).start()

    for part in range(tensor):

        @pl.loop(0, chips)
        def _(source):
            across(part, source, 1 - core).wait_recv()

    def ordered(source, kind):
        cols = slice(kind * share, (kind + 1) * share)
        return jnp.concatenate(
            [land_ref[part, source][:, cols] for part in range(tensor)], axis=1
        )

    if depth % 16:
        for kind in range(4):
            for source in range(dp):
                spare_ref[source * depth : (source + 1) * depth] = ordered(source, kind)[
                    0:depth
                ].astype(jnp.float32)
            weight_ref[kind] = spare_ref[...].astype(weight_ref.dtype)
    else:

        @pl.loop(0, dp)
        def _(source):
            at = pl.ds(pl.multiple_of(source * depth, depth), depth)
            for kind in range(4):
                weight_ref[kind, at] = ordered(source, kind)

    saves[0].start()

    def lanes(pair):
        return pl.ds(pl.multiple_of(pair * 128, 128), 128)

    def project(first, also_queries=False):
        @pl.loop(0, blocks)
        def _(b):
            at = pl.ds(pl.multiple_of(first + b * BRANCH, BRANCH), BRANCH)
            normed = seen_ref[at]
            k_ref[at] = dot_nn(normed, weight_ref[1]).astype(k_ref.dtype)
            v_ref[at] = dot_nn(normed, weight_ref[2]).astype(v_ref.dtype)
            if also_queries:
                here = pl.ds(pl.multiple_of(b * BRANCH, BRANCH), BRANCH)
                q_ref[here] = dot_nn(normed, weight_ref[0]).astype(q_ref.dtype)

    def attend_tiles(pair, tiles_of, opening):
        values, work = {}, [(block, head) for block in range(blocks) for head in range(2)]

        def value_tile(first, head):
            if (first, head) not in values:
                flipped = v_ref[first : first + BRANCH, lanes(pair)].T
                for side in range(2):
                    values[first, side] = jnp.where(
                        head_lanes(flipped.shape, 0, side), flipped, jnp.ones_like(flipped)
                    )
            return values[first, head]

        def start(block, head):
            queries = q_ref[block * BRANCH : (block + 1) * BRANCH, lanes(pair)]
            queries = jnp.where(
                head_lanes(queries.shape, 1, head), queries, jnp.zeros_like(queries)
            )
            scores = []
            for first, masked in tiles_of(block):
                tile = dot_nt(k_ref[first : first + BRANCH, lanes(pair)], queries)
                if masked:
                    keys = lax.broadcasted_iota(jnp.int32, tile.shape, 0)
                    at = lax.broadcasted_iota(jnp.int32, tile.shape, 1)
                    tile = jnp.where(keys <= at, tile, MASKED)
                scores.append(tile)
            top = jnp.max(functools.reduce(jnp.maximum, scores), axis=0, keepdims=True)
            return scores, top

        def middle(block, head, scores, top):
            cols = slice(block * BRANCH, (block + 1) * BRANCH)
            fade = None
            if not opening:
                before = top_ref[pair, head : head + 1, cols]
                top = jnp.maximum(before, top)
                fade = jnp.exp2((before - top) * EXP_SCALE)
            top_ref[pair, head : head + 1, cols] = top
            shift = top * EXP_SCALE
            return [
                jnp.exp2(tile * EXP_SCALE - shift).astype(jnp.bfloat16) for tile in scores
            ], fade

        def finish(block, head, probs, fade):
            cols = slice(block * BRANCH, (block + 1) * BRANCH)
            acc = None if opening else acc_ref[pair, head, :, cols] * fade
            for (first, _), tile in zip(tiles_of(block), probs):
                part = dot_nn(value_tile(first, head), tile)
                acc = part if acc is None else acc + part
            acc_ref[pair, head, :, cols] = acc

        ready, held = start(*work[0]), None
        for at, item in enumerate(work):
            now = ready
            if at + 1 < len(work):
                ready = start(*work[at + 1])
            done = middle(*item, *now)
            if held is not None:
                finish(*held)
            held = (*item, *done)
        finish(*held)

    project(2 * rows, True)
    for index in (1, 3, 4, 5):
        saves[index].start()
    serve(pieces, pieces + 2)

    @pl.loop(0, pairs)
    def _(pair):
        @pl.when(place == 0)
        def _():
            attend_tiles(
                pair,
                lambda block: [
                    (2 * rows + j * BRANCH, j == block) for j in range(block + 1)
                ],
                True,
            )

        @pl.when(place > 0)
        def _():
            attend_tiles(pair, lambda block: [(2 * rows + block * BRANCH, True)], True)

        @pl.when(lax.rem(pair, 2) == 1)
        def _():
            piece = pieces + 2 + pair // 2
            serve(piece, piece + 1)

    project(0)
    for index in (6, 7, 8):
        saves[index].start()
    served = pieces + 2 + pairs // 2
    per_pair = -(-(2 * pieces - served) // pairs)

    @pl.loop(0, pairs)
    def _(pair):
        @pl.when(place > 0)
        def _():
            attend_tiles(pair, lambda block: [(j * BRANCH, False) for j in range(blocks)], False)

        first = served + pair * per_pair
        serve(jnp.minimum(first, 2 * pieces), jnp.minimum(first + per_pair, 2 * pieces))

    @pl.when((place > 0) & (place < tensor - 1))
    def _():
        @pl.loop(0, 2 * pieces)
        def _(piece):
            pass_on(piece, False).wait_send()

    @pl.when(place > 1)
    def _():
        branches = [
            seen_ref[rows + branch * BRANCH : rows + (branch + 1) * BRANCH]
            for branch in range(blocks)
        ]
        for leaf in range(blocks):
            chosen = None
            for branch in range(blocks):
                at = leaf * blocks + branch
                part = branches[branch] * parent_ref[at : at + 1].astype(own_ref.dtype)
                chosen = part if chosen is None else chosen + part
            o_ref[leaf * BRANCH : (leaf + 1) * BRANCH] = chosen
        seen_ref[rows : 2 * rows] = o_ref[...]

    project(rows)
    for index in (9, 10, 11):
        saves[index].start()

    @pl.loop(0, pairs)
    def _(pair):
        @pl.when(place > 1)
        def _():
            attend_tiles(pair, lambda block: [(rows + block * BRANCH, False)], False)

        outs = []
        for head in range(2):
            mine, other = head * HEAD_DIM, (1 - head) * HEAD_DIM
            total = acc_ref[pair, head, other : other + 1]
            outs.append(acc_ref[pair, head, mine : mine + HEAD_DIM] / total)
            lse_ref[pair, head : head + 1] = (
                top_ref[pair, head : head + 1] * EXP_SCALE + jnp.log2(total)
            )
        o_ref[:, lanes(pair)] = jnp.concatenate(outs, axis=0).T.astype(o_ref.dtype)

    saves[2].start()
    for part in range(tensor):

        @pl.loop(0, chips)
        def _(source):
            across(part, source, core).wait_send()

        @pl.loop(1, chips)
        def _(hop):
            plane(part, hop).wait_send()

    for step in range(1, tensor):
        line(step).wait_send()

    @pl.when(place == 0)
    def _():
        @pl.loop(0, pieces)
        def _(piece):
            pass_on(piece, True).wait_send()

    for save in saves:
        save.wait()


def front(tokens, gain, block, parents):
    dp, tensor = lax.axis_size("dp"), lax.axis_size("tensor")
    rows, width = tokens.shape
    depth, cols = block.shape
    pieces, chips, pairs = rows // PIECE, dp // 2, width // 128
    padded = -(-depth // 16) * 16
    block = jnp.pad(block, ((0, padded - depth), (0, 0)))
    low, full = jnp.bfloat16, jnp.float32
    few, many = (rows, width), (3 * rows, width)
    weights = (4, width, width)
    dma = pltpu.SemaphoreType.DMA
    here = pl.BlockSpec(memory_space=pltpu.VMEM)
    anywhere = pl.BlockSpec(memory_space=pl.ANY)
    return pl.pallas_call(
        lambda *refs: front_kernel(dp, tensor, depth, *refs),
        out_shape=tuple(
            jax.ShapeDtypeStruct(shape, low) for shape in (many, weights, few, many, many, few)
        )
        + (jax.ShapeDtypeStruct((pairs, 2, rows), full),),
        in_specs=[here] * 4,
        out_specs=[anywhere] * 6 + [here],
        scratch_shapes=[
            pltpu.VMEM(few, low),
            pltpu.VMEM(many, low),
            pltpu.VMEM((tensor, dp, padded, cols), low),
            pltpu.VMEM(weights, low),
            pltpu.VMEM(few, low),
            pltpu.VMEM(many, low),
            pltpu.VMEM(many, low),
            pltpu.VMEM(few, low),
            pltpu.VMEM((pairs, 2, 128, rows), full),
            pltpu.VMEM((pairs, 2, rows), full),
            pltpu.VMEM((width, width) if depth % 16 else (8, 128), full),
            dma((2 * pieces,)), dma((2 * pieces,)),
            dma((tensor,)), dma((tensor,)),
            dma((tensor, chips)), dma((tensor, chips)),
            dma((tensor, chips)), dma((tensor, chips)),
            dma((12,)),
        ],
        compiler_params=pltpu.CompilerParams(
            collective_id=2, has_side_effects=True, vmem_limit_bytes=58 << 20
        ),
        name="front",
    )(tokens, gain.reshape(1, width), block, parents)


TN = (((0,), (0,)), ((), ()))
GROUP = 256


def dot_tn(a, b):
    return lax.dot_general(a, b, TN, preferred_element_type=jnp.float32)


def back_kernel(
    dp, tensor, depth,
    parent_ref, q_in, k_in, v_in, o_in, grad_in, seen_in, weight_in, lse_ref, small_ref,
    out_ref, sum_ref, total_ref,
    q_ref, k_ref, v_ref, o_ref, bg_ref, g_ref, stage_ref, seen_ref, weight_ref,
    delta_ref, dqt_ref, rows_ref, land_ref, gain_ref,
    slab_ref, pair_land, chip_land, line_out, line_land, part_ref, part_land,
    load_sem, pair_sem, stage_sem, row_send, row_recv,
    pair_send, pair_recv, chip_send, chip_recv,
    line_send, line_recv, small_send, small_recv, spread_send, spread_recv,
):
    spot, place = lax.axis_index("dp"), lax.axis_index("tensor")
    ways = dp * tensor
    me = spot * tensor + place
    scale = HEAD_DIM ** (-0.5)
    rows, width = q_ref.shape
    pairs = width // 128
    groups = width // GROUP
    blocks = rows // BRANCH
    pieces = rows // PIECE
    stage_rows = stage_ref.shape[1]

    def device(index):
        return (index // tensor, lax.rem(index, tensor))

    def along(step):
        return lax.rem(place + step, tensor)

    chips = dp // 2
    chip, core = spot // 2, lax.rem(spot, 2)

    def chip_at(step):
        return lax.rem(chip + step, chips)

    def block_at(b):
        return pl.ds(pl.multiple_of(b * BRANCH, BRANCH), BRANCH)

    barrier = pltpu.get_barrier_semaphore()

    @pl.loop(1, ways)
    def _(step):
        pl.semaphore_signal(
            barrier, inc=1, device_id=device(lax.rem(me + step, ways)), device_id_type=MESH
        )

    def lanes(pair):
        return pl.ds(pl.multiple_of(pair * 128, 128), 128)

    grad_load = pltpu.make_async_copy(grad_in, bg_ref, load_sem.at[0])
    weight_load = pltpu.make_async_copy(weight_in, weight_ref, load_sem.at[1])
    value_load = pltpu.make_async_copy(o_in, o_ref, load_sem.at[2])

    def pair_loads(pair):
        return [
            pltpu.make_async_copy(
                source.at[:, lanes(pair)], held.at[:, lanes(pair)], pair_sem.at[which, pair]
            )
            for which, (source, held) in enumerate(((q_in, q_ref), (k_in, k_ref), (v_in, v_ref)))
        ]

    def stage(part):
        slot = lax.rem(part, 2)
        at = pl.ds(pl.multiple_of(part * stage_rows, stage_rows), stage_rows)
        return pltpu.make_async_copy(seen_in.at[at], stage_ref.at[slot], stage_sem.at[slot])

    grad_load.start()
    weight_load.start()
    value_load.start()

    @pl.loop(0, pairs)
    def _(pair):
        for load in pair_loads(pair):
            load.start()

    grad_load.wait()
    weight_load.wait()
    value_load.wait()

    def keep(held, value, kind):
        cols = slice(kind * GROUP, (kind + 1) * GROUP)
        if depth % 16:
            for target in range(dp):
                held[target, 0:depth, cols] = value[target * depth : (target + 1) * depth].astype(
                    slab_ref.dtype
                )
        else:
            held[:, :, cols] = value.reshape(dp, depth, GROUP).astype(slab_ref.dtype)

    product = dot_tn(bg_ref[...], o_ref[...])
    for group in range(groups):
        keep(slab_ref.at[groups], product[:, group * GROUP : (group + 1) * GROUP], group)

    @pl.loop(0, blocks)
    def _(b):
        at = block_at(b)
        g_ref[at] = dot_nn(bg_ref[at], weight_ref[3]).astype(g_ref.dtype)

    pl.semaphore_wait(barrier, ways - 1)

    def halve(group, source):
        return pltpu.make_async_remote_copy(
            src_ref=slab_ref.at[group, source * 2 + 1 - core],
            dst_ref=pair_land.at[group, source],
            send_sem=pair_send.at[group, source], recv_sem=pair_recv.at[group, source],
            device_id=(chip * 2 + 1 - core, place), device_id_type=MESH,
        )

    def give(group, step):
        to = chip_at(step) * 2 + core
        return pltpu.make_async_remote_copy(
            src_ref=slab_ref.at[group, to], dst_ref=chip_land.at[group, chip],
            send_sem=chip_send.at[group, step], recv_sem=chip_recv.at[group, chip],
            device_id=(to, place), device_id_type=MESH,
        )

    def take(group, step):
        source = chip_at(chips - step)
        return pltpu.make_async_remote_copy(
            src_ref=slab_ref.at[group, source * 2 + core], dst_ref=chip_land.at[group, source],
            send_sem=chip_send.at[group, step], recv_sem=chip_recv.at[group, source],
            device_id=(chip_at(step) * 2 + core, place), device_id_type=MESH,
        )

    def share_slabs(group):
        @pl.loop(0, chips)
        def _(source):
            halve(group, source).start()

    def send_slabs(group):
        @pl.loop(0, chips)
        def _(step):
            to = chip_at(step)
            halve(group, to).wait_recv()
            mine = slab_ref[group, to * 2 + core].astype(jnp.float32)
            mine = mine + pair_land[group, to].astype(jnp.float32)
            slab_ref[group, to * 2 + core] = mine.astype(slab_ref.dtype)

            @pl.when(step > 0)
            def _():
                give(group, step).start()

    share_slabs(groups)

    @pl.loop(0, pairs)
    def _(pair):
        for load in pair_loads(pair):
            load.wait()
        product = g_ref[:, lanes(pair)].astype(jnp.float32)
        product = (product * o_ref[:, lanes(pair)].astype(jnp.float32)).T
        for head in range(2):
            delta_ref[pair, head : head + 1, :] = jnp.sum(
                product[head * HEAD_DIM : (head + 1) * HEAD_DIM], axis=0, keepdims=True
            )
        dqt_ref[pair] = jnp.zeros(dqt_ref.shape[1:], dqt_ref.dtype)

    def sweep(pair, tiles):
        work = [(tile, head) for tile in range(len(tiles)) for head in range(2)]
        sums = [[None, None] for _ in tiles]
        keys, flipped = {}, {}

        def key_block(tile):
            row = tiles[tile][0]
            if id(row) not in keys:
                kb = k_ref[pl.ds(row, BRANCH), lanes(pair)]
                vb = v_ref[pl.ds(row, BRANCH), lanes(pair)]
                masked = []
                for head in range(2):
                    mine = head_lanes(kb.shape, 1, head)
                    masked.append(
                        (
                            jnp.where(mine, kb, jnp.zeros_like(kb)),
                            jnp.where(mine, vb, jnp.zeros_like(vb)),
                        )
                    )
                keys[id(row)] = masked
                flipped[id(row)] = kb.T
            return keys[id(row)], flipped[id(row)]

        def start(tile, head):
            at = pl.ds(tiles[tile][1], BRANCH)
            kb, vb = key_block(tile)[0][head]
            return dot_nt(kb, q_ref[at, lanes(pair)]), dot_nt(vb, g_ref[at, lanes(pair)])

        def middle(tile, head, scores, prob_grad):
            at = pl.ds(tiles[tile][1], BRANCH)
            probs = jnp.exp2(scores * EXP_SCALE - lse_ref[pair, head : head + 1, at])
            if tiles[tile][2] is not None:
                probs = tiles[tile][2](probs)
            score_grad = probs * (prob_grad - delta_ref[pair, head : head + 1, at])
            return probs.astype(jnp.bfloat16), score_grad.astype(jnp.bfloat16)

        def finish(tile, head, probs, score_grad):
            at = pl.ds(tiles[tile][1], BRANCH)
            parts = (
                dot_nn(score_grad, q_ref[at, lanes(pair)]),
                dot_nn(probs, g_ref[at, lanes(pair)]),
            )
            for which in range(2):
                held = sums[tile][which]
                if head == 0:
                    sums[tile][which] = parts[which]
                else:
                    first = head_lanes(held.shape, 1, 0)
                    sums[tile][which] = jnp.where(first, held, parts[which])
            mine = slice(head * HEAD_DIM, (head + 1) * HEAD_DIM)
            dqt_ref[pair, mine, at] += dot_nn(key_block(tile)[1][mine], score_grad)

        ready = start(*work[0])
        held = None
        for at, item in enumerate(work):
            now = ready
            if at + 1 < len(work):
                ready = start(*work[at + 1])
            done = middle(*item, *now)
            if held is not None:
                finish(*held)
            held = (*item, *done)
        finish(*held)
        return sums

    def causal(key_row, query_row):
        def mask_of(probs):
            keys = lax.broadcasted_iota(jnp.int32, probs.shape, 0) + key_row
            at = lax.broadcasted_iota(jnp.int32, probs.shape, 1) + query_row
            return jnp.where(keys <= at, probs, 0.0)

        return mask_of

    def put(pair, row, dk, dv):
        at = pl.ds(row, BRANCH)
        k_ref[at, lanes(pair)] = (dk * scale).astype(k_ref.dtype)
        v_ref[at, lanes(pair)] = dv.astype(v_ref.dtype)

    def pass_down(piece):
        at = pl.ds(pl.multiple_of(piece * PIECE, PIECE), PIECE)
        return pltpu.make_async_remote_copy(
            src_ref=rows_ref.at[at], dst_ref=land_ref.at[at],
            send_sem=row_send.at[piece], recv_sem=row_recv.at[piece],
            device_id=(spot, lax.rem(place + tensor - 1, tensor)), device_id_type=MESH,
        )

    def row_grad(b):
        at = block_at(b)
        return dot_nt(k_ref[at], weight_ref[1]) + dot_nt(v_ref[at], weight_ref[2])

    def hand_down(b, total):
        rows_ref[block_at(b)] = total.astype(rows_ref.dtype)

        @pl.when(place == tensor - 1)
        def _():
            for piece in range(BRANCH // PIECE):
                pass_down(b * (BRANCH // PIECE) + piece).start()

    def joined(piece):
        at = pl.ds(pl.multiple_of(piece * PIECE, PIECE), PIECE)
        return rows_ref[at].astype(jnp.float32) + land_ref[at].astype(jnp.float32)

    middle_place = (place > 0) & (place < tensor - 1)
    late = 3 * jnp.maximum(tensor - 2 - place, 0)
    first_relay = jnp.where(place > 1, 0, pieces)
    last_relay = jnp.where(middle_place, 2 * pieces, first_relay)

    def piece_of(order):
        return lax.rem(order + pieces, 2 * pieces)

    def serve(first, last):
        def one(order, carry):
            piece = piece_of(order)
            pass_down(piece).wait_recv()
            at = pl.ds(pl.multiple_of(piece * PIECE, PIECE), PIECE)
            rows_ref[at] = joined(piece).astype(rows_ref.dtype)
            pass_down(piece).start()
            return carry

        low = jnp.clip(first - late, first_relay, last_relay)
        lax.fori_loop(low, jnp.clip(last - late, low, last_relay), one, 0)

    @pl.loop(0, pairs)
    def _(pair):
        @pl.when(place == 0)
        def _():
            for ref in (k_ref, v_ref):
                ref[rows : 3 * rows, lanes(pair)] = jnp.zeros((2 * rows, 128), ref.dtype)

        @pl.when(place > 0)
        def _():
            def seen_parent(probs):
                return jnp.where(place > 1, probs, 0.0)

            spots = range(0, rows, BRANCH)
            sums = sweep(pair, [(rows + at, at, seen_parent) for at in spots])
            for at, part in zip(spots, sums):
                put(pair, rows + at, *part)

    send_slabs(groups)

    @pl.loop(0, blocks)
    def _(leaf):
        out_ref[block_at(leaf)] = row_grad(blocks + leaf)

    for branch in range(blocks):
        total = None
        for leaf in range(blocks):
            at = leaf * blocks + branch
            part = out_ref[leaf * BRANCH : (leaf + 1) * BRANCH] * parent_ref[at : at + 1]
            total = part if total is None else total + part
        hand_down(blocks + branch, total)

    stage(0).start()

    @pl.loop(0, blocks)
    def _(b):
        row = pl.multiple_of(b * BRANCH, BRANCH)

        @pl.loop(0, pairs)
        def _(pair):
            def finish_block(masked):
                tiles = [
                    (row, first, causal(row, first) if masked else None)
                    for first in range(0, rows, BRANCH)
                ]
                sums = sweep(pair, tiles)
                put(pair, row, sum(part[0] for part in sums), sum(part[1] for part in sums))

            @pl.when(place == 0)
            def _():
                finish_block(True)

            @pl.when(place > 0)
            def _():
                finish_block(False)

            slot = b * pairs + pair
            serve(slot - 1, slot)

        for _half in range(2):
            part = b * 2 + _half

            @pl.when(part < 3 * rows // stage_rows)
            def _():
                stage(part).wait()

                @pl.when(part + 1 < 3 * rows // stage_rows)
                def _():
                    stage(part + 1).start()

                at = pl.ds(pl.multiple_of(part * stage_rows, stage_rows), stage_rows)
                seen_ref[:, at] = stage_ref[lax.rem(part, 2)].T

        hand_down(b, row_grad(b))

    served = blocks * pairs - 1

    gain_ref[...] = jnp.zeros_like(gain_ref)

    @pl.loop(0, groups)
    def _(group):
        base = served + group * 4

        @pl.loop(0, 2)
        def _(half):
            pair = group * 2 + half

            @pl.when(place > 0)
            def _():
                spots = range(0, rows, BRANCH)
                sums = sweep(pair, [(2 * rows + at, at, causal(0, 0)) for at in spots])
                for at, part in zip(spots, sums):
                    put(pair, 2 * rows + at, *part)

            q_ref[:, lanes(pair)] = (dqt_ref[pair] * scale).T.astype(q_ref.dtype)
            serve(base + half, base + half + 1)

        cols = pl.ds(pl.multiple_of(group * GROUP, GROUP), GROUP)
        for kind, value in (
            (0, lambda: dot_nn(seen_ref[:, 2 * rows : 3 * rows], q_ref[:, cols])),
            (1, lambda: dot_nn(seen_ref[...], k_ref[:, cols])),
            (2, lambda: dot_nn(seen_ref[...], v_ref[:, cols])),
        ):
            product = value()
            scaled = product * weight_ref[kind, :, cols].astype(jnp.float32)
            gain_ref[...] += scaled[:, 0:128] + scaled[:, 128:256]
            keep(slab_ref.at[group], product, kind)
            if kind:
                serve(base + 1 + kind, base + 2 + kind)

        share_slabs(group)

        @pl.when(group > 0)
        def _():
            send_slabs(group - 1)

    served += groups * 4

    part_ref[...] = small_ref[...]
    gains = jnp.sum(gain_ref[...].T, axis=0, keepdims=True)
    for row in range(width // 128):
        part_ref[0, row : row + 1, :] = gains[:, row * 128 : (row + 1) * 128]

    def scatter(step):
        to = lax.rem(me + step, ways)
        return pltpu.make_async_remote_copy(
            src_ref=part_ref.at[to], dst_ref=part_land.at[me],
            send_sem=small_send.at[step], recv_sem=small_recv.at[me],
            device_id=device(to), device_id_type=MESH,
        )

    def arrival(step):
        source = lax.rem(me - step + ways, ways)
        return pltpu.make_async_remote_copy(
            src_ref=part_ref.at[source], dst_ref=part_land.at[source],
            send_sem=small_send.at[step], recv_sem=small_recv.at[source],
            device_id=device(lax.rem(me + step, ways)), device_id_type=MESH,
        )

    def spread(step):
        return pltpu.make_async_remote_copy(
            src_ref=total_ref.at[me], dst_ref=total_ref.at[me],
            send_sem=spread_send.at[step], recv_sem=spread_recv.at[me],
            device_id=device(lax.rem(me + step, ways)), device_id_type=MESH,
        )

    def landing(step):
        source = lax.rem(me - step + ways, ways)
        return pltpu.make_async_remote_copy(
            src_ref=total_ref.at[source], dst_ref=total_ref.at[source],
            send_sem=spread_send.at[step], recv_sem=spread_recv.at[source],
            device_id=device(lax.rem(me + step, ways)), device_id_type=MESH,
        )

    @pl.loop(1, ways)
    def _(step):
        scatter(step).start()

    send_slabs(groups - 1)

    @pl.loop(0, blocks)
    def _(b):
        at = block_at(b)
        out_ref[at] = row_grad(2 * blocks + b) + dot_nt(q_ref[at], weight_ref[0])
        serve(served + 2 * b, served + 2 * b + 2)

    served += 2 * blocks

    def add(step, total):
        arrival(step).wait_recv()
        return total + part_land[lax.rem(me - step + ways, ways)]

    total_ref[me] = lax.fori_loop(1, ways, add, part_ref[me])

    @pl.loop(1, ways)
    def _(step):
        spread(step).start()

    serve(served, jnp.maximum(served, 2 * pieces) + late)

    kinds = [[], [], [], []]
    for group in range(groups + 1):

        def add_slab(step, total):
            take(group, step).wait_recv()
            return total + chip_land[group, chip_at(chips - step)].astype(jnp.float32)

        total = lax.fori_loop(1, chips, add_slab, slab_ref[group, spot].astype(jnp.float32))
        for part in range(total.shape[1] // GROUP):
            kinds[3 if group == groups else part].append(
                total[:, part * GROUP : (part + 1) * GROUP]
            )

    share = width // tensor
    kinds = [jnp.concatenate(parts, axis=1) for parts in kinds]
    for target in range(tensor):
        mine = jnp.concatenate(
            [kind[:, target * share : (target + 1) * share] for kind in kinds], axis=1
        )
        line_out[target] = mine.astype(line_out.dtype)

        @pl.when(place == target)
        def _():
            sum_ref[...] = mine

    def line(step):
        return pltpu.make_async_remote_copy(
            src_ref=line_out.at[along(step)], dst_ref=line_land.at[place],
            send_sem=line_send.at[step], recv_sem=line_recv.at[place],
            device_id=(spot, along(step)), device_id_type=MESH,
        )

    def line_in(step):
        source = along(tensor - step)
        return pltpu.make_async_remote_copy(
            src_ref=line_out.at[source], dst_ref=line_land.at[source],
            send_sem=line_send.at[step], recv_sem=line_recv.at[source],
            device_id=(spot, along(step)), device_id_type=MESH,
        )

    for step in range(1, tensor):
        line(step).start()

    @pl.when(place < 2)
    def _():
        @pl.loop(0, pieces)
        def _(piece):
            source = place * pieces + piece
            pass_down(source).wait_recv()
            at = pl.ds(pl.multiple_of(piece * PIECE, PIECE), PIECE)
            out_ref[at] += joined(source)

    for step in range(1, tensor):
        line_in(step).wait_recv()
        sum_ref[...] += line_land[along(tensor - step)].astype(jnp.float32)

    @pl.loop(1, ways)
    def _(step):
        landing(step).wait_recv()

    for step in range(1, tensor):
        line(step).wait_send()

    @pl.loop(1, ways)
    def _(step):
        scatter(step).wait_send()
        spread(step).wait_send()

    for group in range(groups + 1):

        @pl.loop(0, chips)
        def _(step):
            halve(group, step).wait_send()

            @pl.when(step > 0)
            def _():
                give(group, step).wait_send()

    sent = jnp.where(place == tensor - 1, 2 * pieces, last_relay)
    first_sent = jnp.where(place == tensor - 1, 0, first_relay)

    def sent_one(order, carry):
        pass_down(piece_of(order)).wait_send()
        return carry

    lax.fori_loop(first_sent, sent, sent_one, 0)


def backward(parents, q, k, v, o, branch_grad, seen, weights, lse, small):
    dp, tensor = lax.axis_size("dp"), lax.axis_size("tensor")
    ways = dp * tensor
    rows, width = q.shape
    seen_rows = k.shape[0]
    depth = width // dp
    padded = -(-depth // 16) * 16
    pairs, groups, pieces = width // 128, width // GROUP, rows // PIECE
    slab = (padded, width)
    low, full = jnp.bfloat16, jnp.float32
    dma = pltpu.SemaphoreType.DMA
    anywhere = pl.BlockSpec(memory_space=pl.ANY)
    here = pl.BlockSpec(memory_space=pltpu.VMEM)
    out, block, total = pl.pallas_call(
        lambda *refs: back_kernel(dp, tensor, depth, *refs),
        out_shape=(
            jax.ShapeDtypeStruct((rows, width), full),
            jax.ShapeDtypeStruct((padded, width), full),
            jax.ShapeDtypeStruct(small.shape, full),
        ),
        in_specs=[here] + [anywhere] * 7 + [here] * 2,
        out_specs=[here, here, here],
        scratch_shapes=[
            pltpu.VMEM((rows, width), low),
            pltpu.VMEM((seen_rows, width), low),
            pltpu.VMEM((seen_rows, width), low),
            pltpu.VMEM((rows, width), low),
            pltpu.VMEM((rows, width), low),
            pltpu.VMEM((rows, width), low),
            pltpu.VMEM((2, rows // 2, width), low),
            pltpu.VMEM((width, seen_rows), low),
            pltpu.VMEM(weights.shape, low),
            pltpu.VMEM((pairs, 2, rows), full),
            pltpu.VMEM((pairs, 128, rows), full),
            pltpu.VMEM((2 * rows, width), low),
            pltpu.VMEM((2 * rows, width), low),
            pltpu.VMEM((width, 128), full),
            pltpu.VMEM((groups + 1, dp) + slab, low),
            pltpu.VMEM((groups + 1, dp // 2) + slab, low),
            pltpu.VMEM((groups + 1, dp // 2) + slab, low),
            pltpu.VMEM((tensor, padded, width), low),
            pltpu.VMEM((tensor, padded, width), low),
            pltpu.VMEM(small.shape, full),
            pltpu.VMEM(small.shape, full),
            dma((3,)), dma((3, pairs)), dma((2,)),
            dma((2 * pieces,)), dma((2 * pieces,)),
            dma((groups + 1, dp // 2)), dma((groups + 1, dp // 2)),
            dma((groups + 1, dp // 2)), dma((groups + 1, dp // 2)),
            dma((tensor,)), dma((tensor,)),
            dma((ways,)), dma((ways,)), dma((ways,)), dma((ways,)),
        ],
        compiler_params=pltpu.CompilerParams(
            collective_id=3, has_side_effects=True, vmem_limit_bytes=62 << 20
        ),
        name="attend_backward",
    )(parents, q, k, v, o, branch_grad, seen, weights, lse, small)
    return out, block[:depth], total


HALF_ROOT = math.sqrt(0.5)
PDF_SCALE = 1.0 / math.sqrt(2.0 * math.pi)
CHUNK = 512
BAND = 256
NEAR = 512


def expert_kernel(
    dp, tensor, x_in, g_in, w_in, w_out, result_ref, back_ref, in_grad_ref, out_grad_ref,
    x_ref, g_ref, active_ref, slope_ref, keep_ref, part_ref, land_ref, home_ref,
    back_part, back_land, back_home, grad_ref, grad_land,
    x_send, x_recv, x_pair_send, x_pair_recv, g_send, g_recv, g_pair_send, g_pair_recv,
    y_pair_send, y_pair_recv, y_send, y_recv, d_pair_send, d_pair_recv, d_send, d_recv,
    line_send, line_recv,
):
    spot, place = lax.axis_index("dp"), lax.axis_index("tensor")
    chips = dp // 2
    chip, core = spot // 2, lax.rem(spot, 2)
    partner = (chip * 2 + 1 - core, place)
    capacity = x_in.shape[0] // chips

    def ahead(step):
        return (lax.rem(chip + step, chips) * 2 + core, place)

    def behind(step):
        return (lax.rem(chip - step + chips, chips) * 2 + core, place)

    def at(side, step):
        return pl.ds(pl.multiple_of((side * chips + step) * capacity, capacity), capacity)

    def along(step):
        return lax.rem(place + step, tensor)

    greet(
        [ahead(step) for step in range(1, chips)]
        + [partner]
        + [(spot, along(step)) for step in range(1, tensor)]
    )
    share, near = out_grad_ref.shape
    width = x_in.shape[1]

    def line(step):
        return pltpu.make_async_remote_copy(
            src_ref=grad_ref.at[along(step)], dst_ref=grad_land.at[place],
            send_sem=line_send.at[step], recv_sem=line_recv.at[place],
            device_id=(spot, along(step)), device_id_type=MESH,
        )

    def line_in(step):
        source = along(tensor - step)
        return pltpu.make_async_remote_copy(
            src_ref=grad_ref.at[source], dst_ref=grad_land.at[source],
            send_sem=line_send.at[step], recv_sem=line_recv.at[source],
            device_id=(spot, along(step)), device_id_type=MESH,
        )

    def copy(source, target, send, recv, step, where):
        return pltpu.make_async_remote_copy(
            src_ref=source, dst_ref=target, send_sem=send.at[step], recv_sem=recv.at[step],
            device_id=where, device_id_type=MESH,
        )

    def go_x(step):
        return copy(x_in.at[at(0, step)], x_ref.at[at(0, step)], x_send, x_recv, step, ahead(step))

    def go_g(step):
        return copy(g_in.at[at(0, step)], g_ref.at[at(0, step)], g_send, g_recv, step, ahead(step))

    def pair_x(step):
        return copy(
            x_ref.at[at(0, step)], x_ref.at[at(1, step)], x_pair_send, x_pair_recv, step, partner
        )

    def pair_g(step):
        return copy(
            g_ref.at[at(0, step)], g_ref.at[at(1, step)], g_pair_send, g_pair_recv, step, partner
        )

    def pair_y(step):
        here = at(0, step)
        return copy(part_ref.at[here], land_ref.at[here], y_pair_send, y_pair_recv, step, partner)

    def pair_d(step):
        here = at(0, step)
        return copy(back_part.at[here], back_land.at[here], d_pair_send, d_pair_recv, step, partner)

    def home_y(step):
        here = at(0, step)
        return copy(home_ref.at[here], result_ref.at[here], y_send, y_recv, step, behind(step))

    def home_d(step):
        here = at(0, step)
        return copy(back_home.at[here], back_ref.at[here], d_send, d_recv, step, behind(step))

    @pl.loop(1, chips)
    def _(step):
        go_x(step).start()

    x_ref[at(0, 0)] = x_in[at(0, 0)]
    pair_x(0).start()
    g_ref[at(0, 0)] = g_in[at(0, 0)]

    def ahead_pass(side, step):
        rows = x_ref[at(side, step)]
        total = None
        for first in range(0, w_in.shape[1], CHUNK):
            cols = slice(first, first + CHUNK)
            up = dot_nn(rows, w_in[:, cols])
            below = 0.5 * (1.0 + lax.erf(up * HALF_ROOT))
            active = (up * below).astype(jnp.bfloat16)
            slope = below + up * (jnp.exp(-0.5 * up * up) * PDF_SCALE)
            active_ref[at(side, step), cols] = active
            slope_ref[at(side, step), cols] = slope.astype(jnp.bfloat16)
            part = dot_nn(active, w_out[cols])
            total = part if total is None else total + part
        return total

    def back_pass(side, step):
        grads = g_ref[at(side, step)]
        total = None
        for first in range(0, w_in.shape[1], CHUNK):
            cols = slice(first, first + CHUNK)
            active_grad = dot_nt(grads, w_out[cols])
            up_grad = active_grad * slope_ref[at(side, step), cols].astype(jnp.float32)
            up_grad = up_grad.astype(jnp.bfloat16)
            slope_ref[at(side, step), cols] = up_grad
            part = dot_nt(up_grad, w_in[:, cols])
            total = part if total is None else total + part
        return total

    keep_ref[at(0, 0)] = ahead_pass(0, 0)

    @pl.loop(1, chips)
    def _(step):
        go_x(step).wait_recv()
        pair_x(step).start()
        go_g(step).start()
        keep_ref[at(0, step)] = ahead_pass(0, step)

    pair_g(0).start()

    @pl.loop(0, chips)
    def _(step):
        pair_x(step).wait_recv()
        part_ref[at(0, step)] = ahead_pass(1, step).astype(part_ref.dtype)
        pair_y(step).start()

    @pl.loop(1, chips)
    def _(step):
        go_g(step).wait_recv()
        pair_g(step).start()

    @pl.loop(0, chips)
    def _(step):
        pair_y(step).wait_recv()
        here = at(0, step)
        total = keep_ref[here] + land_ref[here].astype(jnp.float32)
        home_ref[here] = total.astype(home_ref.dtype)

        @pl.when(step > 0)
        def _():
            home_y(step).start()

        @pl.when(step == 0)
        def _():
            result_ref[here] = total.astype(result_ref.dtype)

    @pl.loop(0, chips)
    def _(step):
        pair_g(step).wait_recv()

    @pl.loop(1, tensor + 1)
    def _(turn):
        step = lax.rem(turn, tensor)
        part = along(step)
        for first in range(0, share, 128):
            cols = pl.ds(pl.multiple_of(part * share + first, 128), 128)
            product = dot_tn(active_ref[:, cols], g_ref[...]).astype(grad_ref.dtype)
            grad_ref[part, first : first + 128] = product[:, :near]
            in_grad_ref[cols, width:] = product[:, near:]

        @pl.when(step > 0)
        def _():
            line(step).start()

    @pl.loop(0, chips)
    def _(step):
        back_part[at(0, step)] = back_pass(1, step).astype(back_part.dtype)
        pair_d(step).start()

    @pl.loop(0, chips)
    def _(turn):
        step = chips - 1 - turn
        here = at(0, step)
        total = back_pass(0, step)
        pair_d(step).wait_recv()
        total = (total + back_land[here].astype(jnp.float32)).astype(back_home.dtype)
        back_home[here] = total

        @pl.when(step > 0)
        def _():
            home_d(step).start()

        @pl.when(step == 0)
        def _():
            back_ref[here] = total

    @pl.loop(0, w_in.shape[1] // BAND)
    def _(band):
        cols = pl.ds(pl.multiple_of(band * BAND, BAND), BAND)
        product = dot_tn(slope_ref[:, cols], x_ref[...])
        in_grad_ref[cols, 0:width] = product.astype(in_grad_ref.dtype)

    out_grad_ref[...] = grad_ref[place].astype(jnp.float32)
    for step in range(1, tensor):
        line_in(step).wait_recv()
        out_grad_ref[...] += grad_land[along(tensor - step)].astype(jnp.float32)
    for step in range(1, tensor):
        line(step).wait_send()

    @pl.loop(1, chips)
    def _(step):
        home_y(step).wait_recv()
        home_d(step).wait_recv()

    @pl.loop(0, chips)
    def _(step):
        pair_x(step).wait_send()
        pair_g(step).wait_send()
        pair_y(step).wait_send()
        pair_d(step).wait_send()

    @pl.loop(1, chips)
    def _(step):
        go_x(step).wait_send()
        go_g(step).wait_send()
        home_y(step).wait_send()
        home_d(step).wait_send()


def run_experts(slot_rows, slot_grads, w_in, w_out):
    dp, tensor = lax.axis_size("dp"), lax.axis_size("tensor")
    rows, width = slot_rows.shape
    hidden = w_in.shape[1]
    low = jnp.bfloat16
    here = pl.BlockSpec(memory_space=pltpu.VMEM)
    near = pltpu.VMEM((rows, width), low)
    both = pltpu.VMEM((2 * rows, width), low)
    middle = pltpu.VMEM((2 * rows, hidden), low)
    return pl.pallas_call(
        lambda *refs: expert_kernel(dp, tensor, *refs),
        out_shape=(
            jax.ShapeDtypeStruct((rows, width), low),
            jax.ShapeDtypeStruct((rows, width), low),
            jax.ShapeDtypeStruct((hidden, 2 * width - NEAR), low),
            jax.ShapeDtypeStruct((hidden // tensor, NEAR), jnp.float32),
        ),
        in_specs=[here] * 4,
        out_specs=[here] * 4,
        scratch_shapes=[
            both, both, middle, middle, pltpu.VMEM((rows, width), jnp.float32),
            near, near, near, near, near, near,
            pltpu.VMEM((tensor, hidden // tensor, NEAR), low),
            pltpu.VMEM((tensor, hidden // tensor, NEAR), low),
        ]
        + [pltpu.SemaphoreType.DMA((dp // 2,))] * 16
        + [pltpu.SemaphoreType.DMA((tensor,))] * 2,
        compiler_params=pltpu.CompilerParams(
            collective_id=4, has_side_effects=True, vmem_limit_bytes=60 << 20
        ),
        name="run_experts",
    )(slot_rows, slot_grads, w_in, w_out)


norm_eps = 1e-05
route_scale = 3.0
masked_score = -1e30
highest = lax.Precision.HIGHEST


def layer_norm(values, norm_gain):
    centred = values - jnp.mean(values, axis=-1, keepdims=True)
    spread = jnp.mean(centred * centred, axis=-1, keepdims=True)
    return centred * lax.rsqrt(spread + norm_eps) * norm_gain


def unit_rows(values):
    return values * lax.rsqrt(jnp.sum(values * values, axis=-1, keepdims=True) + 1.0)


def router_gate(normed, router_proj, expert_embed, picked):
    routed = jnp.dot(normed, router_proj, precision=highest)
    logits = route_scale * jnp.dot(unit_rows(routed), unit_rows(expert_embed).T, precision=highest)
    return jnp.sum(jax.nn.softmax(logits, axis=-1) * picked, axis=-1)


def gelu_exact(values):
    return jax.nn.gelu(values, approximate=False)


def slot_table(route_ids, order_ids, capacity):
    same_expert = route_ids[:, None] == route_ids[None, :]
    earlier = order_ids[None, :] < order_ids[:, None]
    ranking = jnp.sum(jnp.where(same_expert & earlier, 1, 0), axis=1).astype(jnp.int32)
    kept_mask = ranking < capacity
    column = route_ids * capacity + jnp.minimum(ranking, capacity - 1)
    return (column, kept_mask)


def low_dot(rows, weight):
    return jnp.dot(rows, weight, preferred_element_type=jnp.float32).astype(jnp.bfloat16)


def shards(
    tokens,
    norm1_gain,
    qkv_weight,
    attn_proj,
    norm2_gain,
    router_proj,
    expert_embed,
    expert_in,
    expert_out,
    routes,
    orders,
    leaf_parent,
    cotangent,
):
    rows_here = tokens.shape[0]
    model_width = tokens.shape[1]
    experts = expert_embed.shape[0]
    capacity = rows_here // experts
    dp_size, tensor_size = lax.axis_size("dp"), lax.axis_size("tensor")

    hidden = tokens.astype(jnp.float32)
    norm1_back = jax.vjp(layer_norm, hidden, norm1_gain)[1]
    flat_qkv = qkv_weight.reshape(qkv_weight.shape[0], -1)
    place = lax.axis_index("tensor")
    leaf_blocks = rows_here // BRANCH
    first_leaf = jnp.maximum(place - 2, 0) * leaf_blocks
    leaf_parents = lax.dynamic_slice_in_dim(leaf_parent[0], first_leaf, leaf_blocks, 0) - 1
    parents = (leaf_parents[:, None] == jnp.arange(leaf_blocks)[None, :]).astype(jnp.float32)
    parents = jnp.broadcast_to(parents.reshape(-1, 1), (leaf_blocks * leaf_blocks, model_width))
    seen_in, weights, query_rows, key_rows, value_rows, attended, log_totals = front(
        tokens, norm1_gain, jnp.concatenate([flat_qkv, attn_proj.T], axis=1), parents
    )
    proj_back = weights[3]
    branch_out = jnp.einsum(
        "sc,dc->sd", attended, proj_back, preferred_element_type=jnp.float32
    )
    mid_stream = hidden + branch_out
    normed_mid, norm2_back = jax.vjp(layer_norm, mid_stream, norm2_gain)
    moe_in = normed_mid.astype(jnp.bfloat16)
    route_ids = routes[:, 0]
    near_route = (route_ids - lax.axis_index("dp") // 2) % experts
    column, kept_mask = slot_table(near_route, orders[0], capacity)
    picked = (route_ids[:, None] == jnp.arange(experts)[None, :]).astype(jnp.float32)
    gate_value, gate_back = jax.vjp(
        lambda normed_rows, route_proj, embed_rows: router_gate(
            normed_rows, route_proj, embed_rows, picked
        ),
        moe_in.astype(jnp.float32),
        router_proj,
        expert_embed,
    )
    select = (
        (column[:, None] == jnp.arange(experts * capacity)[None, :]) & kept_mask[:, None]
    ).astype(jnp.bfloat16)
    def to_slots(token_rows):
        return jnp.einsum(
            "ts,td->sd", select, token_rows, preferred_element_type=jnp.float32
        ).astype(jnp.bfloat16)

    def from_slots(slot_rows):
        return jnp.dot(select, slot_rows, preferred_element_type=jnp.float32)

    upstream = cotangent.astype(jnp.float32)
    slot_grads = to_slots((gate_value[:, None] * upstream).astype(jnp.bfloat16))
    result_rows, grad_rows, far_grads, near_grads = run_experts(
        to_slots(moe_in), slot_grads, expert_in, expert_out
    )
    expert_result = from_slots(result_rows)
    output = (mid_stream + gate_value[:, None] * expert_result).astype(jnp.bfloat16)
    moe_grad = from_slots(grad_rows)
    gate_grad = jnp.sum(upstream * expert_result, axis=-1)
    router_part, proj_grad, embed_grad = gate_back(gate_grad)
    mid_part, gain2_grad = norm2_back(moe_grad + router_part)
    mid_grad = upstream + mid_part
    far_grads = lax.psum_scatter(
        far_grads, "tensor", scatter_dimension=0, tiled=True
    ).astype(jnp.float32)
    expert_in_grad = far_grads[:, :model_width].T
    expert_out_grad = jnp.concatenate([near_grads, far_grads[:, model_width:]], axis=1)
    branch_grad = mid_grad.astype(jnp.bfloat16)
    later = [gain2_grad, proj_grad, embed_grad]
    flat = jnp.concatenate([jnp.zeros_like(norm1_gain)] + [part.reshape(-1) for part in later])
    ways = dp_size * tensor_size
    lanes = -(-flat.shape[0] // (ways * 8 * 128)) * 128
    small = jnp.pad(flat, (0, ways * 8 * lanes - flat.shape[0])).reshape(ways, 8, lanes)
    input_grad, grad_block, totals = backward(
        parents, query_rows, key_rows, value_rows, attended, branch_grad, seen_in, weights,
        log_totals, small,
    )
    qkv_grad = grad_block[:, : flat_qkv.shape[1]].reshape(qkv_weight.shape)
    attn_proj_grad = grad_block[:, flat_qkv.shape[1] :].T
    totals = totals.reshape(-1)
    gain1_sum = totals[:model_width] / norm1_gain
    gain2_sum, router_sum, embed_sum = (
        totals[first : first + part.size].reshape(part.shape)
        for first, part in zip(
            (model_width, 2 * model_width, 2 * model_width + proj_grad.size), later
        )
    )
    token_part, _ = norm1_back(input_grad)
    token_grad = mid_grad + token_part
    return (
        output,
        token_grad,
        gain1_sum,
        qkv_grad,
        attn_proj_grad,
        gain2_sum,
        router_sum,
        embed_sum,
        expert_in_grad,
        expert_out_grad,
    )


def solution(mesh):
    in_specs = (
        P(("dp", "tensor"), None),
        P(),
        P("dp", None, "tensor"),
        P("tensor", "dp"),
        P(),
        P(),
        P(),
        P(None, "dp"),
        P("dp", None),
        P(("dp", "tensor"), None),
        P(("dp", "tensor"), None),
        P("dp", None),
        P(("dp", "tensor"), None),
    )
    out_specs = (
        P(("dp", "tensor"), None),
        P(("dp", "tensor"), None),
        P(),
        P("dp", None, "tensor"),
        P("tensor", "dp"),
        P(),
        P(),
        P(),
        P(None, ("dp", "tensor")),
        P(("dp", "tensor"), None),
    )
    return jax.shard_map(shards, mesh=mesh, in_specs=in_specs, out_specs=out_specs, check_vma=False)
```

```python
import functools
import math

import jax
import jax.numpy as jnp
from jax import lax
from jax.experimental import pallas as pl
from jax.experimental.pallas import tpu as pltpu
from jax.sharding import PartitionSpec as P

HEAD_DIM = 64
TRUNK = 1024
BRANCH = 256
MASKED = -1e30
LOG2E = math.log2(math.e)
EXP_SCALE = HEAD_DIM ** (-0.5) * LOG2E

NT = (((1,), (1,)), ((), ()))
NN = (((1,), (0,)), ((), ()))


def dot_nt(a, b):
    return lax.dot_general(a, b, NT, preferred_element_type=jnp.float32)


def dot_nn(a, b):
    return lax.dot_general(a, b, NN, preferred_element_type=jnp.float32)


def head_lanes(shape, dim, head):
    return lax.broadcasted_iota(jnp.int32, shape, dim) // HEAD_DIM == head


MESH = pl.DeviceIdType.MESH
PIECE = 64


def greet(peers):
    barrier = pltpu.get_barrier_semaphore()
    for peer in peers:
        pl.semaphore_signal(barrier, inc=1, device_id=peer, device_id_type=MESH)
    pl.semaphore_wait(barrier, len(peers))


def front_kernel(
    dp, tensor, depth, token_ref, scale_ref, block_ref, parent_ref,
    seen_out, weight_out, q_out, k_out, v_out, o_out, lse_ref,
    own_ref, seen_ref, land_ref, weight_ref, q_ref, k_ref, v_ref, o_ref, acc_ref, top_ref, spare_ref,
    row_send, row_recv, line_send, line_recv, chip_send, chip_recv, pair_send, pair_recv, save_sem,
):
    spot, place = lax.axis_index("dp"), lax.axis_index("tensor")
    chip, core = spot // 2, lax.rem(spot, 2)
    chips = dp // 2
    rows, width = own_ref.shape
    pieces = rows // PIECE
    pairs = width // 128
    blocks = rows // BRANCH
    share = width // tensor

    @pl.loop(0, blocks)
    def _(b):
        at = pl.ds(pl.multiple_of(b * BRANCH, BRANCH), BRANCH)
        normed = layer_norm(token_ref[at].astype(jnp.float32), scale_ref[...])
        own_ref[at] = normed.astype(own_ref.dtype)

    partner = (chip * 2 + 1 - core, place)

    def along(step):
        return lax.rem(place + step, tensor)

    def chip_at(step):
        return lax.rem(chip + step, chips)

    greet(
        [(spot, along(step)) for step in range(1, tensor)]
        + [(chip_at(step) * 2 + core, place) for step in range(1, chips)]
        + [partner]
    )

    def pass_on(piece, fresh):
        at = pl.ds(pl.multiple_of(piece * PIECE, PIECE), PIECE)
        source = seen_ref.at[at]
        if fresh:
            here = lax.rem(piece, pieces) * PIECE
            source = own_ref.at[pl.ds(pl.multiple_of(here, PIECE), PIECE)]
        return pltpu.make_async_remote_copy(
            src_ref=source, dst_ref=seen_ref.at[at],
            send_sem=row_send.at[piece], recv_sem=row_recv.at[piece],
            device_id=(spot, lax.rem(place + 1, tensor)), device_id_type=MESH,
        )

    def line(step):
        return pltpu.make_async_remote_copy(
            src_ref=block_ref, dst_ref=land_ref.at[place, spot],
            send_sem=line_send.at[step], recv_sem=line_recv.at[place],
            device_id=(spot, along(step)), device_id_type=MESH,
        )

    def line_in(step):
        source = along(tensor - step)
        return pltpu.make_async_remote_copy(
            src_ref=block_ref, dst_ref=land_ref.at[source, spot],
            send_sem=line_send.at[step], recv_sem=line_recv.at[source],
            device_id=(spot, along(step)), device_id_type=MESH,
        )

    def plane(part, step):
        block = land_ref.at[part, spot]
        return pltpu.make_async_remote_copy(
            src_ref=block, dst_ref=block,
            send_sem=chip_send.at[part, step], recv_sem=chip_recv.at[part, chip],
            device_id=(chip_at(step) * 2 + core, place), device_id_type=MESH,
        )

    def plane_in(part, step):
        source = chip_at(chips - step)
        block = land_ref.at[part, source * 2 + core]
        return pltpu.make_async_remote_copy(
            src_ref=block, dst_ref=block,
            send_sem=chip_send.at[part, step], recv_sem=chip_recv.at[part, source],
            device_id=(chip_at(step) * 2 + core, place), device_id_type=MESH,
        )

    def across(part, source, source_core):
        block = land_ref.at[part, source * 2 + source_core]
        return pltpu.make_async_remote_copy(
            src_ref=block, dst_ref=block,
            send_sem=pair_send.at[part, source], recv_sem=pair_recv.at[part, source],
            device_id=partner, device_id_type=MESH,
        )

    for step in range(1, tensor):
        line(step).start()

    @pl.when(place == 0)
    def _():
        @pl.loop(0, pieces)
        def _(piece):
            pass_on(piece, True).start()

    land_ref[place, spot] = block_ref[...]
    seen_ref[2 * rows :] = own_ref[...]

    @pl.when(place < 2)
    def _():
        seen_ref[rows : 2 * rows] = own_ref[...]

    @pl.when(place == 0)
    def _():
        seen_ref[0:rows] = own_ref[...]

    def serve(first, last):
        @pl.loop(first, last)
        def _(piece):
            takes = (place > 1) | ((place > 0) & (piece < pieces))

            @pl.when(takes)
            def _():
                pass_on(piece, False).wait_recv()

                @pl.when(place < tensor - 1)
                def _():
                    pass_on(piece, False).start()

    def part_of(index):
        return pl.ds(index * rows, rows)

    saves = [
        pltpu.make_async_copy(source, target, save_sem.at[index])
        for index, (source, target) in enumerate(
            [(weight_ref, weight_out), (q_ref, q_out), (o_ref, o_out)]
            + [
                (held.at[part_of(part)], target.at[part_of(part)])
                for part in (2, 0, 1)
                for held, target in ((seen_ref, seen_out), (k_ref, k_out), (v_ref, v_out))
            ]
        )
    ]

    serve(0, pieces // 8)
    for step in range(tensor):
        part = along(tensor - step)
        if step:
            line_in(step).wait_recv()

        @pl.loop(1, chips)
        def _(hop):
            plane(part, hop).start()

        across(part, chip, core).start()
    serve(pieces // 8, (5 * pieces) // 8)
    for step in range(tensor):
        part = along(tensor - step)

        @pl.loop(1, chips)
        def _(hop):
            plane_in(part, hop).wait_recv()
            across(part, chip_at(chips - hop), core).start()

    serve((5 * pieces) // 8, pieces)

    @pl.when(place == 1)
    def _():
        @pl.loop(pieces, 2 * pieces)
        def _(piece):
            pass_on(piece, True).start()

    for part in range(tensor):

        @pl.loop(0, chips)
        def _(source):
            across(part, source, 1 - core).wait_recv()

    def ordered(source, kind):
        cols = slice(kind * share, (kind + 1) * share)
        return jnp.concatenate(
            [land_ref[part, source][:, cols] for part in range(tensor)], axis=1
        )

    if depth % 16:
        for kind in range(4):
            for source in range(dp):
                spare_ref[source * depth : (source + 1) * depth] = ordered(source, kind)[
                    0:depth
                ].astype(jnp.float32)
            weight_ref[kind] = spare_ref[...].astype(weight_ref.dtype)
    else:

        @pl.loop(0, dp)
        def _(source):
            at = pl.ds(pl.multiple_of(source * depth, depth), depth)
            for kind in range(4):
                weight_ref[kind, at] = ordered(source, kind)

    saves[0].start()

    def lanes(pair):
        return pl.ds(pl.multiple_of(pair * 128, 128), 128)

    def project(first, also_queries=False):
        @pl.loop(0, blocks)
        def _(b):
            at = pl.ds(pl.multiple_of(first + b * BRANCH, BRANCH), BRANCH)
            normed = seen_ref[at]
            k_ref[at] = dot_nn(normed, weight_ref[1]).astype(k_ref.dtype)
            v_ref[at] = dot_nn(normed, weight_ref[2]).astype(v_ref.dtype)
            if also_queries:
                here = pl.ds(pl.multiple_of(b * BRANCH, BRANCH), BRANCH)
                q_ref[here] = dot_nn(normed, weight_ref[0]).astype(q_ref.dtype)

    def attend_tiles(pair, tiles_of, opening):
        values, work = {}, [(block, head) for block in range(blocks) for head in range(2)]

        def value_tile(first, head):
            if (first, head) not in values:
                flipped = v_ref[first : first + BRANCH, lanes(pair)].T
                for side in range(2):
                    values[first, side] = jnp.where(
                        head_lanes(flipped.shape, 0, side), flipped, jnp.ones_like(flipped)
                    )
            return values[first, head]

        def start(block, head):
            queries = q_ref[block * BRANCH : (block + 1) * BRANCH, lanes(pair)]
            queries = jnp.where(
                head_lanes(queries.shape, 1, head), queries, jnp.zeros_like(queries)
            )
            scores = []
            for first, masked in tiles_of(block):
                tile = dot_nt(k_ref[first : first + BRANCH, lanes(pair)], queries)
                if masked:
                    keys = lax.broadcasted_iota(jnp.int32, tile.shape, 0)
                    at = lax.broadcasted_iota(jnp.int32, tile.shape, 1)
                    tile = jnp.where(keys <= at, tile, MASKED)
                scores.append(tile)
            top = jnp.max(functools.reduce(jnp.maximum, scores), axis=0, keepdims=True)
            return scores, top

        def middle(block, head, scores, top):
            cols = slice(block * BRANCH, (block + 1) * BRANCH)
            fade = None
            if not opening:
                before = top_ref[pair, head : head + 1, cols]
                top = jnp.maximum(before, top)
                fade = jnp.exp2((before - top) * EXP_SCALE)
            top_ref[pair, head : head + 1, cols] = top
            shift = top * EXP_SCALE
            return [
                jnp.exp2(tile * EXP_SCALE - shift).astype(jnp.bfloat16) for tile in scores
            ], fade

        def finish(block, head, probs, fade):
            cols = slice(block * BRANCH, (block + 1) * BRANCH)
            acc = None if opening else acc_ref[pair, head, :, cols] * fade
            for (first, _), tile in zip(tiles_of(block), probs):
                part = dot_nn(value_tile(first, head), tile)
                acc = part if acc is None else acc + part
            acc_ref[pair, head, :, cols] = acc

        ready, held = start(*work[0]), None
        for at, item in enumerate(work):
            now = ready
            if at + 1 < len(work):
                ready = start(*work[at + 1])
            done = middle(*item, *now)
            if held is not None:
                finish(*held)
            held = (*item, *done)
        finish(*held)

    project(2 * rows, True)
    for index in (1, 3, 4, 5):
        saves[index].start()
    serve(pieces, pieces + 2)

    @pl.loop(0, pairs)
    def _(pair):
        @pl.when(place == 0)
        def _():
            attend_tiles(
                pair,
                lambda block: [
                    (2 * rows + j * BRANCH, j == block) for j in range(block + 1)
                ],
                True,
            )

        @pl.when(place > 0)
        def _():
            attend_tiles(pair, lambda block: [(2 * rows + block * BRANCH, True)], True)

        @pl.when(lax.rem(pair, 2) == 1)
        def _():
            piece = pieces + 2 + pair // 2
            serve(piece, piece + 1)

    project(0)
    for index in (6, 7, 8):
        saves[index].start()
    served = pieces + 2 + pairs // 2
    per_pair = -(-(2 * pieces - served) // pairs)

    @pl.loop(0, pairs)
    def _(pair):
        @pl.when(place > 0)
        def _():
            attend_tiles(pair, lambda block: [(j * BRANCH, False) for j in range(blocks)], False)

        first = served + pair * per_pair
        serve(jnp.minimum(first, 2 * pieces), jnp.minimum(first + per_pair, 2 * pieces))

    @pl.when((place > 0) & (place < tensor - 1))
    def _():
        @pl.loop(0, 2 * pieces)
        def _(piece):
            pass_on(piece, False).wait_send()

    @pl.when(place > 1)
    def _():
        branches = [
            seen_ref[rows + branch * BRANCH : rows + (branch + 1) * BRANCH]
            for branch in range(blocks)
        ]
        for leaf in range(blocks):
            chosen = None
            for branch in range(blocks):
                at = leaf * blocks + branch
                part = branches[branch] * parent_ref[at : at + 1].astype(own_ref.dtype)
                chosen = part if chosen is None else chosen + part
            o_ref[leaf * BRANCH : (leaf + 1) * BRANCH] = chosen
        seen_ref[rows : 2 * rows] = o_ref[...]

    project(rows)
    for index in (9, 10, 11):
        saves[index].start()

    @pl.loop(0, pairs)
    def _(pair):
        @pl.when(place > 1)
        def _():
            attend_tiles(pair, lambda block: [(rows + block * BRANCH, False)], False)

        outs = []
        for head in range(2):
            mine, other = head * HEAD_DIM, (1 - head) * HEAD_DIM
            total = acc_ref[pair, head, other : other + 1]
            outs.append(acc_ref[pair, head, mine : mine + HEAD_DIM] / total)
            lse_ref[pair, head : head + 1] = (
                top_ref[pair, head : head + 1] * EXP_SCALE + jnp.log2(total)
            )
        o_ref[:, lanes(pair)] = jnp.concatenate(outs, axis=0).T.astype(o_ref.dtype)

    saves[2].start()
    for part in range(tensor):

        @pl.loop(0, chips)
        def _(source):
            across(part, source, core).wait_send()

        @pl.loop(1, chips)
        def _(hop):
            plane(part, hop).wait_send()

    for step in range(1, tensor):
        line(step).wait_send()

    @pl.when(place == 0)
    def _():
        @pl.loop(0, pieces)
        def _(piece):
            pass_on(piece, True).wait_send()

    for save in saves:
        save.wait()


def front(tokens, gain, block, parents):
    dp, tensor = lax.axis_size("dp"), lax.axis_size("tensor")
    rows, width = tokens.shape
    depth, cols = block.shape
    pieces, chips, pairs = rows // PIECE, dp // 2, width // 128
    padded = -(-depth // 16) * 16
    block = jnp.pad(block, ((0, padded - depth), (0, 0)))
    low, full = jnp.bfloat16, jnp.float32
    few, many = (rows, width), (3 * rows, width)
    weights = (4, width, width)
    dma = pltpu.SemaphoreType.DMA
    here = pl.BlockSpec(memory_space=pltpu.VMEM)
    anywhere = pl.BlockSpec(memory_space=pl.ANY)
    return pl.pallas_call(
        lambda *refs: front_kernel(dp, tensor, depth, *refs),
        out_shape=tuple(
            jax.ShapeDtypeStruct(shape, low) for shape in (many, weights, few, many, many, few)
        )
        + (jax.ShapeDtypeStruct((pairs, 2, rows), full),),
        in_specs=[here] * 4,
        out_specs=[anywhere] * 6 + [here],
        scratch_shapes=[
            pltpu.VMEM(few, low),
            pltpu.VMEM(many, low),
            pltpu.VMEM((tensor, dp, padded, cols), low),
            pltpu.VMEM(weights, low),
            pltpu.VMEM(few, low),
            pltpu.VMEM(many, low),
            pltpu.VMEM(many, low),
            pltpu.VMEM(few, low),
            pltpu.VMEM((pairs, 2, 128, rows), full),
            pltpu.VMEM((pairs, 2, rows), full),
            pltpu.VMEM((width, width) if depth % 16 else (8, 128), full),
            dma((2 * pieces,)), dma((2 * pieces,)),
            dma((tensor,)), dma((tensor,)),
            dma((tensor, chips)), dma((tensor, chips)),
            dma((tensor, chips)), dma((tensor, chips)),
            dma((12,)),
        ],
        compiler_params=pltpu.CompilerParams(
            collective_id=2, has_side_effects=True, vmem_limit_bytes=58 << 20
        ),
        name="front",
    )(tokens, gain.reshape(1, width), block, parents)


TN = (((0,), (0,)), ((), ()))
GROUP = 256


def dot_tn(a, b):
    return lax.dot_general(a, b, TN, preferred_element_type=jnp.float32)


def back_kernel(
    dp, tensor, depth,
    parent_ref, q_in, k_in, v_in, o_in, grad_in, seen_in, weight_in, lse_ref, small_ref,
    out_ref, sum_ref, total_ref,
    q_ref, k_ref, v_ref, o_ref, bg_ref, g_ref, stage_ref, seen_ref, weight_ref,
    delta_ref, dqt_ref, rows_ref, land_ref, gain_ref,
    slab_ref, pair_land, chip_land, line_out, line_land, part_ref, part_land,
    load_sem, pair_sem, stage_sem, row_send, row_recv,
    pair_send, pair_recv, chip_send, chip_recv,
    line_send, line_recv, small_send, small_recv, spread_send, spread_recv,
):
    spot, place = lax.axis_index("dp"), lax.axis_index("tensor")
    ways = dp * tensor
    me = spot * tensor + place
    scale = HEAD_DIM ** (-0.5)
    rows, width = q_ref.shape
    pairs = width // 128
    groups = width // GROUP
    blocks = rows // BRANCH
    pieces = rows // PIECE
    stage_rows = stage_ref.shape[1]

    def device(index):
        return (index // tensor, lax.rem(index, tensor))

    def along(step):
        return lax.rem(place + step, tensor)

    chips = dp // 2
    chip, core = spot // 2, lax.rem(spot, 2)

    def chip_at(step):
        return lax.rem(chip + step, chips)

    def block_at(b):
        return pl.ds(pl.multiple_of(b * BRANCH, BRANCH), BRANCH)

    barrier = pltpu.get_barrier_semaphore()

    @pl.loop(1, ways)
    def _(step):
        pl.semaphore_signal(
            barrier, inc=1, device_id=device(lax.rem(me + step, ways)), device_id_type=MESH
        )

    def lanes(pair):
        return pl.ds(pl.multiple_of(pair * 128, 128), 128)

    grad_load = pltpu.make_async_copy(grad_in, bg_ref, load_sem.at[0])
    weight_load = pltpu.make_async_copy(weight_in, weight_ref, load_sem.at[1])
    value_load = pltpu.make_async_copy(o_in, o_ref, load_sem.at[2])

    def pair_loads(pair):
        return [
            pltpu.make_async_copy(
                source.at[:, lanes(pair)], held.at[:, lanes(pair)], pair_sem.at[which, pair]
            )
            for which, (source, held) in enumerate(((q_in, q_ref), (k_in, k_ref), (v_in, v_ref)))
        ]

    def stage(part):
        slot = lax.rem(part, 2)
        at = pl.ds(pl.multiple_of(part * stage_rows, stage_rows), stage_rows)
        return pltpu.make_async_copy(seen_in.at[at], stage_ref.at[slot], stage_sem.at[slot])

    grad_load.start()
    weight_load.start()
    value_load.start()

    @pl.loop(0, pairs)
    def _(pair):
        for load in pair_loads(pair):
            load.start()

    grad_load.wait()
    weight_load.wait()
    value_load.wait()

    def keep(held, value, kind):
        cols = slice(kind * GROUP, (kind + 1) * GROUP)
        if depth % 16:
            for target in range(dp):
                held[target, 0:depth, cols] = value[target * depth : (target + 1) * depth].astype(
                    slab_ref.dtype
                )
        else:
            held[:, :, cols] = value.reshape(dp, depth, GROUP).astype(slab_ref.dtype)

    product = dot_tn(bg_ref[...], o_ref[...])
    for group in range(groups):
        keep(slab_ref.at[groups], product[:, group * GROUP : (group + 1) * GROUP], group)

    @pl.loop(0, blocks)
    def _(b):
        at = block_at(b)
        g_ref[at] = dot_nn(bg_ref[at], weight_ref[3]).astype(g_ref.dtype)

    pl.semaphore_wait(barrier, ways - 1)

    def halve(group, source):
        return pltpu.make_async_remote_copy(
            src_ref=slab_ref.at[group, source * 2 + 1 - core],
            dst_ref=pair_land.at[group, source],
            send_sem=pair_send.at[group, source], recv_sem=pair_recv.at[group, source],
            device_id=(chip * 2 + 1 - core, place), device_id_type=MESH,
        )

    def give(group, step):
        to = chip_at(step) * 2 + core
        return pltpu.make_async_remote_copy(
            src_ref=slab_ref.at[group, to], dst_ref=chip_land.at[group, chip],
            send_sem=chip_send.at[group, step], recv_sem=chip_recv.at[group, chip],
            device_id=(to, place), device_id_type=MESH,
        )

    def take(group, step):
        source = chip_at(chips - step)
        return pltpu.make_async_remote_copy(
            src_ref=slab_ref.at[group, source * 2 + core], dst_ref=chip_land.at[group, source],
            send_sem=chip_send.at[group, step], recv_sem=chip_recv.at[group, source],
            device_id=(chip_at(step) * 2 + core, place), device_id_type=MESH,
        )

    def share_slabs(group):
        @pl.loop(0, chips)
        def _(source):
            halve(group, source).start()

    def send_slabs(group):
        @pl.loop(0, chips)
        def _(step):
            to = chip_at(step)
            halve(group, to).wait_recv()
            mine = slab_ref[group, to * 2 + core].astype(jnp.float32)
            mine = mine + pair_land[group, to].astype(jnp.float32)
            slab_ref[group, to * 2 + core] = mine.astype(slab_ref.dtype)

            @pl.when(step > 0)
            def _():
                give(group, step).start()

    share_slabs(groups)

    @pl.loop(0, pairs)
    def _(pair):
        for load in pair_loads(pair):
            load.wait()
        product = g_ref[:, lanes(pair)].astype(jnp.float32)
        product = (product * o_ref[:, lanes(pair)].astype(jnp.float32)).T
        for head in range(2):
            delta_ref[pair, head : head + 1, :] = jnp.sum(
                product[head * HEAD_DIM : (head + 1) * HEAD_DIM], axis=0, keepdims=True
            )
        dqt_ref[pair] = jnp.zeros(dqt_ref.shape[1:], dqt_ref.dtype)

    def sweep(pair, tiles):
        work = [(tile, head) for tile in range(len(tiles)) for head in range(2)]
        sums = [[None, None] for _ in tiles]
        keys, flipped = {}, {}

        def key_block(tile):
            row = tiles[tile][0]
            if id(row) not in keys:
                kb = k_ref[pl.ds(row, BRANCH), lanes(pair)]
                vb = v_ref[pl.ds(row, BRANCH), lanes(pair)]
                masked = []
                for head in range(2):
                    mine = head_lanes(kb.shape, 1, head)
                    masked.append(
                        (
                            jnp.where(mine, kb, jnp.zeros_like(kb)),
                            jnp.where(mine, vb, jnp.zeros_like(vb)),
                        )
                    )
                keys[id(row)] = masked
                flipped[id(row)] = kb.T
            return keys[id(row)], flipped[id(row)]

        def start(tile, head):
            at = pl.ds(tiles[tile][1], BRANCH)
            kb, vb = key_block(tile)[0][head]
            return dot_nt(kb, q_ref[at, lanes(pair)]), dot_nt(vb, g_ref[at, lanes(pair)])

        def middle(tile, head, scores, prob_grad):
            at = pl.ds(tiles[tile][1], BRANCH)
            probs = jnp.exp2(scores * EXP_SCALE - lse_ref[pair, head : head + 1, at])
            if tiles[tile][2] is not None:
                probs = tiles[tile][2](probs)
            score_grad = probs * (prob_grad - delta_ref[pair, head : head + 1, at])
            return probs.astype(jnp.bfloat16), score_grad.astype(jnp.bfloat16)

        def finish(tile, head, probs, score_grad):
            at = pl.ds(tiles[tile][1], BRANCH)
            parts = (
                dot_nn(score_grad, q_ref[at, lanes(pair)]),
                dot_nn(probs, g_ref[at, lanes(pair)]),
            )
            for which in range(2):
                held = sums[tile][which]
                if head == 0:
                    sums[tile][which] = parts[which]
                else:
                    first = head_lanes(held.shape, 1, 0)
                    sums[tile][which] = jnp.where(first, held, parts[which])
            mine = slice(head * HEAD_DIM, (head + 1) * HEAD_DIM)
            dqt_ref[pair, mine, at] += dot_nn(key_block(tile)[1][mine], score_grad)

        ready = start(*work[0])
        held = None
        for at, item in enumerate(work):
            now = ready
            if at + 1 < len(work):
                ready = start(*work[at + 1])
            done = middle(*item, *now)
            if held is not None:
                finish(*held)
            held = (*item, *done)
        finish(*held)
        return sums

    def causal(key_row, query_row):
        def mask_of(probs):
            keys = lax.broadcasted_iota(jnp.int32, probs.shape, 0) + key_row
            at = lax.broadcasted_iota(jnp.int32, probs.shape, 1) + query_row
            return jnp.where(keys <= at, probs, 0.0)

        return mask_of

    def put(pair, row, dk, dv):
        at = pl.ds(row, BRANCH)
        k_ref[at, lanes(pair)] = (dk * scale).astype(k_ref.dtype)
        v_ref[at, lanes(pair)] = dv.astype(v_ref.dtype)

    def pass_down(piece):
        at = pl.ds(pl.multiple_of(piece * PIECE, PIECE), PIECE)
        return pltpu.make_async_remote_copy(
            src_ref=rows_ref.at[at], dst_ref=land_ref.at[at],
            send_sem=row_send.at[piece], recv_sem=row_recv.at[piece],
            device_id=(spot, lax.rem(place + tensor - 1, tensor)), device_id_type=MESH,
        )

    def row_grad(b):
        at = block_at(b)
        return dot_nt(k_ref[at], weight_ref[1]) + dot_nt(v_ref[at], weight_ref[2])

    def hand_down(b, total):
        rows_ref[block_at(b)] = total.astype(rows_ref.dtype)

        @pl.when(place == tensor - 1)
        def _():
            for piece in range(BRANCH // PIECE):
                pass_down(b * (BRANCH // PIECE) + piece).start()

    def joined(piece):
        at = pl.ds(pl.multiple_of(piece * PIECE, PIECE), PIECE)
        return rows_ref[at].astype(jnp.float32) + land_ref[at].astype(jnp.float32)

    middle_place = (place > 0) & (place < tensor - 1)
    late = 3 * jnp.maximum(tensor - 2 - place, 0)
    first_relay = jnp.where(place > 1, 0, pieces)
    last_relay = jnp.where(middle_place, 2 * pieces, first_relay)

    def piece_of(order):
        return lax.rem(order + pieces, 2 * pieces)

    def serve(first, last):
        def one(order, carry):
            piece = piece_of(order)
            pass_down(piece).wait_recv()
            at = pl.ds(pl.multiple_of(piece * PIECE, PIECE), PIECE)
            rows_ref[at] = joined(piece).astype(rows_ref.dtype)
            pass_down(piece).start()
            return carry

        low = jnp.clip(first - late, first_relay, last_relay)
        lax.fori_loop(low, jnp.clip(last - late, low, last_relay), one, 0)

    @pl.loop(0, pairs)
    def _(pair):
        @pl.when(place == 0)
        def _():
            for ref in (k_ref, v_ref):
                ref[rows : 3 * rows, lanes(pair)] = jnp.zeros((2 * rows, 128), ref.dtype)

        @pl.when(place > 0)
        def _():
            def seen_parent(probs):
                return jnp.where(place > 1, probs, 0.0)

            spots = range(0, rows, BRANCH)
            sums = sweep(pair, [(rows + at, at, seen_parent) for at in spots])
            for at, part in zip(spots, sums):
                put(pair, rows + at, *part)

    send_slabs(groups)

    @pl.loop(0, blocks)
    def _(leaf):
        out_ref[block_at(leaf)] = row_grad(blocks + leaf)

    for branch in range(blocks):
        total = None
        for leaf in range(blocks):
            at = leaf * blocks + branch
            part = out_ref[leaf * BRANCH : (leaf + 1) * BRANCH] * parent_ref[at : at + 1]
            total = part if total is None else total + part
        hand_down(blocks + branch, total)

    stage(0).start()

    @pl.loop(0, blocks)
    def _(b):
        row = pl.multiple_of(b * BRANCH, BRANCH)

        @pl.loop(0, pairs)
        def _(pair):
            def finish_block(masked):
                tiles = [
                    (row, first, causal(row, first) if masked else None)
                    for first in range(0, rows, BRANCH)
                ]
                sums = sweep(pair, tiles)
                put(pair, row, sum(part[0] for part in sums), sum(part[1] for part in sums))

            @pl.when(place == 0)
            def _():
                finish_block(True)

            @pl.when(place > 0)
            def _():
                finish_block(False)

            slot = b * pairs + pair
            serve(slot - 1, slot)

        for _half in range(2):
            part = b * 2 + _half

            @pl.when(part < 3 * rows // stage_rows)
            def _():
                stage(part).wait()

                @pl.when(part + 1 < 3 * rows // stage_rows)
                def _():
                    stage(part + 1).start()

                at = pl.ds(pl.multiple_of(part * stage_rows, stage_rows), stage_rows)
                seen_ref[:, at] = stage_ref[lax.rem(part, 2)].T

        hand_down(b, row_grad(b))

    served = blocks * pairs - 1

    gain_ref[...] = jnp.zeros_like(gain_ref)

    @pl.loop(0, groups)
    def _(group):
        base = served + group * 4

        @pl.loop(0, 2)
        def _(half):
            pair = group * 2 + half

            @pl.when(place > 0)
            def _():
                spots = range(0, rows, BRANCH)
                sums = sweep(pair, [(2 * rows + at, at, causal(0, 0)) for at in spots])
                for at, part in zip(spots, sums):
                    put(pair, 2 * rows + at, *part)

            q_ref[:, lanes(pair)] = (dqt_ref[pair] * scale).T.astype(q_ref.dtype)
            serve(base + half, base + half + 1)

        cols = pl.ds(pl.multiple_of(group * GROUP, GROUP), GROUP)
        for kind, value in (
            (0, lambda: dot_nn(seen_ref[:, 2 * rows : 3 * rows], q_ref[:, cols])),
            (1, lambda: dot_nn(seen_ref[...], k_ref[:, cols])),
            (2, lambda: dot_nn(seen_ref[...], v_ref[:, cols])),
        ):
            product = value()
            scaled = product * weight_ref[kind, :, cols].astype(jnp.float32)
            gain_ref[...] += scaled[:, 0:128] + scaled[:, 128:256]
            keep(slab_ref.at[group], product, kind)
            if kind:
                serve(base + 1 + kind, base + 2 + kind)

        share_slabs(group)

        @pl.when(group > 0)
        def _():
            send_slabs(group - 1)

    served += groups * 4

    part_ref[...] = small_ref[...]
    gains = jnp.sum(gain_ref[...].T, axis=0, keepdims=True)
    for row in range(width // 128):
        part_ref[0, row : row + 1, :] = gains[:, row * 128 : (row + 1) * 128]

    def scatter(step):
        to = lax.rem(me + step, ways)
        return pltpu.make_async_remote_copy(
            src_ref=part_ref.at[to], dst_ref=part_land.at[me],
            send_sem=small_send.at[step], recv_sem=small_recv.at[me],
            device_id=device(to), device_id_type=MESH,
        )

    def arrival(step):
        source = lax.rem(me - step + ways, ways)
        return pltpu.make_async_remote_copy(
            src_ref=part_ref.at[source], dst_ref=part_land.at[source],
            send_sem=small_send.at[step], recv_sem=small_recv.at[source],
            device_id=device(lax.rem(me + step, ways)), device_id_type=MESH,
        )

    def spread(step):
        return pltpu.make_async_remote_copy(
            src_ref=total_ref.at[me], dst_ref=total_ref.at[me],
            send_sem=spread_send.at[step], recv_sem=spread_recv.at[me],
            device_id=device(lax.rem(me + step, ways)), device_id_type=MESH,
        )

    def landing(step):
        source = lax.rem(me - step + ways, ways)
        return pltpu.make_async_remote_copy(
            src_ref=total_ref.at[source], dst_ref=total_ref.at[source],
            send_sem=spread_send.at[step], recv_sem=spread_recv.at[source],
            device_id=device(lax.rem(me + step, ways)), device_id_type=MESH,
        )

    @pl.loop(1, ways)
    def _(step):
        scatter(step).start()

    send_slabs(groups - 1)

    @pl.loop(0, blocks)
    def _(b):
        at = block_at(b)
        out_ref[at] = row_grad(2 * blocks + b) + dot_nt(q_ref[at], weight_ref[0])
        serve(served + 2 * b, served + 2 * b + 2)

    served += 2 * blocks

    def add(step, total):
        arrival(step).wait_recv()
        return total + part_land[lax.rem(me - step + ways, ways)]

    total_ref[me] = lax.fori_loop(1, ways, add, part_ref[me])

    @pl.loop(1, ways)
    def _(step):
        spread(step).start()

    serve(served, jnp.maximum(served, 2 * pieces) + late)

    kinds = [[], [], [], []]
    for group in range(groups + 1):

        def add_slab(step, total):
            take(group, step).wait_recv()
            return total + chip_land[group, chip_at(chips - step)].astype(jnp.float32)

        total = lax.fori_loop(1, chips, add_slab, slab_ref[group, spot].astype(jnp.float32))
        for part in range(total.shape[1] // GROUP):
            kinds[3 if group == groups else part].append(
                total[:, part * GROUP : (part + 1) * GROUP]
            )

    share = width // tensor
    kinds = [jnp.concatenate(parts, axis=1) for parts in kinds]
    for target in range(tensor):
        mine = jnp.concatenate(
            [kind[:, target * share : (target + 1) * share] for kind in kinds], axis=1
        )
        line_out[target] = mine.astype(line_out.dtype)

        @pl.when(place == target)
        def _():
            sum_ref[...] = mine

    def line(step):
        return pltpu.make_async_remote_copy(
            src_ref=line_out.at[along(step)], dst_ref=line_land.at[place],
            send_sem=line_send.at[step], recv_sem=line_recv.at[place],
            device_id=(spot, along(step)), device_id_type=MESH,
        )

    def line_in(step):
        source = along(tensor - step)
        return pltpu.make_async_remote_copy(
            src_ref=line_out.at[source], dst_ref=line_land.at[source],
            send_sem=line_send.at[step], recv_sem=line_recv.at[source],
            device_id=(spot, along(step)), device_id_type=MESH,
        )

    for step in range(1, tensor):
        line(step).start()

    @pl.when(place < 2)
    def _():
        @pl.loop(0, pieces)
        def _(piece):
            source = place * pieces + piece
            pass_down(source).wait_recv()
            at = pl.ds(pl.multiple_of(piece * PIECE, PIECE), PIECE)
            out_ref[at] += joined(source)

    for step in range(1, tensor):
        line_in(step).wait_recv()
        sum_ref[...] += line_land[along(tensor - step)].astype(jnp.float32)

    @pl.loop(1, ways)
    def _(step):
        landing(step).wait_recv()

    for step in range(1, tensor):
        line(step).wait_send()

    @pl.loop(1, ways)
    def _(step):
        scatter(step).wait_send()
        spread(step).wait_send()

    for group in range(groups + 1):

        @pl.loop(0, chips)
        def _(step):
            halve(group, step).wait_send()

            @pl.when(step > 0)
            def _():
                give(group, step).wait_send()

    sent = jnp.where(place == tensor - 1, 2 * pieces, last_relay)
    first_sent = jnp.where(place == tensor - 1, 0, first_relay)

    def sent_one(order, carry):
        pass_down(piece_of(order)).wait_send()
        return carry

    lax.fori_loop(first_sent, sent, sent_one, 0)


def backward(parents, q, k, v, o, branch_grad, seen, weights, lse, small):
    dp, tensor = lax.axis_size("dp"), lax.axis_size("tensor")
    ways = dp * tensor
    rows, width = q.shape
    seen_rows = k.shape[0]
    depth = width // dp
    padded = -(-depth // 16) * 16
    pairs, groups, pieces = width // 128, width // GROUP, rows // PIECE
    slab = (padded, width)
    low, full = jnp.bfloat16, jnp.float32
    dma = pltpu.SemaphoreType.DMA
    anywhere = pl.BlockSpec(memory_space=pl.ANY)
    here = pl.BlockSpec(memory_space=pltpu.VMEM)
    out, block, total = pl.pallas_call(
        lambda *refs: back_kernel(dp, tensor, depth, *refs),
        out_shape=(
            jax.ShapeDtypeStruct((rows, width), full),
            jax.ShapeDtypeStruct((padded, width), full),
            jax.ShapeDtypeStruct(small.shape, full),
        ),
        in_specs=[here] + [anywhere] * 7 + [here] * 2,
        out_specs=[here, here, here],
        scratch_shapes=[
            pltpu.VMEM((rows, width), low),
            pltpu.VMEM((seen_rows, width), low),
            pltpu.VMEM((seen_rows, width), low),
            pltpu.VMEM((rows, width), low),
            pltpu.VMEM((rows, width), low),
            pltpu.VMEM((rows, width), low),
            pltpu.VMEM((2, rows // 2, width), low),
            pltpu.VMEM((width, seen_rows), low),
            pltpu.VMEM(weights.shape, low),
            pltpu.VMEM((pairs, 2, rows), full),
            pltpu.VMEM((pairs, 128, rows), full),
            pltpu.VMEM((2 * rows, width), low),
            pltpu.VMEM((2 * rows, width), low),
            pltpu.VMEM((width, 128), full),
            pltpu.VMEM((groups + 1, dp) + slab, low),
            pltpu.VMEM((groups + 1, dp // 2) + slab, low),
            pltpu.VMEM((groups + 1, dp // 2) + slab, low),
            pltpu.VMEM((tensor, padded, width), low),
            pltpu.VMEM((tensor, padded, width), low),
            pltpu.VMEM(small.shape, full),
            pltpu.VMEM(small.shape, full),
            dma((3,)), dma((3, pairs)), dma((2,)),
            dma((2 * pieces,)), dma((2 * pieces,)),
            dma((groups + 1, dp // 2)), dma((groups + 1, dp // 2)),
            dma((groups + 1, dp // 2)), dma((groups + 1, dp // 2)),
            dma((tensor,)), dma((tensor,)),
            dma((ways,)), dma((ways,)), dma((ways,)), dma((ways,)),
        ],
        compiler_params=pltpu.CompilerParams(
            collective_id=3, has_side_effects=True, vmem_limit_bytes=62 << 20
        ),
        name="attend_backward",
    )(parents, q, k, v, o, branch_grad, seen, weights, lse, small)
    return out, block[:depth], total


HALF_ROOT = math.sqrt(0.5)
PDF_SCALE = 1.0 / math.sqrt(2.0 * math.pi)
CHUNK = 512
BAND = 256
NEAR = 640


def expert_kernel(
    dp, tensor, x_in, g_in, w_in, w_out, result_ref, back_ref, in_grad_ref, out_grad_ref,
    x_ref, g_ref, active_ref, slope_ref, keep_ref, part_ref, land_ref, home_ref,
    back_part, back_land, back_home, grad_ref, grad_land,
    x_send, x_recv, x_pair_send, x_pair_recv, g_send, g_recv, g_pair_send, g_pair_recv,
    y_pair_send, y_pair_recv, y_send, y_recv, d_pair_send, d_pair_recv, d_send, d_recv,
    line_send, line_recv,
):
    spot, place = lax.axis_index("dp"), lax.axis_index("tensor")
    chips = dp // 2
    chip, core = spot // 2, lax.rem(spot, 2)
    partner = (chip * 2 + 1 - core, place)
    capacity = x_in.shape[0] // chips

    def ahead(step):
        return (lax.rem(chip + step, chips) * 2 + core, place)

    def behind(step):
        return (lax.rem(chip - step + chips, chips) * 2 + core, place)

    def at(side, step):
        return pl.ds(pl.multiple_of((side * chips + step) * capacity, capacity), capacity)

    def along(step):
        return lax.rem(place + step, tensor)

    greet(
        [ahead(step) for step in range(1, chips)]
        + [partner]
        + [(spot, along(step)) for step in range(1, tensor)]
    )
    share, near = out_grad_ref.shape
    width = x_in.shape[1]

    def line(step):
        return pltpu.make_async_remote_copy(
            src_ref=grad_ref.at[along(step)], dst_ref=grad_land.at[place],
            send_sem=line_send.at[step], recv_sem=line_recv.at[place],
            device_id=(spot, along(step)), device_id_type=MESH,
        )

    def line_in(step):
        source = along(tensor - step)
        return pltpu.make_async_remote_copy(
            src_ref=grad_ref.at[source], dst_ref=grad_land.at[source],
            send_sem=line_send.at[step], recv_sem=line_recv.at[source],
            device_id=(spot, along(step)), device_id_type=MESH,
        )

    def copy(source, target, send, recv, step, where):
        return pltpu.make_async_remote_copy(
            src_ref=source, dst_ref=target, send_sem=send.at[step], recv_sem=recv.at[step],
            device_id=where, device_id_type=MESH,
        )

    def go_x(step):
        return copy(x_in.at[at(0, step)], x_ref.at[at(0, step)], x_send, x_recv, step, ahead(step))

    def go_g(step):
        return copy(g_in.at[at(0, step)], g_ref.at[at(0, step)], g_send, g_recv, step, ahead(step))

    def pair_x(step):
        return copy(
            x_ref.at[at(0, step)], x_ref.at[at(1, step)], x_pair_send, x_pair_recv, step, partner
        )

    def pair_g(step):
        return copy(
            g_ref.at[at(0, step)], g_ref.at[at(1, step)], g_pair_send, g_pair_recv, step, partner
        )

    def pair_y(step):
        here = at(0, step)
        return copy(part_ref.at[here], land_ref.at[here], y_pair_send, y_pair_recv, step, partner)

    def pair_d(step):
        here = at(0, step)
        return copy(back_part.at[here], back_land.at[here], d_pair_send, d_pair_recv, step, partner)

    def home_y(step):
        here = at(0, step)
        return copy(home_ref.at[here], result_ref.at[here], y_send, y_recv, step, behind(step))

    def home_d(step):
        here = at(0, step)
        return copy(back_home.at[here], back_ref.at[here], d_send, d_recv, step, behind(step))

    @pl.loop(1, chips)
    def _(step):
        go_x(step).start()

    x_ref[at(0, 0)] = x_in[at(0, 0)]
    pair_x(0).start()
    g_ref[at(0, 0)] = g_in[at(0, 0)]

    def ahead_pass(side, step):
        rows = x_ref[at(side, step)]
        total = None
        for first in range(0, w_in.shape[1], CHUNK):
            cols = slice(first, first + CHUNK)
            up = dot_nn(rows, w_in[:, cols])
            below = 0.5 * (1.0 + lax.erf(up * HALF_ROOT))
            active = (up * below).astype(jnp.bfloat16)
            slope = below + up * (jnp.exp(-0.5 * up * up) * PDF_SCALE)
            active_ref[at(side, step), cols] = active
            slope_ref[at(side, step), cols] = slope.astype(jnp.bfloat16)
            part = dot_nn(active, w_out[cols])
            total = part if total is None else total + part
        return total

    def back_pass(side, step):
        grads = g_ref[at(side, step)]
        total = None
        for first in range(0, w_in.shape[1], CHUNK):
            cols = slice(first, first + CHUNK)
            active_grad = dot_nt(grads, w_out[cols])
            up_grad = active_grad * slope_ref[at(side, step), cols].astype(jnp.float32)
            up_grad = up_grad.astype(jnp.bfloat16)
            slope_ref[at(side, step), cols] = up_grad
            part = dot_nt(up_grad, w_in[:, cols])
            total = part if total is None else total + part
        return total

    keep_ref[at(0, 0)] = ahead_pass(0, 0)

    @pl.loop(1, chips)
    def _(step):
        go_x(step).wait_recv()
        pair_x(step).start()
        go_g(step).start()
        keep_ref[at(0, step)] = ahead_pass(0, step)

    pair_g(0).start()

    @pl.loop(0, chips)
    def _(step):
        pair_x(step).wait_recv()
        part_ref[at(0, step)] = ahead_pass(1, step).astype(part_ref.dtype)
        pair_y(step).start()

    @pl.loop(1, chips)
    def _(step):
        go_g(step).wait_recv()
        pair_g(step).start()

    @pl.loop(0, chips)
    def _(step):
        pair_y(step).wait_recv()
        here = at(0, step)
        total = keep_ref[here] + land_ref[here].astype(jnp.float32)
        home_ref[here] = total.astype(home_ref.dtype)

        @pl.when(step > 0)
        def _():
            home_y(step).start()

        @pl.when(step == 0)
        def _():
            result_ref[here] = total.astype(result_ref.dtype)

    @pl.loop(0, chips)
    def _(step):
        pair_g(step).wait_recv()

    @pl.loop(1, tensor + 1)
    def _(turn):
        step = lax.rem(turn, tensor)
        part = along(step)
        for first in range(0, share, 128):
            cols = pl.ds(pl.multiple_of(part * share + first, 128), 128)
            product = dot_tn(active_ref[:, cols], g_ref[...]).astype(grad_ref.dtype)
            grad_ref[part, first : first + 128] = product[:, :near]
            in_grad_ref[cols, width:] = product[:, near:]

        @pl.when(step > 0)
        def _():
            line(step).start()

    @pl.loop(0, chips)
    def _(step):
        back_part[at(0, step)] = back_pass(1, step).astype(back_part.dtype)
        pair_d(step).start()

    @pl.loop(0, chips)
    def _(turn):
        step = chips - 1 - turn
        here = at(0, step)
        total = back_pass(0, step)
        pair_d(step).wait_recv()
        total = (total + back_land[here].astype(jnp.float32)).astype(back_home.dtype)
        back_home[here] = total

        @pl.when(step > 0)
        def _():
            home_d(step).start()

        @pl.when(step == 0)
        def _():
            back_ref[here] = total

    @pl.loop(0, w_in.shape[1] // BAND)
    def _(band):
        cols = pl.ds(pl.multiple_of(band * BAND, BAND), BAND)
        product = dot_tn(slope_ref[:, cols], x_ref[...])
        in_grad_ref[cols, 0:width] = product.astype(in_grad_ref.dtype)

    out_grad_ref[...] = grad_ref[place].astype(jnp.float32)
    for step in range(1, tensor):
        line_in(step).wait_recv()
        out_grad_ref[...] += grad_land[along(tensor - step)].astype(jnp.float32)
    for step in range(1, tensor):
        line(step).wait_send()

    @pl.loop(1, chips)
    def _(step):
        home_y(step).wait_recv()
        home_d(step).wait_recv()

    @pl.loop(0, chips)
    def _(step):
        pair_x(step).wait_send()
        pair_g(step).wait_send()
        pair_y(step).wait_send()
        pair_d(step).wait_send()

    @pl.loop(1, chips)
    def _(step):
        go_x(step).wait_send()
        go_g(step).wait_send()
        home_y(step).wait_send()
        home_d(step).wait_send()


def run_experts(slot_rows, slot_grads, w_in, w_out):
    dp, tensor = lax.axis_size("dp"), lax.axis_size("tensor")
    rows, width = slot_rows.shape
    hidden = w_in.shape[1]
    low = jnp.bfloat16
    here = pl.BlockSpec(memory_space=pltpu.VMEM)
    near = pltpu.VMEM((rows, width), low)
    both = pltpu.VMEM((2 * rows, width), low)
    middle = pltpu.VMEM((2 * rows, hidden), low)
    return pl.pallas_call(
        lambda *refs: expert_kernel(dp, tensor, *refs),
        out_shape=(
            jax.ShapeDtypeStruct((rows, width), low),
            jax.ShapeDtypeStruct((rows, width), low),
            jax.ShapeDtypeStruct((hidden, 2 * width - NEAR), low),
            jax.ShapeDtypeStruct((hidden // tensor, NEAR), jnp.float32),
        ),
        in_specs=[here] * 4,
        out_specs=[here] * 4,
        scratch_shapes=[
            both, both, middle, middle, pltpu.VMEM((rows, width), jnp.float32),
            near, near, near, near, near, near,
            pltpu.VMEM((tensor, hidden // tensor, NEAR), low),
            pltpu.VMEM((tensor, hidden // tensor, NEAR), low),
        ]
        + [pltpu.SemaphoreType.DMA((dp // 2,))] * 16
        + [pltpu.SemaphoreType.DMA((tensor,))] * 2,
        compiler_params=pltpu.CompilerParams(
            collective_id=4, has_side_effects=True, vmem_limit_bytes=60 << 20
        ),
        name="run_experts",
    )(slot_rows, slot_grads, w_in, w_out)


norm_eps = 1e-05
route_scale = 3.0
masked_score = -1e30
highest = lax.Precision.HIGHEST


def layer_norm(values, norm_gain):
    centred = values - jnp.mean(values, axis=-1, keepdims=True)
    spread = jnp.mean(centred * centred, axis=-1, keepdims=True)
    return centred * lax.rsqrt(spread + norm_eps) * norm_gain


def unit_rows(values):
    return values * lax.rsqrt(jnp.sum(values * values, axis=-1, keepdims=True) + 1.0)


def router_gate(normed, router_proj, expert_embed, picked):
    routed = jnp.dot(normed, router_proj, precision=highest)
    logits = route_scale * jnp.dot(unit_rows(routed), unit_rows(expert_embed).T, precision=highest)
    return jnp.sum(jax.nn.softmax(logits, axis=-1) * picked, axis=-1)


def gelu_exact(values):
    return jax.nn.gelu(values, approximate=False)


def slot_table(route_ids, order_ids, capacity):
    same_expert = route_ids[:, None] == route_ids[None, :]
    earlier = order_ids[None, :] < order_ids[:, None]
    ranking = jnp.sum(jnp.where(same_expert & earlier, 1, 0), axis=1).astype(jnp.int32)
    kept_mask = ranking < capacity
    column = route_ids * capacity + jnp.minimum(ranking, capacity - 1)
    return (column, kept_mask)


def low_dot(rows, weight):
    return jnp.dot(rows, weight, preferred_element_type=jnp.float32).astype(jnp.bfloat16)


def shards(
    tokens,
    norm1_gain,
    qkv_weight,
    attn_proj,
    norm2_gain,
    router_proj,
    expert_embed,
    expert_in,
    expert_out,
    routes,
    orders,
    leaf_parent,
    cotangent,
):
    rows_here = tokens.shape[0]
    model_width = tokens.shape[1]
    experts = expert_embed.shape[0]
    capacity = rows_here // experts
    dp_size, tensor_size = lax.axis_size("dp"), lax.axis_size("tensor")

    hidden = tokens.astype(jnp.float32)
    norm1_back = jax.vjp(layer_norm, hidden, norm1_gain)[1]
    flat_qkv = qkv_weight.reshape(qkv_weight.shape[0], -1)
    place = lax.axis_index("tensor")
    leaf_blocks = rows_here // BRANCH
    first_leaf = jnp.maximum(place - 2, 0) * leaf_blocks
    leaf_parents = lax.dynamic_slice_in_dim(leaf_parent[0], first_leaf, leaf_blocks, 0) - 1
    parents = (leaf_parents[:, None] == jnp.arange(leaf_blocks)[None, :]).astype(jnp.float32)
    parents = jnp.broadcast_to(parents.reshape(-1, 1), (leaf_blocks * leaf_blocks, model_width))
    seen_in, weights, query_rows, key_rows, value_rows, attended, log_totals = front(
        tokens, norm1_gain, jnp.concatenate([flat_qkv, attn_proj.T], axis=1), parents
    )
    proj_back = weights[3]
    branch_out = jnp.einsum(
        "sc,dc->sd", attended, proj_back, preferred_element_type=jnp.float32
    )
    mid_stream = hidden + branch_out
    normed_mid, norm2_back = jax.vjp(layer_norm, mid_stream, norm2_gain)
    moe_in = normed_mid.astype(jnp.bfloat16)
    route_ids = routes[:, 0]
    near_route = (route_ids - lax.axis_index("dp") // 2) % experts
    column, kept_mask = slot_table(near_route, orders[0], capacity)
    picked = (route_ids[:, None] == jnp.arange(experts)[None, :]).astype(jnp.float32)
    gate_value, gate_back = jax.vjp(
        lambda normed_rows, route_proj, embed_rows: router_gate(
            normed_rows, route_proj, embed_rows, picked
        ),
        moe_in.astype(jnp.float32),
        router_proj,
        expert_embed,
    )
    select = (
        (column[:, None] == jnp.arange(experts * capacity)[None, :]) & kept_mask[:, None]
    ).astype(jnp.bfloat16)
    def to_slots(token_rows):
        return jnp.einsum(
            "ts,td->sd", select, token_rows, preferred_element_type=jnp.float32
        ).astype(jnp.bfloat16)

    def from_slots(slot_rows):
        return jnp.dot(select, slot_rows, preferred_element_type=jnp.float32)

    upstream = cotangent.astype(jnp.float32)
    slot_grads = to_slots((gate_value[:, None] * upstream).astype(jnp.bfloat16))
    result_rows, grad_rows, far_grads, near_grads = run_experts(
        to_slots(moe_in), slot_grads, expert_in, expert_out
    )
    expert_result = from_slots(result_rows)
    output = (mid_stream + gate_value[:, None] * expert_result).astype(jnp.bfloat16)
    moe_grad = from_slots(grad_rows)
    gate_grad = jnp.sum(upstream * expert_result, axis=-1)
    router_part, proj_grad, embed_grad = gate_back(gate_grad)
    mid_part, gain2_grad = norm2_back(moe_grad + router_part)
    mid_grad = upstream + mid_part
    far_grads = lax.psum_scatter(
        far_grads, "tensor", scatter_dimension=0, tiled=True
    ).astype(jnp.float32)
    expert_in_grad = far_grads[:, :model_width].T
    expert_out_grad = jnp.concatenate([near_grads, far_grads[:, model_width:]], axis=1)
    branch_grad = mid_grad.astype(jnp.bfloat16)
    later = [gain2_grad, proj_grad, embed_grad]
    flat = jnp.concatenate([jnp.zeros_like(norm1_gain)] + [part.reshape(-1) for part in later])
    ways = dp_size * tensor_size
    lanes = -(-flat.shape[0] // (ways * 8 * 128)) * 128
    small = jnp.pad(flat, (0, ways * 8 * lanes - flat.shape[0])).reshape(ways, 8, lanes)
    input_grad, grad_block, totals = backward(
        parents, query_rows, key_rows, value_rows, attended, branch_grad, seen_in, weights,
        log_totals, small,
    )
    qkv_grad = grad_block[:, : flat_qkv.shape[1]].reshape(qkv_weight.shape)
    attn_proj_grad = grad_block[:, flat_qkv.shape[1] :].T
    totals = totals.reshape(-1)
    gain1_sum = totals[:model_width] / norm1_gain
    gain2_sum, router_sum, embed_sum = (
        totals[first : first + part.size].reshape(part.shape)
        for first, part in zip(
            (model_width, 2 * model_width, 2 * model_width + proj_grad.size), later
        )
    )
    token_part, _ = norm1_back(input_grad)
    token_grad = mid_grad + token_part
    return (
        output,
        token_grad,
        gain1_sum,
        qkv_grad,
        attn_proj_grad,
        gain2_sum,
        router_sum,
        embed_sum,
        expert_in_grad,
        expert_out_grad,
    )


def solution(mesh):
    in_specs = (
        P(("dp", "tensor"), None),
        P(),
        P("dp", None, "tensor"),
        P("tensor", "dp"),
        P(),
        P(),
        P(),
        P(None, "dp"),
        P("dp", None),
        P(("dp", "tensor"), None),
        P(("dp", "tensor"), None),
        P("dp", None),
        P(("dp", "tensor"), None),
    )
    out_specs = (
        P(("dp", "tensor"), None),
        P(("dp", "tensor"), None),
        P(),
        P("dp", None, "tensor"),
        P("tensor", "dp"),
        P(),
        P(),
        P(),
        P(None, ("dp", "tensor")),
        P(("dp", "tensor"), None),
    )
    return jax.shard_map(shards, mesh=mesh, in_specs=in_specs, out_specs=out_specs, check_vma=False)
```
